32 devices in a mesh: fsdp: 8 (over z, y), tp: 4 (over x, core).
Axes of the slice: x: 2, y: 2, z: 4, core: 2. Of those that a mesh axis runs over, the one named last changes fastest.
Arguments:
- tokens: bfloat16 [2, 2048, 1024], P(None, 'fsdp'), may hold values from -6 to 6
- cotangent: bfloat16 [2, 2048, 1024], P(None, 'fsdp'), may hold values from -6 to 6
- perm: int32 [2, 2048], replicated, may hold values from 0 to 2047, as said below
- lengths: int32 [2, 8], replicated, may hold values from 1 to 1024, 2048 in all within a row
- w_qkv: bfloat16 [1024, 3, 1024], P('fsdp', None, 'tp'), may hold values from -0.1875 to 0.1875
- w_attn_out: bfloat16 [1024, 1024], P('fsdp', 'tp'), may hold values from -6 to 6
- w_in: bfloat16 [1024, 2, 2624], P('fsdp', None, 'tp'), may hold values from -0.1875 to 0.1875
- w_down: bfloat16 [1024, 2624], P('fsdp', 'tp'), may hold values from -0.125 to 0.125
- gain_one: bfloat16 [1024], P('fsdp'), may hold values from 0.099609375 to 1.8984375
- gain_two: bfloat16 [1024], P('fsdp'), may hold values from 0.099609375 to 1.8984375
Outputs:
- output: bfloat16 [2, 2048, 1024], P(None, 'fsdp')
- input_grad: bfloat16 [2, 2048, 1024], P(None, 'fsdp')
- grad_qkv: float32 [1024, 3, 1024], P('fsdp', None, 'tp')
- grad_attn_out: float32 [1024, 1024], P('fsdp', 'tp')
- grad_in: float32 [1024, 2, 2624], P('fsdp', None, 'tp')
- grad_down: float32 [1024, 2624], P('fsdp', 'tp')
- grad_gain_one: float32 [1024], P('fsdp')
- grad_gain_two: float32 [1024], P('fsdp')
The draws below stay inside these ranges and needn't reach their ends.
Inputs may be any that keep to these rules, and one draw needn't show every extreme that they name: perm[m, d * 256 + j] is the initial token of micro-batch m taken at slot j of fsdp index d; each row is a permutation, and fsdp index d takes exactly 32 tokens from each index's block of 256 initial tokens. lengths[m] sum to 2048; the longest is exactly 1024.
All inputs are finite; a program needn't handle non-finite values.
Results may differ from the reference program's by a relative error of at most 0.025.
Values may be sent and summed in bfloat16 or wider, within the bound.
No kernel may reach another device: no remote copies, remote signals or barrier semaphores. Data moves between devices by JAX's collectives and lax.ppermute only.
A program may use at most 192 MiB of HBM per device.

```python
import math
import jax
import jax.numpy as jnp
import numpy as np
from jax import lax

D = 1024
H = 16
HD = 64
FF = 2624
MB = 2
NSEQ = 8
TOK_MB = 256
TOKENS = 2048
MOST = 1024


def draw_perm(key, part):
    groups = TOKENS // TOK_MB
    per_pair = TOK_MB // groups
    rows = []
    for micro_idx in range(MB):
        first_key, second_key = jax.random.split(jax.random.fold_in(key, micro_idx + 11))
        src_keys = jax.random.split(first_key, groups)
        local = jax.vmap(lambda one_key: jax.random.permutation(one_key, TOK_MB))(src_keys)
        anchor = local + (jnp.arange(groups, dtype=jnp.int32) * TOK_MB)[:, None]
        blocks = anchor.reshape(groups, groups, per_pair)
        per_dest = jnp.transpose(blocks, (1, 0, 2)).reshape(groups, TOK_MB)
        dest_keys = jax.random.split(second_key, groups)
        shuffled = jax.vmap(lambda one_key, row_vals: jax.random.permutation(one_key, row_vals))(dest_keys, per_dest)
        rows.append(shuffled.reshape(TOKENS))
    return jnp.stack(rows).astype(jnp.int32)


def level_of(rng, shape, cuts, smallest, high):
    def one(axis_at, parts):
        heights = jax.random.uniform(jax.random.fold_in(jax.random.fold_in(rng, 6), axis_at), (parts,), jnp.float32, smallest / len(cuts), high / len(cuts))
        return jnp.repeat(jnp.exp(heights), shape[axis_at] // parts).reshape((-1,) + (1,) * (len(shape) - axis_at - 1))

    factor_of = one(*cuts[0])
    for cut in cuts[1:]:
        factor_of = factor_of * one(*cut)
    return factor_of


def profile(number_of, total, reach, lean):
    weights = [(1 << 20) // math.isqrt(rank ** lean) + 1 for rank in range(2, number_of + 1)]
    surplus, counts = total - reach - (number_of - 1), [1] * (number_of - 1)
    while surplus > 0:
        free = [i for i in range(number_of - 1) if counts[i] < reach]
        whole, left = sum([weights[i] for i in free]), surplus
        for i in free:
            addition = min(reach - counts[i], max(1, left * weights[i] // whole), surplus)
            counts[i] = counts[i] + addition
            surplus = surplus - addition
    return np.array([reach] + counts)


def ragged(key, number_of, total, reach, slope):
    if number_of == 2:
        one = jax.random.randint(key, (), max(1, total - reach), min(reach, total - 1) + 1)
        return jnp.stack([one, total - one])
    sizes = jnp.asarray(profile(number_of, total, reach, slope), jnp.int32)
    pairs = (number_of - 1) // 2
    giver, receiver = sizes[1:1 + 2 * pairs:2], sizes[2:2 + 2 * pairs:2]
    slack = jnp.minimum(giver - 1, reach - receiver)
    moved = jax.random.randint(jax.random.fold_in(key, 1), (pairs,), 0, 1 << 20) % (slack + 1)
    sizes = sizes.at[1:1 + 2 * pairs:2].set(giver - moved).at[2:2 + 2 * pairs:2].set(receiver + moved)
    return sizes[jax.random.permutation(jax.random.fold_in(key, 2), number_of)]


def bell_draw(own_key, shape, scale, limit, pieces=(), kind=jnp.bfloat16):
    values = jax.random.normal(own_key, shape, jnp.float32) * scale
    if len(pieces) > 0:
        values = level_of(own_key, shape, pieces, -0.22, 0.18) * values
    return jnp.clip(values, min=-limit, max=limit).astype(kind)


def setup_inputs(seed: int = 0) -> dict:
    splits = jax.random.split(jax.random.key(seed), 11)
    return {
        "tokens": bell_draw(splits[0], (MB, TOKENS, D), 1.0, 6.0, ((1, 8),)),
        "cotangent": bell_draw(splits[1], (MB, TOKENS, D), 1.0, 6.0, ((1, 8),)),
        "perm": draw_perm(jax.random.fold_in(splits[10], 71), 0),
        "lengths": jax.vmap(lambda own: ragged(own, NSEQ, TOKENS, MOST, 2))(jax.random.split(splits[3], MB)).reshape((MB, NSEQ)).astype(jnp.int32),
        "w_qkv": bell_draw(splits[4], (D, 3, D), D ** -0.5, 0.1875, ((0, 8), (2, 4))),
        "w_attn_out": bell_draw(splits[5], (D, D), 1 ** -0.5, 6.0, ((0, 8), (1, 4))),
        "w_in": bell_draw(splits[6], (D, 2, FF), D ** -0.5, 0.1875, ((0, 8), (2, 4))),
        "w_down": bell_draw(splits[7], (D, FF), FF ** -0.5, 0.125, ((0, 8), (1, 4))),
        "gain_one": jnp.clip(1.0 + 0.18 * jax.random.normal(splits[8], (D,), jnp.float32), 0.099609375, 1.8984375).astype(jnp.bfloat16),
        "gain_two": jnp.clip(1.0 + 0.18 * jax.random.normal(splits[9], (D,), jnp.float32), 0.099609375, 1.8984375).astype(jnp.bfloat16),
    }


@jax.custom_vjp
def low(v):
    return lax.optimization_barrier(v.astype(jnp.bfloat16)).astype(jnp.float32)

@jax.custom_vjp
def low_back(v):
    return v

def low_keep(v):
    return (low(v), None)

def low_pass(kept, grad):
    return (grad,)

def back_keep(v):
    return (v, None)

def back_low(kept, grad):
    return (low(grad),)
low.defvjp(low_keep, low_pass)
low_back.defvjp(back_keep, back_low)
EPS = 1e-05
THETA = 160000.0
HIGH = lax.Precision.HIGHEST

def layer_norm(values, gain):
    center = values - lax.optimization_barrier(jnp.mean(values, axis=-1, keepdims=True))
    spread = lax.optimization_barrier(jnp.mean(center * center, axis=-1, keepdims=True))
    return center * lax.rsqrt(spread + EPS) * gain

def rope_tables(position, width):
    freqs = jnp.power(THETA, -jnp.arange(width // 2, dtype=jnp.float32) * 2.0 / width)
    angle = position.astype(jnp.float32)[:, None] * freqs[None, :]
    angle = jnp.concatenate([angle, angle], axis=-1)
    return (jnp.cos(angle), jnp.sin(angle))

def rotate(values, cosine, sine):
    half = values.shape[-1] // 2
    turned = jnp.concatenate([-values[..., half:], values[..., :half]], axis=-1)
    return values * cosine[:, None, :] + turned * sine[:, None, :]

def seq_info(anchor, seq_lens):
    ends = jnp.cumsum(seq_lens).astype(jnp.int32)
    starts = (ends - seq_lens).astype(jnp.int32)
    segment = lax.optimization_barrier(jnp.sum((anchor[:, None] >= ends[None, :]).astype(jnp.int32), axis=1)).astype(jnp.int32)
    onehot = segment[:, None] == jnp.arange(seq_lens.shape[0], dtype=jnp.int32)[None, :]
    position = (anchor - lax.optimization_barrier(jnp.sum(jnp.where(onehot, starts[None, :], 0), axis=1))).astype(jnp.int32)
    return (segment, position)

def attend_block(query_blk, seg_blk, keys, values, segment):
    scores = jnp.einsum('qhe,khe->hqk', query_blk, keys, precision=HIGH) * HD ** (-0.5)
    scores = low_back(scores)
    same_seq = (seg_blk[:, None] == segment[None, :])[None]
    scores = jnp.where(same_seq, scores, -jnp.inf)
    probs = low(jax.nn.softmax(scores, axis=-1))
    return jnp.einsum('hqk,khe->qhe', probs, values, precision=HIGH)

def forward(inputs, w_qkv, w_attn_out, w_in, w_down, gain_one, gain_two, perm, lengths):
    results = []
    for micro_idx in range(MB):
        x_float = inputs[micro_idx]
        anchor = jnp.arange(TOKENS, dtype=jnp.int32)
        segment, position = seq_info(anchor, lengths[micro_idx])
        cosine, sine = rope_tables(position, HD)
        normed = low(layer_norm(x_float, gain_one))
        raw_proj = low_back(jnp.dot(normed, w_qkv.reshape(D, 3 * D), precision=HIGH)).reshape(TOKENS, 3, H, HD)
        queries = low(rotate(raw_proj[:, 0], cosine, sine))
        keys = low(rotate(raw_proj[:, 1], cosine, sine))
        values = low(raw_proj[:, 2])
        block = min(512, TOKENS)
        query_blocks = queries.reshape(TOKENS // block, block, H, HD)
        seg_blocks = segment.reshape(TOKENS // block, block)

        def one_block(pair_args):
            return attend_block(pair_args[0], pair_args[1], keys, values, segment)
        mixed = lax.map(jax.checkpoint(one_block), (query_blocks, seg_blocks)).reshape(TOKENS, D)
        mixed = low(low_back(mixed))
        branch = low_back(jnp.dot(mixed, w_attn_out.T, precision=HIGH))
        hidden = x_float + branch
        normed_two = low(layer_norm(hidden, gain_two))
        ffn_proj = low_back(jnp.dot(normed_two, w_in.reshape(D, 2 * FF), precision=HIGH)).reshape(TOKENS, 2, FF)
        act_low = low(jax.nn.gelu(ffn_proj[:, 0], approximate=False) * ffn_proj[:, 1])
        branch_two = low_back(jnp.dot(act_low, w_down.T, precision=HIGH))
        results.append((hidden + branch_two)[perm[micro_idx]])
    return jnp.stack(results)

def reference(tokens, cotangent, perm, lengths, w_qkv, w_attn_out, w_in, w_down, gain_one, gain_two):
    floats = [a.astype(jnp.float32) for a in (tokens, w_qkv, w_attn_out, w_in, w_down, gain_one, gain_two)]

    def func(inputs, wq_arg, wo_arg, wi_arg, wd_arg, g1_arg, g2_arg):
        return forward(inputs, wq_arg, wo_arg, wi_arg, wd_arg, g1_arg, g2_arg, perm, lengths)
    result, pull = jax.vjp(func, *floats)
    grads = pull(cotangent.astype(jnp.float32))
    return (result.astype(jnp.bfloat16), grads[0].astype(jnp.bfloat16), grads[1], grads[2], grads[3], grads[4], grads[5], grads[6])
```

```python
import jax
import jax.numpy as jnp
from jax import lax
from jax.experimental import pallas as pl
from jax.experimental.pallas import tpu as pltpu
from jax.sharding import PartitionSpec as P

D = 1024
HD = 64


EPS = 1e-05
THETA = 160000.0
key_block = 2048


def layer_norm(values, gain):
    center = values - jnp.mean(values, axis=-1, keepdims=True)
    spread = jnp.mean(center * center, axis=-1, keepdims=True)
    return center * lax.rsqrt(spread + EPS) * gain


def rope_tables(position, width):
    freqs = jnp.power(THETA, -jnp.arange(width // 2, dtype=jnp.float32) * 2.0 / width)
    angle = position.astype(jnp.float32)[:, None] * freqs[None, :]
    angle = jnp.concatenate([angle, angle], axis=-1)
    return (jnp.cos(angle), jnp.sin(angle))


def rotate(values, cosine, sine):
    half = values.shape[-1] // 2
    turned = jnp.concatenate([-values[..., half:], values[..., :half]], axis=-1)
    return values * cosine[:, None, :] + turned * sine[:, None, :]


def running_ends(seq_lens):
    order = jnp.arange(seq_lens.shape[0], dtype=jnp.int32)
    return jnp.sum(jnp.where(order[None, :] <= order[:, None], seq_lens[None, :], 0), axis=1)


def seq_info(anchor, seq_lens):
    ends = running_ends(seq_lens)
    starts = ends - seq_lens
    segment = jnp.sum((anchor[:, None] >= ends[None, :]).astype(jnp.int32), axis=1)
    onehot = segment[:, None] == jnp.arange(seq_lens.shape[0], dtype=jnp.int32)[None, :]
    position = anchor - jnp.sum(jnp.where(onehot, starts[None, :], 0), axis=1)
    return (segment, position)


def blockwise(running, pieces, offset, step_fn):
    piece_len = pieces[0].shape[0]
    if piece_len > key_block and piece_len % key_block == 0:
        block_count = piece_len // key_block
        stacked = tuple((one.reshape((block_count, key_block) + one.shape[1:]) for one in pieces))

        def inner(state_now, scan_item):
            block_index, piece_parts = scan_item
            return (step_fn(state_now, piece_parts, offset + block_index * key_block), None)

        running, _ = lax.scan(inner, running, (jnp.arange(block_count, dtype=jnp.int32), stacked))
        return running
    return step_fn(running, pieces, offset)


def general_layer(
    tokens, cotangent, perm, lengths, w_qkv, w_attn_out, w_in, w_down, gain_one, gain_two
):
    groups = lax.axis_size("fsdp")
    my_index = lax.axis_index("fsdp")
    micro_count = tokens.shape[0]
    tok_rows = tokens.shape[1]
    total_rows = tok_rows * groups
    per_pair = tok_rows // groups
    head_cols = w_qkv.shape[2]
    head_count = head_cols // HD
    unit_cols = w_in.shape[2]
    score_scale = HD ** (-0.5)
    rows_idx = jnp.arange(tok_rows, dtype=jnp.int32)
    f32 = jnp.float32
    bf16 = jnp.bfloat16
    dims_rows = (((0,), (0,)), ((), ()))
    dims_cols = (((1,), (1,)), ((), ()))
    acc_qkv = jnp.zeros((D, 3, head_cols), f32)
    acc_out = jnp.zeros((D, head_cols), f32)
    acc_in = jnp.zeros((D, 2, unit_cols), f32)
    acc_down = jnp.zeros((D, unit_cols), f32)
    acc_gain_one = jnp.zeros((D,), f32)
    acc_gain_two = jnp.zeros((D,), f32)
    outputs = []
    input_grads = []
    for micro_idx in range(micro_count):
        perm_row = perm[micro_idx]
        seq_lens = lengths[micro_idx]
        inverse = (
            jnp.zeros((total_rows,), jnp.int32)
            .at[perm_row]
            .set(jnp.arange(total_rows, dtype=jnp.int32))
        )
        placed = lax.dynamic_slice_in_dim(inverse, my_index * tok_rows, tok_rows)
        send_order = jnp.argsort(placed)
        outgoing = tokens[micro_idx][send_order].reshape(groups, per_pair, D)
        arrived = lax.all_to_all(outgoing, "fsdp", split_axis=0, concat_axis=0, tiled=True).reshape(
            tok_rows, D
        )
        my_tokens = lax.dynamic_slice_in_dim(perm_row, my_index * tok_rows, tok_rows)
        source = my_tokens // tok_rows
        recv_order = jnp.argsort(source * tok_rows + rows_idx)
        recv_slot = jnp.zeros((tok_rows,), jnp.int32).at[recv_order].set(rows_idx)
        dealt = arrived[recv_slot]
        fetched = (
            lax.all_gather(gain_one, "fsdp", axis=0, tiled=True),
            lax.all_gather(gain_two, "fsdp", axis=0, tiled=True),
            lax.all_gather(w_qkv, "fsdp", axis=0, tiled=True),
            lax.all_gather(w_attn_out, "fsdp", axis=0, tiled=True),
            lax.all_gather(w_in, "fsdp", axis=0, tiled=True),
            lax.all_gather(w_down, "fsdp", axis=0, tiled=True),
        )
        gain_first = fetched[0].astype(f32)
        gain_second = fetched[1].astype(f32)
        query_seg, query_pos = seq_info(my_tokens, seq_lens)
        cosine, sine = rope_tables(query_pos, HD)
        x_float = dealt.astype(f32)
        normed_low = layer_norm(x_float, gain_first).astype(bf16)
        raw_proj = jnp.einsum("td,dcf->tcf", normed_low, fetched[2], preferred_element_type=f32)
        raw_heads = raw_proj.reshape(tok_rows, 3, head_count, HD)
        query_low = rotate(raw_heads[:, 0], cosine, sine).astype(bf16)
        key_low = rotate(raw_heads[:, 1], cosine, sine).astype(bf16)
        value_low = raw_heads[:, 2].astype(bf16)

        def forward_step(running, piece_parts, offset):
            run_peak, run_total, run_acc = running
            key_part, value_part = piece_parts
            key_seg, _ = seq_info(
                lax.dynamic_slice_in_dim(perm_row, offset, key_part.shape[0]), seq_lens
            )
            scores = (
                jnp.einsum("qhe,khe->hqk", query_low, key_part, preferred_element_type=f32)
                * score_scale
            )
            same_seq = (query_seg[:, None] == key_seg[None, :])[None]
            block_top = jnp.max(jnp.where(same_seq, scores, -1e30), axis=-1)
            new_peak = jnp.maximum(run_peak, block_top)
            weights = jnp.where(same_seq, jnp.exp(scores - new_peak[..., None]), 0.0)
            fade_factor = jnp.exp(run_peak - new_peak)
            run_acc = run_acc * jnp.transpose(fade_factor)[:, :, None] + jnp.einsum(
                "hqk,khe->qhe", weights.astype(bf16), value_part, preferred_element_type=f32
            )
            run_total = run_total * fade_factor + jnp.sum(weights, axis=-1)
            return (new_peak, run_total, run_acc)

        start_state = (
            jnp.full((head_count, tok_rows), -1e30, f32),
            jnp.zeros((head_count, tok_rows), f32),
            jnp.zeros((tok_rows, head_count, HD), f32),
        )
        run_peak, run_total, run_acc = blockwise(
            start_state,
            (
                lax.all_gather(key_low, "fsdp", axis=0, tiled=True),
                lax.all_gather(value_low, "fsdp", axis=0, tiled=True),
            ),
            jnp.int32(0),
            forward_step,
        )
        log_total = run_peak + jnp.log(run_total)
        mixed_heads = run_acc / jnp.transpose(run_total)[:, :, None]
        mixed_low = mixed_heads.reshape(tok_rows, head_cols).astype(bf16)
        attn_part = lax.dot_general(mixed_low, fetched[3], dims_cols, preferred_element_type=f32)
        branch = lax.psum(attn_part.astype(jnp.bfloat16), "tp").astype(jnp.float32)
        hidden = x_float + branch
        normed_two = layer_norm(hidden, gain_second).astype(bf16)
        ffn_proj = jnp.einsum("td,dcf->tcf", normed_two, fetched[4], preferred_element_type=f32)
        act_low = (jax.nn.gelu(ffn_proj[:, 0], approximate=False) * ffn_proj[:, 1]).astype(bf16)
        ffn_part = lax.dot_general(act_low, fetched[5], dims_cols, preferred_element_type=f32)
        branch_two = lax.psum(ffn_part.astype(jnp.bfloat16), "tp").astype(jnp.float32)
        outputs.append((hidden + branch_two).astype(bf16))
        again = (
            lax.all_gather(gain_one, "fsdp", axis=0, tiled=True),
            lax.all_gather(gain_two, "fsdp", axis=0, tiled=True),
            lax.all_gather(w_qkv, "fsdp", axis=0, tiled=True),
            lax.all_gather(w_attn_out, "fsdp", axis=0, tiled=True),
            lax.all_gather(w_in, "fsdp", axis=0, tiled=True),
            lax.all_gather(w_down, "fsdp", axis=0, tiled=True),
        )
        gain_first = again[0].astype(f32)
        gain_second = again[1].astype(f32)
        grad_low = cotangent[micro_idx]
        grad_float = grad_low.astype(f32)
        acc_down = acc_down + lax.dot_general(
            grad_low, act_low, dims_rows, preferred_element_type=f32
        )
        d_act = jnp.dot(grad_low, again[5], preferred_element_type=f32)
        _, gelu_pull = jax.vjp(
            lambda inputs, gates: jax.nn.gelu(inputs, approximate=False) * gates,
            ffn_proj[:, 0],
            ffn_proj[:, 1],
        )
        d_inputs, d_gates = gelu_pull(d_act)
        d_proj = jnp.stack([d_inputs, d_gates], axis=1).astype(bf16)
        acc_in = acc_in + jnp.einsum("td,tcf->dcf", normed_two, d_proj, preferred_element_type=f32)
        norm_part = jnp.einsum("tcf,dcf->td", d_proj, again[4], preferred_element_type=f32)
        d_norm_two = lax.psum(norm_part.astype(jnp.bfloat16), "tp").astype(jnp.float32)
        _, second_pull = jax.vjp(layer_norm, hidden, gain_second)
        d_hid_norm, d_gain_two = second_pull(d_norm_two)
        acc_gain_two = acc_gain_two + d_gain_two
        d_hidden = grad_float + d_hid_norm
        hidden_low = d_hidden.astype(bf16)
        acc_out = acc_out + lax.dot_general(
            hidden_low, mixed_low, dims_rows, preferred_element_type=f32
        )
        d_mixed = jnp.dot(hidden_low, again[3], preferred_element_type=f32).astype(bf16)
        d_mixed = d_mixed.reshape(tok_rows, head_count, HD)
        delta_rows = jnp.sum(d_mixed.astype(f32) * mixed_heads, axis=-1)
        delta_heads = jnp.transpose(delta_rows)

        def query_step(grad_query, piece_parts, offset):
            key_part, value_part = piece_parts
            key_seg, _ = seq_info(
                lax.dynamic_slice_in_dim(perm_row, offset, key_part.shape[0]), seq_lens
            )
            scores = (
                jnp.einsum("qhe,khe->hqk", query_low, key_part, preferred_element_type=f32)
                * score_scale
            )
            same_seq = (query_seg[:, None] == key_seg[None, :])[None]
            weights = jnp.where(same_seq, jnp.exp(scores - log_total[..., None]), 0.0)
            d_weights = jnp.einsum("qhe,khe->hqk", d_mixed, value_part, preferred_element_type=f32)
            d_scores = (weights * (d_weights - delta_heads[..., None])).astype(bf16)
            return grad_query + score_scale * jnp.einsum(
                "hqk,khe->qhe", d_scores, key_part, preferred_element_type=f32
            )

        query_start = jnp.zeros((tok_rows, head_count, HD), f32)
        grad_query = blockwise(
            query_start,
            (
                lax.all_gather(key_low, "fsdp", axis=0, tiled=True),
                lax.all_gather(value_low, "fsdp", axis=0, tiled=True),
            ),
            jnp.int32(0),
            query_step,
        )
        stat_total, stat_delta = (
            lax.all_gather(jnp.transpose(log_total), "fsdp", axis=0, tiled=True),
            lax.all_gather(delta_rows, "fsdp", axis=0, tiled=True),
        )

        def key_step(running, piece_parts, offset):
            grad_key, grad_value = running
            query_part, dmix_part = piece_parts
            piece_len = query_part.shape[0]
            piece_seg, _ = seq_info(lax.dynamic_slice_in_dim(perm_row, offset, piece_len), seq_lens)
            total_part = jnp.transpose(lax.dynamic_slice_in_dim(stat_total, offset, piece_len))
            delta_part = jnp.transpose(lax.dynamic_slice_in_dim(stat_delta, offset, piece_len))
            scores = (
                jnp.einsum("qhe,khe->hqk", query_part, key_low, preferred_element_type=f32)
                * score_scale
            )
            same_seq = (piece_seg[:, None] == query_seg[None, :])[None]
            weights = jnp.where(same_seq, jnp.exp(scores - total_part[..., None]), 0.0)
            d_weights = jnp.einsum("qhe,khe->hqk", dmix_part, value_low, preferred_element_type=f32)
            d_scores = (weights * (d_weights - delta_part[..., None])).astype(bf16)
            grad_key = grad_key + score_scale * jnp.einsum(
                "hqk,qhe->khe", d_scores, query_part, preferred_element_type=f32
            )
            grad_value = grad_value + jnp.einsum(
                "hqk,qhe->khe", weights.astype(bf16), dmix_part, preferred_element_type=f32
            )
            return (grad_key, grad_value)

        grad_key, grad_value = blockwise(
            (
                jnp.zeros((tok_rows, head_count, HD), f32),
                jnp.zeros((tok_rows, head_count, HD), f32),
            ),
            (
                lax.all_gather(query_low, "fsdp", axis=0, tiled=True),
                lax.all_gather(d_mixed, "fsdp", axis=0, tiled=True),
            ),
            jnp.int32(0),
            key_step,
        )
        _, rope_pull = jax.vjp(lambda heads_in: rotate(heads_in, cosine, sine), raw_heads[:, 0])
        d_raw_query = rope_pull(grad_query)[0]
        d_raw_key = rope_pull(grad_key)[0]
        d_raw = (
            jnp.stack([d_raw_query, d_raw_key, grad_value], axis=1)
            .reshape(tok_rows, 3, head_cols)
            .astype(bf16)
        )
        acc_qkv = acc_qkv + jnp.einsum("td,tcf->dcf", normed_low, d_raw, preferred_element_type=f32)
        first_part = jnp.einsum("tcf,dcf->td", d_raw, again[2], preferred_element_type=f32)
        d_norm_one = lax.psum(first_part.astype(jnp.bfloat16), "tp").astype(jnp.float32)
        _, first_pull = jax.vjp(layer_norm, x_float, gain_first)
        d_x_norm, d_gain_one = first_pull(d_norm_one)
        acc_gain_one = acc_gain_one + d_gain_one
        d_input = (d_hidden + d_x_norm).astype(bf16)
        back_rows = d_input[recv_order].reshape(groups, per_pair, D)
        returned = lax.all_to_all(
            back_rows, "fsdp", split_axis=0, concat_axis=0, tiled=True
        ).reshape(tok_rows, D)
        send_slot = jnp.zeros((tok_rows,), jnp.int32).at[send_order].set(rows_idx)
        input_grads.append(returned[send_slot])
    summed = (
        lax.psum_scatter(acc_qkv, "fsdp", scatter_dimension=0, tiled=True),
        lax.psum_scatter(acc_out, "fsdp", scatter_dimension=0, tiled=True),
        lax.psum_scatter(acc_in, "fsdp", scatter_dimension=0, tiled=True),
        lax.psum_scatter(acc_down, "fsdp", scatter_dimension=0, tiled=True),
        lax.psum_scatter(acc_gain_one, "fsdp", scatter_dimension=0, tiled=True),
        lax.psum_scatter(acc_gain_two, "fsdp", scatter_dimension=0, tiled=True),
    )
    return (
        jnp.stack(outputs),
        jnp.stack(input_grads),
        summed[0],
        summed[1],
        summed[2],
        summed[3],
        summed[4],
        summed[5],
    )


BLOCK = 256
FAR = -1e30
ORDER = (0, 2, 4, 6, 1, 3, 5, 7)
NT = (((1,), (1,)), ((), ()))
TN = (((0,), (0,)), ((), ()))
NN = (((1,), (0,)), ((), ()))


def mm(left, right, dims):
    return lax.dot_general(left, right, dims, preferred_element_type=jnp.float32)


def hop(value, step):
    return lax.ppermute(value, "fsdp", [(i, i ^ step) for i in range(8)])


def twin(value):
    return lax.ppermute(value, "tp", [(i, i ^ 1) for i in range(4)])


def across(value):
    return lax.ppermute(value, "tp", [(i, i ^ 2) for i in range(4)])


def gather_shards(shard):
    same = [shard] + [hop(shard, step) for step in ORDER[1:4]]
    return same + [hop(one, 1) for one in same]


def scatter_sum(total):
    cols = total.shape[1] // 8
    low = total.astype(jnp.bfloat16)
    near = total[:, : 4 * cols] + hop(low[:, 4 * cols :], 1).astype(jnp.float32)
    result = near[:, :cols]
    for place in range(1, 4):
        piece = near[:, place * cols : (place + 1) * cols].astype(jnp.bfloat16)
        result = result + hop(piece, ORDER[place]).astype(jnp.float32)
    return result


def key_range(lens_ref, low, high):
    first = jnp.int32(0)
    last = jnp.int32(0)
    total = jnp.int32(0)
    for index in range(lens_ref.shape[0]):
        start = total
        total = total + lens_ref[index]
        first = jnp.where((start <= low) & (low < total), start, first)
        last = jnp.where((start <= high) & (high < total), total, last)
    return first, last


def query_bounds(lens_ref, base, width):
    place = base + lax.broadcasted_iota(jnp.int32, (1, width), 1)
    first = jnp.zeros((1, width), jnp.int32)
    last = jnp.zeros((1, width), jnp.int32)
    total = jnp.int32(0)
    for index in range(lens_ref.shape[0]):
        start = total
        total = total + lens_ref[index]
        inside = (place >= start) & (place < total)
        first = jnp.where(inside, start, first)
        last = jnp.where(inside, total, last)
    return first, last


def attend_kernel(lens_ref, qkv_ref, mixed_ref, exact_ref, log_ref, key_ref):
    count = qkv_ref.shape[0]

    def turn(index, carry):
        block = qkv_ref[index, HD : 2 * HD, :].astype(jnp.float32)
        key_ref[index] = jnp.transpose(block).astype(jnp.bfloat16)
        return carry

    lax.fori_loop(0, count, turn, 0)

    def one_query(index, carry):
        base = index * BLOCK
        first, last = key_range(lens_ref, base, base + BLOCK - 1)
        low, high = query_bounds(lens_ref, base, BLOCK)
        query = qkv_ref[index, :HD, :] * jnp.bfloat16(HD**-0.5)

        def one_key(at, state):
            peak, total, acc = state
            scores = mm(key_ref[at], query, NN)
            place = at * BLOCK + lax.broadcasted_iota(jnp.int32, (BLOCK, BLOCK), 0)
            scores = jnp.where((place >= low) & (place < high), scores, FAR)
            top = jnp.maximum(peak, jnp.max(scores, axis=0, keepdims=True))
            weights = jnp.exp(scores - top)
            fade = jnp.exp(peak - top)
            total = total * fade + jnp.sum(weights, axis=0, keepdims=True)
            acc = acc * fade + mm(qkv_ref[at, 2 * HD :, :], weights.astype(jnp.bfloat16), NN)
            return top, total, acc

        peak, total, acc = lax.fori_loop(
            first // BLOCK,
            (last + BLOCK - 1) // BLOCK,
            one_key,
            (
                jnp.full((1, BLOCK), FAR, jnp.float32),
                jnp.zeros((1, BLOCK), jnp.float32),
                jnp.zeros((HD, BLOCK), jnp.float32),
            ),
        )
        result = acc / total
        mixed_ref[index] = result.astype(jnp.bfloat16)
        exact_ref[index] = result
        log_ref[index] = peak + jnp.log(total)
        return carry

    lax.fori_loop(0, count, one_query, 0)


def attend(lens, qkv):
    count = qkv.shape[0]
    return pl.pallas_call(
        attend_kernel,
        in_specs=[
            pl.BlockSpec(memory_space=pltpu.SMEM),
            pl.BlockSpec(memory_space=pltpu.VMEM),
        ],
        out_specs=[pl.BlockSpec(memory_space=pltpu.VMEM)] * 3,
        out_shape=[
            jax.ShapeDtypeStruct((count, HD, BLOCK), jnp.bfloat16),
            jax.ShapeDtypeStruct((count, HD, BLOCK), jnp.float32),
            jax.ShapeDtypeStruct((count, 1, BLOCK), jnp.float32),
        ],
        scratch_shapes=[pltpu.VMEM((count, BLOCK, HD), jnp.bfloat16)],
        compiler_params=pltpu.CompilerParams(vmem_limit_bytes=40 * 1024 * 1024),
        name="attend",
    )(lens, qkv)


def attend_back_kernel(
    lens_ref, qkv_ref, exact_ref, log_ref, grad_ref, table_ref, raw_ref,
    key_ref, value_ref, dkey_ref, dvalue_ref,
):
    count = qkv_ref.shape[0]
    half = HD // 2

    def turn(index, carry):
        block = qkv_ref[index, HD : 2 * HD, :].astype(jnp.float32)
        key_ref[index] = jnp.transpose(block).astype(jnp.bfloat16)
        block = qkv_ref[index, 2 * HD :, :].astype(jnp.float32)
        value_ref[index] = jnp.transpose(block).astype(jnp.bfloat16)
        dkey_ref[index] = jnp.zeros((HD, BLOCK), jnp.float32)
        dvalue_ref[index] = jnp.zeros((HD, BLOCK), jnp.float32)
        return carry

    lax.fori_loop(0, count, turn, 0)

    def unturn(index, grad):
        cosine = table_ref[index, :half, :]
        sine = table_ref[index, half:, :]
        upper, lower = grad[:half], grad[half:]
        return upper * cosine + lower * sine, lower * cosine - upper * sine

    def one_query(index, carry):
        base = index * BLOCK
        first, last = key_range(lens_ref, base, base + BLOCK - 1)
        low, high = query_bounds(lens_ref, base, BLOCK)
        query = qkv_ref[index, :HD, :] * jnp.bfloat16(HD**-0.5)
        grad = grad_ref[index]
        logs = log_ref[index]
        delta = jnp.sum(grad.astype(jnp.float32) * exact_ref[index], axis=0, keepdims=True)

        def one_key(at, dquery):
            scores = mm(key_ref[at], query, NN)
            place = at * BLOCK + lax.broadcasted_iota(jnp.int32, (BLOCK, BLOCK), 0)
            weights = jnp.where((place >= low) & (place < high), jnp.exp(scores - logs), 0.0)
            dweights = mm(value_ref[at], grad, NN)
            dscores = (weights * (dweights - delta)).astype(jnp.bfloat16)
            dkey_ref[at] += mm(query, dscores, NT)
            dvalue_ref[at] += mm(grad, weights.astype(jnp.bfloat16), NT)
            return dquery + mm(qkv_ref[at, HD : 2 * HD, :], dscores, NN)

        dquery = lax.fori_loop(
            first // BLOCK,
            (last + BLOCK - 1) // BLOCK,
            one_key,
            jnp.zeros((HD, BLOCK), jnp.float32),
        )
        upper, lower = unturn(index, dquery * (HD**-0.5))
        raw_ref[index, :half, :] = upper.astype(jnp.bfloat16)
        raw_ref[index, half:HD, :] = lower.astype(jnp.bfloat16)
        return carry

    lax.fori_loop(0, count, one_query, 0)

    def finish(index, carry):
        upper, lower = unturn(index, dkey_ref[index])
        raw_ref[index, HD : HD + half, :] = upper.astype(jnp.bfloat16)
        raw_ref[index, HD + half : 2 * HD, :] = lower.astype(jnp.bfloat16)
        raw_ref[index, 2 * HD :, :] = dvalue_ref[index].astype(jnp.bfloat16)
        return carry

    lax.fori_loop(0, count, finish, 0)


def attend_back(lens, qkv, exact, logs, grad, table):
    count = qkv.shape[0]
    return pl.pallas_call(
        attend_back_kernel,
        in_specs=[pl.BlockSpec(memory_space=pltpu.SMEM)] + [pl.BlockSpec(memory_space=pltpu.VMEM)] * 5,
        out_specs=pl.BlockSpec(memory_space=pltpu.VMEM),
        out_shape=jax.ShapeDtypeStruct((count, 3 * HD, BLOCK), jnp.bfloat16),
        scratch_shapes=[
            pltpu.VMEM((count, BLOCK, HD), jnp.bfloat16),
            pltpu.VMEM((count, BLOCK, HD), jnp.bfloat16),
            pltpu.VMEM((count, HD, BLOCK), jnp.float32),
            pltpu.VMEM((count, HD, BLOCK), jnp.float32),
        ],
        compiler_params=pltpu.CompilerParams(vmem_limit_bytes=40 * 1024 * 1024),
        name="attend_back",
    )(lens, qkv, exact, logs, grad, table)


def positions(anchor, seq_lens):
    ends = running_ends(seq_lens)
    starts = ends - seq_lens
    inside = (anchor[:, None] >= starts[None, :]) & (anchor[:, None] < ends[None, :])
    return anchor - jnp.sum(jnp.where(inside, starts[None, :], 0), axis=1)


def turn_tables(place):
    freqs = jnp.power(THETA, -jnp.arange(HD // 2, dtype=jnp.float32) * 2.0 / HD)
    angle = freqs[:, None] * place.astype(jnp.float32)[None, :]
    return jnp.concatenate([jnp.cos(angle), jnp.sin(angle)], axis=0)


def statistics(values):
    center = values - jnp.mean(values, axis=-1, keepdims=True)
    spread = lax.rsqrt(jnp.mean(center * center, axis=-1, keepdims=True) + EPS)
    return center * spread, spread


def norm_back(xhat, spread, gain, grad):
    scaled = grad * gain
    inner = scaled - jnp.mean(scaled, axis=-1, keepdims=True)
    inner = inner - xhat * jnp.mean(scaled * xhat, axis=-1, keepdims=True)
    return inner * spread, jnp.sum(grad * xhat, axis=0)


def paired_layer(
    tokens, cotangent, perm, lengths, w_qkv, w_attn_out, w_in, w_down, gain_one, gain_two
):
    f32, bf16 = jnp.float32, jnp.bfloat16
    mine = lax.axis_index("fsdp")
    part = lax.axis_index("tp")
    core, side = part % 2, part // 2
    rows = tokens.shape[1]
    width = w_qkv.shape[0]
    head_cols = w_qkv.shape[2]
    heads = head_cols // HD
    units = w_in.shape[2]
    per_pair = rows // 8
    order = jnp.bitwise_xor(jnp.array(ORDER, jnp.int32), mine)
    back = jnp.bitwise_xor(jnp.arange(8, dtype=jnp.int32), mine)
    back = (back % 2) * 4 + back // 2

    def reorder(value, index):
        axis = value.ndim - 1
        pieces = [lax.dynamic_slice_in_dim(value, index[at] * width, width, axis) for at in range(8)]
        return jnp.concatenate(pieces, axis=axis)

    def pick(value, index):
        return lax.dynamic_index_in_dim(value, index, 0, keepdims=False)

    def tp_sum(value):
        got = twin(pick(value, 1 - core).astype(bf16))
        half = (pick(value, core) + got.astype(f32)).astype(bf16)
        return half.astype(f32) + across(half).astype(f32)

    def both(value):
        other = twin(value)
        return jnp.stack([jnp.where(core == 0, value, other), jnp.where(core == 0, other, value)])

    turned = jnp.transpose(w_qkv.reshape(width, 3, heads, HD), (2, 1, 3, 0)).reshape(3 * head_cols, width)
    gains = jnp.zeros((16, width), bf16).at[0].set(gain_one).at[1].set(gain_two)
    first_pack = gather_shards(jnp.concatenate([turned, gains], axis=0))
    first_all = jnp.concatenate(first_pack, axis=1)
    qkv_w = first_all[: 3 * head_cols]
    gain_first = first_all[3 * head_cols].astype(f32)
    gain_second = first_all[3 * head_cols + 1].astype(f32)

    x_rel = reorder(tokens, order).astype(f32)
    xhat_one, spread_one = statistics(x_rel)
    n_one = (xhat_one * gain_first).astype(bf16)
    raw = mm(qkv_w, n_one.reshape(2 * rows, 8 * width), NT)
    raw = raw.reshape(heads, 3, HD, 2, rows)
    anchor = mine * rows + jnp.arange(rows, dtype=jnp.int32)
    own_table = jnp.stack([turn_tables(positions(anchor, lengths[m])) for m in range(2)], axis=1)
    cosine, sine = own_table[: HD // 2], own_table[HD // 2 :]

    def spin(value):
        upper, lower = value[:, : HD // 2], value[:, HD // 2 :]
        return jnp.concatenate([upper * cosine - lower * sine, lower * cosine + upper * sine], axis=1)

    turned_qkv = jnp.stack([spin(raw[:, 0]), spin(raw[:, 1]), raw[:, 2]], axis=1).astype(bf16)
    outgoing = jnp.transpose(turned_qkv, (3, 0, 1, 2, 4)).reshape(8, 3 * HD, rows)
    qkv = lax.all_to_all(outgoing, "fsdp", 0, 0, tiled=True)
    my_lens = lengths[mine // heads]
    mixed_out, exact, logs = attend(my_lens, qkv)
    mixed = lax.all_to_all(mixed_out, "fsdp", 0, 0, tiled=True).reshape(2, head_cols, rows)

    second = jnp.concatenate(
        [
            jnp.transpose(w_attn_out),
            jnp.transpose(w_in.reshape(width, 2 * units)),
            jnp.transpose(w_down),
        ],
        axis=0,
    )
    second_all = jnp.concatenate(gather_shards(second), axis=1)
    out_w = second_all[:head_cols]
    in_w = second_all[head_cols : head_cols + 2 * units]
    down_w = second_all[head_cols + 2 * units :]

    slots = perm.reshape(2, 8, rows)
    from_me = (slots // rows == mine).astype(f32)
    slot_no = jnp.arange(rows, dtype=jnp.int32)
    before = (slot_no[:, None] < slot_no[None, :]).astype(f32)
    rank_me = jnp.einsum("mds,st->mdt", from_me, before).astype(jnp.int32)
    ranks = jnp.arange(per_pair, dtype=jnp.int32)
    chosen = (from_me[..., None] > 0) & (rank_me[..., None] == ranks)
    local = jnp.sum(jnp.where(chosen, (slots % rows)[..., None], 0), axis=2)
    my_slots = lax.dynamic_index_in_dim(slots, mine, 1, keepdims=False)
    target = my_slots // rows
    same = (target[:, :, None] == target[:, None, :]) & (slot_no[:, None] < slot_no[None, :])[None]
    rank_own = jnp.sum(same.astype(jnp.int32), axis=1)
    place_own = target * per_pair + rank_own

    quarter = per_pair // 4
    wanted = jnp.arange(8, dtype=jnp.int32)[:, None] * per_pair + part * quarter
    wanted = (wanted + jnp.arange(quarter, dtype=jnp.int32)[None, :]).reshape(-1)
    packer = (place_own[:, None, :] == wanted[None, :, None]).astype(bf16)
    packed = jnp.einsum("mps,msd->mpd", packer, cotangent, preferred_element_type=f32).astype(bf16)
    packed = jnp.transpose(packed.reshape(2, 8, quarter, 8 * width), (1, 0, 2, 3))
    arrived = lax.all_to_all(packed, "fsdp", 0, 0, tiled=True)
    near = twin(arrived)
    pair = jnp.stack([jnp.where(core == 0, arrived, near), jnp.where(core == 0, near, arrived)])
    far = across(pair)
    four = jnp.concatenate([jnp.where(side == 0, pair, far), jnp.where(side == 0, far, pair)])
    four = jnp.transpose(four, (2, 1, 0, 3, 4)).reshape(2, rows, 8 * width)
    spread_rows = (local.reshape(2, 1, rows) == slot_no[None, :, None]).astype(bf16)
    four = four.astype(bf16)
    grad_nat = jnp.einsum("mps,msd->mpd", spread_rows, four, preferred_element_type=f32).astype(bf16)
    grad = reorder(grad_nat, order)

    out_part = jnp.stack([mm(mixed[m], out_w, TN) for m in range(2)])
    hidden = pick(x_rel, core) + tp_sum(out_part)
    xhat_two, spread_two = statistics(hidden)
    n_two = both((xhat_two * gain_second).astype(bf16)).reshape(2 * rows, 8 * width)

    grad_flat = grad.reshape(2 * rows, 8 * width)
    projected = mm(n_two, in_w, NT)
    inp, gate = projected[:, :units], projected[:, units:]
    d_act = mm(grad_flat, down_w, NT)
    cdf = 0.5 * (1.0 + lax.erf(inp * (0.5**0.5)))
    density = jnp.exp(-0.5 * inp * inp) * ((0.5 / jnp.pi) ** 0.5)
    gelu = inp * cdf
    act = (gelu * gate).astype(bf16)
    d_inp = d_act * gate * (cdf + inp * density)
    d_proj = jnp.concatenate([d_inp, d_act * gelu], axis=1).astype(bf16)
    d_two_part = mm(d_proj, in_w, NN).reshape(2, rows, 8 * width)
    d_two = tp_sum(d_two_part)
    d_norm, d_gain_two = norm_back(xhat_two, spread_two, gain_second, d_two)
    d_hidden = pick(grad, core).astype(f32) + d_norm
    low_hidden = both(d_hidden.astype(bf16))

    down_part = mm(act, down_w, NN).reshape(2, rows, 8 * width)
    result = (hidden + tp_sum(down_part)).astype(bf16)
    grad_in = mm(d_proj, n_two, TN)
    grad_down = mm(act, grad_flat, TN)

    result = reorder(result, back)
    local_own = pick(local, core)
    halfway = per_pair // 2
    mine_half = lax.dynamic_slice_in_dim(local_own, side * halfway, halfway, 1).reshape(-1)
    packer = (mine_half[:, None] == slot_no[None, :]).astype(bf16)
    packed = mm(packer, result, NN).astype(bf16).reshape(8, halfway, 8 * width)
    arrived = lax.all_to_all(packed, "fsdp", 0, 0, tiled=True)
    far = across(arrived)
    full = jnp.concatenate(
        [jnp.where(side == 0, arrived, far), jnp.where(side == 0, far, arrived)], axis=1
    ).reshape(rows, 8 * width)
    full = both(full)
    unpack = (place_own[:, :, None] == slot_no[None, None, :]).astype(bf16)
    output = jnp.einsum("msp,mpd->msd", unpack, full, preferred_element_type=f32).astype(bf16)

    d_mixed = mm(out_w, low_hidden.reshape(2 * rows, 8 * width), NT).astype(bf16)
    d_mixed = jnp.transpose(d_mixed.reshape(heads, HD, 2, rows), (2, 0, 1, 3)).reshape(8, HD, rows)
    grad_mixed = lax.all_to_all(d_mixed, "fsdp", 0, 0, tiled=True)
    grad_out = mm(mixed[0], low_hidden[0], NN) + mm(mixed[1], low_hidden[1], NN)
    second_grad = scatter_sum(jnp.concatenate([grad_out, grad_in, grad_down], axis=0))
    all_anchor = jnp.arange(8 * rows, dtype=jnp.int32)
    table = turn_tables(positions(all_anchor, my_lens))
    table = jnp.transpose(table.reshape(HD, 8, rows), (1, 0, 2))
    d_raw_out = attend_back(my_lens, qkv, exact, logs, grad_mixed, table)
    d_raw = lax.all_to_all(d_raw_out, "fsdp", 0, 0, tiled=True).reshape(2, 3 * head_cols, rows)
    d_one_part = jnp.stack([mm(d_raw[m], qkv_w, TN) for m in range(2)])
    d_one = tp_sum(d_one_part)
    grad_qkv = mm(d_raw[0], n_one[0], NN) + mm(d_raw[1], n_one[1], NN)
    d_x, d_gain_one = norm_back(
        pick(xhat_one, core), pick(spread_one, core), gain_first, d_one
    )
    input_grad = both(reorder((d_hidden + d_x).astype(bf16), back))

    gain_grads = jnp.stack([d_gain_one, d_gain_two])
    high = gain_grads.astype(bf16).astype(f32)
    rest = jnp.zeros((12, 8 * width), f32)
    first_grad = scatter_sum(jnp.concatenate([grad_qkv, high, gain_grads - high, rest], axis=0))
    gain_rows = first_grad[3 * head_cols : 3 * head_cols + 2] + first_grad[3 * head_cols + 2 : 3 * head_cols + 4]
    gain_rows = gain_rows + twin(gain_rows)
    qkv_out = first_grad[: 3 * head_cols].reshape(heads, 3, HD, width)
    return (
        output,
        input_grad,
        jnp.transpose(qkv_out, (3, 1, 0, 2)).reshape(width, 3, head_cols),
        jnp.transpose(second_grad[:head_cols]),
        jnp.transpose(second_grad[head_cols : head_cols + 2 * units]).reshape(width, 2, units),
        jnp.transpose(second_grad[head_cols + 2 * units :]),
        gain_rows[0],
        gain_rows[1],
    )


def on_device(*operands):
    micro_count, tok_rows = operands[0].shape[0], operands[0].shape[1]
    groups, parts = lax.axis_size("fsdp"), lax.axis_size("tp")
    heads = operands[4].shape[2] // HD
    if groups == 8 and parts == 4 and micro_count == 2 and micro_count * heads == groups and tok_rows % 256 == 0:
        return paired_layer(*operands)
    return general_layer(*operands)


def solution(mesh):
    placed = (
        P(None, "fsdp", None),
        P(None, "fsdp", None),
        P(),
        P(),
        P("fsdp", None, "tp"),
        P("fsdp", "tp"),
        P("fsdp", None, "tp"),
        P("fsdp", "tp"),
        P("fsdp"),
        P("fsdp"),
    )
    return jax.shard_map(
        on_device,
        mesh=mesh,
        in_specs=placed,
        out_specs=(
            P(None, "fsdp", None),
            P(None, "fsdp", None),
            P("fsdp", None, "tp"),
            P("fsdp", "tp"),
            P("fsdp", None, "tp"),
            P("fsdp", "tp"),
            P("fsdp"),
            P("fsdp"),
        ),
        check_vma=False,
    )
```

```python
import math

import jax
import jax.numpy as jnp
from jax import lax
from jax.experimental import pallas as pl
from jax.experimental.pallas import tpu as pltpu
from jax.sharding import PartitionSpec as P

D = 1024
HD = 64


EPS = 1e-05
THETA = 160000.0
key_block = 2048


def layer_norm(values, gain):
    center = values - jnp.mean(values, axis=-1, keepdims=True)
    spread = jnp.mean(center * center, axis=-1, keepdims=True)
    return center * lax.rsqrt(spread + EPS) * gain


def rope_tables(position, width):
    freqs = jnp.power(THETA, -jnp.arange(width // 2, dtype=jnp.float32) * 2.0 / width)
    angle = position.astype(jnp.float32)[:, None] * freqs[None, :]
    angle = jnp.concatenate([angle, angle], axis=-1)
    return (jnp.cos(angle), jnp.sin(angle))


def rotate(values, cosine, sine):
    half = values.shape[-1] // 2
    turned = jnp.concatenate([-values[..., half:], values[..., :half]], axis=-1)
    return values * cosine[:, None, :] + turned * sine[:, None, :]


def running_ends(seq_lens):
    order = jnp.arange(seq_lens.shape[0], dtype=jnp.int32)
    return jnp.sum(jnp.where(order[None, :] <= order[:, None], seq_lens[None, :], 0), axis=1)


def seq_info(anchor, seq_lens):
    ends = running_ends(seq_lens)
    starts = ends - seq_lens
    segment = jnp.sum((anchor[:, None] >= ends[None, :]).astype(jnp.int32), axis=1)
    onehot = segment[:, None] == jnp.arange(seq_lens.shape[0], dtype=jnp.int32)[None, :]
    position = anchor - jnp.sum(jnp.where(onehot, starts[None, :], 0), axis=1)
    return (segment, position)


def blockwise(running, pieces, offset, step_fn):
    piece_len = pieces[0].shape[0]
    if piece_len > key_block and piece_len % key_block == 0:
        block_count = piece_len // key_block
        stacked = tuple((one.reshape((block_count, key_block) + one.shape[1:]) for one in pieces))

        def inner(state_now, scan_item):
            block_index, piece_parts = scan_item
            return (step_fn(state_now, piece_parts, offset + block_index * key_block), None)

        running, _ = lax.scan(inner, running, (jnp.arange(block_count, dtype=jnp.int32), stacked))
        return running
    return step_fn(running, pieces, offset)


def general_layer(
    tokens, cotangent, perm, lengths, w_qkv, w_attn_out, w_in, w_down, gain_one, gain_two
):
    groups = lax.axis_size("fsdp")
    my_index = lax.axis_index("fsdp")
    micro_count = tokens.shape[0]
    tok_rows = tokens.shape[1]
    total_rows = tok_rows * groups
    per_pair = tok_rows // groups
    head_cols = w_qkv.shape[2]
    head_count = head_cols // HD
    unit_cols = w_in.shape[2]
    score_scale = HD ** (-0.5)
    rows_idx = jnp.arange(tok_rows, dtype=jnp.int32)
    f32 = jnp.float32
    bf16 = jnp.bfloat16
    dims_rows = (((0,), (0,)), ((), ()))
    dims_cols = (((1,), (1,)), ((), ()))
    acc_qkv = jnp.zeros((D, 3, head_cols), f32)
    acc_out = jnp.zeros((D, head_cols), f32)
    acc_in = jnp.zeros((D, 2, unit_cols), f32)
    acc_down = jnp.zeros((D, unit_cols), f32)
    acc_gain_one = jnp.zeros((D,), f32)
    acc_gain_two = jnp.zeros((D,), f32)
    outputs = []
    input_grads = []
    for micro_idx in range(micro_count):
        perm_row = perm[micro_idx]
        seq_lens = lengths[micro_idx]
        inverse = (
            jnp.zeros((total_rows,), jnp.int32)
            .at[perm_row]
            .set(jnp.arange(total_rows, dtype=jnp.int32))
        )
        placed = lax.dynamic_slice_in_dim(inverse, my_index * tok_rows, tok_rows)
        send_order = jnp.argsort(placed)
        outgoing = tokens[micro_idx][send_order].reshape(groups, per_pair, D)
        arrived = lax.all_to_all(outgoing, "fsdp", split_axis=0, concat_axis=0, tiled=True).reshape(
            tok_rows, D
        )
        my_tokens = lax.dynamic_slice_in_dim(perm_row, my_index * tok_rows, tok_rows)
        source = my_tokens // tok_rows
        recv_order = jnp.argsort(source * tok_rows + rows_idx)
        recv_slot = jnp.zeros((tok_rows,), jnp.int32).at[recv_order].set(rows_idx)
        dealt = arrived[recv_slot]
        fetched = (
            lax.all_gather(gain_one, "fsdp", axis=0, tiled=True),
            lax.all_gather(gain_two, "fsdp", axis=0, tiled=True),
            lax.all_gather(w_qkv, "fsdp", axis=0, tiled=True),
            lax.all_gather(w_attn_out, "fsdp", axis=0, tiled=True),
            lax.all_gather(w_in, "fsdp", axis=0, tiled=True),
            lax.all_gather(w_down, "fsdp", axis=0, tiled=True),
        )
        gain_first = fetched[0].astype(f32)
        gain_second = fetched[1].astype(f32)
        query_seg, query_pos = seq_info(my_tokens, seq_lens)
        cosine, sine = rope_tables(query_pos, HD)
        x_float = dealt.astype(f32)
        normed_low = layer_norm(x_float, gain_first).astype(bf16)
        raw_proj = jnp.einsum("td,dcf->tcf", normed_low, fetched[2], preferred_element_type=f32)
        raw_heads = raw_proj.reshape(tok_rows, 3, head_count, HD)
        query_low = rotate(raw_heads[:, 0], cosine, sine).astype(bf16)
        key_low = rotate(raw_heads[:, 1], cosine, sine).astype(bf16)
        value_low = raw_heads[:, 2].astype(bf16)

        def forward_step(running, piece_parts, offset):
            run_peak, run_total, run_acc = running
            key_part, value_part = piece_parts
            key_seg, _ = seq_info(
                lax.dynamic_slice_in_dim(perm_row, offset, key_part.shape[0]), seq_lens
            )
            scores = (
                jnp.einsum("qhe,khe->hqk", query_low, key_part, preferred_element_type=f32)
                * score_scale
            )
            same_seq = (query_seg[:, None] == key_seg[None, :])[None]
            block_top = jnp.max(jnp.where(same_seq, scores, -1e30), axis=-1)
            new_peak = jnp.maximum(run_peak, block_top)
            weights = jnp.where(same_seq, jnp.exp(scores - new_peak[..., None]), 0.0)
            fade_factor = jnp.exp(run_peak - new_peak)
            run_acc = run_acc * jnp.transpose(fade_factor)[:, :, None] + jnp.einsum(
                "hqk,khe->qhe", weights.astype(bf16), value_part, preferred_element_type=f32
            )
            run_total = run_total * fade_factor + jnp.sum(weights, axis=-1)
            return (new_peak, run_total, run_acc)

        start_state = (
            jnp.full((head_count, tok_rows), -1e30, f32),
            jnp.zeros((head_count, tok_rows), f32),
            jnp.zeros((tok_rows, head_count, HD), f32),
        )
        run_peak, run_total, run_acc = blockwise(
            start_state,
            (
                lax.all_gather(key_low, "fsdp", axis=0, tiled=True),
                lax.all_gather(value_low, "fsdp", axis=0, tiled=True),
            ),
            jnp.int32(0),
            forward_step,
        )
        log_total = run_peak + jnp.log(run_total)
        mixed_heads = run_acc / jnp.transpose(run_total)[:, :, None]
        mixed_low = mixed_heads.reshape(tok_rows, head_cols).astype(bf16)
        attn_part = lax.dot_general(mixed_low, fetched[3], dims_cols, preferred_element_type=f32)
        branch = lax.psum(attn_part.astype(jnp.bfloat16), "tp").astype(jnp.float32)
        hidden = x_float + branch
        normed_two = layer_norm(hidden, gain_second).astype(bf16)
        ffn_proj = jnp.einsum("td,dcf->tcf", normed_two, fetched[4], preferred_element_type=f32)
        act_low = (jax.nn.gelu(ffn_proj[:, 0], approximate=False) * ffn_proj[:, 1]).astype(bf16)
        ffn_part = lax.dot_general(act_low, fetched[5], dims_cols, preferred_element_type=f32)
        branch_two = lax.psum(ffn_part.astype(jnp.bfloat16), "tp").astype(jnp.float32)
        outputs.append((hidden + branch_two).astype(bf16))
        again = (
            lax.all_gather(gain_one, "fsdp", axis=0, tiled=True),
            lax.all_gather(gain_two, "fsdp", axis=0, tiled=True),
            lax.all_gather(w_qkv, "fsdp", axis=0, tiled=True),
            lax.all_gather(w_attn_out, "fsdp", axis=0, tiled=True),
            lax.all_gather(w_in, "fsdp", axis=0, tiled=True),
            lax.all_gather(w_down, "fsdp", axis=0, tiled=True),
        )
        gain_first = again[0].astype(f32)
        gain_second = again[1].astype(f32)
        grad_low = cotangent[micro_idx]
        grad_float = grad_low.astype(f32)
        acc_down = acc_down + lax.dot_general(
            grad_low, act_low, dims_rows, preferred_element_type=f32
        )
        d_act = jnp.dot(grad_low, again[5], preferred_element_type=f32)
        _, gelu_pull = jax.vjp(
            lambda inputs, gates: jax.nn.gelu(inputs, approximate=False) * gates,
            ffn_proj[:, 0],
            ffn_proj[:, 1],
        )
        d_inputs, d_gates = gelu_pull(d_act)
        d_proj = jnp.stack([d_inputs, d_gates], axis=1).astype(bf16)
        acc_in = acc_in + jnp.einsum("td,tcf->dcf", normed_two, d_proj, preferred_element_type=f32)
        norm_part = jnp.einsum("tcf,dcf->td", d_proj, again[4], preferred_element_type=f32)
        d_norm_two = lax.psum(norm_part.astype(jnp.bfloat16), "tp").astype(jnp.float32)
        _, second_pull = jax.vjp(layer_norm, hidden, gain_second)
        d_hid_norm, d_gain_two = second_pull(d_norm_two)
        acc_gain_two = acc_gain_two + d_gain_two
        d_hidden = grad_float + d_hid_norm
        hidden_low = d_hidden.astype(bf16)
        acc_out = acc_out + lax.dot_general(
            hidden_low, mixed_low, dims_rows, preferred_element_type=f32
        )
        d_mixed = jnp.dot(hidden_low, again[3], preferred_element_type=f32).astype(bf16)
        d_mixed = d_mixed.reshape(tok_rows, head_count, HD)
        delta_rows = jnp.sum(d_mixed.astype(f32) * mixed_heads, axis=-1)
        delta_heads = jnp.transpose(delta_rows)

        def query_step(grad_query, piece_parts, offset):
            key_part, value_part = piece_parts
            key_seg, _ = seq_info(
                lax.dynamic_slice_in_dim(perm_row, offset, key_part.shape[0]), seq_lens
            )
            scores = (
                jnp.einsum("qhe,khe->hqk", query_low, key_part, preferred_element_type=f32)
                * score_scale
            )
            same_seq = (query_seg[:, None] == key_seg[None, :])[None]
            weights = jnp.where(same_seq, jnp.exp(scores - log_total[..., None]), 0.0)
            d_weights = jnp.einsum("qhe,khe->hqk", d_mixed, value_part, preferred_element_type=f32)
            d_scores = (weights * (d_weights - delta_heads[..., None])).astype(bf16)
            return grad_query + score_scale * jnp.einsum(
                "hqk,khe->qhe", d_scores, key_part, preferred_element_type=f32
            )

        query_start = jnp.zeros((tok_rows, head_count, HD), f32)
        grad_query = blockwise(
            query_start,
            (
                lax.all_gather(key_low, "fsdp", axis=0, tiled=True),
                lax.all_gather(value_low, "fsdp", axis=0, tiled=True),
            ),
            jnp.int32(0),
            query_step,
        )
        stat_total, stat_delta = (
            lax.all_gather(jnp.transpose(log_total), "fsdp", axis=0, tiled=True),
            lax.all_gather(delta_rows, "fsdp", axis=0, tiled=True),
        )

        def key_step(running, piece_parts, offset):
            grad_key, grad_value = running
            query_part, dmix_part = piece_parts
            piece_len = query_part.shape[0]
            piece_seg, _ = seq_info(lax.dynamic_slice_in_dim(perm_row, offset, piece_len), seq_lens)
            total_part = jnp.transpose(lax.dynamic_slice_in_dim(stat_total, offset, piece_len))
            delta_part = jnp.transpose(lax.dynamic_slice_in_dim(stat_delta, offset, piece_len))
            scores = (
                jnp.einsum("qhe,khe->hqk", query_part, key_low, preferred_element_type=f32)
                * score_scale
            )
            same_seq = (piece_seg[:, None] == query_seg[None, :])[None]
            weights = jnp.where(same_seq, jnp.exp(scores - total_part[..., None]), 0.0)
            d_weights = jnp.einsum("qhe,khe->hqk", dmix_part, value_low, preferred_element_type=f32)
            d_scores = (weights * (d_weights - delta_part[..., None])).astype(bf16)
            grad_key = grad_key + score_scale * jnp.einsum(
                "hqk,qhe->khe", d_scores, query_part, preferred_element_type=f32
            )
            grad_value = grad_value + jnp.einsum(
                "hqk,qhe->khe", weights.astype(bf16), dmix_part, preferred_element_type=f32
            )
            return (grad_key, grad_value)

        grad_key, grad_value = blockwise(
            (
                jnp.zeros((tok_rows, head_count, HD), f32),
                jnp.zeros((tok_rows, head_count, HD), f32),
            ),
            (
                lax.all_gather(query_low, "fsdp", axis=0, tiled=True),
                lax.all_gather(d_mixed, "fsdp", axis=0, tiled=True),
            ),
            jnp.int32(0),
            key_step,
        )
        _, rope_pull = jax.vjp(lambda heads_in: rotate(heads_in, cosine, sine), raw_heads[:, 0])
        d_raw_query = rope_pull(grad_query)[0]
        d_raw_key = rope_pull(grad_key)[0]
        d_raw = (
            jnp.stack([d_raw_query, d_raw_key, grad_value], axis=1)
            .reshape(tok_rows, 3, head_cols)
            .astype(bf16)
        )
        acc_qkv = acc_qkv + jnp.einsum("td,tcf->dcf", normed_low, d_raw, preferred_element_type=f32)
        first_part = jnp.einsum("tcf,dcf->td", d_raw, again[2], preferred_element_type=f32)
        d_norm_one = lax.psum(first_part.astype(jnp.bfloat16), "tp").astype(jnp.float32)
        _, first_pull = jax.vjp(layer_norm, x_float, gain_first)
        d_x_norm, d_gain_one = first_pull(d_norm_one)
        acc_gain_one = acc_gain_one + d_gain_one
        d_input = (d_hidden + d_x_norm).astype(bf16)
        back_rows = d_input[recv_order].reshape(groups, per_pair, D)
        returned = lax.all_to_all(
            back_rows, "fsdp", split_axis=0, concat_axis=0, tiled=True
        ).reshape(tok_rows, D)
        send_slot = jnp.zeros((tok_rows,), jnp.int32).at[send_order].set(rows_idx)
        input_grads.append(returned[send_slot])
    summed = (
        lax.psum_scatter(acc_qkv, "fsdp", scatter_dimension=0, tiled=True),
        lax.psum_scatter(acc_out, "fsdp", scatter_dimension=0, tiled=True),
        lax.psum_scatter(acc_in, "fsdp", scatter_dimension=0, tiled=True),
        lax.psum_scatter(acc_down, "fsdp", scatter_dimension=0, tiled=True),
        lax.psum_scatter(acc_gain_one, "fsdp", scatter_dimension=0, tiled=True),
        lax.psum_scatter(acc_gain_two, "fsdp", scatter_dimension=0, tiled=True),
    )
    return (
        jnp.stack(outputs),
        jnp.stack(input_grads),
        summed[0],
        summed[1],
        summed[2],
        summed[3],
        summed[4],
        summed[5],
    )


JOIN = 2
FAR = -1e30
ORDER = (0, 2, 4, 6, 1, 3, 5, 7)
NT = (((1,), (1,)), ((), ()))
TN = (((0,), (0,)), ((), ()))
NN = (((1,), (0,)), ((), ()))
ROOM = 10 * 1024 * 1024


def partial(kernel, *given):
    return lambda *refs: kernel(*given, *refs)


def mm(left, right, dims):
    return lax.dot_general(left, right, dims, preferred_element_type=jnp.float32)


def hop(value, step):
    return lax.ppermute(value, "fsdp", [(i, i ^ step) for i in range(8)])


def twin(value):
    return lax.ppermute(value, "tp", [(i, i ^ 1) for i in range(4)])


def across(value):
    return lax.ppermute(value, "tp", [(i, i ^ 2) for i in range(4)])


def deal_out(value):
    return lax.all_to_all(value, "fsdp", 0, 0, tiled=True)


def after(value, *earlier):
    return lax.optimization_barrier((value,) + earlier)[0]


def sync(values):
    return lax.optimization_barrier(values)


def z_phase(shard):
    return [shard] + [hop(shard, step) for step in ORDER[1:4]]


def y_phase(shards):
    return [hop(one, 1) for one in shards]


def local_call(kernel, name, scalars, arrays, outs, scratch=(), shards=(), copies=8, far_in=(), far_out=()):
    shapes = [(one.shape, one.dtype) for one in arrays]
    staged = [shapes[at] for at in far_in] + [outs[at] for at in far_out]
    sems = [pltpu.SemaphoreType.DMA((copies,))] if shards else []
    room = ROOM + sum(math.prod(shape) * jnp.dtype(kind).itemsize for shape, kind in [*shapes, *outs, *scratch])
    counts = (len(scalars), len(arrays), len(shards), len(outs), len(scratch) + len(sems))

    def body(*refs):
        groups = []
        for count in counts:
            groups.append(list(refs[:count]))
            refs = refs[count:]
        given, ins, pieces, results, extra = groups
        if not staged:
            return kernel(*given, *ins, *pieces, *results, *extra)
        stage, sem = refs[:-1], refs[-1]
        incoming, outgoing = [], []
        for slot, at in enumerate(far_in):
            incoming.append(pltpu.make_async_copy(ins[at], stage[slot], sem.at[slot]))
            incoming[-1].start()
            ins[at] = stage[slot]
        for slot, at in enumerate(far_out, len(far_in)):
            outgoing.append(pltpu.make_async_copy(stage[slot], results[at], sem.at[slot]))
            results[at] = stage[slot]
        for copy in incoming:
            copy.wait()
        kernel(*given, *ins, *pieces, *results, *extra)
        for copy in outgoing:
            copy.start()
        for copy in outgoing:
            copy.wait()

    def space(at, far):
        return pl.BlockSpec(memory_space=pltpu.HBM if at in far else pltpu.VMEM)

    result = pl.pallas_call(
        body,
        in_specs=[pl.BlockSpec(memory_space=pltpu.SMEM)] * len(scalars)
        + [space(at, far_in) for at in range(len(arrays))]
        + [pl.BlockSpec(memory_space=pl.ANY)] * len(shards),
        out_specs=[space(at, far_out) for at in range(len(outs))],
        out_shape=[jax.ShapeDtypeStruct(shape, kind) for shape, kind in outs],
        scratch_shapes=[pltpu.VMEM(shape, kind) for shape, kind in scratch]
        + sems
        + [pltpu.VMEM(shape, kind) for shape, kind in staged]
        + ([pltpu.SemaphoreType.DMA((len(staged),))] if staged else []),
        compiler_params=pltpu.CompilerParams(vmem_limit_bytes=room),
        name=name,
    )(*scalars, *arrays, *shards)
    return result if len(outs) > 1 else result[0]


def block_at(order_ref, place, width):
    return pl.ds(pl.multiple_of(order_ref[place] * width, width), width)


def shard_copies(shards, low, high, into_ref, sem_ref, base=0):
    width = shards[0].shape[1]
    copies = []
    for place, shard in enumerate(shards):
        span = pl.ds(place * width, width)
        source = shard.at[pl.ds(low, high - low), :]
        copies.append(pltpu.make_async_copy(source, into_ref.at[:, span], sem_ref.at[base + place]))
        copies[-1].start()
    return copies


def gathered_copies(order_ref, source, low, high, into_ref, sem_ref):
    width = source.shape[2]
    copies = []
    for place in range(8):
        copies.append(
            pltpu.make_async_copy(
                source.at[order_ref[place], pl.ds(low, high - low), :],
                into_ref.at[:, pl.ds(place * width, width)],
                sem_ref.at[place],
            )
        )
        copies[-1].start()
    return copies


def finish(copies):
    for copy in copies:
        copy.wait()


def project_kernel(order_ref, x_ref, table_ref, *refs):
    shards = refs[:8]
    norm_ref, gains_ref, send_ref, w_ref, sem_ref = refs[8:]
    width = shards[0].shape[1]
    rows = x_ref.shape[1]
    wide = w_ref.shape[0] - 16
    heads = wide // (3 * HD)
    half = HD // 2
    finish(shard_copies(shards, 0, wide + 16, w_ref, sem_ref))
    gains_ref[...] = w_ref[wide:, :].astype(jnp.float32)[:2]
    for micro in range(2):
        x = x_ref[micro].astype(jnp.float32)
        mean = jnp.mean(x, axis=-1, keepdims=True)
        center = x - mean
        spread = lax.rsqrt(jnp.mean(center * center, axis=-1, keepdims=True) + EPS)
        for place in range(8):
            piece = x_ref[micro, :, block_at(order_ref, place, width)].astype(jnp.float32)
            span = slice(place * width, (place + 1) * width)
            value = (piece - mean) * spread * gains_ref[0:1, span]
            norm_ref[micro * rows : (micro + 1) * rows, span] = value.astype(jnp.bfloat16)
    raw = mm(w_ref[:wide, :], norm_ref[...], NT)
    cosine, sine = table_ref[:half, :], table_ref[half:, :]
    for head in range(heads):
        base = head * 3 * HD
        for kind in range(2):
            upper = raw[base + kind * HD : base + kind * HD + half]
            lower = raw[base + kind * HD + half : base + (kind + 1) * HD]
            first = (upper * cosine - lower * sine).astype(jnp.bfloat16)
            second = (lower * cosine + upper * sine).astype(jnp.bfloat16)
            for micro in range(2):
                span = slice(micro * rows, (micro + 1) * rows)
                send_ref[micro * heads + head, kind * HD : kind * HD + half, :] = first[:, span]
                send_ref[micro * heads + head, kind * HD + half : (kind + 1) * HD, :] = second[:, span]
        value = raw[base + 2 * HD : base + 3 * HD].astype(jnp.bfloat16)
        for micro in range(2):
            send_ref[micro * heads + head, 2 * HD :, :] = value[:, micro * rows : (micro + 1) * rows]


def key_range(lens_ref, low, high):
    first = jnp.int32(0)
    last = jnp.int32(0)
    total = jnp.int32(0)
    for index in range(lens_ref.shape[0]):
        start = total
        total = total + lens_ref[index]
        first = jnp.where((start <= low) & (low < total), start, first)
        last = jnp.where((start <= high) & (high < total), total, last)
    return first, last


def query_bounds(lens_ref, base, width):
    place = base + lax.broadcasted_iota(jnp.int32, (1, width), 1)
    first = jnp.zeros((1, width), jnp.int32)
    last = jnp.zeros((1, width), jnp.int32)
    total = jnp.int32(0)
    for index in range(lens_ref.shape[0]):
        start = total
        total = total + lens_ref[index]
        inside = (place >= start) & (place < total)
        first = jnp.where(inside, start, first)
        last = jnp.where(inside, total, last)
    return first, last


def lanes(ref, index, count, rows):
    return jnp.concatenate([ref[index * count + at, rows, :] for at in range(count)], axis=1)


def attend_kernel(lens_ref, qkv_ref, mixed_ref, exact_ref, log_ref, key_ref):
    blocks, _, small = qkv_ref.shape
    wide = JOIN * small
    for at in range(blocks):
        block = qkv_ref[at, HD : 2 * HD, :].astype(jnp.float32)
        key_ref[at * small : (at + 1) * small, :] = jnp.transpose(block).astype(jnp.bfloat16)

    def one_query(index, carry):
        base = index * wide
        first, last = key_range(lens_ref, base, base + wide - 1)
        low, high = query_bounds(lens_ref, base, wide)
        query = lanes(qkv_ref, index, JOIN, slice(0, HD)) * jnp.bfloat16(HD**-0.5)

        def one_key(at, state):
            peak, total, acc = state
            start = pl.multiple_of(at * wide, wide)
            scores = mm(key_ref[pl.ds(start, wide), :], query, NN)
            place = start + lax.broadcasted_iota(jnp.int32, (wide, wide), 0)
            scores = jnp.where((place >= low) & (place < high), scores, FAR)
            top = jnp.maximum(peak, jnp.max(scores, axis=0, keepdims=True))
            weights = jnp.exp(scores - top)
            fade = jnp.exp(peak - top)
            total = total * fade + jnp.sum(weights, axis=0, keepdims=True)
            value = lanes(qkv_ref, at, JOIN, slice(2 * HD, 3 * HD))
            acc = acc * fade + mm(value, weights.astype(jnp.bfloat16), NN)
            return top, total, acc

        peak, total, acc = lax.fori_loop(
            first // wide,
            (last + wide - 1) // wide,
            one_key,
            (
                jnp.full((1, wide), FAR, jnp.float32),
                jnp.zeros((1, wide), jnp.float32),
                jnp.zeros((HD, wide), jnp.float32),
            ),
        )
        result = acc / total
        logs = peak + jnp.log(total)
        for at in range(JOIN):
            span = slice(at * small, (at + 1) * small)
            mixed_ref[index * JOIN + at] = result[:, span].astype(jnp.bfloat16)
            exact_ref[index * JOIN + at] = result[:, span]
            log_ref[index * JOIN + at] = logs[:, span]
        return carry

    lax.fori_loop(0, blocks // JOIN, one_query, 0)


def attend_back_kernel(
    lens_ref, qkv_ref, exact_ref, log_ref, grad_ref, table_ref, raw_ref, pair_ref, dkey_ref, dvalue_ref
):
    blocks, _, small = qkv_ref.shape
    wide = JOIN * small
    half = HD // 2
    for at in range(blocks):
        block = qkv_ref[at, HD : 3 * HD, :].astype(jnp.float32)
        pair_ref[at * small : (at + 1) * small, :] = jnp.transpose(block).astype(jnp.bfloat16)
    dkey_ref[...] = jnp.zeros(dkey_ref.shape, jnp.float32)
    dvalue_ref[...] = jnp.zeros(dvalue_ref.shape, jnp.float32)

    def unturn(index, grad):
        cosine = table_ref[index, :half, :]
        sine = table_ref[index, half:, :]
        upper, lower = grad[:half], grad[half:]
        return upper * cosine + lower * sine, lower * cosine - upper * sine

    def one_query(index, carry):
        base = index * wide
        first, last = key_range(lens_ref, base, base + wide - 1)
        low, high = query_bounds(lens_ref, base, wide)
        query = lanes(qkv_ref, index, JOIN, slice(0, HD)) * jnp.bfloat16(HD**-0.5)
        grad = lanes(grad_ref, index, JOIN, slice(0, HD))
        logs = lanes(log_ref, index, JOIN, slice(0, 1))
        exact = lanes(exact_ref, index, JOIN, slice(0, HD))
        delta = jnp.sum(grad.astype(jnp.float32) * exact, axis=0, keepdims=True)

        def one_key(at, dquery):
            start = pl.multiple_of(at * wide, wide)
            span = pl.ds(start, wide)
            scores = mm(pair_ref[span, :HD], query, NN)
            dweights = mm(pair_ref[span, HD:], grad, NN)
            place = start + lax.broadcasted_iota(jnp.int32, (wide, wide), 0)
            weights = jnp.where((place >= low) & (place < high), jnp.exp(scores - logs), 0.0)
            dscores = (weights * (dweights - delta)).astype(jnp.bfloat16)
            dkey_ref[:, span] += mm(query, dscores, NT)
            dvalue_ref[:, span] += mm(grad, weights.astype(jnp.bfloat16), NT)
            return dquery + mm(lanes(qkv_ref, at, JOIN, slice(HD, 2 * HD)), dscores, NN)

        dquery = lax.fori_loop(
            first // wide,
            (last + wide - 1) // wide,
            one_key,
            jnp.zeros((HD, wide), jnp.float32),
        ) * (HD**-0.5)
        for at in range(JOIN):
            upper, lower = unturn(index * JOIN + at, dquery[:, at * small : (at + 1) * small])
            raw_ref[index * JOIN + at, :half, :] = upper.astype(jnp.bfloat16)
            raw_ref[index * JOIN + at, half:HD, :] = lower.astype(jnp.bfloat16)
        return carry

    lax.fori_loop(0, blocks // JOIN, one_query, 0)
    for at in range(blocks):
        span = slice(at * small, (at + 1) * small)
        upper, lower = unturn(at, dkey_ref[:, span])
        raw_ref[at, HD : HD + half, :] = upper.astype(jnp.bfloat16)
        raw_ref[at, HD + half : 2 * HD, :] = lower.astype(jnp.bfloat16)
        raw_ref[at, 2 * HD :, :] = dvalue_ref[:, span].astype(jnp.bfloat16)


def mix_out_kernel(core_ref, order_ref, mixed_ref, all_ref, send_ref, keep_ref, w_ref, sem_ref):
    last = all_ref.shape[1]
    finish(gathered_copies(order_ref, all_ref, last - mixed_ref.shape[1], last, w_ref, sem_ref))
    core = core_ref[0]
    send_ref[...] = mm(mixed_ref[1 - core], w_ref[...], TN).astype(jnp.bfloat16)
    keep_ref[...] = mm(mixed_ref[core], w_ref[...], TN)


def norm_two_kernel(core_ref, order_ref, x_ref, half_ref, far_ref, gains_ref, hidden_ref, norm_ref):
    core = core_ref[0]
    width = x_ref.shape[2] // 8
    for place in range(8):
        span = slice(place * width, (place + 1) * width)
        piece = x_ref[core, :, block_at(order_ref, place, width)].astype(jnp.float32)
        branch = half_ref[:, span].astype(jnp.float32) + far_ref[:, span].astype(jnp.float32)
        hidden_ref[:, span] = piece + branch
    hidden = hidden_ref[...]
    center = hidden - jnp.mean(hidden, axis=-1, keepdims=True)
    spread = lax.rsqrt(jnp.mean(center * center, axis=-1, keepdims=True) + EPS)
    norm_ref[...] = (center * spread * gains_ref[1:2, :]).astype(jnp.bfloat16)


def feed_kernel(
    order_ref, own_ref, other_ref, grad_ref, all_ref, send_ref, keep_ref, act_ref, dinp_ref, dgate_ref, w_ref, sem_ref
):
    units = w_ref.shape[0] // 3
    inp_w, gate_w, down_w = [w_ref.at[pl.ds(at * units, units), :] for at in range(3)]
    rows = own_ref.shape[0]
    finish(gathered_copies(order_ref, all_ref, 0, 3 * units, w_ref, sem_ref))
    for micro, norm_ref in ((1, other_ref), (0, own_ref)):
        span = slice(micro * rows, (micro + 1) * rows)
        inp = mm(norm_ref[...], inp_w[...], NT)
        gate = mm(norm_ref[...], gate_w[...], NT)
        dact = mm(grad_ref[micro], down_w[...], NT)
        cdf = 0.5 * (1.0 + lax.erf(inp * (0.5**0.5)))
        density = jnp.exp(-0.5 * inp * inp) * ((0.5 / jnp.pi) ** 0.5)
        gelu = inp * cdf
        act_ref[span, :] = (gelu * gate).astype(jnp.bfloat16)
        dinp = (dact * gate * (cdf + inp * density)).astype(jnp.bfloat16)
        dgate = (dact * gelu).astype(jnp.bfloat16)
        dinp_ref[span, :] = dinp
        dgate_ref[span, :] = dgate
        part = mm(dinp, inp_w[...], NN) + mm(dgate, gate_w[...], NN)
        if micro:
            send_ref[...] = part.astype(jnp.bfloat16)
        else:
            keep_ref[...] = part


def weight_grad_kernel(order_ref, dinp_ref, dgate_ref, act_ref, own_ref, other_ref, grad_ref, out_ref):
    units = act_ref.shape[1]
    rows = own_ref.shape[0]
    width = out_ref.shape[2]
    for at, (left_ref, rights) in enumerate((
        (dinp_ref, (own_ref, other_ref)),
        (dgate_ref, (own_ref, other_ref)),
        (act_ref, (grad_ref.at[0], grad_ref.at[1])),
    )):
        total = mm(left_ref[:rows, :], rights[0][...], TN) + mm(left_ref[rows:, :], rights[1][...], TN)
        for place in range(8):
            piece = total[:, place * width : (place + 1) * width].astype(jnp.bfloat16)
            out_ref[order_ref[place], at * units : (at + 1) * units, :] = piece


def near_sum_kernel(near_ref, far_ref, own_ref, *low_refs):
    own_ref[...] = near_ref[0] + far_ref[0].astype(jnp.float32)
    for at, low_ref in enumerate(low_refs):
        low_ref[...] = (near_ref[at + 1] + far_ref[at + 1].astype(jnp.float32)).astype(jnp.bfloat16)


def down_kernel(order_ref, act_ref, all_ref, send_ref, keep_ref, w_ref, sem_ref):
    rows = send_ref.shape[0]
    units = w_ref.shape[0]
    finish(gathered_copies(order_ref, all_ref, 2 * units, 3 * units, w_ref, sem_ref))
    send_ref[...] = mm(act_ref[rows:, :], w_ref[...], NN).astype(jnp.bfloat16)
    keep_ref[...] = mm(act_ref[:rows, :], w_ref[...], NN)


def norm_two_back_kernel(hidden_ref, half_ref, far_ref, grad_ref, gains_ref, dhidden_ref, low_ref):
    hidden = hidden_ref[...]
    center = hidden - jnp.mean(hidden, axis=-1, keepdims=True)
    spread = lax.rsqrt(jnp.mean(center * center, axis=-1, keepdims=True) + EPS)
    xhat = center * spread
    dnorm = half_ref[...].astype(jnp.float32) + far_ref[...].astype(jnp.float32)
    scaled = dnorm * gains_ref[1:2, :]
    inner = scaled - jnp.mean(scaled, axis=-1, keepdims=True)
    inner = inner - xhat * jnp.mean(scaled * xhat, axis=-1, keepdims=True)
    total = grad_ref[0].astype(jnp.float32) + inner * spread
    dhidden_ref[...] = total
    low_ref[...] = total.astype(jnp.bfloat16)


def mix_back_kernel(core_ref, own_ref, other_ref, w_ref, send_ref):
    cols = w_ref.shape[0]
    heads = cols // HD
    core = core_ref[0]
    for micro, low_ref in ((core, own_ref), (1 - core, other_ref)):
        total = mm(w_ref[...], low_ref[...], NT).astype(jnp.bfloat16)
        for head in range(heads):
            send_ref[micro * heads + head] = total[head * HD : (head + 1) * HD, :]


def mix_grad_kernel(core_ref, mixed_ref, own_ref, other_ref, far_ref, near_ref):
    core = core_ref[0]
    width = far_ref.shape[2]
    total = mm(mixed_ref[core], own_ref[...], NN) + mm(mixed_ref[1 - core], other_ref[...], NN)
    for place in range(4):
        near_ref[place] = total[:, place * width : (place + 1) * width]
        far_ref[place] = total[:, (4 + place) * width : (5 + place) * width].astype(jnp.bfloat16)


def project_back_kernel(core_ref, raw_ref, w_ref, send_ref, keep_ref):
    core = core_ref[0]
    weights = w_ref[: raw_ref.shape[1], :]
    send_ref[...] = mm(raw_ref[1 - core], weights, TN).astype(jnp.bfloat16)
    keep_ref[...] = mm(raw_ref[core], weights, TN)


def project_grad_kernel(first, raw_ref, norm_ref, far_ref, near_ref):
    count, width = far_ref.shape[1:]
    rows = raw_ref.shape[2]
    span = slice(first, first + count)
    total = mm(raw_ref[0, span, :], norm_ref[:rows, :], NN) + mm(raw_ref[1, span, :], norm_ref[rows:, :], NN)
    for place in range(4):
        near_ref[place] = total[:, place * width : (place + 1) * width]
        far_ref[place] = total[:, (4 + place) * width : (5 + place) * width].astype(jnp.bfloat16)


def norm_one_back_kernel(
    core_ref, order_ref, x_ref, half_ref, far_ref, dhidden_ref, gains_ref, grad_ref, xhat_ref
):
    core = core_ref[0]
    width = x_ref.shape[2] // 8
    x = x_ref[core].astype(jnp.float32)
    mean = jnp.mean(x, axis=-1, keepdims=True)
    center = x - mean
    spread = lax.rsqrt(jnp.mean(center * center, axis=-1, keepdims=True) + EPS)
    for place in range(8):
        span = slice(place * width, (place + 1) * width)
        piece = x_ref[core, :, block_at(order_ref, place, width)].astype(jnp.float32)
        xhat_ref[:, span] = (piece - mean) * spread
    xhat = xhat_ref[...]
    dnorm = half_ref[...].astype(jnp.float32) + far_ref[...].astype(jnp.float32)
    scaled = dnorm * gains_ref[0:1, :]
    inner = scaled - jnp.mean(scaled, axis=-1, keepdims=True)
    inner = inner - xhat * jnp.mean(scaled * xhat, axis=-1, keepdims=True)
    total = (dhidden_ref[...] + inner * spread).astype(jnp.bfloat16)
    for place in range(8):
        grad_ref[:, block_at(order_ref, place, width)] = total[:, place * width : (place + 1) * width]


def place_grad_kernel(core_ref, order_ref, local_ref, four_ref, grad_ref, natural_ref):
    rows = grad_ref.shape[1]
    width = grad_ref.shape[2] // 8
    core = core_ref[0]
    for at in range(2):
        micro = core if at == 0 else 1 - core
        place = lax.broadcasted_iota(jnp.int32, (rows, rows), 0)
        onehot = jnp.where(local_ref[pl.ds(micro, 1), :] == place, 1.0, 0.0).astype(jnp.bfloat16)
        natural_ref[...] = mm(onehot, four_ref[micro], NN).astype(jnp.bfloat16)
        for block in range(8):
            span = slice(block * width, (block + 1) * width)
            grad_ref[at, :, span] = natural_ref[:, block_at(order_ref, block, width)]


def result_kernel(order_ref, picks_ref, hidden_ref, half_ref, far_ref, packed_ref, natural_ref):
    rows = hidden_ref.shape[0]
    width = hidden_ref.shape[1] // 8
    branch = half_ref[...].astype(jnp.float32) + far_ref[...].astype(jnp.float32)
    total = (hidden_ref[...] + branch).astype(jnp.bfloat16)
    for block in range(8):
        natural_ref[:, block_at(order_ref, block, width)] = total[:, block * width : (block + 1) * width]
    count = packed_ref.shape[0]
    place = lax.broadcasted_iota(jnp.int32, (rows, count), 0)
    onehot = jnp.where(picks_ref[...] == place, 1.0, 0.0).astype(jnp.bfloat16)
    packed_ref[...] = mm(onehot, natural_ref[...], TN).astype(jnp.bfloat16)


def positions(anchor, seq_lens):
    ends = running_ends(seq_lens)
    starts = ends - seq_lens
    inside = (anchor[:, None] >= starts[None, :]) & (anchor[:, None] < ends[None, :])
    return anchor - jnp.sum(jnp.where(inside, starts[None, :], 0), axis=1)


def turn_tables(place):
    freqs = jnp.power(THETA, -jnp.arange(HD // 2, dtype=jnp.float32) * 2.0 / HD)
    angle = freqs[:, None] * place.astype(jnp.float32)[None, :]
    return jnp.concatenate([jnp.cos(angle), jnp.sin(angle)], axis=0)


def paired_layer(
    tokens, cotangent, perm, lengths, w_qkv, w_attn_out, w_in, w_down, gain_one, gain_two
):
    f32, bf16, i32 = jnp.float32, jnp.bfloat16, jnp.int32
    mine = lax.axis_index("fsdp")
    part = lax.axis_index("tp")
    core, side = part & 1, part >> 1
    core_at = core.reshape(1).astype(i32)
    rows = tokens.shape[1]
    width = w_qkv.shape[0]
    full = 8 * width
    cols = w_qkv.shape[2]
    heads = cols // HD
    units = w_in.shape[2]
    per_pair = rows // 8
    order = jnp.bitwise_xor(jnp.array(ORDER, i32), mine)

    def pick(value, index):
        return lax.dynamic_index_in_dim(value, index, 0, keepdims=False)

    def both(value, other):
        return jnp.stack([jnp.where(core == 0, value, other), jnp.where(core == 0, other, value)])

    def add_half(keep, got):
        return (keep + got.astype(f32)).astype(bf16)

    def near_sum(near, far, name):
        shape = near.shape[1:]
        own, *lows = local_call(near_sum_kernel, name, (), (near, far), [(shape, f32)] + [(shape, bf16)] * 3, far_in=(0, 1), far_out=(0,))
        return own, lows

    def y_join(same):
        return same + [hop(jnp.concatenate(same, axis=0), 1)]

    def z_send(lows):
        return [hop(low, ORDER[at + 1]) for at, low in enumerate(lows)]

    def far_sum(own, got):
        return own + sum(one.astype(f32) for one in got)

    turned = jnp.transpose(w_qkv.reshape(width, 3, heads, HD), (2, 1, 3, 0)).reshape(3 * cols, width)
    gains_rows = jnp.concatenate([gain_one[None], gain_two[None], jnp.zeros((14, width), bf16)])
    first_same = z_phase(jnp.concatenate([turned, gains_rows], axis=0))
    first = first_same + y_phase(first_same)

    slots = perm.reshape(2, 8, rows)
    from_me = (slots // rows == mine).astype(f32)
    slot_no = jnp.arange(rows, dtype=i32)
    before = (slot_no[:, None] < slot_no[None, :]).astype(f32)
    rank_me = jnp.einsum("mds,st->mdt", from_me, before).astype(i32)
    ranks = jnp.arange(per_pair, dtype=i32)
    chosen = (from_me[..., None] > 0) & (rank_me[..., None] == ranks)
    local = jnp.sum(jnp.where(chosen, (slots % rows)[..., None], 0), axis=2)
    my_slots = lax.dynamic_index_in_dim(slots, mine, 1, keepdims=False)
    target = my_slots // rows
    same = (target[:, :, None] == target[:, None, :]) & (slot_no[:, None] < slot_no[None, :])[None]
    rank_own = jnp.sum(same.astype(i32), axis=1)
    place_own = target * per_pair + rank_own
    quarter = per_pair // 4
    wanted = jnp.arange(8, dtype=i32)[:, None] * per_pair + part * quarter
    wanted = (wanted + jnp.arange(quarter, dtype=i32)[None, :]).reshape(-1)
    packer = (place_own[:, None, :] == wanted[None, :, None]).astype(bf16)
    packed = jnp.einsum("mps,msd->mpd", packer, cotangent, preferred_element_type=f32).astype(bf16)
    packed = jnp.transpose(packed.reshape(2, 8, quarter, full), (1, 0, 2, 3))
    anchor = mine * rows + jnp.arange(rows, dtype=i32)
    own_table = jnp.concatenate([turn_tables(positions(anchor, lengths[m])) for m in range(2)], axis=1)
    inp_turned, gate_turned = jnp.transpose(w_in[:, 0]), jnp.transpose(w_in[:, 1])
    second = jnp.concatenate([inp_turned, gate_turned, jnp.transpose(w_down), jnp.transpose(w_attn_out)], axis=0)
    second_all = lax.all_gather(second, "fsdp", axis=0, tiled=False)
    halfway = per_pair // 2
    picks = lax.dynamic_slice_in_dim(pick(local, core), side * halfway, halfway, 1).reshape(1, -1)
    unpack = (place_own[:, :, None] == slot_no[None, None, :]).astype(bf16)
    my_lens = lengths[mine // heads]
    all_anchor = jnp.arange(8 * rows, dtype=i32)
    table = turn_tables(positions(all_anchor, my_lens))
    table = jnp.transpose(table.reshape(HD, 8, rows), (1, 0, 2))
    arrived = deal_out(packed)
    first, arrived, own_table, picks, unpack, table, local, order, core_at, core, side, my_lens = sync(
        (first, arrived, own_table, picks, unpack, table, local, order, core_at, core, side, my_lens)
    )

    norm_one, gains, outgoing, qkv_w = local_call(
        project_kernel, "project", (order,), (tokens, own_table),
        [((2 * rows, full), bf16), ((2, full), f32), ((2 * heads, 3 * HD, rows), bf16), ((3 * cols + 16, full), bf16)],
        (), first, far_in=(0, 1), far_out=(0, 1, 2, 3),
    )
    near = twin(arrived)
    outgoing, near = sync((outgoing, near))
    qkv = deal_out(outgoing)
    pair = jnp.stack([jnp.where(core == 0, arrived, near), jnp.where(core == 0, near, arrived)])
    far = across(pair)
    qkv, far = sync((qkv, far))

    mixed_out, exact, logs = local_call(
        attend_kernel, "attend", (my_lens,), (qkv,),
        [((8, HD, rows), bf16), ((8, HD, rows), f32), ((8, 1, rows), f32)],
        [((8 * rows, HD), bf16)], far_in=(0,), far_out=(0, 1, 2),
    )
    mixed_out, far = sync((mixed_out, far))
    mixed = deal_out(mixed_out).reshape(2, cols, rows)
    four = jnp.concatenate([jnp.where(side == 0, pair, far), jnp.where(side == 0, far, pair)])
    four = jnp.transpose(four, (2, 1, 0, 3, 4)).reshape(2, rows, full)
    grad = local_call(
        place_grad_kernel, "place_grad", (core_at, order), (local.reshape(2, rows), four),
        [((2, rows, full), bf16)], [((rows, full), bf16)],
    )
    mixed, grad = sync((mixed, grad))

    send, keep, out_w = local_call(
        mix_out_kernel, "mix_out", (core_at, order), (mixed,),
        [((rows, full), bf16), ((rows, full), f32), ((cols, full), bf16)], (), (second_all,), far_in=(0,),
    )
    half = add_half(keep, twin(send))
    far = across(half)
    hidden, two_own = local_call(
        norm_two_kernel, "norm_two", (core_at, order), (tokens, half, far, gains),
        [((rows, full), f32), ((rows, full), bf16)], far_in=(0, 3),
    )
    two_other = twin(two_own)

    send, keep, act, d_inp, d_gate = local_call(
        feed_kernel, "feed", (order,), (two_own, two_other, grad),
        [((rows, full), bf16), ((rows, full), f32)] + [((2 * rows, units), bf16)] * 3,
        [((3 * units, full), bf16)], (second_all,),
    )
    half_two = add_half(keep, twin(send))
    half_two, act, d_inp, d_gate = sync((half_two, act, d_inp, d_gate))
    far_two = across(half_two)
    feed_grad = local_call(
        weight_grad_kernel, "feed_grad", (order,), (d_inp, d_gate, act, two_own, two_other, grad),
        [((8, 3 * units, width), bf16)], far_out=(0,),
    )
    feed_sum = lax.psum_scatter(feed_grad, "fsdp", scatter_dimension=0, tiled=False)
    far_two, feed_grad = sync((far_two, feed_grad))
    d_hidden, low_own = local_call(
        norm_two_back_kernel, "norm_two_back", (), (hidden, half_two, far_two, grad, gains),
        [((rows, full), f32), ((rows, full), bf16)], far_in=(4,), far_out=(0,),
    )
    low_other = twin(low_own)
    d_mixed = local_call(
        mix_back_kernel, "mix_back", (core_at,), (low_own, low_other, out_w),
        [((8, HD, rows), bf16)], far_out=(0,),
    )
    d_mixed, low_other, act = sync((d_mixed, low_other, act))
    grad_mixed = deal_out(d_mixed)
    send, keep = local_call(
        down_kernel, "down", (order,), (act,),
        [((rows, full), bf16), ((rows, full), f32)], [((units, full), bf16)], (second_all,),
    )
    res_half = add_half(keep, twin(send))
    grad_mixed, res_half = sync((grad_mixed, res_half))

    res_far = across(res_half)
    d_raw_out = local_call(
        attend_back_kernel, "attend_back", (my_lens,), (qkv, exact, logs, grad_mixed, table),
        [((8, 3 * HD, rows), bf16)],
        [((8 * rows, 2 * HD), bf16), ((HD, 8 * rows), f32), ((HD, 8 * rows), f32)],
        far_in=(0, 1, 2, 3, 4), far_out=(0,),
    )
    d_raw_out, res_far = sync((d_raw_out, res_far))
    d_raw = deal_out(d_raw_out).reshape(2, 3 * cols, rows)
    out_far, out_near = local_call(
        mix_grad_kernel, "mix_grad", (core_at,), (mixed, low_own, low_other),
        [((4, cols, width), bf16), ((4, cols, width), f32)], far_in=(0, 1, 2), far_out=(1,),
    )
    out_got = hop(out_far, 1)
    packed = local_call(
        result_kernel, "result", (order,), (picks, hidden, res_half, res_far),
        [((8 * halfway, full), bf16)], [((rows, full), bf16)], far_in=(1, 2, 3), far_out=(0,),
    )
    d_raw, out_got, packed = sync((d_raw, out_got, packed))

    qkv_far, qkv_near = local_call(
        partial(project_grad_kernel, 0), "project_grad", (), (d_raw, norm_one),
        [((4, 3 * cols, width), bf16), ((4, 3 * cols, width), f32)], far_in=(0, 1), far_out=(1,),
    )
    qkv_far, d_raw = sync((qkv_far, d_raw))
    qkv_got = hop(qkv_far, 1)
    send, keep = local_call(
        project_back_kernel, "project_back", (core_at,), (d_raw, qkv_w),
        [((rows, full), bf16), ((rows, full), f32)], far_in=(0, 1),
    )
    half = add_half(keep, twin(send))
    half, packed, out_got = sync((half, packed, out_got))
    far = across(half)
    arrived = deal_out(packed.reshape(8, halfway, full))
    out_own, out_lows = near_sum(out_near, out_got, "out_near")
    out_got = z_send(out_lows)
    qkv_got, far, arrived, out_got = sync((qkv_got, far, arrived, out_got))
    qkv_own, qkv_lows = near_sum(qkv_near, qkv_got, "qkv_near")
    qkv_got = z_send(qkv_lows)
    input_own = local_call(
        norm_one_back_kernel, "norm_one_back", (core_at, order), (tokens, half, far, d_hidden, gains),
        [((rows, full), bf16)], [((rows, full), f32)], far_in=(0, 3, 4),
    )
    input_grad = both(input_own, twin(input_own))
    other_side = across(arrived)
    whole = jnp.concatenate(
        [jnp.where(side == 0, arrived, other_side), jnp.where(side == 0, other_side, arrived)], axis=1
    ).reshape(rows, full)
    whole = both(whole, twin(whole))
    output = jnp.einsum("msp,mpd->msd", unpack, whole, preferred_element_type=f32).astype(bf16)
    out_sum = far_sum(out_own, out_got)
    qkv_got, output, input_grad, out_sum = sync((qkv_got, output, input_grad, out_sum))
    qkv_sum = far_sum(qkv_own, qkv_got)
    inp_sum, gate_sum, down_sum = [feed_sum[at * units : (at + 1) * units].astype(f32) for at in range(3)]

    one_row = jnp.sum(qkv_sum * turned.astype(f32), axis=0) / gain_one.astype(f32)
    two_row = jnp.sum(inp_sum * inp_turned.astype(f32) + gate_sum * gate_turned.astype(f32), axis=0)
    gain_rows = jnp.stack([one_row, two_row / gain_two.astype(f32)])
    gain_rows = gain_rows + twin(gain_rows)
    gain_rows = gain_rows + across(gain_rows)
    return (
        output,
        input_grad,
        jnp.transpose(qkv_sum.reshape(heads, 3, HD, width), (3, 1, 0, 2)).reshape(width, 3, cols),
        jnp.transpose(out_sum),
        jnp.stack([jnp.transpose(inp_sum), jnp.transpose(gate_sum)], axis=1),
        jnp.transpose(down_sum),
        gain_rows[0],
        gain_rows[1],
    )


def on_device(*operands):
    micro_count, tok_rows = operands[0].shape[0], operands[0].shape[1]
    groups, parts = lax.axis_size("fsdp"), lax.axis_size("tp")
    heads = operands[4].shape[2] // HD
    if groups == 8 and parts == 4 and micro_count == 2 and micro_count * heads == groups and tok_rows % 256 == 0:
        return paired_layer(*operands)
    return general_layer(*operands)


def solution(mesh):
    placed = (
        P(None, "fsdp", None),
        P(None, "fsdp", None),
        P(),
        P(),
        P("fsdp", None, "tp"),
        P("fsdp", "tp"),
        P("fsdp", None, "tp"),
        P("fsdp", "tp"),
        P("fsdp"),
        P("fsdp"),
    )
    return jax.shard_map(
        on_device,
        mesh=mesh,
        in_specs=placed,
        out_specs=(
            P(None, "fsdp", None),
            P(None, "fsdp", None),
            P("fsdp", None, "tp"),
            P("fsdp", "tp"),
            P("fsdp", None, "tp"),
            P("fsdp", "tp"),
            P("fsdp"),
            P("fsdp"),
        ),
        check_vma=False,
    )
```

```python
import math

import jax
import jax.numpy as jnp
from jax import lax
from jax.experimental import pallas as pl
from jax.experimental.pallas import tpu as pltpu
from jax.sharding import PartitionSpec as P

D = 1024
HD = 64


EPS = 1e-05
THETA = 160000.0
key_block = 2048


def layer_norm(values, gain):
    center = values - jnp.mean(values, axis=-1, keepdims=True)
    spread = jnp.mean(center * center, axis=-1, keepdims=True)
    return center * lax.rsqrt(spread + EPS) * gain


def rope_tables(position, width):
    freqs = jnp.power(THETA, -jnp.arange(width // 2, dtype=jnp.float32) * 2.0 / width)
    angle = position.astype(jnp.float32)[:, None] * freqs[None, :]
    angle = jnp.concatenate([angle, angle], axis=-1)
    return (jnp.cos(angle), jnp.sin(angle))


def rotate(values, cosine, sine):
    half = values.shape[-1] // 2
    turned = jnp.concatenate([-values[..., half:], values[..., :half]], axis=-1)
    return values * cosine[:, None, :] + turned * sine[:, None, :]


def running_ends(seq_lens):
    order = jnp.arange(seq_lens.shape[0], dtype=jnp.int32)
    return jnp.sum(jnp.where(order[None, :] <= order[:, None], seq_lens[None, :], 0), axis=1)


def seq_info(anchor, seq_lens):
    ends = running_ends(seq_lens)
    starts = ends - seq_lens
    segment = jnp.sum((anchor[:, None] >= ends[None, :]).astype(jnp.int32), axis=1)
    onehot = segment[:, None] == jnp.arange(seq_lens.shape[0], dtype=jnp.int32)[None, :]
    position = anchor - jnp.sum(jnp.where(onehot, starts[None, :], 0), axis=1)
    return (segment, position)


def blockwise(running, pieces, offset, step_fn):
    piece_len = pieces[0].shape[0]
    if piece_len > key_block and piece_len % key_block == 0:
        block_count = piece_len // key_block
        stacked = tuple((one.reshape((block_count, key_block) + one.shape[1:]) for one in pieces))

        def inner(state_now, scan_item):
            block_index, piece_parts = scan_item
            return (step_fn(state_now, piece_parts, offset + block_index * key_block), None)

        running, _ = lax.scan(inner, running, (jnp.arange(block_count, dtype=jnp.int32), stacked))
        return running
    return step_fn(running, pieces, offset)


def general_layer(
    tokens, cotangent, perm, lengths, w_qkv, w_attn_out, w_in, w_down, gain_one, gain_two
):
    groups = lax.axis_size("fsdp")
    my_index = lax.axis_index("fsdp")
    micro_count = tokens.shape[0]
    tok_rows = tokens.shape[1]
    total_rows = tok_rows * groups
    per_pair = tok_rows // groups
    head_cols = w_qkv.shape[2]
    head_count = head_cols // HD
    unit_cols = w_in.shape[2]
    score_scale = HD ** (-0.5)
    rows_idx = jnp.arange(tok_rows, dtype=jnp.int32)
    f32 = jnp.float32
    bf16 = jnp.bfloat16
    dims_rows = (((0,), (0,)), ((), ()))
    dims_cols = (((1,), (1,)), ((), ()))
    acc_qkv = jnp.zeros((D, 3, head_cols), f32)
    acc_out = jnp.zeros((D, head_cols), f32)
    acc_in = jnp.zeros((D, 2, unit_cols), f32)
    acc_down = jnp.zeros((D, unit_cols), f32)
    acc_gain_one = jnp.zeros((D,), f32)
    acc_gain_two = jnp.zeros((D,), f32)
    outputs = []
    input_grads = []
    for micro_idx in range(micro_count):
        perm_row = perm[micro_idx]
        seq_lens = lengths[micro_idx]
        inverse = (
            jnp.zeros((total_rows,), jnp.int32)
            .at[perm_row]
            .set(jnp.arange(total_rows, dtype=jnp.int32))
        )
        placed = lax.dynamic_slice_in_dim(inverse, my_index * tok_rows, tok_rows)
        send_order = jnp.argsort(placed)
        outgoing = tokens[micro_idx][send_order].reshape(groups, per_pair, D)
        arrived = lax.all_to_all(outgoing, "fsdp", split_axis=0, concat_axis=0, tiled=True).reshape(
            tok_rows, D
        )
        my_tokens = lax.dynamic_slice_in_dim(perm_row, my_index * tok_rows, tok_rows)
        source = my_tokens // tok_rows
        recv_order = jnp.argsort(source * tok_rows + rows_idx)
        recv_slot = jnp.zeros((tok_rows,), jnp.int32).at[recv_order].set(rows_idx)
        dealt = arrived[recv_slot]
        fetched = (
            lax.all_gather(gain_one, "fsdp", axis=0, tiled=True),
            lax.all_gather(gain_two, "fsdp", axis=0, tiled=True),
            lax.all_gather(w_qkv, "fsdp", axis=0, tiled=True),
            lax.all_gather(w_attn_out, "fsdp", axis=0, tiled=True),
            lax.all_gather(w_in, "fsdp", axis=0, tiled=True),
            lax.all_gather(w_down, "fsdp", axis=0, tiled=True),
        )
        gain_first = fetched[0].astype(f32)
        gain_second = fetched[1].astype(f32)
        query_seg, query_pos = seq_info(my_tokens, seq_lens)
        cosine, sine = rope_tables(query_pos, HD)
        x_float = dealt.astype(f32)
        normed_low = layer_norm(x_float, gain_first).astype(bf16)
        raw_proj = jnp.einsum("td,dcf->tcf", normed_low, fetched[2], preferred_element_type=f32)
        raw_heads = raw_proj.reshape(tok_rows, 3, head_count, HD)
        query_low = rotate(raw_heads[:, 0], cosine, sine).astype(bf16)
        key_low = rotate(raw_heads[:, 1], cosine, sine).astype(bf16)
        value_low = raw_heads[:, 2].astype(bf16)

        def forward_step(running, piece_parts, offset):
            run_peak, run_total, run_acc = running
            key_part, value_part = piece_parts
            key_seg, _ = seq_info(
                lax.dynamic_slice_in_dim(perm_row, offset, key_part.shape[0]), seq_lens
            )
            scores = (
                jnp.einsum("qhe,khe->hqk", query_low, key_part, preferred_element_type=f32)
                * score_scale
            )
            same_seq = (query_seg[:, None] == key_seg[None, :])[None]
            block_top = jnp.max(jnp.where(same_seq, scores, -1e30), axis=-1)
            new_peak = jnp.maximum(run_peak, block_top)
            weights = jnp.where(same_seq, jnp.exp(scores - new_peak[..., None]), 0.0)
            fade_factor = jnp.exp(run_peak - new_peak)
            run_acc = run_acc * jnp.transpose(fade_factor)[:, :, None] + jnp.einsum(
                "hqk,khe->qhe", weights.astype(bf16), value_part, preferred_element_type=f32
            )
            run_total = run_total * fade_factor + jnp.sum(weights, axis=-1)
            return (new_peak, run_total, run_acc)

        start_state = (
            jnp.full((head_count, tok_rows), -1e30, f32),
            jnp.zeros((head_count, tok_rows), f32),
            jnp.zeros((tok_rows, head_count, HD), f32),
        )
        run_peak, run_total, run_acc = blockwise(
            start_state,
            (
                lax.all_gather(key_low, "fsdp", axis=0, tiled=True),
                lax.all_gather(value_low, "fsdp", axis=0, tiled=True),
            ),
            jnp.int32(0),
            forward_step,
        )
        log_total = run_peak + jnp.log(run_total)
        mixed_heads = run_acc / jnp.transpose(run_total)[:, :, None]
        mixed_low = mixed_heads.reshape(tok_rows, head_cols).astype(bf16)
        attn_part = lax.dot_general(mixed_low, fetched[3], dims_cols, preferred_element_type=f32)
        branch = lax.psum(attn_part.astype(jnp.bfloat16), "tp").astype(jnp.float32)
        hidden = x_float + branch
        normed_two = layer_norm(hidden, gain_second).astype(bf16)
        ffn_proj = jnp.einsum("td,dcf->tcf", normed_two, fetched[4], preferred_element_type=f32)
        act_low = (jax.nn.gelu(ffn_proj[:, 0], approximate=False) * ffn_proj[:, 1]).astype(bf16)
        ffn_part = lax.dot_general(act_low, fetched[5], dims_cols, preferred_element_type=f32)
        branch_two = lax.psum(ffn_part.astype(jnp.bfloat16), "tp").astype(jnp.float32)
        outputs.append((hidden + branch_two).astype(bf16))
        again = (
            lax.all_gather(gain_one, "fsdp", axis=0, tiled=True),
            lax.all_gather(gain_two, "fsdp", axis=0, tiled=True),
            lax.all_gather(w_qkv, "fsdp", axis=0, tiled=True),
            lax.all_gather(w_attn_out, "fsdp", axis=0, tiled=True),
            lax.all_gather(w_in, "fsdp", axis=0, tiled=True),
            lax.all_gather(w_down, "fsdp", axis=0, tiled=True),
        )
        gain_first = again[0].astype(f32)
        gain_second = again[1].astype(f32)
        grad_low = cotangent[micro_idx]
        grad_float = grad_low.astype(f32)
        acc_down = acc_down + lax.dot_general(
            grad_low, act_low, dims_rows, preferred_element_type=f32
        )
        d_act = jnp.dot(grad_low, again[5], preferred_element_type=f32)
        _, gelu_pull = jax.vjp(
            lambda inputs, gates: jax.nn.gelu(inputs, approximate=False) * gates,
            ffn_proj[:, 0],
            ffn_proj[:, 1],
        )
        d_inputs, d_gates = gelu_pull(d_act)
        d_proj = jnp.stack([d_inputs, d_gates], axis=1).astype(bf16)
        acc_in = acc_in + jnp.einsum("td,tcf->dcf", normed_two, d_proj, preferred_element_type=f32)
        norm_part = jnp.einsum("tcf,dcf->td", d_proj, again[4], preferred_element_type=f32)
        d_norm_two = lax.psum(norm_part.astype(jnp.bfloat16), "tp").astype(jnp.float32)
        _, second_pull = jax.vjp(layer_norm, hidden, gain_second)
        d_hid_norm, d_gain_two = second_pull(d_norm_two)
        acc_gain_two = acc_gain_two + d_gain_two
        d_hidden = grad_float + d_hid_norm
        hidden_low = d_hidden.astype(bf16)
        acc_out = acc_out + lax.dot_general(
            hidden_low, mixed_low, dims_rows, preferred_element_type=f32
        )
        d_mixed = jnp.dot(hidden_low, again[3], preferred_element_type=f32).astype(bf16)
        d_mixed = d_mixed.reshape(tok_rows, head_count, HD)
        delta_rows = jnp.sum(d_mixed.astype(f32) * mixed_heads, axis=-1)
        delta_heads = jnp.transpose(delta_rows)

        def query_step(grad_query, piece_parts, offset):
            key_part, value_part = piece_parts
            key_seg, _ = seq_info(
                lax.dynamic_slice_in_dim(perm_row, offset, key_part.shape[0]), seq_lens
            )
            scores = (
                jnp.einsum("qhe,khe->hqk", query_low, key_part, preferred_element_type=f32)
                * score_scale
            )
            same_seq = (query_seg[:, None] == key_seg[None, :])[None]
            weights = jnp.where(same_seq, jnp.exp(scores - log_total[..., None]), 0.0)
            d_weights = jnp.einsum("qhe,khe->hqk", d_mixed, value_part, preferred_element_type=f32)
            d_scores = (weights * (d_weights - delta_heads[..., None])).astype(bf16)
            return grad_query + score_scale * jnp.einsum(
                "hqk,khe->qhe", d_scores, key_part, preferred_element_type=f32
            )

        query_start = jnp.zeros((tok_rows, head_count, HD), f32)
        grad_query = blockwise(
            query_start,
            (
                lax.all_gather(key_low, "fsdp", axis=0, tiled=True),
                lax.all_gather(value_low, "fsdp", axis=0, tiled=True),
            ),
            jnp.int32(0),
            query_step,
        )
        stat_total, stat_delta = (
            lax.all_gather(jnp.transpose(log_total), "fsdp", axis=0, tiled=True),
            lax.all_gather(delta_rows, "fsdp", axis=0, tiled=True),
        )

        def key_step(running, piece_parts, offset):
            grad_key, grad_value = running
            query_part, dmix_part = piece_parts
            piece_len = query_part.shape[0]
            piece_seg, _ = seq_info(lax.dynamic_slice_in_dim(perm_row, offset, piece_len), seq_lens)
            total_part = jnp.transpose(lax.dynamic_slice_in_dim(stat_total, offset, piece_len))
            delta_part = jnp.transpose(lax.dynamic_slice_in_dim(stat_delta, offset, piece_len))
            scores = (
                jnp.einsum("qhe,khe->hqk", query_part, key_low, preferred_element_type=f32)
                * score_scale
            )
            same_seq = (piece_seg[:, None] == query_seg[None, :])[None]
            weights = jnp.where(same_seq, jnp.exp(scores - total_part[..., None]), 0.0)
            d_weights = jnp.einsum("qhe,khe->hqk", dmix_part, value_low, preferred_element_type=f32)
            d_scores = (weights * (d_weights - delta_part[..., None])).astype(bf16)
            grad_key = grad_key + score_scale * jnp.einsum(
                "hqk,qhe->khe", d_scores, query_part, preferred_element_type=f32
            )
            grad_value = grad_value + jnp.einsum(
                "hqk,qhe->khe", weights.astype(bf16), dmix_part, preferred_element_type=f32
            )
            return (grad_key, grad_value)

        grad_key, grad_value = blockwise(
            (
                jnp.zeros((tok_rows, head_count, HD), f32),
                jnp.zeros((tok_rows, head_count, HD), f32),
            ),
            (
                lax.all_gather(query_low, "fsdp", axis=0, tiled=True),
                lax.all_gather(d_mixed, "fsdp", axis=0, tiled=True),
            ),
            jnp.int32(0),
            key_step,
        )
        _, rope_pull = jax.vjp(lambda heads_in: rotate(heads_in, cosine, sine), raw_heads[:, 0])
        d_raw_query = rope_pull(grad_query)[0]
        d_raw_key = rope_pull(grad_key)[0]
        d_raw = (
            jnp.stack([d_raw_query, d_raw_key, grad_value], axis=1)
            .reshape(tok_rows, 3, head_cols)
            .astype(bf16)
        )
        acc_qkv = acc_qkv + jnp.einsum("td,tcf->dcf", normed_low, d_raw, preferred_element_type=f32)
        first_part = jnp.einsum("tcf,dcf->td", d_raw, again[2], preferred_element_type=f32)
        d_norm_one = lax.psum(first_part.astype(jnp.bfloat16), "tp").astype(jnp.float32)
        _, first_pull = jax.vjp(layer_norm, x_float, gain_first)
        d_x_norm, d_gain_one = first_pull(d_norm_one)
        acc_gain_one = acc_gain_one + d_gain_one
        d_input = (d_hidden + d_x_norm).astype(bf16)
        back_rows = d_input[recv_order].reshape(groups, per_pair, D)
        returned = lax.all_to_all(
            back_rows, "fsdp", split_axis=0, concat_axis=0, tiled=True
        ).reshape(tok_rows, D)
        send_slot = jnp.zeros((tok_rows,), jnp.int32).at[send_order].set(rows_idx)
        input_grads.append(returned[send_slot])
    summed = (
        lax.psum_scatter(acc_qkv, "fsdp", scatter_dimension=0, tiled=True),
        lax.psum_scatter(acc_out, "fsdp", scatter_dimension=0, tiled=True),
        lax.psum_scatter(acc_in, "fsdp", scatter_dimension=0, tiled=True),
        lax.psum_scatter(acc_down, "fsdp", scatter_dimension=0, tiled=True),
        lax.psum_scatter(acc_gain_one, "fsdp", scatter_dimension=0, tiled=True),
        lax.psum_scatter(acc_gain_two, "fsdp", scatter_dimension=0, tiled=True),
    )
    return (
        jnp.stack(outputs),
        jnp.stack(input_grads),
        summed[0],
        summed[1],
        summed[2],
        summed[3],
        summed[4],
        summed[5],
    )


JOIN = 2
COST = 5 * 10**9
FAR = -1e30
ORDER = (0, 2, 4, 6, 1, 3, 5, 7)
NT = (((1,), (1,)), ((), ()))
TN = (((0,), (0,)), ((), ()))
NN = (((1,), (0,)), ((), ()))
ROOM = 10 * 1024 * 1024


def partial(kernel, *given):
    return lambda *refs: kernel(*given, *refs)


def mm(left, right, dims):
    return lax.dot_general(left, right, dims, preferred_element_type=jnp.float32)


def hop(value, step):
    return lax.ppermute(value, "fsdp", [(i, i ^ step) for i in range(8)])


def twin(value):
    return lax.ppermute(value, "tp", [(i, i ^ 1) for i in range(4)])


def across(value):
    return lax.ppermute(value, "tp", [(i, i ^ 2) for i in range(4)])


def deal_out(value):
    return lax.all_to_all(value, "fsdp", 0, 0, tiled=True)


def after(value, *earlier):
    return lax.optimization_barrier((value,) + earlier)[0]


def sync(values):
    return lax.optimization_barrier(values)


def z_phase(shard):
    return [shard] + [hop(shard, step) for step in ORDER[1:4]]


def y_phase(shards):
    return [hop(one, 1) for one in shards]


def local_call(kernel, name, scalars, arrays, outs, scratch=(), shards=(), copies=8, far_in=(), far_out=(), far_shards=True):
    shapes = [(one.shape, one.dtype) for one in arrays]
    staged = [shapes[at] for at in far_in] + [outs[at] for at in far_out]
    sems = [pltpu.SemaphoreType.DMA((copies,))] if shards else []
    room = ROOM + sum(math.prod(shape) * jnp.dtype(kind).itemsize for shape, kind in [*shapes, *outs, *scratch])
    counts = (len(scalars), len(arrays), len(shards), len(outs), len(scratch) + len(sems))

    def body(*refs):
        groups = []
        for count in counts:
            groups.append(list(refs[:count]))
            refs = refs[count:]
        given, ins, pieces, results, extra = groups
        if not staged:
            return kernel(*given, *ins, *pieces, *results, *extra)
        stage, sem = refs[:-1], refs[-1]
        incoming, outgoing = [], []
        for slot, at in enumerate(far_in):
            incoming.append(pltpu.make_async_copy(ins[at], stage[slot], sem.at[slot]))
            incoming[-1].start()
            ins[at] = stage[slot]
        for slot, at in enumerate(far_out, len(far_in)):
            outgoing.append(pltpu.make_async_copy(stage[slot], results[at], sem.at[slot]))
            results[at] = stage[slot]
        for copy in incoming:
            copy.wait()
        kernel(*given, *ins, *pieces, *results, *extra)
        for copy in outgoing:
            copy.start()
        for copy in outgoing:
            copy.wait()

    arrays = [pltpu.with_memory_space_constraint(one, pltpu.HBM) if at in far_in else one for at, one in enumerate(arrays)]
    shards = [pltpu.with_memory_space_constraint(one, pltpu.HBM) if far_shards else one for one in shards]

    def space(at, far):
        return pl.BlockSpec(memory_space=pltpu.HBM if at in far else pltpu.VMEM)

    result = pl.pallas_call(
        body,
        in_specs=[pl.BlockSpec(memory_space=pltpu.SMEM)] * len(scalars)
        + [space(at, far_in) for at in range(len(arrays))]
        + [pl.BlockSpec(memory_space=pltpu.HBM if far_shards else pl.ANY)] * len(shards),
        out_specs=[space(at, far_out) for at in range(len(outs))],
        out_shape=[
            pltpu.HBM(shape, kind) if at in far_out else jax.ShapeDtypeStruct(shape, kind)
            for at, (shape, kind) in enumerate(outs)
        ],
        scratch_shapes=[pltpu.VMEM(shape, kind) for shape, kind in scratch]
        + sems
        + [pltpu.VMEM(shape, kind) for shape, kind in staged]
        + ([pltpu.SemaphoreType.DMA((len(staged),))] if staged else []),
        compiler_params=pltpu.CompilerParams(vmem_limit_bytes=room),
        cost_estimate=pl.CostEstimate(flops=COST, transcendentals=0, bytes_accessed=8 * 1024 * 1024),
        name=name,
    )(*scalars, *arrays, *shards)
    return result if len(outs) > 1 else result[0]


def block_at(order_ref, place, width):
    return pl.ds(pl.multiple_of(order_ref[place] * width, width), width)


def shard_copies(shards, low, high, into_ref, sem_ref, base=0):
    width = shards[0].shape[1]
    copies = []
    for place, shard in enumerate(shards):
        span = pl.ds(place * width, width)
        source = shard.at[pl.ds(low, high - low), :]
        copies.append(pltpu.make_async_copy(source, into_ref.at[:, span], sem_ref.at[base + place]))
        copies[-1].start()
    return copies


def gathered_copies(order_ref, source, low, high, into_ref, sem_ref, base=0):
    width = source.shape[2]
    copies = []
    for place in range(8):
        copies.append(
            pltpu.make_async_copy(
                source.at[order_ref[place], pl.ds(low, high - low), :],
                into_ref.at[:, pl.ds(place * width, width)],
                sem_ref.at[base + place],
            )
        )
        copies[-1].start()
    return copies


def finish(copies):
    for copy in copies:
        copy.wait()


def project_kernel(order_ref, x_ref, table_ref, *refs):
    shards = refs[:8]
    norm_ref, gains_ref, send_ref, w_ref, sem_ref = refs[8:]
    width = shards[0].shape[1]
    rows = x_ref.shape[1]
    wide = w_ref.shape[0] - 16
    heads = wide // (3 * HD)
    half = HD // 2
    finish(shard_copies(shards, 0, wide + 16, w_ref, sem_ref))
    gains_ref[...] = w_ref[wide:, :].astype(jnp.float32)[:2]
    for micro in range(2):
        x = x_ref[micro].astype(jnp.float32)
        mean = jnp.mean(x, axis=-1, keepdims=True)
        center = x - mean
        spread = lax.rsqrt(jnp.mean(center * center, axis=-1, keepdims=True) + EPS)
        for place in range(8):
            piece = x_ref[micro, :, block_at(order_ref, place, width)].astype(jnp.float32)
            span = slice(place * width, (place + 1) * width)
            value = (piece - mean) * spread * gains_ref[0:1, span]
            norm_ref[micro * rows : (micro + 1) * rows, span] = value.astype(jnp.bfloat16)
    raw = mm(w_ref[:wide, :], norm_ref[...], NT)
    cosine, sine = table_ref[:half, :], table_ref[half:, :]
    for head in range(heads):
        base = head * 3 * HD
        for kind in range(2):
            upper = raw[base + kind * HD : base + kind * HD + half]
            lower = raw[base + kind * HD + half : base + (kind + 1) * HD]
            first = (upper * cosine - lower * sine).astype(jnp.bfloat16)
            second = (lower * cosine + upper * sine).astype(jnp.bfloat16)
            for micro in range(2):
                span = slice(micro * rows, (micro + 1) * rows)
                send_ref[micro * heads + head, kind * HD : kind * HD + half, :] = first[:, span]
                send_ref[micro * heads + head, kind * HD + half : (kind + 1) * HD, :] = second[:, span]
        value = raw[base + 2 * HD : base + 3 * HD].astype(jnp.bfloat16)
        for micro in range(2):
            send_ref[micro * heads + head, 2 * HD :, :] = value[:, micro * rows : (micro + 1) * rows]


def key_range(lens_ref, low, high):
    first = jnp.int32(0)
    last = jnp.int32(0)
    total = jnp.int32(0)
    for index in range(lens_ref.shape[0]):
        start = total
        total = total + lens_ref[index]
        first = jnp.where((start <= low) & (low < total), start, first)
        last = jnp.where((start <= high) & (high < total), total, last)
    return first, last


def query_bounds(lens_ref, base, width):
    place = base + lax.broadcasted_iota(jnp.int32, (1, width), 1)
    first = jnp.zeros((1, width), jnp.int32)
    last = jnp.zeros((1, width), jnp.int32)
    total = jnp.int32(0)
    for index in range(lens_ref.shape[0]):
        start = total
        total = total + lens_ref[index]
        inside = (place >= start) & (place < total)
        first = jnp.where(inside, start, first)
        last = jnp.where(inside, total, last)
    return first, last


def lanes(ref, index, count, rows):
    return jnp.concatenate([ref[index * count + at, rows, :] for at in range(count)], axis=1)


def attend_kernel(lens_ref, qkv_ref, mixed_ref, exact_ref, log_ref, key_ref):
    blocks, _, small = qkv_ref.shape
    wide = JOIN * small
    for at in range(blocks):
        block = qkv_ref[at, HD : 2 * HD, :].astype(jnp.float32)
        key_ref[at * small : (at + 1) * small, :] = jnp.transpose(block).astype(jnp.bfloat16)

    def one_query(index, carry):
        base = index * wide
        first, last = key_range(lens_ref, base, base + wide - 1)
        low, high = query_bounds(lens_ref, base, wide)
        query = lanes(qkv_ref, index, JOIN, slice(0, HD)) * jnp.bfloat16(HD**-0.5)

        def one_key(at, state):
            peak, total, acc = state
            start = pl.multiple_of(at * wide, wide)
            scores = mm(key_ref[pl.ds(start, wide), :], query, NN)
            place = start + lax.broadcasted_iota(jnp.int32, (wide, wide), 0)
            scores = jnp.where((place >= low) & (place < high), scores, FAR)
            top = jnp.maximum(peak, jnp.max(scores, axis=0, keepdims=True))
            weights = jnp.exp(scores - top)
            fade = jnp.exp(peak - top)
            total = total * fade + jnp.sum(weights, axis=0, keepdims=True)
            value = lanes(qkv_ref, at, JOIN, slice(2 * HD, 3 * HD))
            acc = acc * fade + mm(value, weights.astype(jnp.bfloat16), NN)
            return top, total, acc

        peak, total, acc = lax.fori_loop(
            first // wide,
            (last + wide - 1) // wide,
            one_key,
            (
                jnp.full((1, wide), FAR, jnp.float32),
                jnp.zeros((1, wide), jnp.float32),
                jnp.zeros((HD, wide), jnp.float32),
            ),
        )
        result = acc / total
        logs = peak + jnp.log(total)
        for at in range(JOIN):
            span = slice(at * small, (at + 1) * small)
            mixed_ref[index * JOIN + at] = result[:, span].astype(jnp.bfloat16)
            exact_ref[index * JOIN + at] = result[:, span]
            log_ref[index * JOIN + at] = logs[:, span]
        return carry

    lax.fori_loop(0, blocks // JOIN, one_query, 0)


def attend_back_kernel(
    lens_ref, qkv_ref, exact_ref, log_ref, grad_ref, table_ref, raw_ref, pair_ref, dkey_ref, dvalue_ref
):
    blocks, _, small = qkv_ref.shape
    wide = JOIN * small
    half = HD // 2
    for at in range(blocks):
        block = qkv_ref[at, HD : 3 * HD, :].astype(jnp.float32)
        pair_ref[at * small : (at + 1) * small, :] = jnp.transpose(block).astype(jnp.bfloat16)
    dkey_ref[...] = jnp.zeros(dkey_ref.shape, jnp.float32)
    dvalue_ref[...] = jnp.zeros(dvalue_ref.shape, jnp.float32)

    def unturn(index, grad):
        cosine = table_ref[index, :half, :]
        sine = table_ref[index, half:, :]
        upper, lower = grad[:half], grad[half:]
        return upper * cosine + lower * sine, lower * cosine - upper * sine

    def one_query(index, carry):
        base = index * wide
        first, last = key_range(lens_ref, base, base + wide - 1)
        low, high = query_bounds(lens_ref, base, wide)
        query = lanes(qkv_ref, index, JOIN, slice(0, HD)) * jnp.bfloat16(HD**-0.5)
        grad = lanes(grad_ref, index, JOIN, slice(0, HD))
        logs = lanes(log_ref, index, JOIN, slice(0, 1))
        exact = lanes(exact_ref, index, JOIN, slice(0, HD))
        delta = jnp.sum(grad.astype(jnp.float32) * exact, axis=0, keepdims=True)

        def one_key(at, dquery):
            start = pl.multiple_of(at * wide, wide)
            span = pl.ds(start, wide)
            scores = mm(pair_ref[span, :HD], query, NN)
            dweights = mm(pair_ref[span, HD:], grad, NN)
            place = start + lax.broadcasted_iota(jnp.int32, (wide, wide), 0)
            weights = jnp.where((place >= low) & (place < high), jnp.exp(scores - logs), 0.0)
            dscores = (weights * (dweights - delta)).astype(jnp.bfloat16)
            dkey_ref[:, span] += mm(query, dscores, NT)
            dvalue_ref[:, span] += mm(grad, weights.astype(jnp.bfloat16), NT)
            return dquery + mm(lanes(qkv_ref, at, JOIN, slice(HD, 2 * HD)), dscores, NN)

        dquery = lax.fori_loop(
            first // wide,
            (last + wide - 1) // wide,
            one_key,
            jnp.zeros((HD, wide), jnp.float32),
        ) * (HD**-0.5)
        for at in range(JOIN):
            upper, lower = unturn(index * JOIN + at, dquery[:, at * small : (at + 1) * small])
            raw_ref[index * JOIN + at, :half, :] = upper.astype(jnp.bfloat16)
            raw_ref[index * JOIN + at, half:HD, :] = lower.astype(jnp.bfloat16)
        return carry

    lax.fori_loop(0, blocks // JOIN, one_query, 0)
    for at in range(blocks):
        span = slice(at * small, (at + 1) * small)
        upper, lower = unturn(at, dkey_ref[:, span])
        raw_ref[at, HD : HD + half, :] = upper.astype(jnp.bfloat16)
        raw_ref[at, HD + half : 2 * HD, :] = lower.astype(jnp.bfloat16)
        raw_ref[at, 2 * HD :, :] = dvalue_ref[:, span].astype(jnp.bfloat16)


def mix_out_kernel(core_ref, order_ref, mixed_ref, all_ref, send_ref, keep_ref, w_ref, sem_ref):
    last = all_ref.shape[1]
    finish(gathered_copies(order_ref, all_ref, last - mixed_ref.shape[1], last, w_ref, sem_ref))
    core = core_ref[0]
    send_ref[...] = mm(mixed_ref[1 - core], w_ref[...], TN).astype(jnp.bfloat16)
    keep_ref[...] = mm(mixed_ref[core], w_ref[...], TN)


def norm_two_kernel(core_ref, order_ref, x_ref, half_ref, far_ref, gains_ref, hidden_ref, norm_ref):
    core = core_ref[0]
    width = x_ref.shape[2] // 8
    for place in range(8):
        span = slice(place * width, (place + 1) * width)
        piece = x_ref[core, :, block_at(order_ref, place, width)].astype(jnp.float32)
        branch = half_ref[:, span].astype(jnp.float32) + far_ref[:, span].astype(jnp.float32)
        hidden_ref[:, span] = piece + branch
    hidden = hidden_ref[...]
    center = hidden - jnp.mean(hidden, axis=-1, keepdims=True)
    spread = lax.rsqrt(jnp.mean(center * center, axis=-1, keepdims=True) + EPS)
    norm_ref[...] = (center * spread * gains_ref[1:2, :]).astype(jnp.bfloat16)


def feed_kernel(
    order_ref, own_ref, other_ref, grad_ref, all_ref, down_ref, send_ref, keep_ref, act_ref, dinp_ref, dgate_ref, w_ref, sem_ref
):
    units = w_ref.shape[0] // 3
    inp_w, gate_w, down_w = [w_ref.at[pl.ds(at * units, units), :] for at in range(3)]
    rows = own_ref.shape[0]
    first_copies = gathered_copies(order_ref, all_ref, 0, 2 * units, w_ref.at[pl.ds(0, 2 * units), :], sem_ref)
    finish(gathered_copies(order_ref, down_ref, 0, units, down_w, sem_ref, 8))
    finish(first_copies)
    for micro, norm_ref in ((1, other_ref), (0, own_ref)):
        span = slice(micro * rows, (micro + 1) * rows)
        inp = mm(norm_ref[...], inp_w[...], NT)
        gate = mm(norm_ref[...], gate_w[...], NT)
        dact = mm(grad_ref[micro], down_w[...], NT)
        cdf = 0.5 * (1.0 + lax.erf(inp * (0.5**0.5)))
        density = jnp.exp(-0.5 * inp * inp) * ((0.5 / jnp.pi) ** 0.5)
        gelu = inp * cdf
        act_ref[span, :] = (gelu * gate).astype(jnp.bfloat16)
        dinp = (dact * gate * (cdf + inp * density)).astype(jnp.bfloat16)
        dgate = (dact * gelu).astype(jnp.bfloat16)
        dinp_ref[span, :] = dinp
        dgate_ref[span, :] = dgate
        part = mm(dinp, inp_w[...], NN) + mm(dgate, gate_w[...], NN)
        if micro:
            send_ref[...] = part.astype(jnp.bfloat16)
        else:
            keep_ref[...] = part


def weight_grad_kernel(order_ref, dinp_ref, dgate_ref, act_ref, own_ref, other_ref, grad_ref, out_ref):
    units = act_ref.shape[1]
    rows = own_ref.shape[0]
    width = out_ref.shape[2]
    for at, (left_ref, rights) in enumerate((
        (dinp_ref, (own_ref, other_ref)),
        (dgate_ref, (own_ref, other_ref)),
        (act_ref, (grad_ref.at[0], grad_ref.at[1])),
    )):
        total = mm(left_ref[:rows, :], rights[0][...], TN) + mm(left_ref[rows:, :], rights[1][...], TN)
        for place in range(8):
            piece = total[:, place * width : (place + 1) * width].astype(jnp.bfloat16)
            out_ref[order_ref[place], at * units : (at + 1) * units, :] = piece


def near_sum_kernel(near_ref, far_ref, own_ref, *low_refs):
    own_ref[...] = near_ref[0] + far_ref[0].astype(jnp.float32)
    for at, low_ref in enumerate(low_refs):
        low_ref[...] = (near_ref[at + 1] + far_ref[at + 1].astype(jnp.float32)).astype(jnp.bfloat16)


def down_kernel(order_ref, act_ref, all_ref, send_ref, keep_ref, w_ref, sem_ref):
    rows = send_ref.shape[0]
    units = w_ref.shape[0]
    finish(gathered_copies(order_ref, all_ref, 0, units, w_ref, sem_ref))
    send_ref[...] = mm(act_ref[rows:, :], w_ref[...], NN).astype(jnp.bfloat16)
    keep_ref[...] = mm(act_ref[:rows, :], w_ref[...], NN)


def norm_two_back_kernel(hidden_ref, half_ref, far_ref, grad_ref, gains_ref, dhidden_ref, low_ref):
    hidden = hidden_ref[...]
    center = hidden - jnp.mean(hidden, axis=-1, keepdims=True)
    spread = lax.rsqrt(jnp.mean(center * center, axis=-1, keepdims=True) + EPS)
    xhat = center * spread
    dnorm = half_ref[...].astype(jnp.float32) + far_ref[...].astype(jnp.float32)
    scaled = dnorm * gains_ref[1:2, :]
    inner = scaled - jnp.mean(scaled, axis=-1, keepdims=True)
    inner = inner - xhat * jnp.mean(scaled * xhat, axis=-1, keepdims=True)
    total = grad_ref[0].astype(jnp.float32) + inner * spread
    dhidden_ref[...] = total
    low_ref[...] = total.astype(jnp.bfloat16)


def mix_back_kernel(core_ref, own_ref, other_ref, w_ref, send_ref):
    cols = w_ref.shape[0]
    heads = cols // HD
    core = core_ref[0]
    for micro, low_ref in ((core, own_ref), (1 - core, other_ref)):
        total = mm(w_ref[...], low_ref[...], NT).astype(jnp.bfloat16)
        for head in range(heads):
            send_ref[micro * heads + head] = total[head * HD : (head + 1) * HD, :]


def mix_grad_kernel(core_ref, mixed_ref, own_ref, other_ref, far_ref, near_ref):
    core = core_ref[0]
    width = far_ref.shape[2]
    total = mm(mixed_ref[core], own_ref[...], NN) + mm(mixed_ref[1 - core], other_ref[...], NN)
    for place in range(4):
        near_ref[place] = total[:, place * width : (place + 1) * width]
        far_ref[place] = total[:, (4 + place) * width : (5 + place) * width].astype(jnp.bfloat16)


def project_back_kernel(core_ref, raw_ref, w_ref, send_ref, keep_ref):
    core = core_ref[0]
    weights = w_ref[: raw_ref.shape[1], :]
    send_ref[...] = mm(raw_ref[1 - core], weights, TN).astype(jnp.bfloat16)
    keep_ref[...] = mm(raw_ref[core], weights, TN)


def project_grad_kernel(first, raw_ref, norm_ref, far_ref, near_ref):
    count, width = far_ref.shape[1:]
    rows = raw_ref.shape[2]
    span = slice(first, first + count)
    total = mm(raw_ref[0, span, :], norm_ref[:rows, :], NN) + mm(raw_ref[1, span, :], norm_ref[rows:, :], NN)
    for place in range(4):
        near_ref[place] = total[:, place * width : (place + 1) * width]
        far_ref[place] = total[:, (4 + place) * width : (5 + place) * width].astype(jnp.bfloat16)


def norm_one_back_kernel(
    core_ref, order_ref, x_ref, half_ref, far_ref, dhidden_ref, gains_ref, grad_ref, dgain_ref, xhat_ref
):
    core = core_ref[0]
    width = x_ref.shape[2] // 8
    x = x_ref[core].astype(jnp.float32)
    mean = jnp.mean(x, axis=-1, keepdims=True)
    center = x - mean
    spread = lax.rsqrt(jnp.mean(center * center, axis=-1, keepdims=True) + EPS)
    for place in range(8):
        span = slice(place * width, (place + 1) * width)
        piece = x_ref[core, :, block_at(order_ref, place, width)].astype(jnp.float32)
        xhat_ref[:, span] = (piece - mean) * spread
    xhat = xhat_ref[...]
    dnorm = half_ref[...].astype(jnp.float32) + far_ref[...].astype(jnp.float32)
    dgain_ref[...] = jnp.sum(dnorm * xhat, axis=0, keepdims=True)
    scaled = dnorm * gains_ref[0:1, :]
    inner = scaled - jnp.mean(scaled, axis=-1, keepdims=True)
    inner = inner - xhat * jnp.mean(scaled * xhat, axis=-1, keepdims=True)
    total = (dhidden_ref[...] + inner * spread).astype(jnp.bfloat16)
    for place in range(8):
        grad_ref[:, block_at(order_ref, place, width)] = total[:, place * width : (place + 1) * width]


def place_grad_kernel(core_ref, order_ref, local_ref, four_ref, grad_ref, natural_ref):
    rows = grad_ref.shape[1]
    width = grad_ref.shape[2] // 8
    core = core_ref[0]
    for at in range(2):
        micro = core if at == 0 else 1 - core
        place = lax.broadcasted_iota(jnp.int32, (rows, rows), 0)
        onehot = jnp.where(local_ref[pl.ds(micro, 1), :] == place, 1.0, 0.0).astype(jnp.bfloat16)
        natural_ref[...] = mm(onehot, four_ref[micro], NN).astype(jnp.bfloat16)
        for block in range(8):
            span = slice(block * width, (block + 1) * width)
            grad_ref[at, :, span] = natural_ref[:, block_at(order_ref, block, width)]


def result_kernel(order_ref, picks_ref, hidden_ref, half_ref, far_ref, packed_ref, natural_ref):
    rows = hidden_ref.shape[0]
    width = hidden_ref.shape[1] // 8
    branch = half_ref[...].astype(jnp.float32) + far_ref[...].astype(jnp.float32)
    total = (hidden_ref[...] + branch).astype(jnp.bfloat16)
    for block in range(8):
        natural_ref[:, block_at(order_ref, block, width)] = total[:, block * width : (block + 1) * width]
    count = packed_ref.shape[0]
    place = lax.broadcasted_iota(jnp.int32, (rows, count), 0)
    onehot = jnp.where(picks_ref[...] == place, 1.0, 0.0).astype(jnp.bfloat16)
    packed_ref[...] = mm(onehot, natural_ref[...], TN).astype(jnp.bfloat16)


def positions(anchor, seq_lens):
    ends = running_ends(seq_lens)
    starts = ends - seq_lens
    inside = (anchor[:, None] >= starts[None, :]) & (anchor[:, None] < ends[None, :])
    return anchor - jnp.sum(jnp.where(inside, starts[None, :], 0), axis=1)


def turn_tables(place):
    freqs = jnp.power(THETA, -jnp.arange(HD // 2, dtype=jnp.float32) * 2.0 / HD)
    angle = freqs[:, None] * place.astype(jnp.float32)[None, :]
    return jnp.concatenate([jnp.cos(angle), jnp.sin(angle)], axis=0)


def paired_layer(
    tokens, cotangent, perm, lengths, w_qkv, w_attn_out, w_in, w_down, gain_one, gain_two
):
    f32, bf16, i32 = jnp.float32, jnp.bfloat16, jnp.int32
    mine = lax.axis_index("fsdp")
    part = lax.axis_index("tp")
    core, side = part & 1, part >> 1
    core_at = core.reshape(1).astype(i32)
    rows = tokens.shape[1]
    width = w_qkv.shape[0]
    full = 8 * width
    cols = w_qkv.shape[2]
    heads = cols // HD
    units = w_in.shape[2]
    per_pair = rows // 8
    order = jnp.bitwise_xor(jnp.array(ORDER, i32), mine)

    def pick(value, index):
        return lax.dynamic_index_in_dim(value, index, 0, keepdims=False)

    def both(value, other):
        return jnp.stack([jnp.where(core == 0, value, other), jnp.where(core == 0, other, value)])

    def add_half(keep, got):
        return (keep + got.astype(f32)).astype(bf16)

    def near_sum(near, far, name):
        shape = near.shape[1:]
        own, *lows = local_call(near_sum_kernel, name, (), (near, far), [(shape, f32)] + [(shape, bf16)] * 3, far_in=(0, 1), far_out=(0,))
        return own, lows

    def y_join(same):
        return same + [hop(jnp.concatenate(same, axis=0), 1)]

    def z_send(lows):
        return [hop(low, ORDER[at + 1]) for at, low in enumerate(lows)]

    def far_sum(own, got):
        return own + sum(one.astype(f32) for one in got)

    turned = jnp.transpose(w_qkv.reshape(width, 3, heads, HD), (2, 1, 3, 0)).reshape(3 * cols, width)
    gains_rows = jnp.concatenate([gain_one[None], gain_two[None], jnp.zeros((14, width), bf16)])
    first_same = z_phase(jnp.concatenate([turned, gains_rows], axis=0))
    first = first_same + y_phase(first_same)

    slots = perm.reshape(2, 8, rows)
    from_me = (slots // rows == mine).astype(f32)
    slot_no = jnp.arange(rows, dtype=i32)
    before = (slot_no[:, None] < slot_no[None, :]).astype(f32)
    rank_me = jnp.einsum("mds,st->mdt", from_me, before).astype(i32)
    ranks = jnp.arange(per_pair, dtype=i32)
    chosen = (from_me[..., None] > 0) & (rank_me[..., None] == ranks)
    local = jnp.sum(jnp.where(chosen, (slots % rows)[..., None], 0), axis=2)
    my_slots = lax.dynamic_index_in_dim(slots, mine, 1, keepdims=False)
    target = my_slots // rows
    same = (target[:, :, None] == target[:, None, :]) & (slot_no[:, None] < slot_no[None, :])[None]
    rank_own = jnp.sum(same.astype(i32), axis=1)
    place_own = target * per_pair + rank_own
    quarter = per_pair // 4
    wanted = order[:, None] * per_pair + part * quarter
    wanted = (wanted + jnp.arange(quarter, dtype=i32)[None, :]).reshape(-1)
    packer = (place_own[:, None, :] == wanted[None, :, None]).astype(bf16)
    packed = jnp.einsum("mps,msd->mpd", packer, cotangent, preferred_element_type=f32).astype(bf16)
    packed = packed.reshape(2, 8, quarter, full)
    packed = [packed[:, at] for at in range(8)]
    chosen = order[:, None] == jnp.arange(8, dtype=i32)[None, :]
    local_own = jnp.sum(jnp.where(chosen[None, :, :, None], local[:, None], 0), axis=2)
    anchor = mine * rows + jnp.arange(rows, dtype=i32)
    own_table = jnp.concatenate([turn_tables(positions(anchor, lengths[m])) for m in range(2)], axis=1)
    inp_turned, gate_turned = jnp.transpose(w_in[:, 0]), jnp.transpose(w_in[:, 1])
    second = jnp.concatenate([jnp.transpose(w_down), jnp.transpose(w_attn_out)], axis=0)
    second_all = lax.all_gather(second, "fsdp", axis=0, tiled=False)
    third_all = lax.all_gather(jnp.concatenate([inp_turned, gate_turned], axis=0), "fsdp", axis=0, tiled=False)
    halfway = per_pair // 2
    picks = lax.dynamic_slice_in_dim(pick(local, core), side * halfway, halfway, 1).reshape(1, -1)
    unpack = (place_own[:, :, None] == slot_no[None, None, :]).astype(bf16)
    my_lens = lengths[mine // heads]
    all_anchor = jnp.arange(8 * rows, dtype=i32)
    table = turn_tables(positions(all_anchor, my_lens))
    table = jnp.transpose(table.reshape(HD, 8, rows), (1, 0, 2))
    first, packed, own_table, picks, unpack, table, local_own, order, core_at, core, side, my_lens = sync(
        (first, packed, own_table, picks, unpack, table, local_own, order, core_at, core, side, my_lens)
    )

    norm_one, gains, outgoing, qkv_w = local_call(
        project_kernel, "project", (order,), (tokens, own_table),
        [((2 * rows, full), bf16), ((2, full), f32), ((2 * heads, 3 * HD, rows), bf16), ((3 * cols + 16, full), bf16)],
        (), first, far_in=(0, 1), far_out=(0, 1, 2, 3), far_shards=False,
    )
    outgoing, packed = sync((outgoing, packed))
    qkv = deal_out(outgoing)
    arrived = [hop(one, ORDER[at]) if at else one for at, one in enumerate(packed)]
    qkv = sync((qkv,))[0]
    mixed_out, exact, logs = local_call(
        attend_kernel, "attend", (my_lens,), (qkv,),
        [((8, HD, rows), bf16), ((8, HD, rows), f32), ((8, 1, rows), f32)],
        [((8 * rows, HD), bf16)], far_in=(0,), far_out=(0, 1, 2),
    )
    mixed_out, arrived = sync((mixed_out, arrived))
    mixed = deal_out(mixed_out).reshape(2, cols, rows)
    arrived = jnp.stack(arrived)
    near = twin(arrived)
    pair = jnp.stack([jnp.where(core == 0, arrived, near), jnp.where(core == 0, near, arrived)])
    far = across(pair)
    mixed, far = sync((mixed, far))
    four = jnp.concatenate([jnp.where(side == 0, pair, far), jnp.where(side == 0, far, pair)])
    four = jnp.transpose(four, (2, 1, 0, 3, 4)).reshape(2, rows, full)
    grad = local_call(
        place_grad_kernel, "place_grad", (core_at, order), (local_own.reshape(2, rows), four),
        [((2, rows, full), bf16)], [((rows, full), bf16)],
    )

    send, keep, out_w = local_call(
        mix_out_kernel, "mix_out", (core_at, order), (mixed,),
        [((rows, full), bf16), ((rows, full), f32), ((cols, full), bf16)], (), (second_all,), far_in=(0,),
    )
    half = add_half(keep, twin(send))
    far = across(half)
    far, grad = sync((far, grad))
    hidden, two_own = local_call(
        norm_two_kernel, "norm_two", (core_at, order), (tokens, half, far, gains),
        [((rows, full), f32), ((rows, full), bf16)], far_in=(0, 3),
    )
    two_other = twin(two_own)

    send, keep, act, d_inp, d_gate = local_call(
        feed_kernel, "feed", (order,), (two_own, two_other, grad),
        [((rows, full), bf16), ((rows, full), f32)] + [((2 * rows, units), bf16)] * 3,
        [((3 * units, full), bf16)], (third_all, second_all), copies=16,
    )
    half_two = add_half(keep, twin(send))
    half_two, act, d_inp, d_gate = sync((half_two, act, d_inp, d_gate))
    far_two = across(half_two)
    feed_grad = local_call(
        weight_grad_kernel, "feed_grad", (order,), (d_inp, d_gate, act, two_own, two_other, grad),
        [((8, 3 * units, width), bf16)], far_out=(0,),
    )
    feed_sum = lax.psum_scatter(feed_grad, "fsdp", scatter_dimension=0, tiled=False)
    send, keep = local_call(
        down_kernel, "down", (order,), (act,),
        [((rows, full), bf16), ((rows, full), f32)], [((units, full), bf16)], (second_all,),
    )
    res_half = add_half(keep, twin(send))
    far_two, feed_grad, res_half = sync((far_two, feed_grad, res_half))
    d_hidden, low_own = local_call(
        norm_two_back_kernel, "norm_two_back", (), (hidden, half_two, far_two, grad, gains),
        [((rows, full), f32), ((rows, full), bf16)], far_in=(4,), far_out=(0,),
    )
    low_other = twin(low_own)
    d_mixed = local_call(
        mix_back_kernel, "mix_back", (core_at,), (low_own, low_other, out_w),
        [((8, HD, rows), bf16)], far_out=(0,),
    )
    out_far, out_near = local_call(
        mix_grad_kernel, "mix_grad", (core_at,), (mixed, low_own, low_other),
        [((4, cols, width), bf16), ((4, cols, width), f32)], far_in=(0,), far_out=(1,),
    )
    d_mixed, out_far = sync((d_mixed, out_far))
    grad_mixed = deal_out(d_mixed)
    res_far = across(res_half)
    grad_mixed, res_far = sync((grad_mixed, res_far))

    out_got = hop(out_far, 1)
    d_raw_out = local_call(
        attend_back_kernel, "attend_back", (my_lens,), (qkv, exact, logs, grad_mixed, table),
        [((8, 3 * HD, rows), bf16)],
        [((8 * rows, 2 * HD), bf16), ((HD, 8 * rows), f32), ((HD, 8 * rows), f32)],
        far_in=(0, 1, 2, 3, 4), far_out=(0,),
    )
    d_raw_out, out_got = sync((d_raw_out, out_got))
    d_raw = deal_out(d_raw_out).reshape(2, 3 * cols, rows)
    out_own, out_lows = near_sum(out_near, out_got, "out_near")
    packed = local_call(
        result_kernel, "result", (order,), (picks, hidden, res_half, res_far),
        [((8 * halfway, full), bf16)], [((rows, full), bf16)], far_in=(1, 2, 3), far_out=(0,),
    )
    d_raw, out_lows, packed = sync((d_raw, out_lows, packed))

    qkv_far, qkv_near = local_call(
        partial(project_grad_kernel, 0), "project_grad", (), (d_raw, norm_one),
        [((4, 3 * cols, width), bf16), ((4, 3 * cols, width), f32)], far_in=(0, 1), far_out=(1,),
    )
    qkv_far, d_raw = sync((qkv_far, d_raw))
    qkv_got = hop(qkv_far, 1)
    send, keep = local_call(
        project_back_kernel, "project_back", (core_at,), (d_raw, qkv_w),
        [((rows, full), bf16), ((rows, full), f32)], far_in=(0, 1),
    )
    half = add_half(keep, twin(send))
    half, packed, out_lows = sync((half, packed, out_lows))
    far = across(half)
    arrived = deal_out(packed.reshape(8, halfway, full))
    out_got = z_send(out_lows)
    qkv_got, far, arrived = sync((qkv_got, far, arrived))
    qkv_own, qkv_lows = near_sum(qkv_near, qkv_got, "qkv_near")
    qkv_got = z_send(qkv_lows)
    input_own, d_gain_one = local_call(
        norm_one_back_kernel, "norm_one_back", (core_at, order), (tokens, half, far, d_hidden, gains),
        [((rows, full), bf16), ((1, full), f32)], [((rows, full), f32)], far_in=(0, 3, 4),
    )
    input_grad = both(input_own, twin(input_own))
    high = d_gain_one.astype(bf16).astype(f32)
    gain_parts = jnp.concatenate([high, d_gain_one - high, jnp.zeros((14, full), f32)], axis=0)
    gain_parts = jnp.transpose(gain_parts.reshape(16, 8, width), (1, 0, 2))
    gain_near = gain_parts[:4] + hop(gain_parts[4:].astype(bf16), 1).astype(f32)
    gain_got = z_send([gain_near[at].astype(bf16) for at in range(1, 4)])
    gain_row = far_sum(gain_near[0], gain_got)
    gain_row = gain_row[0] + gain_row[1]
    grad_gain_one = gain_row + twin(gain_row)
    other_side = across(arrived)
    whole = jnp.concatenate(
        [jnp.where(side == 0, arrived, other_side), jnp.where(side == 0, other_side, arrived)], axis=1
    ).reshape(rows, full)
    whole = both(whole, twin(whole))
    output = jnp.einsum("msp,mpd->msd", unpack, whole, preferred_element_type=f32).astype(bf16)
    out_sum = far_sum(out_own, out_got)
    inp_sum, gate_sum, down_sum = [feed_sum[at * units : (at + 1) * units].astype(f32) for at in range(3)]
    two_row = jnp.sum(inp_sum * inp_turned.astype(f32) + gate_sum * gate_turned.astype(f32), axis=0)
    two_row = two_row + twin(two_row)
    grad_gain_two = (two_row + across(two_row)) / gain_two.astype(f32)
    grad_attn_out = jnp.transpose(out_sum)
    grad_in = jnp.stack([jnp.transpose(inp_sum), jnp.transpose(gate_sum)], axis=1)
    grad_down = jnp.transpose(down_sum)
    qkv_got, output, input_grad, grad_attn_out, grad_in, grad_down, grad_gain_one, grad_gain_two = sync(
        (qkv_got, output, input_grad, grad_attn_out, grad_in, grad_down, grad_gain_one, grad_gain_two)
    )
    qkv_sum = far_sum(qkv_own, qkv_got)
    return (
        output,
        input_grad,
        jnp.transpose(qkv_sum.reshape(heads, 3, HD, width), (3, 1, 0, 2)).reshape(width, 3, cols),
        grad_attn_out,
        grad_in,
        grad_down,
        grad_gain_one,
        grad_gain_two,
    )


def on_device(*operands):
    micro_count, tok_rows = operands[0].shape[0], operands[0].shape[1]
    groups, parts = lax.axis_size("fsdp"), lax.axis_size("tp")
    heads = operands[4].shape[2] // HD
    if groups == 8 and parts == 4 and micro_count == 2 and micro_count * heads == groups and tok_rows % 256 == 0:
        return paired_layer(*operands)
    return general_layer(*operands)


def solution(mesh):
    placed = (
        P(None, "fsdp", None),
        P(None, "fsdp", None),
        P(),
        P(),
        P("fsdp", None, "tp"),
        P("fsdp", "tp"),
        P("fsdp", None, "tp"),
        P("fsdp", "tp"),
        P("fsdp"),
        P("fsdp"),
    )
    return jax.shard_map(
        on_device,
        mesh=mesh,
        in_specs=placed,
        out_specs=(
            P(None, "fsdp", None),
            P(None, "fsdp", None),
            P("fsdp", None, "tp"),
            P("fsdp", "tp"),
            P("fsdp", None, "tp"),
            P("fsdp", "tp"),
            P("fsdp"),
            P("fsdp"),
        ),
        check_vma=False,
    )
```

```python
import math

import jax
import jax.numpy as jnp
from jax import lax
from jax.experimental import pallas as pl
from jax.experimental.pallas import tpu as pltpu
from jax.sharding import PartitionSpec as P

D = 1024
HD = 64


EPS = 1e-05
THETA = 160000.0
key_block = 2048


def layer_norm(values, gain):
    center = values - jnp.mean(values, axis=-1, keepdims=True)
    spread = jnp.mean(center * center, axis=-1, keepdims=True)
    return center * lax.rsqrt(spread + EPS) * gain


def rope_tables(position, width):
    freqs = jnp.power(THETA, -jnp.arange(width // 2, dtype=jnp.float32) * 2.0 / width)
    angle = position.astype(jnp.float32)[:, None] * freqs[None, :]
    angle = jnp.concatenate([angle, angle], axis=-1)
    return (jnp.cos(angle), jnp.sin(angle))


def rotate(values, cosine, sine):
    half = values.shape[-1] // 2
    turned = jnp.concatenate([-values[..., half:], values[..., :half]], axis=-1)
    return values * cosine[:, None, :] + turned * sine[:, None, :]


def running_ends(seq_lens):
    order = jnp.arange(seq_lens.shape[0], dtype=jnp.int32)
    return jnp.sum(jnp.where(order[None, :] <= order[:, None], seq_lens[None, :], 0), axis=1)


def seq_info(anchor, seq_lens):
    ends = running_ends(seq_lens)
    starts = ends - seq_lens
    segment = jnp.sum((anchor[:, None] >= ends[None, :]).astype(jnp.int32), axis=1)
    onehot = segment[:, None] == jnp.arange(seq_lens.shape[0], dtype=jnp.int32)[None, :]
    position = anchor - jnp.sum(jnp.where(onehot, starts[None, :], 0), axis=1)
    return (segment, position)


def blockwise(running, pieces, offset, step_fn):
    piece_len = pieces[0].shape[0]
    if piece_len > key_block and piece_len % key_block == 0:
        block_count = piece_len // key_block
        stacked = tuple((one.reshape((block_count, key_block) + one.shape[1:]) for one in pieces))

        def inner(state_now, scan_item):
            block_index, piece_parts = scan_item
            return (step_fn(state_now, piece_parts, offset + block_index * key_block), None)

        running, _ = lax.scan(inner, running, (jnp.arange(block_count, dtype=jnp.int32), stacked))
        return running
    return step_fn(running, pieces, offset)


def general_layer(
    tokens, cotangent, perm, lengths, w_qkv, w_attn_out, w_in, w_down, gain_one, gain_two
):
    groups = lax.axis_size("fsdp")
    my_index = lax.axis_index("fsdp")
    micro_count = tokens.shape[0]
    tok_rows = tokens.shape[1]
    total_rows = tok_rows * groups
    per_pair = tok_rows // groups
    head_cols = w_qkv.shape[2]
    head_count = head_cols // HD
    unit_cols = w_in.shape[2]
    score_scale = HD ** (-0.5)
    rows_idx = jnp.arange(tok_rows, dtype=jnp.int32)
    f32 = jnp.float32
    bf16 = jnp.bfloat16
    dims_rows = (((0,), (0,)), ((), ()))
    dims_cols = (((1,), (1,)), ((), ()))
    acc_qkv = jnp.zeros((D, 3, head_cols), f32)
    acc_out = jnp.zeros((D, head_cols), f32)
    acc_in = jnp.zeros((D, 2, unit_cols), f32)
    acc_down = jnp.zeros((D, unit_cols), f32)
    acc_gain_one = jnp.zeros((D,), f32)
    acc_gain_two = jnp.zeros((D,), f32)
    outputs = []
    input_grads = []
    for micro_idx in range(micro_count):
        perm_row = perm[micro_idx]
        seq_lens = lengths[micro_idx]
        inverse = (
            jnp.zeros((total_rows,), jnp.int32)
            .at[perm_row]
            .set(jnp.arange(total_rows, dtype=jnp.int32))
        )
        placed = lax.dynamic_slice_in_dim(inverse, my_index * tok_rows, tok_rows)
        send_order = jnp.argsort(placed)
        outgoing = tokens[micro_idx][send_order].reshape(groups, per_pair, D)
        arrived = lax.all_to_all(outgoing, "fsdp", split_axis=0, concat_axis=0, tiled=True).reshape(
            tok_rows, D
        )
        my_tokens = lax.dynamic_slice_in_dim(perm_row, my_index * tok_rows, tok_rows)
        source = my_tokens // tok_rows
        recv_order = jnp.argsort(source * tok_rows + rows_idx)
        recv_slot = jnp.zeros((tok_rows,), jnp.int32).at[recv_order].set(rows_idx)
        dealt = arrived[recv_slot]
        fetched = (
            lax.all_gather(gain_one, "fsdp", axis=0, tiled=True),
            lax.all_gather(gain_two, "fsdp", axis=0, tiled=True),
            lax.all_gather(w_qkv, "fsdp", axis=0, tiled=True),
            lax.all_gather(w_attn_out, "fsdp", axis=0, tiled=True),
            lax.all_gather(w_in, "fsdp", axis=0, tiled=True),
            lax.all_gather(w_down, "fsdp", axis=0, tiled=True),
        )
        gain_first = fetched[0].astype(f32)
        gain_second = fetched[1].astype(f32)
        query_seg, query_pos = seq_info(my_tokens, seq_lens)
        cosine, sine = rope_tables(query_pos, HD)
        x_float = dealt.astype(f32)
        normed_low = layer_norm(x_float, gain_first).astype(bf16)
        raw_proj = jnp.einsum("td,dcf->tcf", normed_low, fetched[2], preferred_element_type=f32)
        raw_heads = raw_proj.reshape(tok_rows, 3, head_count, HD)
        query_low = rotate(raw_heads[:, 0], cosine, sine).astype(bf16)
        key_low = rotate(raw_heads[:, 1], cosine, sine).astype(bf16)
        value_low = raw_heads[:, 2].astype(bf16)

        def forward_step(running, piece_parts, offset):
            run_peak, run_total, run_acc = running
            key_part, value_part = piece_parts
            key_seg, _ = seq_info(
                lax.dynamic_slice_in_dim(perm_row, offset, key_part.shape[0]), seq_lens
            )
            scores = (
                jnp.einsum("qhe,khe->hqk", query_low, key_part, preferred_element_type=f32)
                * score_scale
            )
            same_seq = (query_seg[:, None] == key_seg[None, :])[None]
            block_top = jnp.max(jnp.where(same_seq, scores, -1e30), axis=-1)
            new_peak = jnp.maximum(run_peak, block_top)
            weights = jnp.where(same_seq, jnp.exp(scores - new_peak[..., None]), 0.0)
            fade_factor = jnp.exp(run_peak - new_peak)
            run_acc = run_acc * jnp.transpose(fade_factor)[:, :, None] + jnp.einsum(
                "hqk,khe->qhe", weights.astype(bf16), value_part, preferred_element_type=f32
            )
            run_total = run_total * fade_factor + jnp.sum(weights, axis=-1)
            return (new_peak, run_total, run_acc)

        start_state = (
            jnp.full((head_count, tok_rows), -1e30, f32),
            jnp.zeros((head_count, tok_rows), f32),
            jnp.zeros((tok_rows, head_count, HD), f32),
        )
        run_peak, run_total, run_acc = blockwise(
            start_state,
            (
                lax.all_gather(key_low, "fsdp", axis=0, tiled=True),
                lax.all_gather(value_low, "fsdp", axis=0, tiled=True),
            ),
            jnp.int32(0),
            forward_step,
        )
        log_total = run_peak + jnp.log(run_total)
        mixed_heads = run_acc / jnp.transpose(run_total)[:, :, None]
        mixed_low = mixed_heads.reshape(tok_rows, head_cols).astype(bf16)
        attn_part = lax.dot_general(mixed_low, fetched[3], dims_cols, preferred_element_type=f32)
        branch = lax.psum(attn_part.astype(jnp.bfloat16), "tp").astype(jnp.float32)
        hidden = x_float + branch
        normed_two = layer_norm(hidden, gain_second).astype(bf16)
        ffn_proj = jnp.einsum("td,dcf->tcf", normed_two, fetched[4], preferred_element_type=f32)
        act_low = (jax.nn.gelu(ffn_proj[:, 0], approximate=False) * ffn_proj[:, 1]).astype(bf16)
        ffn_part = lax.dot_general(act_low, fetched[5], dims_cols, preferred_element_type=f32)
        branch_two = lax.psum(ffn_part.astype(jnp.bfloat16), "tp").astype(jnp.float32)
        outputs.append((hidden + branch_two).astype(bf16))
        again = (
            lax.all_gather(gain_one, "fsdp", axis=0, tiled=True),
            lax.all_gather(gain_two, "fsdp", axis=0, tiled=True),
            lax.all_gather(w_qkv, "fsdp", axis=0, tiled=True),
            lax.all_gather(w_attn_out, "fsdp", axis=0, tiled=True),
            lax.all_gather(w_in, "fsdp", axis=0, tiled=True),
            lax.all_gather(w_down, "fsdp", axis=0, tiled=True),
        )
        gain_first = again[0].astype(f32)
        gain_second = again[1].astype(f32)
        grad_low = cotangent[micro_idx]
        grad_float = grad_low.astype(f32)
        acc_down = acc_down + lax.dot_general(
            grad_low, act_low, dims_rows, preferred_element_type=f32
        )
        d_act = jnp.dot(grad_low, again[5], preferred_element_type=f32)
        _, gelu_pull = jax.vjp(
            lambda inputs, gates: jax.nn.gelu(inputs, approximate=False) * gates,
            ffn_proj[:, 0],
            ffn_proj[:, 1],
        )
        d_inputs, d_gates = gelu_pull(d_act)
        d_proj = jnp.stack([d_inputs, d_gates], axis=1).astype(bf16)
        acc_in = acc_in + jnp.einsum("td,tcf->dcf", normed_two, d_proj, preferred_element_type=f32)
        norm_part = jnp.einsum("tcf,dcf->td", d_proj, again[4], preferred_element_type=f32)
        d_norm_two = lax.psum(norm_part.astype(jnp.bfloat16), "tp").astype(jnp.float32)
        _, second_pull = jax.vjp(layer_norm, hidden, gain_second)
        d_hid_norm, d_gain_two = second_pull(d_norm_two)
        acc_gain_two = acc_gain_two + d_gain_two
        d_hidden = grad_float + d_hid_norm
        hidden_low = d_hidden.astype(bf16)
        acc_out = acc_out + lax.dot_general(
            hidden_low, mixed_low, dims_rows, preferred_element_type=f32
        )
        d_mixed = jnp.dot(hidden_low, again[3], preferred_element_type=f32).astype(bf16)
        d_mixed = d_mixed.reshape(tok_rows, head_count, HD)
        delta_rows = jnp.sum(d_mixed.astype(f32) * mixed_heads, axis=-1)
        delta_heads = jnp.transpose(delta_rows)

        def query_step(grad_query, piece_parts, offset):
            key_part, value_part = piece_parts
            key_seg, _ = seq_info(
                lax.dynamic_slice_in_dim(perm_row, offset, key_part.shape[0]), seq_lens
            )
            scores = (
                jnp.einsum("qhe,khe->hqk", query_low, key_part, preferred_element_type=f32)
                * score_scale
            )
            same_seq = (query_seg[:, None] == key_seg[None, :])[None]
            weights = jnp.where(same_seq, jnp.exp(scores - log_total[..., None]), 0.0)
            d_weights = jnp.einsum("qhe,khe->hqk", d_mixed, value_part, preferred_element_type=f32)
            d_scores = (weights * (d_weights - delta_heads[..., None])).astype(bf16)
            return grad_query + score_scale * jnp.einsum(
                "hqk,khe->qhe", d_scores, key_part, preferred_element_type=f32
            )

        query_start = jnp.zeros((tok_rows, head_count, HD), f32)
        grad_query = blockwise(
            query_start,
            (
                lax.all_gather(key_low, "fsdp", axis=0, tiled=True),
                lax.all_gather(value_low, "fsdp", axis=0, tiled=True),
            ),
            jnp.int32(0),
            query_step,
        )
        stat_total, stat_delta = (
            lax.all_gather(jnp.transpose(log_total), "fsdp", axis=0, tiled=True),
            lax.all_gather(delta_rows, "fsdp", axis=0, tiled=True),
        )

        def key_step(running, piece_parts, offset):
            grad_key, grad_value = running
            query_part, dmix_part = piece_parts
            piece_len = query_part.shape[0]
            piece_seg, _ = seq_info(lax.dynamic_slice_in_dim(perm_row, offset, piece_len), seq_lens)
            total_part = jnp.transpose(lax.dynamic_slice_in_dim(stat_total, offset, piece_len))
            delta_part = jnp.transpose(lax.dynamic_slice_in_dim(stat_delta, offset, piece_len))
            scores = (
                jnp.einsum("qhe,khe->hqk", query_part, key_low, preferred_element_type=f32)
                * score_scale
            )
            same_seq = (piece_seg[:, None] == query_seg[None, :])[None]
            weights = jnp.where(same_seq, jnp.exp(scores - total_part[..., None]), 0.0)
            d_weights = jnp.einsum("qhe,khe->hqk", dmix_part, value_low, preferred_element_type=f32)
            d_scores = (weights * (d_weights - delta_part[..., None])).astype(bf16)
            grad_key = grad_key + score_scale * jnp.einsum(
                "hqk,qhe->khe", d_scores, query_part, preferred_element_type=f32
            )
            grad_value = grad_value + jnp.einsum(
                "hqk,qhe->khe", weights.astype(bf16), dmix_part, preferred_element_type=f32
            )
            return (grad_key, grad_value)

        grad_key, grad_value = blockwise(
            (
                jnp.zeros((tok_rows, head_count, HD), f32),
                jnp.zeros((tok_rows, head_count, HD), f32),
            ),
            (
                lax.all_gather(query_low, "fsdp", axis=0, tiled=True),
                lax.all_gather(d_mixed, "fsdp", axis=0, tiled=True),
            ),
            jnp.int32(0),
            key_step,
        )
        _, rope_pull = jax.vjp(lambda heads_in: rotate(heads_in, cosine, sine), raw_heads[:, 0])
        d_raw_query = rope_pull(grad_query)[0]
        d_raw_key = rope_pull(grad_key)[0]
        d_raw = (
            jnp.stack([d_raw_query, d_raw_key, grad_value], axis=1)
            .reshape(tok_rows, 3, head_cols)
            .astype(bf16)
        )
        acc_qkv = acc_qkv + jnp.einsum("td,tcf->dcf", normed_low, d_raw, preferred_element_type=f32)
        first_part = jnp.einsum("tcf,dcf->td", d_raw, again[2], preferred_element_type=f32)
        d_norm_one = lax.psum(first_part.astype(jnp.bfloat16), "tp").astype(jnp.float32)
        _, first_pull = jax.vjp(layer_norm, x_float, gain_first)
        d_x_norm, d_gain_one = first_pull(d_norm_one)
        acc_gain_one = acc_gain_one + d_gain_one
        d_input = (d_hidden + d_x_norm).astype(bf16)
        back_rows = d_input[recv_order].reshape(groups, per_pair, D)
        returned = lax.all_to_all(
            back_rows, "fsdp", split_axis=0, concat_axis=0, tiled=True
        ).reshape(tok_rows, D)
        send_slot = jnp.zeros((tok_rows,), jnp.int32).at[send_order].set(rows_idx)
        input_grads.append(returned[send_slot])
    summed = (
        lax.psum_scatter(acc_qkv, "fsdp", scatter_dimension=0, tiled=True),
        lax.psum_scatter(acc_out, "fsdp", scatter_dimension=0, tiled=True),
        lax.psum_scatter(acc_in, "fsdp", scatter_dimension=0, tiled=True),
        lax.psum_scatter(acc_down, "fsdp", scatter_dimension=0, tiled=True),
        lax.psum_scatter(acc_gain_one, "fsdp", scatter_dimension=0, tiled=True),
        lax.psum_scatter(acc_gain_two, "fsdp", scatter_dimension=0, tiled=True),
    )
    return (
        jnp.stack(outputs),
        jnp.stack(input_grads),
        summed[0],
        summed[1],
        summed[2],
        summed[3],
        summed[4],
        summed[5],
    )


JOIN = 2
COSTS = {"attend": 10, "attend_back": 15, "feed": 8, "feed_grad": 5, "down": 3}
FAR = -1e30
ORDER = (0, 2, 4, 6, 1, 3, 5, 7)
NT = (((1,), (1,)), ((), ()))
TN = (((0,), (0,)), ((), ()))
NN = (((1,), (0,)), ((), ()))
ROOM = 10 * 1024 * 1024


def partial(kernel, *given):
    return lambda *refs: kernel(*given, *refs)


def mm(left, right, dims):
    return lax.dot_general(left, right, dims, preferred_element_type=jnp.float32)


def hop(value, step):
    return lax.ppermute(value, "fsdp", [(i, i ^ step) for i in range(8)])


def twin(value):
    return lax.ppermute(value, "tp", [(i, i ^ 1) for i in range(4)])


def across(value):
    return lax.ppermute(value, "tp", [(i, i ^ 2) for i in range(4)])


def deal_out(value):
    return lax.all_to_all(value, "fsdp", 0, 0, tiled=True)


def after(value, *earlier):
    return lax.optimization_barrier((value,) + earlier)[0]


def sync(values):
    return lax.optimization_barrier(values)


def z_phase(shard):
    return [shard] + [hop(shard, step) for step in ORDER[1:4]]


def y_phase(shards):
    return [hop(one, 1) for one in shards]


def local_call(kernel, name, scalars, arrays, outs, scratch=(), shards=(), copies=8, far_in=(), far_out=(), far_shards=True):
    shapes = [(one.shape, one.dtype) for one in arrays]
    staged = [shapes[at] for at in far_in] + [outs[at] for at in far_out]
    sems = [pltpu.SemaphoreType.DMA((copies,))] if shards else []
    room = ROOM + sum(math.prod(shape) * jnp.dtype(kind).itemsize for shape, kind in [*shapes, *outs, *scratch])
    counts = (len(scalars), len(arrays), len(shards), len(outs), len(scratch) + len(sems))

    def body(*refs):
        groups = []
        for count in counts:
            groups.append(list(refs[:count]))
            refs = refs[count:]
        given, ins, pieces, results, extra = groups
        if not staged:
            return kernel(*given, *ins, *pieces, *results, *extra)
        stage, sem = refs[:-1], refs[-1]
        incoming, outgoing = [], []
        for slot, at in enumerate(far_in):
            incoming.append(pltpu.make_async_copy(ins[at], stage[slot], sem.at[slot]))
            incoming[-1].start()
            ins[at] = stage[slot]
        for slot, at in enumerate(far_out, len(far_in)):
            outgoing.append(pltpu.make_async_copy(stage[slot], results[at], sem.at[slot]))
            results[at] = stage[slot]
        for copy in incoming:
            copy.wait()
        kernel(*given, *ins, *pieces, *results, *extra)
        for copy in outgoing:
            copy.start()
        for copy in outgoing:
            copy.wait()

    arrays = [pltpu.with_memory_space_constraint(one, pltpu.HBM) if at in far_in else one for at, one in enumerate(arrays)]
    shards = [pltpu.with_memory_space_constraint(one, pltpu.HBM) if far_shards else one for one in shards]

    def space(at, far):
        return pl.BlockSpec(memory_space=pltpu.HBM if at in far else pltpu.VMEM)

    result = pl.pallas_call(
        body,
        in_specs=[pl.BlockSpec(memory_space=pltpu.SMEM)] * len(scalars)
        + [space(at, far_in) for at in range(len(arrays))]
        + [pl.BlockSpec(memory_space=pltpu.HBM if far_shards else pl.ANY)] * len(shards),
        out_specs=[space(at, far_out) for at in range(len(outs))],
        out_shape=[
            pltpu.HBM(shape, kind) if at in far_out else jax.ShapeDtypeStruct(shape, kind)
            for at, (shape, kind) in enumerate(outs)
        ],
        scratch_shapes=[pltpu.VMEM(shape, kind) for shape, kind in scratch]
        + sems
        + [pltpu.VMEM(shape, kind) for shape, kind in staged]
        + ([pltpu.SemaphoreType.DMA((len(staged),))] if staged else []),
        compiler_params=pltpu.CompilerParams(vmem_limit_bytes=room),
        cost_estimate=pl.CostEstimate(flops=COSTS.get(name, 3) * 10**9, transcendentals=0, bytes_accessed=8 * 1024 * 1024),
        name=name,
    )(*scalars, *arrays, *shards)
    return result if len(outs) > 1 else result[0]


def block_at(order_ref, place, width):
    return pl.ds(pl.multiple_of(order_ref[place] * width, width), width)


def shard_copies(shards, low, high, into_ref, sem_ref, base=0):
    width = shards[0].shape[1]
    copies = []
    for place, shard in enumerate(shards):
        span = pl.ds(place * width, width)
        source = shard.at[pl.ds(low, high - low), :]
        copies.append(pltpu.make_async_copy(source, into_ref.at[:, span], sem_ref.at[base + place]))
        copies[-1].start()
    return copies


def gathered_copies(order_ref, source, low, high, into_ref, sem_ref, base=0):
    width = source.shape[2]
    copies = []
    for place in range(8):
        copies.append(
            pltpu.make_async_copy(
                source.at[order_ref[place], pl.ds(low, high - low), :],
                into_ref.at[:, pl.ds(place * width, width)],
                sem_ref.at[base + place],
            )
        )
        copies[-1].start()
    return copies


def finish(copies):
    for copy in copies:
        copy.wait()


def project_kernel(order_ref, x_ref, table_ref, *refs):
    shards = refs[:8]
    norm_ref, gains_ref, send_ref, w_ref, sem_ref = refs[8:]
    width = shards[0].shape[1]
    rows = x_ref.shape[1]
    wide = w_ref.shape[0] - 16
    heads = wide // (3 * HD)
    half = HD // 2
    finish(shard_copies(shards, 0, wide + 16, w_ref, sem_ref))
    gains_ref[...] = w_ref[wide:, :].astype(jnp.float32)[:2]
    for micro in range(2):
        x = x_ref[micro].astype(jnp.float32)
        mean = jnp.mean(x, axis=-1, keepdims=True)
        center = x - mean
        spread = lax.rsqrt(jnp.mean(center * center, axis=-1, keepdims=True) + EPS)
        for place in range(8):
            piece = x_ref[micro, :, block_at(order_ref, place, width)].astype(jnp.float32)
            span = slice(place * width, (place + 1) * width)
            value = (piece - mean) * spread * gains_ref[0:1, span]
            norm_ref[micro * rows : (micro + 1) * rows, span] = value.astype(jnp.bfloat16)
    raw = mm(w_ref[:wide, :], norm_ref[...], NT)
    cosine, sine = table_ref[:half, :], table_ref[half:, :]
    for head in range(heads):
        base = head * 3 * HD
        for kind in range(2):
            upper = raw[base + kind * HD : base + kind * HD + half]
            lower = raw[base + kind * HD + half : base + (kind + 1) * HD]
            first = (upper * cosine - lower * sine).astype(jnp.bfloat16)
            second = (lower * cosine + upper * sine).astype(jnp.bfloat16)
            for micro in range(2):
                span = slice(micro * rows, (micro + 1) * rows)
                send_ref[micro * heads + head, kind * HD : kind * HD + half, :] = first[:, span]
                send_ref[micro * heads + head, kind * HD + half : (kind + 1) * HD, :] = second[:, span]
        value = raw[base + 2 * HD : base + 3 * HD].astype(jnp.bfloat16)
        for micro in range(2):
            send_ref[micro * heads + head, 2 * HD :, :] = value[:, micro * rows : (micro + 1) * rows]


def key_range(lens_ref, low, high):
    first = jnp.int32(0)
    last = jnp.int32(0)
    total = jnp.int32(0)
    for index in range(lens_ref.shape[0]):
        start = total
        total = total + lens_ref[index]
        first = jnp.where((start <= low) & (low < total), start, first)
        last = jnp.where((start <= high) & (high < total), total, last)
    return first, last


def query_bounds(lens_ref, base, width):
    place = base + lax.broadcasted_iota(jnp.int32, (1, width), 1)
    first = jnp.zeros((1, width), jnp.int32)
    last = jnp.zeros((1, width), jnp.int32)
    total = jnp.int32(0)
    for index in range(lens_ref.shape[0]):
        start = total
        total = total + lens_ref[index]
        inside = (place >= start) & (place < total)
        first = jnp.where(inside, start, first)
        last = jnp.where(inside, total, last)
    return first, last


def lanes(ref, index, count, rows):
    return jnp.concatenate([ref[index * count + at, rows, :] for at in range(count)], axis=1)


def attend_kernel(lens_ref, qkv_ref, mixed_ref, exact_ref, log_ref, key_ref):
    blocks, _, small = qkv_ref.shape
    wide = JOIN * small
    for at in range(blocks):
        block = qkv_ref[at, HD : 2 * HD, :].astype(jnp.float32)
        key_ref[at * small : (at + 1) * small, :] = jnp.transpose(block).astype(jnp.bfloat16)

    def one_query(index, carry):
        base = index * wide
        first, last = key_range(lens_ref, base, base + wide - 1)
        low, high = query_bounds(lens_ref, base, wide)
        query = lanes(qkv_ref, index, JOIN, slice(0, HD)) * jnp.bfloat16(HD**-0.5)

        def one_key(at, state):
            peak, total, acc = state
            start = pl.multiple_of(at * wide, wide)
            scores = mm(key_ref[pl.ds(start, wide), :], query, NN)
            place = start + lax.broadcasted_iota(jnp.int32, (wide, wide), 0)
            scores = jnp.where((place >= low) & (place < high), scores, FAR)
            top = jnp.maximum(peak, jnp.max(scores, axis=0, keepdims=True))
            weights = jnp.exp(scores - top)
            fade = jnp.exp(peak - top)
            total = total * fade + jnp.sum(weights, axis=0, keepdims=True)
            value = lanes(qkv_ref, at, JOIN, slice(2 * HD, 3 * HD))
            acc = acc * fade + mm(value, weights.astype(jnp.bfloat16), NN)
            return top, total, acc

        peak, total, acc = lax.fori_loop(
            first // wide,
            (last + wide - 1) // wide,
            one_key,
            (
                jnp.full((1, wide), FAR, jnp.float32),
                jnp.zeros((1, wide), jnp.float32),
                jnp.zeros((HD, wide), jnp.float32),
            ),
        )
        result = acc / total
        logs = peak + jnp.log(total)
        for at in range(JOIN):
            span = slice(at * small, (at + 1) * small)
            mixed_ref[index * JOIN + at] = result[:, span].astype(jnp.bfloat16)
            exact_ref[index * JOIN + at] = result[:, span]
            log_ref[index * JOIN + at] = logs[:, span]
        return carry

    lax.fori_loop(0, blocks // JOIN, one_query, 0)


def attend_back_kernel(
    lens_ref, qkv_ref, exact_ref, log_ref, grad_ref, table_ref, raw_ref, pair_ref, dkey_ref, dvalue_ref
):
    blocks, _, small = qkv_ref.shape
    wide = JOIN * small
    half = HD // 2
    for at in range(blocks):
        block = qkv_ref[at, HD : 3 * HD, :].astype(jnp.float32)
        pair_ref[at * small : (at + 1) * small, :] = jnp.transpose(block).astype(jnp.bfloat16)
    dkey_ref[...] = jnp.zeros(dkey_ref.shape, jnp.float32)
    dvalue_ref[...] = jnp.zeros(dvalue_ref.shape, jnp.float32)

    def unturn(index, grad):
        cosine = table_ref[index, :half, :]
        sine = table_ref[index, half:, :]
        upper, lower = grad[:half], grad[half:]
        return upper * cosine + lower * sine, lower * cosine - upper * sine

    def one_query(index, carry):
        base = index * wide
        first, last = key_range(lens_ref, base, base + wide - 1)
        low, high = query_bounds(lens_ref, base, wide)
        query = lanes(qkv_ref, index, JOIN, slice(0, HD)) * jnp.bfloat16(HD**-0.5)
        grad = lanes(grad_ref, index, JOIN, slice(0, HD))
        logs = lanes(log_ref, index, JOIN, slice(0, 1))
        exact = lanes(exact_ref, index, JOIN, slice(0, HD))
        delta = jnp.sum(grad.astype(jnp.float32) * exact, axis=0, keepdims=True)

        def one_key(at, dquery):
            start = pl.multiple_of(at * wide, wide)
            span = pl.ds(start, wide)
            scores = mm(pair_ref[span, :HD], query, NN)
            dweights = mm(pair_ref[span, HD:], grad, NN)
            place = start + lax.broadcasted_iota(jnp.int32, (wide, wide), 0)
            weights = jnp.where((place >= low) & (place < high), jnp.exp(scores - logs), 0.0)
            dscores = (weights * (dweights - delta)).astype(jnp.bfloat16)
            dkey_ref[:, span] += mm(query, dscores, NT)
            dvalue_ref[:, span] += mm(grad, weights.astype(jnp.bfloat16), NT)
            return dquery + mm(lanes(qkv_ref, at, JOIN, slice(HD, 2 * HD)), dscores, NN)

        dquery = lax.fori_loop(
            first // wide,
            (last + wide - 1) // wide,
            one_key,
            jnp.zeros((HD, wide), jnp.float32),
        ) * (HD**-0.5)
        for at in range(JOIN):
            upper, lower = unturn(index * JOIN + at, dquery[:, at * small : (at + 1) * small])
            raw_ref[index * JOIN + at, :half, :] = upper.astype(jnp.bfloat16)
            raw_ref[index * JOIN + at, half:HD, :] = lower.astype(jnp.bfloat16)
        return carry

    lax.fori_loop(0, blocks // JOIN, one_query, 0)
    for at in range(blocks):
        span = slice(at * small, (at + 1) * small)
        upper, lower = unturn(at, dkey_ref[:, span])
        raw_ref[at, HD : HD + half, :] = upper.astype(jnp.bfloat16)
        raw_ref[at, HD + half : 2 * HD, :] = lower.astype(jnp.bfloat16)
        raw_ref[at, 2 * HD :, :] = dvalue_ref[:, span].astype(jnp.bfloat16)


def mix_out_kernel(core_ref, order_ref, mixed_ref, all_ref, send_ref, keep_ref, w_ref, sem_ref):
    last = all_ref.shape[1]
    finish(gathered_copies(order_ref, all_ref, last - mixed_ref.shape[1], last, w_ref, sem_ref))
    core = core_ref[0]
    send_ref[...] = mm(mixed_ref[1 - core], w_ref[...], TN).astype(jnp.bfloat16)
    keep_ref[...] = mm(mixed_ref[core], w_ref[...], TN)


def norm_two_kernel(core_ref, order_ref, x_ref, half_ref, far_ref, gains_ref, hidden_ref, norm_ref):
    core = core_ref[0]
    width = x_ref.shape[2] // 8
    for place in range(8):
        span = slice(place * width, (place + 1) * width)
        piece = x_ref[core, :, block_at(order_ref, place, width)].astype(jnp.float32)
        branch = half_ref[:, span].astype(jnp.float32) + far_ref[:, span].astype(jnp.float32)
        hidden_ref[:, span] = piece + branch
    hidden = hidden_ref[...]
    center = hidden - jnp.mean(hidden, axis=-1, keepdims=True)
    spread = lax.rsqrt(jnp.mean(center * center, axis=-1, keepdims=True) + EPS)
    norm_ref[...] = (center * spread * gains_ref[1:2, :]).astype(jnp.bfloat16)


def feed_kernel(
    order_ref, own_ref, other_ref, grad_ref, all_ref, down_ref, send_ref, keep_ref, act_ref, dinp_ref, dgate_ref, w_ref, sem_ref
):
    units = w_ref.shape[0] // 3
    inp_w, gate_w, down_w = [w_ref.at[pl.ds(at * units, units), :] for at in range(3)]
    rows = own_ref.shape[0]
    first_copies = gathered_copies(order_ref, all_ref, 0, 2 * units, w_ref.at[pl.ds(0, 2 * units), :], sem_ref)
    finish(gathered_copies(order_ref, down_ref, 0, units, down_w, sem_ref, 8))
    finish(first_copies)
    for micro, norm_ref in ((1, other_ref), (0, own_ref)):
        span = slice(micro * rows, (micro + 1) * rows)
        inp = mm(norm_ref[...], inp_w[...], NT)
        gate = mm(norm_ref[...], gate_w[...], NT)
        dact = mm(grad_ref[micro], down_w[...], NT)
        cdf = 0.5 * (1.0 + lax.erf(inp * (0.5**0.5)))
        density = jnp.exp(-0.5 * inp * inp) * ((0.5 / jnp.pi) ** 0.5)
        gelu = inp * cdf
        act_ref[span, :] = (gelu * gate).astype(jnp.bfloat16)
        dinp = (dact * gate * (cdf + inp * density)).astype(jnp.bfloat16)
        dgate = (dact * gelu).astype(jnp.bfloat16)
        dinp_ref[span, :] = dinp
        dgate_ref[span, :] = dgate
        part = mm(dinp, inp_w[...], NN) + mm(dgate, gate_w[...], NN)
        if micro:
            send_ref[...] = part.astype(jnp.bfloat16)
        else:
            keep_ref[...] = part


def weight_grad_kernel(order_ref, dinp_ref, dgate_ref, act_ref, own_ref, other_ref, grad_ref, out_ref):
    units = act_ref.shape[1]
    rows = own_ref.shape[0]
    width = out_ref.shape[2]
    for at, (left_ref, rights) in enumerate((
        (dinp_ref, (own_ref, other_ref)),
        (dgate_ref, (own_ref, other_ref)),
        (act_ref, (grad_ref.at[0], grad_ref.at[1])),
    )):
        total = mm(left_ref[:rows, :], rights[0][...], TN) + mm(left_ref[rows:, :], rights[1][...], TN)
        for place in range(8):
            piece = total[:, place * width : (place + 1) * width].astype(jnp.bfloat16)
            out_ref[order_ref[place], at * units : (at + 1) * units, :] = piece


def near_sum_kernel(near_ref, far_ref, own_ref, *low_refs):
    own_ref[...] = near_ref[0] + far_ref[0].astype(jnp.float32)
    for at, low_ref in enumerate(low_refs):
        low_ref[...] = (near_ref[at + 1] + far_ref[at + 1].astype(jnp.float32)).astype(jnp.bfloat16)


def down_kernel(order_ref, act_ref, all_ref, send_ref, keep_ref, w_ref, sem_ref):
    rows = send_ref.shape[0]
    units = w_ref.shape[0]
    finish(gathered_copies(order_ref, all_ref, 0, units, w_ref, sem_ref))
    send_ref[...] = mm(act_ref[rows:, :], w_ref[...], NN).astype(jnp.bfloat16)
    keep_ref[...] = mm(act_ref[:rows, :], w_ref[...], NN)


def norm_two_back_kernel(hidden_ref, half_ref, far_ref, grad_ref, gains_ref, dhidden_ref, low_ref):
    hidden = hidden_ref[...]
    center = hidden - jnp.mean(hidden, axis=-1, keepdims=True)
    spread = lax.rsqrt(jnp.mean(center * center, axis=-1, keepdims=True) + EPS)
    xhat = center * spread
    dnorm = half_ref[...].astype(jnp.float32) + far_ref[...].astype(jnp.float32)
    scaled = dnorm * gains_ref[1:2, :]
    inner = scaled - jnp.mean(scaled, axis=-1, keepdims=True)
    inner = inner - xhat * jnp.mean(scaled * xhat, axis=-1, keepdims=True)
    total = grad_ref[0].astype(jnp.float32) + inner * spread
    dhidden_ref[...] = total
    low_ref[...] = total.astype(jnp.bfloat16)


def mix_back_kernel(core_ref, own_ref, other_ref, w_ref, send_ref):
    cols = w_ref.shape[0]
    heads = cols // HD
    core = core_ref[0]
    for micro, low_ref in ((core, own_ref), (1 - core, other_ref)):
        total = mm(w_ref[...], low_ref[...], NT).astype(jnp.bfloat16)
        for head in range(heads):
            send_ref[micro * heads + head] = total[head * HD : (head + 1) * HD, :]


def mix_grad_kernel(core_ref, mixed_ref, own_ref, other_ref, far_ref, near_ref):
    core = core_ref[0]
    width = far_ref.shape[2]
    total = mm(mixed_ref[core], own_ref[...], NN) + mm(mixed_ref[1 - core], other_ref[...], NN)
    for place in range(4):
        near_ref[place] = total[:, place * width : (place + 1) * width]
        far_ref[place] = total[:, (4 + place) * width : (5 + place) * width].astype(jnp.bfloat16)


def project_back_kernel(core_ref, raw_ref, w_ref, send_ref, keep_ref):
    core = core_ref[0]
    weights = w_ref[: raw_ref.shape[1], :]
    send_ref[...] = mm(raw_ref[1 - core], weights, TN).astype(jnp.bfloat16)
    keep_ref[...] = mm(raw_ref[core], weights, TN)


def project_grad_kernel(first, raw_ref, norm_ref, far_ref, near_ref):
    count, width = far_ref.shape[1:]
    rows = raw_ref.shape[2]
    span = slice(first, first + count)
    total = mm(raw_ref[0, span, :], norm_ref[:rows, :], NN) + mm(raw_ref[1, span, :], norm_ref[rows:, :], NN)
    for place in range(4):
        near_ref[place] = total[:, place * width : (place + 1) * width]
        far_ref[place] = total[:, (4 + place) * width : (5 + place) * width].astype(jnp.bfloat16)


def norm_one_back_kernel(
    core_ref, order_ref, x_ref, half_ref, far_ref, dhidden_ref, gains_ref, grad_ref, xhat_ref
):
    core = core_ref[0]
    width = x_ref.shape[2] // 8
    x = x_ref[core].astype(jnp.float32)
    mean = jnp.mean(x, axis=-1, keepdims=True)
    center = x - mean
    spread = lax.rsqrt(jnp.mean(center * center, axis=-1, keepdims=True) + EPS)
    for place in range(8):
        span = slice(place * width, (place + 1) * width)
        piece = x_ref[core, :, block_at(order_ref, place, width)].astype(jnp.float32)
        xhat_ref[:, span] = (piece - mean) * spread
    xhat = xhat_ref[...]
    dnorm = half_ref[...].astype(jnp.float32) + far_ref[...].astype(jnp.float32)
    scaled = dnorm * gains_ref[0:1, :]
    inner = scaled - jnp.mean(scaled, axis=-1, keepdims=True)
    inner = inner - xhat * jnp.mean(scaled * xhat, axis=-1, keepdims=True)
    total = (dhidden_ref[...] + inner * spread).astype(jnp.bfloat16)
    for place in range(8):
        grad_ref[:, block_at(order_ref, place, width)] = total[:, place * width : (place + 1) * width]


def place_grad_kernel(core_ref, order_ref, local_ref, four_ref, grad_ref, natural_ref):
    rows = grad_ref.shape[1]
    width = grad_ref.shape[2] // 8
    core = core_ref[0]
    for at in range(2):
        micro = core if at == 0 else 1 - core
        place = lax.broadcasted_iota(jnp.int32, (rows, rows), 0)
        onehot = jnp.where(local_ref[pl.ds(micro, 1), :] == place, 1.0, 0.0).astype(jnp.bfloat16)
        natural_ref[...] = mm(onehot, four_ref[micro], NN).astype(jnp.bfloat16)
        for block in range(8):
            span = slice(block * width, (block + 1) * width)
            grad_ref[at, :, span] = natural_ref[:, block_at(order_ref, block, width)]


def result_kernel(order_ref, picks_ref, hidden_ref, half_ref, far_ref, packed_ref, natural_ref):
    rows = hidden_ref.shape[0]
    width = hidden_ref.shape[1] // 8
    branch = half_ref[...].astype(jnp.float32) + far_ref[...].astype(jnp.float32)
    total = (hidden_ref[...] + branch).astype(jnp.bfloat16)
    for block in range(8):
        natural_ref[:, block_at(order_ref, block, width)] = total[:, block * width : (block + 1) * width]
    count = packed_ref.shape[0]
    place = lax.broadcasted_iota(jnp.int32, (rows, count), 0)
    onehot = jnp.where(picks_ref[...] == place, 1.0, 0.0).astype(jnp.bfloat16)
    packed_ref[...] = mm(onehot, natural_ref[...], TN).astype(jnp.bfloat16)


def positions(anchor, seq_lens):
    ends = running_ends(seq_lens)
    starts = ends - seq_lens
    inside = (anchor[:, None] >= starts[None, :]) & (anchor[:, None] < ends[None, :])
    return anchor - jnp.sum(jnp.where(inside, starts[None, :], 0), axis=1)


def turn_tables(place):
    freqs = jnp.power(THETA, -jnp.arange(HD // 2, dtype=jnp.float32) * 2.0 / HD)
    angle = freqs[:, None] * place.astype(jnp.float32)[None, :]
    return jnp.concatenate([jnp.cos(angle), jnp.sin(angle)], axis=0)


def paired_layer(
    tokens, cotangent, perm, lengths, w_qkv, w_attn_out, w_in, w_down, gain_one, gain_two
):
    f32, bf16, i32 = jnp.float32, jnp.bfloat16, jnp.int32
    mine = lax.axis_index("fsdp")
    part = lax.axis_index("tp")
    core, side = part & 1, part >> 1
    core_at = core.reshape(1).astype(i32)
    rows = tokens.shape[1]
    width = w_qkv.shape[0]
    full = 8 * width
    cols = w_qkv.shape[2]
    heads = cols // HD
    units = w_in.shape[2]
    per_pair = rows // 8
    order = jnp.bitwise_xor(jnp.array(ORDER, i32), mine)

    def pick(value, index):
        return lax.dynamic_index_in_dim(value, index, 0, keepdims=False)

    def both(value, other):
        return jnp.stack([jnp.where(core == 0, value, other), jnp.where(core == 0, other, value)])

    def add_half(keep, got):
        return (keep + got.astype(f32)).astype(bf16)

    def near_sum(near, far, name):
        shape = near.shape[1:]
        own, *lows = local_call(near_sum_kernel, name, (), (near, far), [(shape, f32)] + [(shape, bf16)] * 3, far_in=(0, 1), far_out=(0,))
        return own, lows

    def y_join(same):
        return same + [hop(jnp.concatenate(same, axis=0), 1)]

    def z_send(lows):
        return [hop(low, ORDER[at + 1]) for at, low in enumerate(lows)]

    def far_sum(own, got):
        return own + sum(one.astype(f32) for one in got)

    turned = jnp.transpose(w_qkv.reshape(width, 3, heads, HD), (2, 1, 3, 0)).reshape(3 * cols, width)
    gains_rows = jnp.concatenate([gain_one[None], gain_two[None], jnp.zeros((14, width), bf16)])
    first_same = z_phase(jnp.concatenate([turned, gains_rows], axis=0))
    first = first_same + y_phase(first_same)

    slots = perm.reshape(2, 8, rows)
    from_me = (slots // rows == mine).astype(f32)
    slot_no = jnp.arange(rows, dtype=i32)
    before = (slot_no[:, None] < slot_no[None, :]).astype(f32)
    rank_me = jnp.einsum("mds,st->mdt", from_me, before).astype(i32)
    ranks = jnp.arange(per_pair, dtype=i32)
    chosen = (from_me[..., None] > 0) & (rank_me[..., None] == ranks)
    local = jnp.sum(jnp.where(chosen, (slots % rows)[..., None], 0), axis=2)
    my_slots = lax.dynamic_index_in_dim(slots, mine, 1, keepdims=False)
    target = my_slots // rows
    same = (target[:, :, None] == target[:, None, :]) & (slot_no[:, None] < slot_no[None, :])[None]
    rank_own = jnp.sum(same.astype(i32), axis=1)
    place_own = target * per_pair + rank_own
    quarter = per_pair // 4
    wanted = order[:, None] * per_pair + part * quarter
    wanted = (wanted + jnp.arange(quarter, dtype=i32)[None, :]).reshape(-1)
    packer = (place_own[:, None, :] == wanted[None, :, None]).astype(bf16)
    packed = jnp.einsum("mps,msd->mpd", packer, cotangent, preferred_element_type=f32).astype(bf16)
    packed = packed.reshape(2, 8, quarter, full)
    packed = [packed[:, at] for at in range(8)]
    chosen = order[:, None] == jnp.arange(8, dtype=i32)[None, :]
    local_own = jnp.sum(jnp.where(chosen[None, :, :, None], local[:, None], 0), axis=2)
    anchor = mine * rows + jnp.arange(rows, dtype=i32)
    own_table = jnp.concatenate([turn_tables(positions(anchor, lengths[m])) for m in range(2)], axis=1)
    inp_turned, gate_turned = jnp.transpose(w_in[:, 0]), jnp.transpose(w_in[:, 1])
    second = jnp.concatenate([jnp.transpose(w_down), jnp.transpose(w_attn_out)], axis=0)
    second_all = lax.all_gather(second, "fsdp", axis=0, tiled=False)
    third_all = lax.all_gather(jnp.concatenate([inp_turned, gate_turned], axis=0), "fsdp", axis=0, tiled=False)
    halfway = per_pair // 2
    picks = lax.dynamic_slice_in_dim(pick(local_own, core), side * halfway, halfway, 1).reshape(1, -1)
    row_of = (order[:, None] * per_pair + jnp.arange(per_pair, dtype=i32)[None, :]).reshape(-1)
    unpack = (place_own[:, :, None] == row_of[None, None, :]).astype(bf16)
    my_lens = lengths[mine // heads]
    all_anchor = jnp.arange(8 * rows, dtype=i32)
    table = turn_tables(positions(all_anchor, my_lens))
    table = jnp.transpose(table.reshape(HD, 8, rows), (1, 0, 2))
    first, packed, own_table, picks, unpack, table, local_own, order, core_at, core, side, my_lens = sync(
        (first, packed, own_table, picks, unpack, table, local_own, order, core_at, core, side, my_lens)
    )

    norm_one, gains, outgoing, qkv_w = local_call(
        project_kernel, "project", (order,), (tokens, own_table),
        [((2 * rows, full), bf16), ((2, full), f32), ((2 * heads, 3 * HD, rows), bf16), ((3 * cols + 16, full), bf16)],
        (), first, far_in=(0, 1), far_out=(0, 1, 2, 3), far_shards=False,
    )
    outgoing, packed = sync((outgoing, packed))
    qkv = deal_out(outgoing)
    arrived = [hop(one, ORDER[at]) if at else one for at, one in enumerate(packed)]
    qkv = sync((qkv,))[0]
    mixed_out, exact, logs = local_call(
        attend_kernel, "attend", (my_lens,), (qkv,),
        [((8, HD, rows), bf16), ((8, HD, rows), f32), ((8, 1, rows), f32)],
        [((8 * rows, HD), bf16)], far_in=(0,), far_out=(0, 1, 2),
    )
    mixed_out, arrived = sync((mixed_out, arrived))
    mixed = deal_out(mixed_out).reshape(2, cols, rows)
    arrived = jnp.stack(arrived)
    near = twin(arrived)
    pair = jnp.stack([jnp.where(core == 0, arrived, near), jnp.where(core == 0, near, arrived)])
    far = across(pair)
    mixed, far = sync((mixed, far))
    four = jnp.concatenate([jnp.where(side == 0, pair, far), jnp.where(side == 0, far, pair)])
    four = jnp.transpose(four, (2, 1, 0, 3, 4)).reshape(2, rows, full)
    grad = local_call(
        place_grad_kernel, "place_grad", (core_at, order), (local_own.reshape(2, rows), four),
        [((2, rows, full), bf16)], [((rows, full), bf16)],
    )

    send, keep, out_w = local_call(
        mix_out_kernel, "mix_out", (core_at, order), (mixed,),
        [((rows, full), bf16), ((rows, full), f32), ((cols, full), bf16)], (), (second_all,), far_in=(0,),
    )
    half = add_half(keep, twin(send))
    far = across(half)
    far, grad = sync((far, grad))
    hidden, two_own = local_call(
        norm_two_kernel, "norm_two", (core_at, order), (tokens, half, far, gains),
        [((rows, full), f32), ((rows, full), bf16)], far_in=(0, 3),
    )
    two_other = twin(two_own)

    send, keep, act, d_inp, d_gate = local_call(
        feed_kernel, "feed", (order,), (two_own, two_other, grad),
        [((rows, full), bf16), ((rows, full), f32)] + [((2 * rows, units), bf16)] * 3,
        [((3 * units, full), bf16)], (third_all, second_all), copies=16,
    )
    half_two = add_half(keep, twin(send))
    half_two, act, d_inp, d_gate = sync((half_two, act, d_inp, d_gate))
    far_two = across(half_two)
    feed_grad = local_call(
        weight_grad_kernel, "feed_grad", (order,), (d_inp, d_gate, act, two_own, two_other, grad),
        [((8, 3 * units, width), bf16)], far_out=(0,),
    )
    feed_sum = lax.psum_scatter(feed_grad, "fsdp", scatter_dimension=0, tiled=False)
    send, keep = local_call(
        down_kernel, "down", (order,), (act,),
        [((rows, full), bf16), ((rows, full), f32)], [((units, full), bf16)], (second_all,),
    )
    res_half = add_half(keep, twin(send))
    far_two, feed_grad, res_half = sync((far_two, feed_grad, res_half))
    d_hidden, low_own = local_call(
        norm_two_back_kernel, "norm_two_back", (), (hidden, half_two, far_two, grad, gains),
        [((rows, full), f32), ((rows, full), bf16)], far_in=(4,), far_out=(0,),
    )
    low_other = twin(low_own)
    d_mixed = local_call(
        mix_back_kernel, "mix_back", (core_at,), (low_own, low_other, out_w),
        [((8, HD, rows), bf16)], far_out=(0,),
    )
    out_far, out_near = local_call(
        mix_grad_kernel, "mix_grad", (core_at,), (mixed, low_own, low_other),
        [((4, cols, width), bf16), ((4, cols, width), f32)], far_in=(0,), far_out=(1,),
    )
    d_mixed, out_far = sync((d_mixed, out_far))
    grad_mixed = deal_out(d_mixed)
    res_far = across(res_half)
    grad_mixed, res_far = sync((grad_mixed, res_far))

    out_got = hop(out_far, 1)
    d_raw_out = local_call(
        attend_back_kernel, "attend_back", (my_lens,), (qkv, exact, logs, grad_mixed, table),
        [((8, 3 * HD, rows), bf16)],
        [((8 * rows, 2 * HD), bf16), ((HD, 8 * rows), f32), ((HD, 8 * rows), f32)],
        far_in=(0, 1, 2, 3, 4), far_out=(0,),
    )
    d_raw_out, out_got = sync((d_raw_out, out_got))
    d_raw = deal_out(d_raw_out).reshape(2, 3 * cols, rows)
    out_own, out_lows = near_sum(out_near, out_got, "out_near")
    packed = local_call(
        result_kernel, "result", (order,), (picks, hidden, res_half, res_far),
        [((8 * halfway, full), bf16)], [((rows, full), bf16)], far_in=(1, 2, 3), far_out=(0,),
    )
    packed = packed.reshape(8, halfway, full)
    arrived = [hop(packed[at], ORDER[at]) if at else packed[at] for at in range(8)]
    d_raw, out_lows, arrived = sync((d_raw, out_lows, arrived))

    qkv_far, qkv_near = local_call(
        partial(project_grad_kernel, 0), "project_grad", (), (d_raw, norm_one),
        [((4, 3 * cols, width), bf16), ((4, 3 * cols, width), f32)], far_in=(0, 1), far_out=(1,),
    )
    qkv_far, d_raw = sync((qkv_far, d_raw))
    qkv_got = hop(qkv_far, 1)
    send, keep = local_call(
        project_back_kernel, "project_back", (core_at,), (d_raw, qkv_w),
        [((rows, full), bf16), ((rows, full), f32)], far_in=(0, 1),
    )
    half = add_half(keep, twin(send))
    far = across(half)
    out_got = z_send(out_lows)
    arrived = jnp.stack(arrived)
    qkv_got, far, arrived = sync((qkv_got, far, arrived))
    qkv_own, qkv_lows = near_sum(qkv_near, qkv_got, "qkv_near")
    qkv_lows, arrived, far, feed_sum, out_got = sync((qkv_lows, arrived, far, feed_sum, out_got))
    input_own = local_call(
        norm_one_back_kernel, "norm_one_back", (core_at, order), (tokens, half, far, d_hidden, gains),
        [((rows, full), bf16)], [((rows, full), f32)], far_in=(0, 3, 4),
    )
    input_own, feed_sum, out_got = sync((input_own, feed_sum, out_got))
    input_grad = both(input_own, twin(input_own))
    out_sum = far_sum(out_own, out_got)
    inp_sum, gate_sum, down_sum = [feed_sum[at * units : (at + 1) * units].astype(f32) for at in range(3)]
    two_row = jnp.sum(inp_sum * inp_turned.astype(f32) + gate_sum * gate_turned.astype(f32), axis=0)
    grad_attn_out = jnp.transpose(out_sum)
    grad_in = jnp.stack([jnp.transpose(inp_sum), jnp.transpose(gate_sum)], axis=1)
    grad_down = jnp.transpose(down_sum)
    other_side = across(arrived)
    whole = jnp.concatenate(
        [jnp.where(side == 0, arrived, other_side), jnp.where(side == 0, other_side, arrived)], axis=1
    ).reshape(rows, full)
    whole = both(whole, twin(whole))
    output = jnp.einsum("msp,mpd->msd", unpack, whole, preferred_element_type=f32).astype(bf16)
    qkv_got = z_send(qkv_lows)
    qkv_got, output, input_grad, grad_attn_out, grad_in, grad_down, two_row = sync(
        (qkv_got, output, input_grad, grad_attn_out, grad_in, grad_down, two_row)
    )
    qkv_sum = far_sum(qkv_own, qkv_got)
    one_row = jnp.sum(qkv_sum * turned.astype(f32), axis=0)
    gain_rows = jnp.stack([one_row / gain_one.astype(f32), two_row / gain_two.astype(f32)])
    beyond = lax.ppermute(gain_rows, "tp", [(i, i ^ 3) for i in range(4)])
    gain_rows = (gain_rows + twin(gain_rows)) + (across(gain_rows) + beyond)
    grad_gain_one, grad_gain_two = gain_rows[0], gain_rows[1]
    return (
        output,
        input_grad,
        jnp.transpose(qkv_sum.reshape(heads, 3, HD, width), (3, 1, 0, 2)).reshape(width, 3, cols),
        grad_attn_out,
        grad_in,
        grad_down,
        grad_gain_one,
        grad_gain_two,
    )


def on_device(*operands):
    micro_count, tok_rows = operands[0].shape[0], operands[0].shape[1]
    groups, parts = lax.axis_size("fsdp"), lax.axis_size("tp")
    heads = operands[4].shape[2] // HD
    if groups == 8 and parts == 4 and micro_count == 2 and micro_count * heads == groups and tok_rows % 256 == 0:
        return paired_layer(*operands)
    return general_layer(*operands)


def solution(mesh):
    placed = (
        P(None, "fsdp", None),
        P(None, "fsdp", None),
        P(),
        P(),
        P("fsdp", None, "tp"),
        P("fsdp", "tp"),
        P("fsdp", None, "tp"),
        P("fsdp", "tp"),
        P("fsdp"),
        P("fsdp"),
    )
    return jax.shard_map(
        on_device,
        mesh=mesh,
        in_specs=placed,
        out_specs=(
            P(None, "fsdp", None),
            P(None, "fsdp", None),
            P("fsdp", None, "tp"),
            P("fsdp", "tp"),
            P("fsdp", None, "tp"),
            P("fsdp", "tp"),
            P("fsdp"),
            P("fsdp"),
        ),
        check_vma=False,
    )
```

```python
import math

import jax
import jax.numpy as jnp
from jax import lax
from jax.experimental import pallas as pl
from jax.experimental.pallas import tpu as pltpu
from jax.sharding import PartitionSpec as P

D = 1024
HD = 64


EPS = 1e-05
THETA = 160000.0
key_block = 2048


def layer_norm(values, gain):
    center = values - jnp.mean(values, axis=-1, keepdims=True)
    spread = jnp.mean(center * center, axis=-1, keepdims=True)
    return center * lax.rsqrt(spread + EPS) * gain


def rope_tables(position, width):
    freqs = jnp.power(THETA, -jnp.arange(width // 2, dtype=jnp.float32) * 2.0 / width)
    angle = position.astype(jnp.float32)[:, None] * freqs[None, :]
    angle = jnp.concatenate([angle, angle], axis=-1)
    return (jnp.cos(angle), jnp.sin(angle))


def rotate(values, cosine, sine):
    half = values.shape[-1] // 2
    turned = jnp.concatenate([-values[..., half:], values[..., :half]], axis=-1)
    return values * cosine[:, None, :] + turned * sine[:, None, :]


def running_ends(seq_lens):
    order = jnp.arange(seq_lens.shape[0], dtype=jnp.int32)
    return jnp.sum(jnp.where(order[None, :] <= order[:, None], seq_lens[None, :], 0), axis=1)


def seq_info(anchor, seq_lens):
    ends = running_ends(seq_lens)
    starts = ends - seq_lens
    segment = jnp.sum((anchor[:, None] >= ends[None, :]).astype(jnp.int32), axis=1)
    onehot = segment[:, None] == jnp.arange(seq_lens.shape[0], dtype=jnp.int32)[None, :]
    position = anchor - jnp.sum(jnp.where(onehot, starts[None, :], 0), axis=1)
    return (segment, position)


def blockwise(running, pieces, offset, step_fn):
    piece_len = pieces[0].shape[0]
    if piece_len > key_block and piece_len % key_block == 0:
        block_count = piece_len // key_block
        stacked = tuple((one.reshape((block_count, key_block) + one.shape[1:]) for one in pieces))

        def inner(state_now, scan_item):
            block_index, piece_parts = scan_item
            return (step_fn(state_now, piece_parts, offset + block_index * key_block), None)

        running, _ = lax.scan(inner, running, (jnp.arange(block_count, dtype=jnp.int32), stacked))
        return running
    return step_fn(running, pieces, offset)


def general_layer(
    tokens, cotangent, perm, lengths, w_qkv, w_attn_out, w_in, w_down, gain_one, gain_two
):
    groups = lax.axis_size("fsdp")
    my_index = lax.axis_index("fsdp")
    micro_count = tokens.shape[0]
    tok_rows = tokens.shape[1]
    total_rows = tok_rows * groups
    per_pair = tok_rows // groups
    head_cols = w_qkv.shape[2]
    head_count = head_cols // HD
    unit_cols = w_in.shape[2]
    score_scale = HD ** (-0.5)
    rows_idx = jnp.arange(tok_rows, dtype=jnp.int32)
    f32 = jnp.float32
    bf16 = jnp.bfloat16
    dims_rows = (((0,), (0,)), ((), ()))
    dims_cols = (((1,), (1,)), ((), ()))
    acc_qkv = jnp.zeros((D, 3, head_cols), f32)
    acc_out = jnp.zeros((D, head_cols), f32)
    acc_in = jnp.zeros((D, 2, unit_cols), f32)
    acc_down = jnp.zeros((D, unit_cols), f32)
    acc_gain_one = jnp.zeros((D,), f32)
    acc_gain_two = jnp.zeros((D,), f32)
    outputs = []
    input_grads = []
    for micro_idx in range(micro_count):
        perm_row = perm[micro_idx]
        seq_lens = lengths[micro_idx]
        inverse = (
            jnp.zeros((total_rows,), jnp.int32)
            .at[perm_row]
            .set(jnp.arange(total_rows, dtype=jnp.int32))
        )
        placed = lax.dynamic_slice_in_dim(inverse, my_index * tok_rows, tok_rows)
        send_order = jnp.argsort(placed)
        outgoing = tokens[micro_idx][send_order].reshape(groups, per_pair, D)
        arrived = lax.all_to_all(outgoing, "fsdp", split_axis=0, concat_axis=0, tiled=True).reshape(
            tok_rows, D
        )
        my_tokens = lax.dynamic_slice_in_dim(perm_row, my_index * tok_rows, tok_rows)
        source = my_tokens // tok_rows
        recv_order = jnp.argsort(source * tok_rows + rows_idx)
        recv_slot = jnp.zeros((tok_rows,), jnp.int32).at[recv_order].set(rows_idx)
        dealt = arrived[recv_slot]
        fetched = (
            lax.all_gather(gain_one, "fsdp", axis=0, tiled=True),
            lax.all_gather(gain_two, "fsdp", axis=0, tiled=True),
            lax.all_gather(w_qkv, "fsdp", axis=0, tiled=True),
            lax.all_gather(w_attn_out, "fsdp", axis=0, tiled=True),
            lax.all_gather(w_in, "fsdp", axis=0, tiled=True),
            lax.all_gather(w_down, "fsdp", axis=0, tiled=True),
        )
        gain_first = fetched[0].astype(f32)
        gain_second = fetched[1].astype(f32)
        query_seg, query_pos = seq_info(my_tokens, seq_lens)
        cosine, sine = rope_tables(query_pos, HD)
        x_float = dealt.astype(f32)
        normed_low = layer_norm(x_float, gain_first).astype(bf16)
        raw_proj = jnp.einsum("td,dcf->tcf", normed_low, fetched[2], preferred_element_type=f32)
        raw_heads = raw_proj.reshape(tok_rows, 3, head_count, HD)
        query_low = rotate(raw_heads[:, 0], cosine, sine).astype(bf16)
        key_low = rotate(raw_heads[:, 1], cosine, sine).astype(bf16)
        value_low = raw_heads[:, 2].astype(bf16)

        def forward_step(running, piece_parts, offset):
            run_peak, run_total, run_acc = running
            key_part, value_part = piece_parts
            key_seg, _ = seq_info(
                lax.dynamic_slice_in_dim(perm_row, offset, key_part.shape[0]), seq_lens
            )
            scores = (
                jnp.einsum("qhe,khe->hqk", query_low, key_part, preferred_element_type=f32)
                * score_scale
            )
            same_seq = (query_seg[:, None] == key_seg[None, :])[None]
            block_top = jnp.max(jnp.where(same_seq, scores, -1e30), axis=-1)
            new_peak = jnp.maximum(run_peak, block_top)
            weights = jnp.where(same_seq, jnp.exp(scores - new_peak[..., None]), 0.0)
            fade_factor = jnp.exp(run_peak - new_peak)
            run_acc = run_acc * jnp.transpose(fade_factor)[:, :, None] + jnp.einsum(
                "hqk,khe->qhe", weights.astype(bf16), value_part, preferred_element_type=f32
            )
            run_total = run_total * fade_factor + jnp.sum(weights, axis=-1)
            return (new_peak, run_total, run_acc)

        start_state = (
            jnp.full((head_count, tok_rows), -1e30, f32),
            jnp.zeros((head_count, tok_rows), f32),
            jnp.zeros((tok_rows, head_count, HD), f32),
        )
        run_peak, run_total, run_acc = blockwise(
            start_state,
            (
                lax.all_gather(key_low, "fsdp", axis=0, tiled=True),
                lax.all_gather(value_low, "fsdp", axis=0, tiled=True),
            ),
            jnp.int32(0),
            forward_step,
        )
        log_total = run_peak + jnp.log(run_total)
        mixed_heads = run_acc / jnp.transpose(run_total)[:, :, None]
        mixed_low = mixed_heads.reshape(tok_rows, head_cols).astype(bf16)
        attn_part = lax.dot_general(mixed_low, fetched[3], dims_cols, preferred_element_type=f32)
        branch = lax.psum(attn_part.astype(jnp.bfloat16), "tp").astype(jnp.float32)
        hidden = x_float + branch
        normed_two = layer_norm(hidden, gain_second).astype(bf16)
        ffn_proj = jnp.einsum("td,dcf->tcf", normed_two, fetched[4], preferred_element_type=f32)
        act_low = (jax.nn.gelu(ffn_proj[:, 0], approximate=False) * ffn_proj[:, 1]).astype(bf16)
        ffn_part = lax.dot_general(act_low, fetched[5], dims_cols, preferred_element_type=f32)
        branch_two = lax.psum(ffn_part.astype(jnp.bfloat16), "tp").astype(jnp.float32)
        outputs.append((hidden + branch_two).astype(bf16))
        again = (
            lax.all_gather(gain_one, "fsdp", axis=0, tiled=True),
            lax.all_gather(gain_two, "fsdp", axis=0, tiled=True),
            lax.all_gather(w_qkv, "fsdp", axis=0, tiled=True),
            lax.all_gather(w_attn_out, "fsdp", axis=0, tiled=True),
            lax.all_gather(w_in, "fsdp", axis=0, tiled=True),
            lax.all_gather(w_down, "fsdp", axis=0, tiled=True),
        )
        gain_first = again[0].astype(f32)
        gain_second = again[1].astype(f32)
        grad_low = cotangent[micro_idx]
        grad_float = grad_low.astype(f32)
        acc_down = acc_down + lax.dot_general(
            grad_low, act_low, dims_rows, preferred_element_type=f32
        )
        d_act = jnp.dot(grad_low, again[5], preferred_element_type=f32)
        _, gelu_pull = jax.vjp(
            lambda inputs, gates: jax.nn.gelu(inputs, approximate=False) * gates,
            ffn_proj[:, 0],
            ffn_proj[:, 1],
        )
        d_inputs, d_gates = gelu_pull(d_act)
        d_proj = jnp.stack([d_inputs, d_gates], axis=1).astype(bf16)
        acc_in = acc_in + jnp.einsum("td,tcf->dcf", normed_two, d_proj, preferred_element_type=f32)
        norm_part = jnp.einsum("tcf,dcf->td", d_proj, again[4], preferred_element_type=f32)
        d_norm_two = lax.psum(norm_part.astype(jnp.bfloat16), "tp").astype(jnp.float32)
        _, second_pull = jax.vjp(layer_norm, hidden, gain_second)
        d_hid_norm, d_gain_two = second_pull(d_norm_two)
        acc_gain_two = acc_gain_two + d_gain_two
        d_hidden = grad_float + d_hid_norm
        hidden_low = d_hidden.astype(bf16)
        acc_out = acc_out + lax.dot_general(
            hidden_low, mixed_low, dims_rows, preferred_element_type=f32
        )
        d_mixed = jnp.dot(hidden_low, again[3], preferred_element_type=f32).astype(bf16)
        d_mixed = d_mixed.reshape(tok_rows, head_count, HD)
        delta_rows = jnp.sum(d_mixed.astype(f32) * mixed_heads, axis=-1)
        delta_heads = jnp.transpose(delta_rows)

        def query_step(grad_query, piece_parts, offset):
            key_part, value_part = piece_parts
            key_seg, _ = seq_info(
                lax.dynamic_slice_in_dim(perm_row, offset, key_part.shape[0]), seq_lens
            )
            scores = (
                jnp.einsum("qhe,khe->hqk", query_low, key_part, preferred_element_type=f32)
                * score_scale
            )
            same_seq = (query_seg[:, None] == key_seg[None, :])[None]
            weights = jnp.where(same_seq, jnp.exp(scores - log_total[..., None]), 0.0)
            d_weights = jnp.einsum("qhe,khe->hqk", d_mixed, value_part, preferred_element_type=f32)
            d_scores = (weights * (d_weights - delta_heads[..., None])).astype(bf16)
            return grad_query + score_scale * jnp.einsum(
                "hqk,khe->qhe", d_scores, key_part, preferred_element_type=f32
            )

        query_start = jnp.zeros((tok_rows, head_count, HD), f32)
        grad_query = blockwise(
            query_start,
            (
                lax.all_gather(key_low, "fsdp", axis=0, tiled=True),
                lax.all_gather(value_low, "fsdp", axis=0, tiled=True),
            ),
            jnp.int32(0),
            query_step,
        )
        stat_total, stat_delta = (
            lax.all_gather(jnp.transpose(log_total), "fsdp", axis=0, tiled=True),
            lax.all_gather(delta_rows, "fsdp", axis=0, tiled=True),
        )

        def key_step(running, piece_parts, offset):
            grad_key, grad_value = running
            query_part, dmix_part = piece_parts
            piece_len = query_part.shape[0]
            piece_seg, _ = seq_info(lax.dynamic_slice_in_dim(perm_row, offset, piece_len), seq_lens)
            total_part = jnp.transpose(lax.dynamic_slice_in_dim(stat_total, offset, piece_len))
            delta_part = jnp.transpose(lax.dynamic_slice_in_dim(stat_delta, offset, piece_len))
            scores = (
                jnp.einsum("qhe,khe->hqk", query_part, key_low, preferred_element_type=f32)
                * score_scale
            )
            same_seq = (piece_seg[:, None] == query_seg[None, :])[None]
            weights = jnp.where(same_seq, jnp.exp(scores - total_part[..., None]), 0.0)
            d_weights = jnp.einsum("qhe,khe->hqk", dmix_part, value_low, preferred_element_type=f32)
            d_scores = (weights * (d_weights - delta_part[..., None])).astype(bf16)
            grad_key = grad_key + score_scale * jnp.einsum(
                "hqk,qhe->khe", d_scores, query_part, preferred_element_type=f32
            )
            grad_value = grad_value + jnp.einsum(
                "hqk,qhe->khe", weights.astype(bf16), dmix_part, preferred_element_type=f32
            )
            return (grad_key, grad_value)

        grad_key, grad_value = blockwise(
            (
                jnp.zeros((tok_rows, head_count, HD), f32),
                jnp.zeros((tok_rows, head_count, HD), f32),
            ),
            (
                lax.all_gather(query_low, "fsdp", axis=0, tiled=True),
                lax.all_gather(d_mixed, "fsdp", axis=0, tiled=True),
            ),
            jnp.int32(0),
            key_step,
        )
        _, rope_pull = jax.vjp(lambda heads_in: rotate(heads_in, cosine, sine), raw_heads[:, 0])
        d_raw_query = rope_pull(grad_query)[0]
        d_raw_key = rope_pull(grad_key)[0]
        d_raw = (
            jnp.stack([d_raw_query, d_raw_key, grad_value], axis=1)
            .reshape(tok_rows, 3, head_cols)
            .astype(bf16)
        )
        acc_qkv = acc_qkv + jnp.einsum("td,tcf->dcf", normed_low, d_raw, preferred_element_type=f32)
        first_part = jnp.einsum("tcf,dcf->td", d_raw, again[2], preferred_element_type=f32)
        d_norm_one = lax.psum(first_part.astype(jnp.bfloat16), "tp").astype(jnp.float32)
        _, first_pull = jax.vjp(layer_norm, x_float, gain_first)
        d_x_norm, d_gain_one = first_pull(d_norm_one)
        acc_gain_one = acc_gain_one + d_gain_one
        d_input = (d_hidden + d_x_norm).astype(bf16)
        back_rows = d_input[recv_order].reshape(groups, per_pair, D)
        returned = lax.all_to_all(
            back_rows, "fsdp", split_axis=0, concat_axis=0, tiled=True
        ).reshape(tok_rows, D)
        send_slot = jnp.zeros((tok_rows,), jnp.int32).at[send_order].set(rows_idx)
        input_grads.append(returned[send_slot])
    summed = (
        lax.psum_scatter(acc_qkv, "fsdp", scatter_dimension=0, tiled=True),
        lax.psum_scatter(acc_out, "fsdp", scatter_dimension=0, tiled=True),
        lax.psum_scatter(acc_in, "fsdp", scatter_dimension=0, tiled=True),
        lax.psum_scatter(acc_down, "fsdp", scatter_dimension=0, tiled=True),
        lax.psum_scatter(acc_gain_one, "fsdp", scatter_dimension=0, tiled=True),
        lax.psum_scatter(acc_gain_two, "fsdp", scatter_dimension=0, tiled=True),
    )
    return (
        jnp.stack(outputs),
        jnp.stack(input_grads),
        summed[0],
        summed[1],
        summed[2],
        summed[3],
        summed[4],
        summed[5],
    )


JOIN = 2
COSTS = {"attend": 10, "attend_back": 28, "feed": 8, "feed_grad": 5}
FAR = -1e30
ORDER = (0, 2, 4, 6, 1, 3, 5, 7)
NT = (((1,), (1,)), ((), ()))
TN = (((0,), (0,)), ((), ()))
NN = (((1,), (0,)), ((), ()))
ROOM = 10 * 1024 * 1024


def partial(kernel, *given):
    return lambda *refs: kernel(*given, *refs)


def mm(left, right, dims):
    return lax.dot_general(left, right, dims, preferred_element_type=jnp.float32)


def hop(value, step):
    return lax.ppermute(value, "fsdp", [(i, i ^ step) for i in range(8)])


def twin(value):
    return lax.ppermute(value, "tp", [(i, i ^ 1) for i in range(4)])


def across(value):
    return lax.ppermute(value, "tp", [(i, i ^ 2) for i in range(4)])


def deal_out(value):
    return lax.all_to_all(value, "fsdp", 0, 0, tiled=True)


def after(value, *earlier):
    return lax.optimization_barrier((value,) + earlier)[0]


def sync(values):
    return lax.optimization_barrier(values)


def z_phase(shard):
    return [shard] + [hop(shard, step) for step in ORDER[1:4]]


def y_phase(shards):
    return [hop(one, 1) for one in shards]


def local_call(kernel, name, scalars, arrays, outs, scratch=(), shards=(), copies=8, far_in=(), far_out=(), far_shards=True):
    shapes = [(one.shape, one.dtype) for one in arrays]
    staged = [shapes[at] for at in far_in] + [outs[at] for at in far_out]
    sems = [pltpu.SemaphoreType.DMA((copies,))] if shards else []
    room = ROOM + sum(math.prod(shape) * jnp.dtype(kind).itemsize for shape, kind in [*shapes, *outs, *scratch])
    counts = (len(scalars), len(arrays), len(shards), len(outs), len(scratch) + len(sems))

    def body(*refs):
        groups = []
        for count in counts:
            groups.append(list(refs[:count]))
            refs = refs[count:]
        given, ins, pieces, results, extra = groups
        if not staged:
            return kernel(*given, *ins, *pieces, *results, *extra)
        stage, sem = refs[:-1], refs[-1]
        incoming, outgoing = [], []
        for slot, at in enumerate(far_in):
            incoming.append(pltpu.make_async_copy(ins[at], stage[slot], sem.at[slot]))
            incoming[-1].start()
            ins[at] = stage[slot]
        for slot, at in enumerate(far_out, len(far_in)):
            outgoing.append(pltpu.make_async_copy(stage[slot], results[at], sem.at[slot]))
            results[at] = stage[slot]
        for copy in incoming:
            copy.wait()
        kernel(*given, *ins, *pieces, *results, *extra)
        for copy in outgoing:
            copy.start()
        for copy in outgoing:
            copy.wait()

    arrays = [pltpu.with_memory_space_constraint(one, pltpu.HBM) if at in far_in else one for at, one in enumerate(arrays)]
    shards = [pltpu.with_memory_space_constraint(one, pltpu.HBM) if far_shards else one for one in shards]

    def space(at, far):
        return pl.BlockSpec(memory_space=pltpu.HBM if at in far else pltpu.VMEM)

    result = pl.pallas_call(
        body,
        in_specs=[pl.BlockSpec(memory_space=pltpu.SMEM)] * len(scalars)
        + [space(at, far_in) for at in range(len(arrays))]
        + [pl.BlockSpec(memory_space=pltpu.HBM if far_shards else pl.ANY)] * len(shards),
        out_specs=[space(at, far_out) for at in range(len(outs))],
        out_shape=[
            pltpu.HBM(shape, kind) if at in far_out else jax.ShapeDtypeStruct(shape, kind)
            for at, (shape, kind) in enumerate(outs)
        ],
        scratch_shapes=[pltpu.VMEM(shape, kind) for shape, kind in scratch]
        + sems
        + [pltpu.VMEM(shape, kind) for shape, kind in staged]
        + ([pltpu.SemaphoreType.DMA((len(staged),))] if staged else []),
        compiler_params=pltpu.CompilerParams(vmem_limit_bytes=room),
        cost_estimate=pl.CostEstimate(flops=COSTS.get(name, 3) * 10**9, transcendentals=0, bytes_accessed=8 * 1024 * 1024),
        name=name,
    )(*scalars, *arrays, *shards)
    return result if len(outs) > 1 else result[0]


def block_at(order_ref, place, width):
    return pl.ds(pl.multiple_of(order_ref[place] * width, width), width)


def shard_copies(shards, low, high, into_ref, sem_ref, base=0):
    width = shards[0].shape[1]
    copies = []
    for place, shard in enumerate(shards):
        span = pl.ds(place * width, width)
        source = shard.at[pl.ds(low, high - low), :]
        copies.append(pltpu.make_async_copy(source, into_ref.at[:, span], sem_ref.at[base + place]))
        copies[-1].start()
    return copies


def gathered_copies(order_ref, source, low, high, into_ref, sem_ref, base=0):
    width = source.shape[2]
    copies = []
    for place in range(8):
        copies.append(
            pltpu.make_async_copy(
                source.at[order_ref[place], pl.ds(low, high - low), :],
                into_ref.at[:, pl.ds(place * width, width)],
                sem_ref.at[base + place],
            )
        )
        copies[-1].start()
    return copies


def finish(copies):
    for copy in copies:
        copy.wait()


def project_kernel(order_ref, x_ref, table_ref, *refs):
    shards = refs[:8]
    norm_ref, gains_ref, send_ref, w_ref, sem_ref = refs[8:]
    width = shards[0].shape[1]
    rows = x_ref.shape[1]
    wide = w_ref.shape[0] - 16
    heads = wide // (3 * HD)
    half = HD // 2
    finish(shard_copies(shards, 0, wide + 16, w_ref, sem_ref))
    gains_ref[...] = w_ref[wide:, :].astype(jnp.float32)[:2]
    for micro in range(2):
        x = x_ref[micro].astype(jnp.float32)
        mean = jnp.mean(x, axis=-1, keepdims=True)
        center = x - mean
        spread = lax.rsqrt(jnp.mean(center * center, axis=-1, keepdims=True) + EPS)
        for place in range(8):
            piece = x_ref[micro, :, block_at(order_ref, place, width)].astype(jnp.float32)
            span = slice(place * width, (place + 1) * width)
            value = (piece - mean) * spread * gains_ref[0:1, span]
            norm_ref[micro * rows : (micro + 1) * rows, span] = value.astype(jnp.bfloat16)
    raw = mm(w_ref[:wide, :], norm_ref[...], NT)
    cosine, sine = table_ref[:half, :], table_ref[half:, :]
    for head in range(heads):
        base = head * 3 * HD
        for kind in range(2):
            upper = raw[base + kind * HD : base + kind * HD + half]
            lower = raw[base + kind * HD + half : base + (kind + 1) * HD]
            first = (upper * cosine - lower * sine).astype(jnp.bfloat16)
            second = (lower * cosine + upper * sine).astype(jnp.bfloat16)
            for micro in range(2):
                span = slice(micro * rows, (micro + 1) * rows)
                send_ref[micro * heads + head, kind * HD : kind * HD + half, :] = first[:, span]
                send_ref[micro * heads + head, kind * HD + half : (kind + 1) * HD, :] = second[:, span]
        value = raw[base + 2 * HD : base + 3 * HD].astype(jnp.bfloat16)
        for micro in range(2):
            send_ref[micro * heads + head, 2 * HD :, :] = value[:, micro * rows : (micro + 1) * rows]


def key_range(lens_ref, low, high):
    first = jnp.int32(0)
    last = jnp.int32(0)
    total = jnp.int32(0)
    for index in range(lens_ref.shape[0]):
        start = total
        total = total + lens_ref[index]
        first = jnp.where((start <= low) & (low < total), start, first)
        last = jnp.where((start <= high) & (high < total), total, last)
    return first, last


def query_bounds(lens_ref, base, width):
    place = base + lax.broadcasted_iota(jnp.int32, (1, width), 1)
    first = jnp.zeros((1, width), jnp.int32)
    last = jnp.zeros((1, width), jnp.int32)
    total = jnp.int32(0)
    for index in range(lens_ref.shape[0]):
        start = total
        total = total + lens_ref[index]
        inside = (place >= start) & (place < total)
        first = jnp.where(inside, start, first)
        last = jnp.where(inside, total, last)
    return first, last


def lanes(ref, index, count, rows):
    return jnp.concatenate([ref[index * count + at, rows, :] for at in range(count)], axis=1)


def attend_kernel(lens_ref, qkv_ref, mixed_ref, exact_ref, log_ref, key_ref):
    blocks, _, small = qkv_ref.shape
    wide = JOIN * small
    for at in range(blocks):
        block = qkv_ref[at, HD : 2 * HD, :].astype(jnp.float32)
        key_ref[at * small : (at + 1) * small, :] = jnp.transpose(block).astype(jnp.bfloat16)

    def one_query(index, carry):
        base = index * wide
        first, last = key_range(lens_ref, base, base + wide - 1)
        low, high = query_bounds(lens_ref, base, wide)
        query = lanes(qkv_ref, index, JOIN, slice(0, HD)) * jnp.bfloat16(HD**-0.5)

        def one_key(at, state):
            peak, total, acc = state
            start = pl.multiple_of(at * wide, wide)
            scores = mm(key_ref[pl.ds(start, wide), :], query, NN)
            place = start + lax.broadcasted_iota(jnp.int32, (wide, wide), 0)
            scores = jnp.where((place >= low) & (place < high), scores, FAR)
            top = jnp.maximum(peak, jnp.max(scores, axis=0, keepdims=True))
            weights = jnp.exp(scores - top)
            fade = jnp.exp(peak - top)
            total = total * fade + jnp.sum(weights, axis=0, keepdims=True)
            value = lanes(qkv_ref, at, JOIN, slice(2 * HD, 3 * HD))
            acc = acc * fade + mm(value, weights.astype(jnp.bfloat16), NN)
            return top, total, acc

        peak, total, acc = lax.fori_loop(
            first // wide,
            (last + wide - 1) // wide,
            one_key,
            (
                jnp.full((1, wide), FAR, jnp.float32),
                jnp.zeros((1, wide), jnp.float32),
                jnp.zeros((HD, wide), jnp.float32),
            ),
        )
        result = acc / total
        logs = peak + jnp.log(total)
        for at in range(JOIN):
            span = slice(at * small, (at + 1) * small)
            mixed_ref[index * JOIN + at] = result[:, span].astype(jnp.bfloat16)
            exact_ref[index * JOIN + at] = result[:, span]
            log_ref[index * JOIN + at] = logs[:, span]
        return carry

    lax.fori_loop(0, blocks // JOIN, one_query, 0)


def attend_back_kernel(
    lens_ref, qkv_ref, exact_ref, log_ref, grad_ref, table_ref, raw_ref, pair_ref, dkey_ref, dvalue_ref
):
    blocks, _, small = qkv_ref.shape
    wide = JOIN * small
    half = HD // 2
    for at in range(blocks):
        block = qkv_ref[at, HD : 3 * HD, :].astype(jnp.float32)
        pair_ref[at * small : (at + 1) * small, :] = jnp.transpose(block).astype(jnp.bfloat16)
    dkey_ref[...] = jnp.zeros(dkey_ref.shape, jnp.float32)
    dvalue_ref[...] = jnp.zeros(dvalue_ref.shape, jnp.float32)

    def unturn(index, grad):
        cosine = table_ref[index, :half, :]
        sine = table_ref[index, half:, :]
        upper, lower = grad[:half], grad[half:]
        return upper * cosine + lower * sine, lower * cosine - upper * sine

    def one_query(index, carry):
        base = index * wide
        first, last = key_range(lens_ref, base, base + wide - 1)
        low, high = query_bounds(lens_ref, base, wide)
        query = lanes(qkv_ref, index, JOIN, slice(0, HD)) * jnp.bfloat16(HD**-0.5)
        grad = lanes(grad_ref, index, JOIN, slice(0, HD))
        logs = lanes(log_ref, index, JOIN, slice(0, 1))
        exact = lanes(exact_ref, index, JOIN, slice(0, HD))
        delta = jnp.sum(grad.astype(jnp.float32) * exact, axis=0, keepdims=True)

        def one_key(at, dquery):
            start = pl.multiple_of(at * wide, wide)
            span = pl.ds(start, wide)
            scores = mm(pair_ref[span, :HD], query, NN)
            dweights = mm(pair_ref[span, HD:], grad, NN)
            place = start + lax.broadcasted_iota(jnp.int32, (wide, wide), 0)
            weights = jnp.where((place >= low) & (place < high), jnp.exp(scores - logs), 0.0)
            dscores = (weights * (dweights - delta)).astype(jnp.bfloat16)
            dkey_ref[:, span] += mm(query, dscores, NT)
            dvalue_ref[:, span] += mm(grad, weights.astype(jnp.bfloat16), NT)
            return dquery + mm(lanes(qkv_ref, at, JOIN, slice(HD, 2 * HD)), dscores, NN)

        dquery = lax.fori_loop(
            first // wide,
            (last + wide - 1) // wide,
            one_key,
            jnp.zeros((HD, wide), jnp.float32),
        ) * (HD**-0.5)
        for at in range(JOIN):
            upper, lower = unturn(index * JOIN + at, dquery[:, at * small : (at + 1) * small])
            raw_ref[index * JOIN + at, :half, :] = upper.astype(jnp.bfloat16)
            raw_ref[index * JOIN + at, half:HD, :] = lower.astype(jnp.bfloat16)
        return carry

    lax.fori_loop(0, blocks // JOIN, one_query, 0)
    for at in range(blocks):
        span = slice(at * small, (at + 1) * small)
        upper, lower = unturn(at, dkey_ref[:, span])
        raw_ref[at, HD : HD + half, :] = upper.astype(jnp.bfloat16)
        raw_ref[at, HD + half : 2 * HD, :] = lower.astype(jnp.bfloat16)
        raw_ref[at, 2 * HD :, :] = dvalue_ref[:, span].astype(jnp.bfloat16)


def mix_out_kernel(core_ref, order_ref, mixed_ref, all_ref, send_ref, keep_ref, w_ref, sem_ref):
    last = all_ref.shape[1]
    finish(gathered_copies(order_ref, all_ref, last - mixed_ref.shape[1], last, w_ref, sem_ref))
    core = core_ref[0]
    send_ref[...] = mm(mixed_ref[1 - core], w_ref[...], TN).astype(jnp.bfloat16)
    keep_ref[...] = mm(mixed_ref[core], w_ref[...], TN)


def norm_two_kernel(core_ref, order_ref, x_ref, half_ref, far_ref, gains_ref, hidden_ref, norm_ref):
    core = core_ref[0]
    width = x_ref.shape[2] // 8
    for place in range(8):
        span = slice(place * width, (place + 1) * width)
        piece = x_ref[core, :, block_at(order_ref, place, width)].astype(jnp.float32)
        branch = half_ref[:, span].astype(jnp.float32) + far_ref[:, span].astype(jnp.float32)
        hidden_ref[:, span] = piece + branch
    hidden = hidden_ref[...]
    center = hidden - jnp.mean(hidden, axis=-1, keepdims=True)
    spread = lax.rsqrt(jnp.mean(center * center, axis=-1, keepdims=True) + EPS)
    norm_ref[...] = (center * spread * gains_ref[1:2, :]).astype(jnp.bfloat16)


def feed_kernel(
    order_ref, own_ref, other_ref, grad_ref, all_ref, down_ref,
    send_ref, keep_ref, act_ref, dinp_ref, dgate_ref, result_send_ref, result_keep_ref, w_ref, sem_ref
):
    units = w_ref.shape[0] // 3
    inp_w, gate_w, down_w = [w_ref.at[pl.ds(at * units, units), :] for at in range(3)]
    rows = own_ref.shape[0]
    first_copies = gathered_copies(order_ref, all_ref, 0, 2 * units, w_ref.at[pl.ds(0, 2 * units), :], sem_ref)
    finish(gathered_copies(order_ref, down_ref, 0, units, down_w, sem_ref, 8))
    finish(first_copies)
    for micro, norm_ref in ((1, other_ref), (0, own_ref)):
        span = slice(micro * rows, (micro + 1) * rows)
        inp = mm(norm_ref[...], inp_w[...], NT)
        gate = mm(norm_ref[...], gate_w[...], NT)
        dact = mm(grad_ref[micro], down_w[...], NT)
        cdf = 0.5 * (1.0 + lax.erf(inp * (0.5**0.5)))
        density = jnp.exp(-0.5 * inp * inp) * ((0.5 / jnp.pi) ** 0.5)
        gelu = inp * cdf
        act = (gelu * gate).astype(jnp.bfloat16)
        act_ref[span, :] = act
        dinp = (dact * gate * (cdf + inp * density)).astype(jnp.bfloat16)
        dgate = (dact * gelu).astype(jnp.bfloat16)
        dinp_ref[span, :] = dinp
        dgate_ref[span, :] = dgate
        part = mm(dinp, inp_w[...], NN) + mm(dgate, gate_w[...], NN)
        result = mm(act, down_w[...], NN)
        if micro:
            send_ref[...] = part.astype(jnp.bfloat16)
            result_send_ref[...] = result.astype(jnp.bfloat16)
        else:
            keep_ref[...] = part
            result_keep_ref[...] = result


def weight_grad_kernel(order_ref, dinp_ref, dgate_ref, act_ref, own_ref, other_ref, grad_ref, out_ref):
    units = act_ref.shape[1]
    rows = own_ref.shape[0]
    width = out_ref.shape[2]
    for at, (left_ref, rights) in enumerate((
        (dinp_ref, (own_ref, other_ref)),
        (dgate_ref, (own_ref, other_ref)),
        (act_ref, (grad_ref.at[0], grad_ref.at[1])),
    )):
        total = mm(left_ref[:rows, :], rights[0][...], TN) + mm(left_ref[rows:, :], rights[1][...], TN)
        for place in range(8):
            piece = total[:, place * width : (place + 1) * width].astype(jnp.bfloat16)
            out_ref[order_ref[place], at * units : (at + 1) * units, :] = piece


def near_sum_kernel(near_ref, far_ref, own_ref, *low_refs):
    own_ref[...] = near_ref[0] + far_ref[0].astype(jnp.float32)
    for at, low_ref in enumerate(low_refs):
        low_ref[...] = (near_ref[at + 1] + far_ref[at + 1].astype(jnp.float32)).astype(jnp.bfloat16)


def norm_two_back_kernel(hidden_ref, half_ref, far_ref, grad_ref, gains_ref, dhidden_ref, low_ref):
    hidden = hidden_ref[...]
    center = hidden - jnp.mean(hidden, axis=-1, keepdims=True)
    spread = lax.rsqrt(jnp.mean(center * center, axis=-1, keepdims=True) + EPS)
    xhat = center * spread
    dnorm = half_ref[...].astype(jnp.float32) + far_ref[...].astype(jnp.float32)
    scaled = dnorm * gains_ref[1:2, :]
    inner = scaled - jnp.mean(scaled, axis=-1, keepdims=True)
    inner = inner - xhat * jnp.mean(scaled * xhat, axis=-1, keepdims=True)
    total = grad_ref[0].astype(jnp.float32) + inner * spread
    dhidden_ref[...] = total
    low_ref[...] = total.astype(jnp.bfloat16)


def mix_back_kernel(core_ref, own_ref, other_ref, w_ref, send_ref):
    cols = w_ref.shape[0]
    heads = cols // HD
    core = core_ref[0]
    for micro, low_ref in ((core, own_ref), (1 - core, other_ref)):
        total = mm(w_ref[...], low_ref[...], NT).astype(jnp.bfloat16)
        for head in range(heads):
            send_ref[micro * heads + head] = total[head * HD : (head + 1) * HD, :]


def mix_grad_kernel(core_ref, mixed_ref, own_ref, other_ref, far_ref, near_ref):
    core = core_ref[0]
    width = far_ref.shape[2]
    total = mm(mixed_ref[core], own_ref[...], NN) + mm(mixed_ref[1 - core], other_ref[...], NN)
    for place in range(4):
        near_ref[place] = total[:, place * width : (place + 1) * width]
        far_ref[place] = total[:, (4 + place) * width : (5 + place) * width].astype(jnp.bfloat16)


def project_back_kernel(core_ref, raw_ref, norm_ref, w_ref, far_ref, near_ref, send_ref, keep_ref):
    wide, width = far_ref.shape[1:]
    rows = raw_ref.shape[2]
    core = core_ref[0]
    total = mm(raw_ref[0], norm_ref[:rows, :], NN) + mm(raw_ref[1], norm_ref[rows:, :], NN)
    for place in range(4):
        near_ref[place] = total[:, place * width : (place + 1) * width]
        far_ref[place] = total[:, (4 + place) * width : (5 + place) * width].astype(jnp.bfloat16)
    send_ref[...] = mm(raw_ref[1 - core], w_ref[:wide, :], TN).astype(jnp.bfloat16)
    keep_ref[...] = mm(raw_ref[core], w_ref[:wide, :], TN)


def norm_one_back_kernel(
    core_ref, order_ref, x_ref, half_ref, far_ref, dhidden_ref, gains_ref, grad_ref, xhat_ref
):
    core = core_ref[0]
    width = x_ref.shape[2] // 8
    x = x_ref[core].astype(jnp.float32)
    mean = jnp.mean(x, axis=-1, keepdims=True)
    center = x - mean
    spread = lax.rsqrt(jnp.mean(center * center, axis=-1, keepdims=True) + EPS)
    for place in range(8):
        span = slice(place * width, (place + 1) * width)
        piece = x_ref[core, :, block_at(order_ref, place, width)].astype(jnp.float32)
        xhat_ref[:, span] = (piece - mean) * spread
    xhat = xhat_ref[...]
    dnorm = half_ref[...].astype(jnp.float32) + far_ref[...].astype(jnp.float32)
    scaled = dnorm * gains_ref[0:1, :]
    inner = scaled - jnp.mean(scaled, axis=-1, keepdims=True)
    inner = inner - xhat * jnp.mean(scaled * xhat, axis=-1, keepdims=True)
    total = (dhidden_ref[...] + inner * spread).astype(jnp.bfloat16)
    for place in range(8):
        grad_ref[:, block_at(order_ref, place, width)] = total[:, place * width : (place + 1) * width]


def place_grad_kernel(core_ref, order_ref, local_ref, four_ref, grad_ref, natural_ref):
    rows = grad_ref.shape[1]
    width = grad_ref.shape[2] // 8
    core = core_ref[0]
    for at in range(2):
        micro = core if at == 0 else 1 - core
        place = lax.broadcasted_iota(jnp.int32, (rows, rows), 0)
        onehot = jnp.where(local_ref[pl.ds(micro, 1), :] == place, 1.0, 0.0).astype(jnp.bfloat16)
        natural_ref[...] = mm(onehot, four_ref[micro], NN).astype(jnp.bfloat16)
        for block in range(8):
            span = slice(block * width, (block + 1) * width)
            grad_ref[at, :, span] = natural_ref[:, block_at(order_ref, block, width)]


def result_kernel(order_ref, picks_ref, hidden_ref, half_ref, far_ref, packed_ref, natural_ref):
    rows = hidden_ref.shape[0]
    width = hidden_ref.shape[1] // 8
    branch = half_ref[...].astype(jnp.float32) + far_ref[...].astype(jnp.float32)
    total = (hidden_ref[...] + branch).astype(jnp.bfloat16)
    for block in range(8):
        natural_ref[:, block_at(order_ref, block, width)] = total[:, block * width : (block + 1) * width]
    count = packed_ref.shape[0]
    place = lax.broadcasted_iota(jnp.int32, (rows, count), 0)
    onehot = jnp.where(picks_ref[...] == place, 1.0, 0.0).astype(jnp.bfloat16)
    packed_ref[...] = mm(onehot, natural_ref[...], TN).astype(jnp.bfloat16)


def positions(anchor, seq_lens):
    ends = running_ends(seq_lens)
    starts = ends - seq_lens
    inside = (anchor[:, None] >= starts[None, :]) & (anchor[:, None] < ends[None, :])
    return anchor - jnp.sum(jnp.where(inside, starts[None, :], 0), axis=1)


def turn_tables(place):
    freqs = jnp.power(THETA, -jnp.arange(HD // 2, dtype=jnp.float32) * 2.0 / HD)
    angle = freqs[:, None] * place.astype(jnp.float32)[None, :]
    return jnp.concatenate([jnp.cos(angle), jnp.sin(angle)], axis=0)


def paired_layer(
    tokens, cotangent, perm, lengths, w_qkv, w_attn_out, w_in, w_down, gain_one, gain_two
):
    f32, bf16, i32 = jnp.float32, jnp.bfloat16, jnp.int32
    mine = lax.axis_index("fsdp")
    part = lax.axis_index("tp")
    core, side = part & 1, part >> 1
    core_at = core.reshape(1).astype(i32)
    rows = tokens.shape[1]
    width = w_qkv.shape[0]
    full = 8 * width
    cols = w_qkv.shape[2]
    heads = cols // HD
    units = w_in.shape[2]
    per_pair = rows // 8
    order = jnp.bitwise_xor(jnp.array(ORDER, i32), mine)

    def pick(value, index):
        return lax.dynamic_index_in_dim(value, index, 0, keepdims=False)

    def both(value, other):
        return jnp.stack([jnp.where(core == 0, value, other), jnp.where(core == 0, other, value)])

    def add_half(keep, got):
        return (keep + got.astype(f32)).astype(bf16)

    def near_sum(near, far, name):
        shape = near.shape[1:]
        own, *lows = local_call(near_sum_kernel, name, (), (near, far), [(shape, f32)] + [(shape, bf16)] * 3, far_in=(0, 1), far_out=(0,))
        return own, lows

    def y_join(same):
        return same + [hop(jnp.concatenate(same, axis=0), 1)]

    def z_send(lows):
        return [hop(low, ORDER[at + 1]) for at, low in enumerate(lows)]

    def far_sum(own, got):
        return own + sum(one.astype(f32) for one in got)

    turned = jnp.transpose(w_qkv.reshape(width, 3, heads, HD), (2, 1, 3, 0)).reshape(3 * cols, width)
    gains_rows = jnp.concatenate([gain_one[None], gain_two[None], jnp.zeros((14, width), bf16)])
    first_same = z_phase(jnp.concatenate([turned, gains_rows], axis=0))
    first = first_same + y_phase(first_same)

    slots = perm.reshape(2, 8, rows)
    from_me = (slots // rows == mine).astype(f32)
    slot_no = jnp.arange(rows, dtype=i32)
    before = (slot_no[:, None] < slot_no[None, :]).astype(f32)
    rank_me = jnp.einsum("mds,st->mdt", from_me, before).astype(i32)
    ranks = jnp.arange(per_pair, dtype=i32)
    chosen = (from_me[..., None] > 0) & (rank_me[..., None] == ranks)
    local = jnp.sum(jnp.where(chosen, (slots % rows)[..., None], 0), axis=2)
    my_slots = lax.dynamic_index_in_dim(slots, mine, 1, keepdims=False)
    target = my_slots // rows
    same = (target[:, :, None] == target[:, None, :]) & (slot_no[:, None] < slot_no[None, :])[None]
    rank_own = jnp.sum(same.astype(i32), axis=1)
    place_own = target * per_pair + rank_own
    quarter = per_pair // 4
    wanted = order[:, None] * per_pair + part * quarter
    wanted = (wanted + jnp.arange(quarter, dtype=i32)[None, :]).reshape(-1)
    packer = (place_own[:, None, :] == wanted[None, :, None]).astype(bf16)
    packed = jnp.einsum("mps,msd->mpd", packer, cotangent, preferred_element_type=f32).astype(bf16)
    packed = packed.reshape(2, 8, quarter, full)
    packed = [packed[:, at] for at in range(8)]
    chosen = order[:, None] == jnp.arange(8, dtype=i32)[None, :]
    local_own = jnp.sum(jnp.where(chosen[None, :, :, None], local[:, None], 0), axis=2)
    anchor = mine * rows + jnp.arange(rows, dtype=i32)
    own_table = jnp.concatenate([turn_tables(positions(anchor, lengths[m])) for m in range(2)], axis=1)
    inp_turned, gate_turned = jnp.transpose(w_in[:, 0]), jnp.transpose(w_in[:, 1])
    second = jnp.concatenate([jnp.transpose(w_down), jnp.transpose(w_attn_out)], axis=0)
    second_all = lax.all_gather(second, "fsdp", axis=0, tiled=False)
    third_all = lax.all_gather(jnp.concatenate([inp_turned, gate_turned], axis=0), "fsdp", axis=0, tiled=False)
    halfway = per_pair // 2
    picks = lax.dynamic_slice_in_dim(pick(local, core), side * halfway, halfway, 1).reshape(1, -1)
    unpack = (place_own[:, :, None] == slot_no[None, None, :]).astype(bf16)
    my_lens = lengths[mine // heads]
    all_anchor = jnp.arange(8 * rows, dtype=i32)
    table = turn_tables(positions(all_anchor, my_lens))
    table = jnp.transpose(table.reshape(HD, 8, rows), (1, 0, 2))
    first, packed, own_table, picks, unpack, table, local_own, order, core_at, core, side, my_lens = sync(
        (first, packed, own_table, picks, unpack, table, local_own, order, core_at, core, side, my_lens)
    )

    norm_one, gains, outgoing, qkv_w = local_call(
        project_kernel, "project", (order,), (tokens, own_table),
        [((2 * rows, full), bf16), ((2, full), f32), ((2 * heads, 3 * HD, rows), bf16), ((3 * cols + 16, full), bf16)],
        (), first, far_in=(0, 1), far_out=(0, 1, 2, 3), far_shards=False,
    )
    outgoing, packed = sync((outgoing, packed))
    qkv = deal_out(outgoing)
    arrived = [hop(one, ORDER[at]) if at else one for at, one in enumerate(packed)]
    qkv = sync((qkv,))[0]
    mixed_out, exact, logs = local_call(
        attend_kernel, "attend", (my_lens,), (qkv,),
        [((8, HD, rows), bf16), ((8, HD, rows), f32), ((8, 1, rows), f32)],
        [((8 * rows, HD), bf16)], far_in=(0,), far_out=(0, 1, 2),
    )
    mixed_out, arrived = sync((mixed_out, arrived))
    mixed = deal_out(mixed_out).reshape(2, cols, rows)
    arrived = jnp.stack(arrived)
    near = twin(arrived)
    pair = jnp.stack([jnp.where(core == 0, arrived, near), jnp.where(core == 0, near, arrived)])
    far = across(pair)
    mixed, far = sync((mixed, far))
    four = jnp.concatenate([jnp.where(side == 0, pair, far), jnp.where(side == 0, far, pair)])
    four = jnp.transpose(four, (2, 1, 0, 3, 4)).reshape(2, rows, full)
    grad = local_call(
        place_grad_kernel, "place_grad", (core_at, order), (local_own.reshape(2, rows), four),
        [((2, rows, full), bf16)], [((rows, full), bf16)],
    )

    send, keep, out_w = local_call(
        mix_out_kernel, "mix_out", (core_at, order), (mixed,),
        [((rows, full), bf16), ((rows, full), f32), ((cols, full), bf16)], (), (second_all,), far_in=(0,),
    )
    half = add_half(keep, twin(send))
    far = across(half)
    far, grad = sync((far, grad))
    hidden, two_own = local_call(
        norm_two_kernel, "norm_two", (core_at, order), (tokens, half, far, gains),
        [((rows, full), f32), ((rows, full), bf16)], far_in=(0, 3),
    )
    two_other = twin(two_own)

    send, keep, act, d_inp, d_gate, result_send, result_keep = local_call(
        feed_kernel, "feed", (order,), (two_own, two_other, grad),
        [((rows, full), bf16), ((rows, full), f32)]
        + [((2 * rows, units), bf16)] * 3
        + [((rows, full), bf16), ((rows, full), f32)],
        [((3 * units, full), bf16)], (third_all, second_all), copies=16, far_out=(5, 6),
    )
    half_two = add_half(keep, twin(send))
    half_two, act, d_inp, d_gate = sync((half_two, act, d_inp, d_gate))
    far_two = across(half_two)
    feed_grad = local_call(
        weight_grad_kernel, "feed_grad", (order,), (d_inp, d_gate, act, two_own, two_other, grad),
        [((8, 3 * units, width), bf16)], far_out=(0,),
    )
    feed_sum = lax.psum_scatter(feed_grad, "fsdp", scatter_dimension=0, tiled=False)
    far_two, feed_grad = sync((far_two, feed_grad))
    d_hidden, low_own = local_call(
        norm_two_back_kernel, "norm_two_back", (), (hidden, half_two, far_two, grad, gains),
        [((rows, full), f32), ((rows, full), bf16)], far_in=(4,), far_out=(0,),
    )
    low_other = twin(low_own)
    d_mixed = local_call(
        mix_back_kernel, "mix_back", (core_at,), (low_own, low_other, out_w),
        [((8, HD, rows), bf16)], far_out=(0,),
    )
    d_mixed, low_own, low_other, result_send, result_keep = sync(
        (d_mixed, low_own, low_other, result_send, result_keep)
    )
    grad_mixed = deal_out(d_mixed)
    out_far, out_near = local_call(
        mix_grad_kernel, "mix_grad", (core_at,), (mixed, low_own, low_other),
        [((4, cols, width), bf16), ((4, cols, width), f32)], far_in=(0, 1, 2), far_out=(1,),
    )
    res_half = add_half(result_keep, twin(result_send))
    grad_mixed, out_far, res_half = sync((grad_mixed, out_far, res_half))

    out_got = hop(out_far, 1)
    res_far = across(res_half)
    d_raw_out = local_call(
        attend_back_kernel, "attend_back", (my_lens,), (qkv, exact, logs, grad_mixed, table),
        [((8, 3 * HD, rows), bf16)],
        [((8 * rows, 2 * HD), bf16), ((HD, 8 * rows), f32), ((HD, 8 * rows), f32)],
        far_in=(0, 1, 2, 3, 4), far_out=(0,),
    )
    d_raw_out, out_got, res_far = sync((d_raw_out, out_got, res_far))
    d_raw = deal_out(d_raw_out).reshape(2, 3 * cols, rows)
    out_own, out_lows = near_sum(out_near, out_got, "out_near")
    packed = local_call(
        result_kernel, "result", (order,), (picks, hidden, res_half, res_far),
        [((8 * halfway, full), bf16)], [((rows, full), bf16)], far_in=(1, 2, 3), far_out=(0,),
    )
    d_raw, out_lows, packed = sync((d_raw, out_lows, packed))

    qkv_far, qkv_near, send, keep = local_call(
        project_back_kernel, "project_back", (core_at,), (d_raw, norm_one, qkv_w),
        [((4, 3 * cols, width), bf16), ((4, 3 * cols, width), f32), ((rows, full), bf16), ((rows, full), f32)],
        far_in=(0, 1, 2), far_out=(1,),
    )
    qkv_got = hop(qkv_far, 1)
    half = add_half(keep, twin(send))
    far = across(half)
    out_got = z_send(out_lows)
    arrived = deal_out(packed.reshape(8, halfway, full))
    qkv_got, far, arrived = sync((qkv_got, far, arrived))
    qkv_own, qkv_lows = near_sum(qkv_near, qkv_got, "qkv_near")
    qkv_lows, arrived, far, feed_sum, out_got = sync((qkv_lows, arrived, far, feed_sum, out_got))
    input_own = local_call(
        norm_one_back_kernel, "norm_one_back", (core_at, order), (tokens, half, far, d_hidden, gains),
        [((rows, full), bf16)], [((rows, full), f32)], far_in=(0, 3, 4),
    )
    input_own, feed_sum, out_got = sync((input_own, feed_sum, out_got))
    input_grad = both(input_own, twin(input_own))
    out_sum = far_sum(out_own, out_got)
    inp_sum, gate_sum, down_sum = [feed_sum[at * units : (at + 1) * units].astype(f32) for at in range(3)]
    two_row = jnp.sum(inp_sum * inp_turned.astype(f32) + gate_sum * gate_turned.astype(f32), axis=0)
    grad_attn_out = jnp.transpose(out_sum)
    grad_in = jnp.stack([jnp.transpose(inp_sum), jnp.transpose(gate_sum)], axis=1)
    grad_down = jnp.transpose(down_sum)
    other_side = across(arrived)
    whole = jnp.concatenate(
        [jnp.where(side == 0, arrived, other_side), jnp.where(side == 0, other_side, arrived)], axis=1
    ).reshape(rows, full)
    whole = both(whole, twin(whole))
    output = jnp.einsum("msp,mpd->msd", unpack, whole, preferred_element_type=f32).astype(bf16)
    qkv_got = z_send(qkv_lows)
    qkv_got, output, input_grad, grad_attn_out, grad_in, grad_down, two_row = sync(
        (qkv_got, output, input_grad, grad_attn_out, grad_in, grad_down, two_row)
    )
    qkv_sum = far_sum(qkv_own, qkv_got)
    one_row = jnp.sum(qkv_sum * turned.astype(f32), axis=0)
    gain_rows = jnp.stack([one_row / gain_one.astype(f32), two_row / gain_two.astype(f32)])
    beyond = lax.ppermute(gain_rows, "tp", [(i, i ^ 3) for i in range(4)])
    gain_rows = (gain_rows + twin(gain_rows)) + (across(gain_rows) + beyond)
    grad_gain_one, grad_gain_two = gain_rows[0], gain_rows[1]
    return (
        output,
        input_grad,
        jnp.transpose(qkv_sum.reshape(heads, 3, HD, width), (3, 1, 0, 2)).reshape(width, 3, cols),
        grad_attn_out,
        grad_in,
        grad_down,
        grad_gain_one,
        grad_gain_two,
    )


def on_device(*operands):
    micro_count, tok_rows = operands[0].shape[0], operands[0].shape[1]
    groups, parts = lax.axis_size("fsdp"), lax.axis_size("tp")
    heads = operands[4].shape[2] // HD
    if groups == 8 and parts == 4 and micro_count == 2 and micro_count * heads == groups and tok_rows % 256 == 0:
        return paired_layer(*operands)
    return general_layer(*operands)


def solution(mesh):
    placed = (
        P(None, "fsdp", None),
        P(None, "fsdp", None),
        P(),
        P(),
        P("fsdp", None, "tp"),
        P("fsdp", "tp"),
        P("fsdp", None, "tp"),
        P("fsdp", "tp"),
        P("fsdp"),
        P("fsdp"),
    )
    return jax.shard_map(
        on_device,
        mesh=mesh,
        in_specs=placed,
        out_specs=(
            P(None, "fsdp", None),
            P(None, "fsdp", None),
            P("fsdp", None, "tp"),
            P("fsdp", "tp"),
            P("fsdp", None, "tp"),
            P("fsdp", "tp"),
            P("fsdp"),
            P("fsdp"),
        ),
        check_vma=False,
    )
```

```python
import math

import jax
import jax.numpy as jnp
from jax import lax
from jax.experimental import pallas as pl
from jax.experimental.pallas import tpu as pltpu
from jax.sharding import PartitionSpec as P

D = 1024
HD = 64


EPS = 1e-05
THETA = 160000.0
key_block = 2048


def layer_norm(values, gain):
    center = values - jnp.mean(values, axis=-1, keepdims=True)
    spread = jnp.mean(center * center, axis=-1, keepdims=True)
    return center * lax.rsqrt(spread + EPS) * gain


def rope_tables(position, width):
    freqs = jnp.power(THETA, -jnp.arange(width // 2, dtype=jnp.float32) * 2.0 / width)
    angle = position.astype(jnp.float32)[:, None] * freqs[None, :]
    angle = jnp.concatenate([angle, angle], axis=-1)
    return (jnp.cos(angle), jnp.sin(angle))


def rotate(values, cosine, sine):
    half = values.shape[-1] // 2
    turned = jnp.concatenate([-values[..., half:], values[..., :half]], axis=-1)
    return values * cosine[:, None, :] + turned * sine[:, None, :]


def running_ends(seq_lens):
    order = jnp.arange(seq_lens.shape[0], dtype=jnp.int32)
    return jnp.sum(jnp.where(order[None, :] <= order[:, None], seq_lens[None, :], 0), axis=1)


def seq_info(anchor, seq_lens):
    ends = running_ends(seq_lens)
    starts = ends - seq_lens
    segment = jnp.sum((anchor[:, None] >= ends[None, :]).astype(jnp.int32), axis=1)
    onehot = segment[:, None] == jnp.arange(seq_lens.shape[0], dtype=jnp.int32)[None, :]
    position = anchor - jnp.sum(jnp.where(onehot, starts[None, :], 0), axis=1)
    return (segment, position)


def blockwise(running, pieces, offset, step_fn):
    piece_len = pieces[0].shape[0]
    if piece_len > key_block and piece_len % key_block == 0:
        block_count = piece_len // key_block
        stacked = tuple((one.reshape((block_count, key_block) + one.shape[1:]) for one in pieces))

        def inner(state_now, scan_item):
            block_index, piece_parts = scan_item
            return (step_fn(state_now, piece_parts, offset + block_index * key_block), None)

        running, _ = lax.scan(inner, running, (jnp.arange(block_count, dtype=jnp.int32), stacked))
        return running
    return step_fn(running, pieces, offset)


def general_layer(
    tokens, cotangent, perm, lengths, w_qkv, w_attn_out, w_in, w_down, gain_one, gain_two
):
    groups = lax.axis_size("fsdp")
    my_index = lax.axis_index("fsdp")
    micro_count = tokens.shape[0]
    tok_rows = tokens.shape[1]
    total_rows = tok_rows * groups
    per_pair = tok_rows // groups
    head_cols = w_qkv.shape[2]
    head_count = head_cols // HD
    unit_cols = w_in.shape[2]
    score_scale = HD ** (-0.5)
    rows_idx = jnp.arange(tok_rows, dtype=jnp.int32)
    f32 = jnp.float32
    bf16 = jnp.bfloat16
    dims_rows = (((0,), (0,)), ((), ()))
    dims_cols = (((1,), (1,)), ((), ()))
    acc_qkv = jnp.zeros((D, 3, head_cols), f32)
    acc_out = jnp.zeros((D, head_cols), f32)
    acc_in = jnp.zeros((D, 2, unit_cols), f32)
    acc_down = jnp.zeros((D, unit_cols), f32)
    acc_gain_one = jnp.zeros((D,), f32)
    acc_gain_two = jnp.zeros((D,), f32)
    outputs = []
    input_grads = []
    for micro_idx in range(micro_count):
        perm_row = perm[micro_idx]
        seq_lens = lengths[micro_idx]
        inverse = (
            jnp.zeros((total_rows,), jnp.int32)
            .at[perm_row]
            .set(jnp.arange(total_rows, dtype=jnp.int32))
        )
        placed = lax.dynamic_slice_in_dim(inverse, my_index * tok_rows, tok_rows)
        send_order = jnp.argsort(placed)
        outgoing = tokens[micro_idx][send_order].reshape(groups, per_pair, D)
        arrived = lax.all_to_all(outgoing, "fsdp", split_axis=0, concat_axis=0, tiled=True).reshape(
            tok_rows, D
        )
        my_tokens = lax.dynamic_slice_in_dim(perm_row, my_index * tok_rows, tok_rows)
        source = my_tokens // tok_rows
        recv_order = jnp.argsort(source * tok_rows + rows_idx)
        recv_slot = jnp.zeros((tok_rows,), jnp.int32).at[recv_order].set(rows_idx)
        dealt = arrived[recv_slot]
        fetched = (
            lax.all_gather(gain_one, "fsdp", axis=0, tiled=True),
            lax.all_gather(gain_two, "fsdp", axis=0, tiled=True),
            lax.all_gather(w_qkv, "fsdp", axis=0, tiled=True),
            lax.all_gather(w_attn_out, "fsdp", axis=0, tiled=True),
            lax.all_gather(w_in, "fsdp", axis=0, tiled=True),
            lax.all_gather(w_down, "fsdp", axis=0, tiled=True),
        )
        gain_first = fetched[0].astype(f32)
        gain_second = fetched[1].astype(f32)
        query_seg, query_pos = seq_info(my_tokens, seq_lens)
        cosine, sine = rope_tables(query_pos, HD)
        x_float = dealt.astype(f32)
        normed_low = layer_norm(x_float, gain_first).astype(bf16)
        raw_proj = jnp.einsum("td,dcf->tcf", normed_low, fetched[2], preferred_element_type=f32)
        raw_heads = raw_proj.reshape(tok_rows, 3, head_count, HD)
        query_low = rotate(raw_heads[:, 0], cosine, sine).astype(bf16)
        key_low = rotate(raw_heads[:, 1], cosine, sine).astype(bf16)
        value_low = raw_heads[:, 2].astype(bf16)

        def forward_step(running, piece_parts, offset):
            run_peak, run_total, run_acc = running
            key_part, value_part = piece_parts
            key_seg, _ = seq_info(
                lax.dynamic_slice_in_dim(perm_row, offset, key_part.shape[0]), seq_lens
            )
            scores = (
                jnp.einsum("qhe,khe->hqk", query_low, key_part, preferred_element_type=f32)
                * score_scale
            )
            same_seq = (query_seg[:, None] == key_seg[None, :])[None]
            block_top = jnp.max(jnp.where(same_seq, scores, -1e30), axis=-1)
            new_peak = jnp.maximum(run_peak, block_top)
            weights = jnp.where(same_seq, jnp.exp(scores - new_peak[..., None]), 0.0)
            fade_factor = jnp.exp(run_peak - new_peak)
            run_acc = run_acc * jnp.transpose(fade_factor)[:, :, None] + jnp.einsum(
                "hqk,khe->qhe", weights.astype(bf16), value_part, preferred_element_type=f32
            )
            run_total = run_total * fade_factor + jnp.sum(weights, axis=-1)
            return (new_peak, run_total, run_acc)

        start_state = (
            jnp.full((head_count, tok_rows), -1e30, f32),
            jnp.zeros((head_count, tok_rows), f32),
            jnp.zeros((tok_rows, head_count, HD), f32),
        )
        run_peak, run_total, run_acc = blockwise(
            start_state,
            (
                lax.all_gather(key_low, "fsdp", axis=0, tiled=True),
                lax.all_gather(value_low, "fsdp", axis=0, tiled=True),
            ),
            jnp.int32(0),
            forward_step,
        )
        log_total = run_peak + jnp.log(run_total)
        mixed_heads = run_acc / jnp.transpose(run_total)[:, :, None]
        mixed_low = mixed_heads.reshape(tok_rows, head_cols).astype(bf16)
        attn_part = lax.dot_general(mixed_low, fetched[3], dims_cols, preferred_element_type=f32)
        branch = lax.psum(attn_part.astype(jnp.bfloat16), "tp").astype(jnp.float32)
        hidden = x_float + branch
        normed_two = layer_norm(hidden, gain_second).astype(bf16)
        ffn_proj = jnp.einsum("td,dcf->tcf", normed_two, fetched[4], preferred_element_type=f32)
        act_low = (jax.nn.gelu(ffn_proj[:, 0], approximate=False) * ffn_proj[:, 1]).astype(bf16)
        ffn_part = lax.dot_general(act_low, fetched[5], dims_cols, preferred_element_type=f32)
        branch_two = lax.psum(ffn_part.astype(jnp.bfloat16), "tp").astype(jnp.float32)
        outputs.append((hidden + branch_two).astype(bf16))
        again = (
            lax.all_gather(gain_one, "fsdp", axis=0, tiled=True),
            lax.all_gather(gain_two, "fsdp", axis=0, tiled=True),
            lax.all_gather(w_qkv, "fsdp", axis=0, tiled=True),
            lax.all_gather(w_attn_out, "fsdp", axis=0, tiled=True),
            lax.all_gather(w_in, "fsdp", axis=0, tiled=True),
            lax.all_gather(w_down, "fsdp", axis=0, tiled=True),
        )
        gain_first = again[0].astype(f32)
        gain_second = again[1].astype(f32)
        grad_low = cotangent[micro_idx]
        grad_float = grad_low.astype(f32)
        acc_down = acc_down + lax.dot_general(
            grad_low, act_low, dims_rows, preferred_element_type=f32
        )
        d_act = jnp.dot(grad_low, again[5], preferred_element_type=f32)
        _, gelu_pull = jax.vjp(
            lambda inputs, gates: jax.nn.gelu(inputs, approximate=False) * gates,
            ffn_proj[:, 0],
            ffn_proj[:, 1],
        )
        d_inputs, d_gates = gelu_pull(d_act)
        d_proj = jnp.stack([d_inputs, d_gates], axis=1).astype(bf16)
        acc_in = acc_in + jnp.einsum("td,tcf->dcf", normed_two, d_proj, preferred_element_type=f32)
        norm_part = jnp.einsum("tcf,dcf->td", d_proj, again[4], preferred_element_type=f32)
        d_norm_two = lax.psum(norm_part.astype(jnp.bfloat16), "tp").astype(jnp.float32)
        _, second_pull = jax.vjp(layer_norm, hidden, gain_second)
        d_hid_norm, d_gain_two = second_pull(d_norm_two)
        acc_gain_two = acc_gain_two + d_gain_two
        d_hidden = grad_float + d_hid_norm
        hidden_low = d_hidden.astype(bf16)
        acc_out = acc_out + lax.dot_general(
            hidden_low, mixed_low, dims_rows, preferred_element_type=f32
        )
        d_mixed = jnp.dot(hidden_low, again[3], preferred_element_type=f32).astype(bf16)
        d_mixed = d_mixed.reshape(tok_rows, head_count, HD)
        delta_rows = jnp.sum(d_mixed.astype(f32) * mixed_heads, axis=-1)
        delta_heads = jnp.transpose(delta_rows)

        def query_step(grad_query, piece_parts, offset):
            key_part, value_part = piece_parts
            key_seg, _ = seq_info(
                lax.dynamic_slice_in_dim(perm_row, offset, key_part.shape[0]), seq_lens
            )
            scores = (
                jnp.einsum("qhe,khe->hqk", query_low, key_part, preferred_element_type=f32)
                * score_scale
            )
            same_seq = (query_seg[:, None] == key_seg[None, :])[None]
            weights = jnp.where(same_seq, jnp.exp(scores - log_total[..., None]), 0.0)
            d_weights = jnp.einsum("qhe,khe->hqk", d_mixed, value_part, preferred_element_type=f32)
            d_scores = (weights * (d_weights - delta_heads[..., None])).astype(bf16)
            return grad_query + score_scale * jnp.einsum(
                "hqk,khe->qhe", d_scores, key_part, preferred_element_type=f32
            )

        query_start = jnp.zeros((tok_rows, head_count, HD), f32)
        grad_query = blockwise(
            query_start,
            (
                lax.all_gather(key_low, "fsdp", axis=0, tiled=True),
                lax.all_gather(value_low, "fsdp", axis=0, tiled=True),
            ),
            jnp.int32(0),
            query_step,
        )
        stat_total, stat_delta = (
            lax.all_gather(jnp.transpose(log_total), "fsdp", axis=0, tiled=True),
            lax.all_gather(delta_rows, "fsdp", axis=0, tiled=True),
        )

        def key_step(running, piece_parts, offset):
            grad_key, grad_value = running
            query_part, dmix_part = piece_parts
            piece_len = query_part.shape[0]
            piece_seg, _ = seq_info(lax.dynamic_slice_in_dim(perm_row, offset, piece_len), seq_lens)
            total_part = jnp.transpose(lax.dynamic_slice_in_dim(stat_total, offset, piece_len))
            delta_part = jnp.transpose(lax.dynamic_slice_in_dim(stat_delta, offset, piece_len))
            scores = (
                jnp.einsum("qhe,khe->hqk", query_part, key_low, preferred_element_type=f32)
                * score_scale
            )
            same_seq = (piece_seg[:, None] == query_seg[None, :])[None]
            weights = jnp.where(same_seq, jnp.exp(scores - total_part[..., None]), 0.0)
            d_weights = jnp.einsum("qhe,khe->hqk", dmix_part, value_low, preferred_element_type=f32)
            d_scores = (weights * (d_weights - delta_part[..., None])).astype(bf16)
            grad_key = grad_key + score_scale * jnp.einsum(
                "hqk,qhe->khe", d_scores, query_part, preferred_element_type=f32
            )
            grad_value = grad_value + jnp.einsum(
                "hqk,qhe->khe", weights.astype(bf16), dmix_part, preferred_element_type=f32
            )
            return (grad_key, grad_value)

        grad_key, grad_value = blockwise(
            (
                jnp.zeros((tok_rows, head_count, HD), f32),
                jnp.zeros((tok_rows, head_count, HD), f32),
            ),
            (
                lax.all_gather(query_low, "fsdp", axis=0, tiled=True),
                lax.all_gather(d_mixed, "fsdp", axis=0, tiled=True),
            ),
            jnp.int32(0),
            key_step,
        )
        _, rope_pull = jax.vjp(lambda heads_in: rotate(heads_in, cosine, sine), raw_heads[:, 0])
        d_raw_query = rope_pull(grad_query)[0]
        d_raw_key = rope_pull(grad_key)[0]
        d_raw = (
            jnp.stack([d_raw_query, d_raw_key, grad_value], axis=1)
            .reshape(tok_rows, 3, head_cols)
            .astype(bf16)
        )
        acc_qkv = acc_qkv + jnp.einsum("td,tcf->dcf", normed_low, d_raw, preferred_element_type=f32)
        first_part = jnp.einsum("tcf,dcf->td", d_raw, again[2], preferred_element_type=f32)
        d_norm_one = lax.psum(first_part.astype(jnp.bfloat16), "tp").astype(jnp.float32)
        _, first_pull = jax.vjp(layer_norm, x_float, gain_first)
        d_x_norm, d_gain_one = first_pull(d_norm_one)
        acc_gain_one = acc_gain_one + d_gain_one
        d_input = (d_hidden + d_x_norm).astype(bf16)
        back_rows = d_input[recv_order].reshape(groups, per_pair, D)
        returned = lax.all_to_all(
            back_rows, "fsdp", split_axis=0, concat_axis=0, tiled=True
        ).reshape(tok_rows, D)
        send_slot = jnp.zeros((tok_rows,), jnp.int32).at[send_order].set(rows_idx)
        input_grads.append(returned[send_slot])
    summed = (
        lax.psum_scatter(acc_qkv, "fsdp", scatter_dimension=0, tiled=True),
        lax.psum_scatter(acc_out, "fsdp", scatter_dimension=0, tiled=True),
        lax.psum_scatter(acc_in, "fsdp", scatter_dimension=0, tiled=True),
        lax.psum_scatter(acc_down, "fsdp", scatter_dimension=0, tiled=True),
        lax.psum_scatter(acc_gain_one, "fsdp", scatter_dimension=0, tiled=True),
        lax.psum_scatter(acc_gain_two, "fsdp", scatter_dimension=0, tiled=True),
    )
    return (
        jnp.stack(outputs),
        jnp.stack(input_grads),
        summed[0],
        summed[1],
        summed[2],
        summed[3],
        summed[4],
        summed[5],
    )


JOIN = 2
COSTS = {"attend": 10, "attend_back": 28, "feed": 8, "norm_one_back": 0, "qkv_near": 0, "feed_grad": 5}
FAR = -1e30
ORDER = (0, 2, 4, 6, 1, 3, 5, 7)
NT = (((1,), (1,)), ((), ()))
TN = (((0,), (0,)), ((), ()))
NN = (((1,), (0,)), ((), ()))
ROOM = 10 * 1024 * 1024


def partial(kernel, *given):
    return lambda *refs: kernel(*given, *refs)


def mm(left, right, dims):
    return lax.dot_general(left, right, dims, preferred_element_type=jnp.float32)


def hop(value, step):
    return lax.ppermute(value, "fsdp", [(i, i ^ step) for i in range(8)])


def twin(value):
    return lax.ppermute(value, "tp", [(i, i ^ 1) for i in range(4)])


def across(value):
    return lax.ppermute(value, "tp", [(i, i ^ 2) for i in range(4)])


def deal_out(value):
    return lax.all_to_all(value, "fsdp", 0, 0, tiled=True)


def after(value, *earlier):
    return lax.optimization_barrier((value,) + earlier)[0]


def sync(values):
    return lax.optimization_barrier(values)


def z_phase(shard):
    return [shard] + [hop(shard, step) for step in ORDER[1:4]]


def y_phase(shards):
    return [hop(one, 1) for one in shards]


def local_call(kernel, name, scalars, arrays, outs, scratch=(), shards=(), copies=8, far_in=(), far_out=(), far_shards=True, raw_out=()):
    shapes = [(one.shape, one.dtype) for one in arrays]
    staged = [shapes[at] for at in far_in] + [outs[at] for at in far_out]
    sems = [pltpu.SemaphoreType.DMA((copies,))] if shards else []
    room = ROOM + sum(math.prod(shape) * jnp.dtype(kind).itemsize for shape, kind in [*shapes, *outs, *scratch])
    counts = (len(scalars), len(arrays), len(shards), len(outs), len(scratch) + len(sems))

    def body(*refs):
        groups = []
        for count in counts:
            groups.append(list(refs[:count]))
            refs = refs[count:]
        given, ins, pieces, results, extra = groups
        if not staged:
            return kernel(*given, *ins, *pieces, *results, *extra)
        stage, sem = refs[:-1], refs[-1]
        incoming, outgoing = [], []
        for slot, at in enumerate(far_in):
            incoming.append(pltpu.make_async_copy(ins[at], stage[slot], sem.at[slot]))
            incoming[-1].start()
            ins[at] = stage[slot]
        for slot, at in enumerate(far_out, len(far_in)):
            outgoing.append(pltpu.make_async_copy(stage[slot], results[at], sem.at[slot]))
            results[at] = stage[slot]
        for copy in incoming:
            copy.wait()
        kernel(*given, *ins, *pieces, *results, *extra)
        for copy in outgoing:
            copy.start()
        for copy in outgoing:
            copy.wait()

    arrays = [pltpu.with_memory_space_constraint(one, pltpu.HBM) if at in far_in else one for at, one in enumerate(arrays)]
    shards = [pltpu.with_memory_space_constraint(one, pltpu.HBM) if far_shards else one for one in shards]

    def space(at, far):
        return pl.BlockSpec(memory_space=pltpu.HBM if at in far else pltpu.VMEM)

    result = pl.pallas_call(
        body,
        in_specs=[pl.BlockSpec(memory_space=pltpu.SMEM)] * len(scalars)
        + [space(at, far_in) for at in range(len(arrays))]
        + [pl.BlockSpec(memory_space=pltpu.HBM if far_shards else pl.ANY)] * len(shards),
        out_specs=[space(at, (*far_out, *raw_out)) for at in range(len(outs))],
        out_shape=[
            pltpu.HBM(shape, kind) if at in (*far_out, *raw_out) else jax.ShapeDtypeStruct(shape, kind)
            for at, (shape, kind) in enumerate(outs)
        ],
        scratch_shapes=[pltpu.VMEM(shape, kind) for shape, kind in scratch]
        + sems
        + [pltpu.VMEM(shape, kind) for shape, kind in staged]
        + ([pltpu.SemaphoreType.DMA((len(staged),))] if staged else []),
        compiler_params=pltpu.CompilerParams(vmem_limit_bytes=room),
        cost_estimate=pl.CostEstimate(flops=COSTS.get(name, 3) * 10**9, transcendentals=0, bytes_accessed=8 * 1024 * 1024),
        name=name,
    )(*scalars, *arrays, *shards)
    return result if len(outs) > 1 else result[0]


def block_at(order_ref, place, width):
    return pl.ds(pl.multiple_of(order_ref[place] * width, width), width)


def shard_copies(shards, low, high, into_ref, sem_ref, base=0):
    width = shards[0].shape[1]
    copies = []
    for place, shard in enumerate(shards):
        span = pl.ds(place * width, width)
        source = shard.at[pl.ds(low, high - low), :]
        copies.append(pltpu.make_async_copy(source, into_ref.at[:, span], sem_ref.at[base + place]))
        copies[-1].start()
    return copies


def gathered_copies(order_ref, source, low, high, into_ref, sem_ref, base=0):
    width = source.shape[2]
    copies = []
    for place in range(8):
        copies.append(
            pltpu.make_async_copy(
                source.at[order_ref[place], pl.ds(low, high - low), :],
                into_ref.at[:, pl.ds(place * width, width)],
                sem_ref.at[base + place],
            )
        )
        copies[-1].start()
    return copies


def finish(copies):
    for copy in copies:
        copy.wait()


def project_kernel(order_ref, x_ref, table_ref, *refs):
    shards = refs[:8]
    norm_out_ref, gains_ref, send_ref, w_out_ref, norm_ref, w_ref, sem_ref = refs[8:]
    width = shards[0].shape[1]
    rows = x_ref.shape[1]
    wide = w_ref.shape[0] - 16
    heads = wide // (3 * HD)
    half = HD // 2
    finish(shard_copies(shards, 0, wide + 16, w_ref, sem_ref))
    outgoing = [pltpu.make_async_copy(w_ref, w_out_ref, sem_ref.at[8]), pltpu.make_async_copy(norm_ref, norm_out_ref, sem_ref.at[9])]
    outgoing[0].start()
    gains_ref[...] = w_ref[wide:, :].astype(jnp.float32)[:2]
    for micro in range(2):
        x = x_ref[micro].astype(jnp.float32)
        mean = jnp.mean(x, axis=-1, keepdims=True)
        center = x - mean
        spread = lax.rsqrt(jnp.mean(center * center, axis=-1, keepdims=True) + EPS)
        for place in range(8):
            piece = x_ref[micro, :, block_at(order_ref, place, width)].astype(jnp.float32)
            span = slice(place * width, (place + 1) * width)
            value = (piece - mean) * spread * gains_ref[0:1, span]
            norm_ref[micro * rows : (micro + 1) * rows, span] = value.astype(jnp.bfloat16)
    outgoing[1].start()
    raw = mm(w_ref[:wide, :], norm_ref[...], NT)
    cosine, sine = table_ref[:half, :], table_ref[half:, :]
    for head in range(heads):
        base = head * 3 * HD
        for kind in range(2):
            upper = raw[base + kind * HD : base + kind * HD + half]
            lower = raw[base + kind * HD + half : base + (kind + 1) * HD]
            first = (upper * cosine - lower * sine).astype(jnp.bfloat16)
            second = (lower * cosine + upper * sine).astype(jnp.bfloat16)
            for micro in range(2):
                span = slice(micro * rows, (micro + 1) * rows)
                send_ref[micro * heads + head, kind * HD : kind * HD + half, :] = first[:, span]
                send_ref[micro * heads + head, kind * HD + half : (kind + 1) * HD, :] = second[:, span]
        value = raw[base + 2 * HD : base + 3 * HD].astype(jnp.bfloat16)
        for micro in range(2):
            send_ref[micro * heads + head, 2 * HD :, :] = value[:, micro * rows : (micro + 1) * rows]
    finish(outgoing)


def key_range(lens_ref, low, high):
    first = jnp.int32(0)
    last = jnp.int32(0)
    total = jnp.int32(0)
    for index in range(lens_ref.shape[0]):
        start = total
        total = total + lens_ref[index]
        first = jnp.where((start <= low) & (low < total), start, first)
        last = jnp.where((start <= high) & (high < total), total, last)
    return first, last


def query_bounds(lens_ref, base, width):
    place = base + lax.broadcasted_iota(jnp.int32, (1, width), 1)
    first = jnp.zeros((1, width), jnp.int32)
    last = jnp.zeros((1, width), jnp.int32)
    total = jnp.int32(0)
    for index in range(lens_ref.shape[0]):
        start = total
        total = total + lens_ref[index]
        inside = (place >= start) & (place < total)
        first = jnp.where(inside, start, first)
        last = jnp.where(inside, total, last)
    return first, last


def lanes(ref, index, count, rows):
    return jnp.concatenate([ref[index * count + at, rows, :] for at in range(count)], axis=1)


def attend_kernel(lens_ref, qkv_ref, mixed_ref, exact_ref, log_ref, key_ref):
    blocks, _, small = qkv_ref.shape
    wide = JOIN * small
    for at in range(blocks):
        block = qkv_ref[at, HD : 2 * HD, :].astype(jnp.float32)
        key_ref[at * small : (at + 1) * small, :] = jnp.transpose(block).astype(jnp.bfloat16)

    def one_query(index, carry):
        base = index * wide
        first, last = key_range(lens_ref, base, base + wide - 1)
        low, high = query_bounds(lens_ref, base, wide)
        query = lanes(qkv_ref, index, JOIN, slice(0, HD)) * jnp.bfloat16(HD**-0.5)

        def one_key(at, state):
            peak, total, acc = state
            start = pl.multiple_of(at * wide, wide)
            scores = mm(key_ref[pl.ds(start, wide), :], query, NN)
            place = start + lax.broadcasted_iota(jnp.int32, (wide, wide), 0)
            scores = jnp.where((place >= low) & (place < high), scores, FAR)
            top = jnp.maximum(peak, jnp.max(scores, axis=0, keepdims=True))
            weights = jnp.exp(scores - top)
            fade = jnp.exp(peak - top)
            total = total * fade + jnp.sum(weights, axis=0, keepdims=True)
            value = lanes(qkv_ref, at, JOIN, slice(2 * HD, 3 * HD))
            acc = acc * fade + mm(value, weights.astype(jnp.bfloat16), NN)
            return top, total, acc

        peak, total, acc = lax.fori_loop(
            first // wide,
            (last + wide - 1) // wide,
            one_key,
            (
                jnp.full((1, wide), FAR, jnp.float32),
                jnp.zeros((1, wide), jnp.float32),
                jnp.zeros((HD, wide), jnp.float32),
            ),
        )
        result = acc / total
        logs = peak + jnp.log(total)
        for at in range(JOIN):
            span = slice(at * small, (at + 1) * small)
            mixed_ref[index * JOIN + at] = result[:, span].astype(jnp.bfloat16)
            exact_ref[index * JOIN + at] = result[:, span]
            log_ref[index * JOIN + at] = logs[:, span]
        return carry

    lax.fori_loop(0, blocks // JOIN, one_query, 0)


def attend_back_kernel(
    lens_ref, qkv_ref, exact_ref, log_ref, grad_ref, table_ref, raw_ref, pair_ref, dkey_ref, dvalue_ref
):
    blocks, _, small = qkv_ref.shape
    wide = JOIN * small
    half = HD // 2
    for at in range(blocks):
        block = qkv_ref[at, HD : 3 * HD, :].astype(jnp.float32)
        pair_ref[at * small : (at + 1) * small, :] = jnp.transpose(block).astype(jnp.bfloat16)
    dkey_ref[...] = jnp.zeros(dkey_ref.shape, jnp.float32)
    dvalue_ref[...] = jnp.zeros(dvalue_ref.shape, jnp.float32)

    def unturn(index, grad):
        cosine = table_ref[index, :half, :]
        sine = table_ref[index, half:, :]
        upper, lower = grad[:half], grad[half:]
        return upper * cosine + lower * sine, lower * cosine - upper * sine

    def one_query(index, carry):
        base = index * wide
        first, last = key_range(lens_ref, base, base + wide - 1)
        low, high = query_bounds(lens_ref, base, wide)
        query = lanes(qkv_ref, index, JOIN, slice(0, HD)) * jnp.bfloat16(HD**-0.5)
        grad = lanes(grad_ref, index, JOIN, slice(0, HD))
        logs = lanes(log_ref, index, JOIN, slice(0, 1))
        exact = lanes(exact_ref, index, JOIN, slice(0, HD))
        delta = jnp.sum(grad.astype(jnp.float32) * exact, axis=0, keepdims=True)

        def one_key(at, dquery):
            start = pl.multiple_of(at * wide, wide)
            span = pl.ds(start, wide)
            scores = mm(pair_ref[span, :HD], query, NN)
            dweights = mm(pair_ref[span, HD:], grad, NN)
            place = start + lax.broadcasted_iota(jnp.int32, (wide, wide), 0)
            weights = jnp.where((place >= low) & (place < high), jnp.exp(scores - logs), 0.0)
            dscores = (weights * (dweights - delta)).astype(jnp.bfloat16)
            dkey_ref[:, span] += mm(query, dscores, NT)
            dvalue_ref[:, span] += mm(grad, weights.astype(jnp.bfloat16), NT)
            return dquery + mm(lanes(qkv_ref, at, JOIN, slice(HD, 2 * HD)), dscores, NN)

        dquery = lax.fori_loop(
            first // wide,
            (last + wide - 1) // wide,
            one_key,
            jnp.zeros((HD, wide), jnp.float32),
        ) * (HD**-0.5)
        for at in range(JOIN):
            upper, lower = unturn(index * JOIN + at, dquery[:, at * small : (at + 1) * small])
            raw_ref[index * JOIN + at, :half, :] = upper.astype(jnp.bfloat16)
            raw_ref[index * JOIN + at, half:HD, :] = lower.astype(jnp.bfloat16)
        return carry

    lax.fori_loop(0, blocks // JOIN, one_query, 0)
    for at in range(blocks):
        span = slice(at * small, (at + 1) * small)
        upper, lower = unturn(at, dkey_ref[:, span])
        raw_ref[at, HD : HD + half, :] = upper.astype(jnp.bfloat16)
        raw_ref[at, HD + half : 2 * HD, :] = lower.astype(jnp.bfloat16)
        raw_ref[at, 2 * HD :, :] = dvalue_ref[:, span].astype(jnp.bfloat16)


def mix_out_kernel(core_ref, order_ref, mixed_ref, all_ref, send_ref, keep_ref, w_ref, sem_ref):
    last = all_ref.shape[1]
    finish(gathered_copies(order_ref, all_ref, last - mixed_ref.shape[1], last, w_ref, sem_ref))
    core = core_ref[0]
    send_ref[...] = mm(mixed_ref[1 - core], w_ref[...], TN).astype(jnp.bfloat16)
    keep_ref[...] = mm(mixed_ref[core], w_ref[...], TN)


def norm_two_kernel(core_ref, order_ref, x_ref, half_ref, far_ref, gains_ref, hidden_ref, norm_ref):
    core = core_ref[0]
    width = x_ref.shape[2] // 8
    for place in range(8):
        span = slice(place * width, (place + 1) * width)
        piece = x_ref[core, :, block_at(order_ref, place, width)].astype(jnp.float32)
        branch = half_ref[:, span].astype(jnp.float32) + far_ref[:, span].astype(jnp.float32)
        hidden_ref[:, span] = piece + branch
    hidden = hidden_ref[...]
    center = hidden - jnp.mean(hidden, axis=-1, keepdims=True)
    spread = lax.rsqrt(jnp.mean(center * center, axis=-1, keepdims=True) + EPS)
    norm_ref[...] = (center * spread * gains_ref[1:2, :]).astype(jnp.bfloat16)


def feed_kernel(
    order_ref, own_ref, other_ref, all_ref, down_ref, source_ref,
    send_ref, keep_ref, act_ref, dinp_ref, dgate_ref, result_send_ref, result_keep_ref, w_ref, grad_ref, sem_ref
):
    units = w_ref.shape[0] // 3
    inp_w, gate_w, down_w = [w_ref.at[pl.ds(at * units, units), :] for at in range(3)]
    rows = own_ref.shape[0]
    inp_copies = gathered_copies(order_ref, all_ref, 0, units, inp_w, sem_ref)
    grad_copy = pltpu.make_async_copy(source_ref, grad_ref, sem_ref.at[24])
    grad_copy.start()
    gate_copies = gathered_copies(order_ref, all_ref, units, 2 * units, gate_w, sem_ref, 16)
    down_copies = gathered_copies(order_ref, down_ref, 0, units, down_w, sem_ref, 8)
    finish(inp_copies)
    for micro, norm_ref in ((1, other_ref), (0, own_ref)):
        span = slice(micro * rows, (micro + 1) * rows)
        inp = mm(norm_ref[...], inp_w[...], NT)
        if micro:
            finish(gate_copies)
        gate = mm(norm_ref[...], gate_w[...], NT)
        if micro:
            finish(down_copies + [grad_copy])
        dact = mm(grad_ref[micro], down_w[...], NT)
        cdf = 0.5 * (1.0 + lax.erf(inp * (0.5**0.5)))
        density = jnp.exp(-0.5 * inp * inp) * ((0.5 / jnp.pi) ** 0.5)
        gelu = inp * cdf
        act = (gelu * gate).astype(jnp.bfloat16)
        act_ref[span, :] = act
        dinp = (dact * gate * (cdf + inp * density)).astype(jnp.bfloat16)
        dgate = (dact * gelu).astype(jnp.bfloat16)
        dinp_ref[span, :] = dinp
        dgate_ref[span, :] = dgate
        part = mm(dinp, inp_w[...], NN) + mm(dgate, gate_w[...], NN)
        result = mm(act, down_w[...], NN)
        if micro:
            send_ref[...] = part.astype(jnp.bfloat16)
            result_send_ref[...] = result.astype(jnp.bfloat16)
        else:
            keep_ref[...] = part
            result_keep_ref[...] = result


def weight_grad_kernel(order_ref, dinp_ref, dgate_ref, act_ref, own_ref, other_ref, grad_ref, out_ref):
    units = act_ref.shape[1]
    rows = own_ref.shape[0]
    width = out_ref.shape[2]
    for at, (left_ref, rights) in enumerate((
        (dinp_ref, (own_ref, other_ref)),
        (dgate_ref, (own_ref, other_ref)),
        (act_ref, (grad_ref.at[0], grad_ref.at[1])),
    )):
        total = mm(left_ref[:rows, :], rights[0][...], TN) + mm(left_ref[rows:, :], rights[1][...], TN)
        for place in range(8):
            piece = total[:, place * width : (place + 1) * width].astype(jnp.bfloat16)
            out_ref[order_ref[place], at * units : (at + 1) * units, :] = piece


def near_sum_kernel(near_ref, far_ref, *low_refs):
    for at, low_ref in enumerate(low_refs):
        low_ref[...] = (near_ref[at + 1] + far_ref[at + 1].astype(jnp.float32)).astype(jnp.bfloat16)


def norm_two_back_kernel(hidden_ref, half_ref, far_ref, grad_ref, gains_ref, dhidden_ref, low_ref):
    hidden = hidden_ref[...]
    center = hidden - jnp.mean(hidden, axis=-1, keepdims=True)
    spread = lax.rsqrt(jnp.mean(center * center, axis=-1, keepdims=True) + EPS)
    xhat = center * spread
    dnorm = half_ref[...].astype(jnp.float32) + far_ref[...].astype(jnp.float32)
    scaled = dnorm * gains_ref[1:2, :]
    inner = scaled - jnp.mean(scaled, axis=-1, keepdims=True)
    inner = inner - xhat * jnp.mean(scaled * xhat, axis=-1, keepdims=True)
    total = grad_ref[0].astype(jnp.float32) + inner * spread
    dhidden_ref[...] = total
    low_ref[...] = total.astype(jnp.bfloat16)


def mix_back_kernel(core_ref, own_ref, other_ref, w_ref, send_ref):
    cols = w_ref.shape[0]
    heads = cols // HD
    core = core_ref[0]
    for micro, low_ref in ((core, own_ref), (1 - core, other_ref)):
        total = mm(w_ref[...], low_ref[...], NT).astype(jnp.bfloat16)
        for head in range(heads):
            send_ref[micro * heads + head] = total[head * HD : (head + 1) * HD, :]


def mix_grad_kernel(core_ref, mixed_ref, own_ref, other_ref, far_ref, near_ref):
    core = core_ref[0]
    width = far_ref.shape[2]
    total = mm(mixed_ref[core], own_ref[...], NN) + mm(mixed_ref[1 - core], other_ref[...], NN)
    for place in range(4):
        near_ref[place] = total[:, place * width : (place + 1) * width]
        far_ref[place] = total[:, (4 + place) * width : (5 + place) * width].astype(jnp.bfloat16)


def project_back_kernel(core_ref, raw_ref, norm_ref, w_ref, far_ref, near_ref, send_ref, keep_ref):
    wide, width = far_ref.shape[1:]
    rows = raw_ref.shape[2]
    core = core_ref[0]
    total = mm(raw_ref[0], norm_ref[:rows, :], NN) + mm(raw_ref[1], norm_ref[rows:, :], NN)
    for place in range(4):
        near_ref[place] = total[:, place * width : (place + 1) * width]
        far_ref[place] = total[:, (4 + place) * width : (5 + place) * width].astype(jnp.bfloat16)
    send_ref[...] = mm(raw_ref[1 - core], w_ref[:wide, :], TN).astype(jnp.bfloat16)
    keep_ref[...] = mm(raw_ref[core], w_ref[:wide, :], TN)


def norm_one_back_kernel(
    core_ref, order_ref, x_ref, half_ref, far_ref, dhidden_ref, gains_ref, grad_ref, xhat_ref
):
    core = core_ref[0]
    width = x_ref.shape[2] // 8
    x = x_ref[core].astype(jnp.float32)
    mean = jnp.mean(x, axis=-1, keepdims=True)
    center = x - mean
    spread = lax.rsqrt(jnp.mean(center * center, axis=-1, keepdims=True) + EPS)
    for place in range(8):
        span = slice(place * width, (place + 1) * width)
        piece = x_ref[core, :, block_at(order_ref, place, width)].astype(jnp.float32)
        xhat_ref[:, span] = (piece - mean) * spread
    xhat = xhat_ref[...]
    dnorm = half_ref[...].astype(jnp.float32) + far_ref[...].astype(jnp.float32)
    scaled = dnorm * gains_ref[0:1, :]
    inner = scaled - jnp.mean(scaled, axis=-1, keepdims=True)
    inner = inner - xhat * jnp.mean(scaled * xhat, axis=-1, keepdims=True)
    total = (dhidden_ref[...] + inner * spread).astype(jnp.bfloat16)
    for place in range(8):
        grad_ref[:, block_at(order_ref, place, width)] = total[:, place * width : (place + 1) * width]


def place_grad_kernel(core_ref, order_ref, local_ref, four_ref, grad_ref, natural_ref):
    rows = grad_ref.shape[1]
    width = grad_ref.shape[2] // 8
    core = core_ref[0]
    for at in range(2):
        micro = core if at == 0 else 1 - core
        place = lax.broadcasted_iota(jnp.int32, (rows, rows), 0)
        onehot = jnp.where(local_ref[pl.ds(micro, 1), :] == place, 1.0, 0.0).astype(jnp.bfloat16)
        natural_ref[...] = mm(onehot, four_ref[micro], NN).astype(jnp.bfloat16)
        for block in range(8):
            span = slice(block * width, (block + 1) * width)
            grad_ref[at, :, span] = natural_ref[:, block_at(order_ref, block, width)]


def result_kernel(order_ref, picks_ref, hidden_ref, half_ref, far_ref, packed_ref, natural_ref):
    rows = hidden_ref.shape[0]
    width = hidden_ref.shape[1] // 8
    branch = half_ref[...].astype(jnp.float32) + far_ref[...].astype(jnp.float32)
    total = (hidden_ref[...] + branch).astype(jnp.bfloat16)
    for block in range(8):
        natural_ref[:, block_at(order_ref, block, width)] = total[:, block * width : (block + 1) * width]
    count = packed_ref.shape[0]
    place = lax.broadcasted_iota(jnp.int32, (rows, count), 0)
    onehot = jnp.where(picks_ref[...] == place, 1.0, 0.0).astype(jnp.bfloat16)
    packed_ref[...] = mm(onehot, natural_ref[...], TN).astype(jnp.bfloat16)


def join_kernel(
    core_ref, side_ref, place_ref, own_ref, far_ref, near_ref, cross_ref, input_own_ref, input_other_ref,
    output_ref, input_ref,
):
    rows = output_ref.shape[1]
    count = own_ref.shape[0]
    halfway = count // 8
    core, side = core_ref[0], side_ref[0]
    row = lax.broadcasted_iota(jnp.int32, (count, rows), 0)
    row = (row // halfway) * (2 * halfway) + row % halfway
    for micro, pieces in ((core, (own_ref, far_ref)), (1 - core, (near_ref, cross_ref))):
        total = jnp.zeros((rows, output_ref.shape[2]), jnp.float32)
        for half, piece in ((side, pieces[0]), (1 - side, pieces[1])):
            wanted = place_ref[pl.ds(micro, 1), :] - half * halfway
            onehot = jnp.where(row == wanted, 1.0, 0.0).astype(jnp.bfloat16)
            total = total + mm(onehot, piece[...], TN)
        output_ref[micro] = total.astype(jnp.bfloat16)
    input_ref[core] = input_own_ref[...]
    input_ref[1 - core] = input_other_ref[...]


def positions(anchor, seq_lens):
    ends = running_ends(seq_lens)
    starts = ends - seq_lens
    inside = (anchor[:, None] >= starts[None, :]) & (anchor[:, None] < ends[None, :])
    return anchor - jnp.sum(jnp.where(inside, starts[None, :], 0), axis=1)


def turn_tables(place):
    freqs = jnp.power(THETA, -jnp.arange(HD // 2, dtype=jnp.float32) * 2.0 / HD)
    angle = freqs[:, None] * place.astype(jnp.float32)[None, :]
    return jnp.concatenate([jnp.cos(angle), jnp.sin(angle)], axis=0)


def paired_layer(
    tokens, cotangent, perm, lengths, w_qkv, w_attn_out, w_in, w_down, gain_one, gain_two
):
    f32, bf16, i32 = jnp.float32, jnp.bfloat16, jnp.int32
    mine = lax.axis_index("fsdp")
    part = lax.axis_index("tp")
    core, side = part & 1, part >> 1
    core_at = core.reshape(1).astype(i32)
    side_at = side.reshape(1).astype(i32)
    rows = tokens.shape[1]
    width = w_qkv.shape[0]
    full = 8 * width
    cols = w_qkv.shape[2]
    heads = cols // HD
    units = w_in.shape[2]
    per_pair = rows // 8
    order = jnp.bitwise_xor(jnp.array(ORDER, i32), mine)

    def pick(value, index):
        return lax.dynamic_index_in_dim(value, index, 0, keepdims=False)

    def add_half(keep, got):
        return (keep + got.astype(f32)).astype(bf16)

    def near_sum(near, far, name):
        shape = near.shape[1:]
        lows = local_call(near_sum_kernel, name, (), (near, far), [(shape, bf16)] * 3, far_in=(0, 1))
        return near[0] + far[0].astype(f32), lows

    def z_send(lows):
        return [hop(low, ORDER[at + 1]) for at, low in enumerate(lows)]

    def far_sum(own, got):
        return own + sum(one.astype(f32) for one in got)

    turned = jnp.transpose(w_qkv.reshape(width, 3, heads, HD), (2, 1, 3, 0)).reshape(3 * cols, width)
    gains_rows = jnp.concatenate([gain_one[None], gain_two[None], jnp.zeros((14, width), bf16)])
    first_same = z_phase(jnp.concatenate([turned, gains_rows], axis=0))
    first = first_same + y_phase(first_same)

    slots = perm.reshape(2, 8, rows)
    from_me = (slots // rows == mine).astype(f32)
    slot_no = jnp.arange(rows, dtype=i32)
    before = (slot_no[:, None] < slot_no[None, :]).astype(f32)
    rank_me = jnp.einsum("mds,st->mdt", from_me, before).astype(i32)
    ranks = jnp.arange(per_pair, dtype=i32)
    chosen = (from_me[..., None] > 0) & (rank_me[..., None] == ranks)
    local = jnp.sum(jnp.where(chosen, (slots % rows)[..., None], 0), axis=2)
    my_slots = lax.dynamic_index_in_dim(slots, mine, 1, keepdims=False)
    target = my_slots // rows
    same = (target[:, :, None] == target[:, None, :]) & (slot_no[:, None] < slot_no[None, :])[None]
    rank_own = jnp.sum(same.astype(i32), axis=1)
    place_own = target * per_pair + rank_own
    quarter = per_pair // 4
    wanted = order[:, None] * per_pair + part * quarter
    wanted = (wanted + jnp.arange(quarter, dtype=i32)[None, :]).reshape(-1)
    packer = (place_own[:, None, :] == wanted[None, :, None]).astype(bf16)
    packed = jnp.einsum("mps,msd->mpd", packer, cotangent, preferred_element_type=f32).astype(bf16)
    packed = packed.reshape(2, 8, quarter, full)
    packed = [packed[:, at] for at in range(8)]
    chosen = order[:, None] == jnp.arange(8, dtype=i32)[None, :]
    local_own = jnp.sum(jnp.where(chosen[None, :, :, None], local[:, None], 0), axis=2)
    anchor = mine * rows + jnp.arange(rows, dtype=i32)
    own_table = jnp.concatenate([turn_tables(positions(anchor, lengths[m])) for m in range(2)], axis=1)
    inp_turned, gate_turned = jnp.transpose(w_in[:, 0]), jnp.transpose(w_in[:, 1])
    second = jnp.concatenate([jnp.transpose(w_down), jnp.transpose(w_attn_out)], axis=0)
    second_all = lax.all_gather(second, "fsdp", axis=0, tiled=False)
    third_all = lax.all_gather(jnp.concatenate([inp_turned, gate_turned], axis=0), "fsdp", axis=0, tiled=False)
    halfway = per_pair // 2
    picks = lax.dynamic_slice_in_dim(pick(local, core), side * halfway, halfway, 1).reshape(1, -1)
    my_lens = lengths[mine // heads]
    all_anchor = jnp.arange(8 * rows, dtype=i32)
    table = turn_tables(positions(all_anchor, my_lens))
    table = jnp.transpose(table.reshape(HD, 8, rows), (1, 0, 2))
    first, packed, own_table, picks, place_own, side_at, table, local_own, order, core_at, core, side, my_lens = sync(
        (first, packed, own_table, picks, place_own, side_at, table, local_own, order, core_at, core, side, my_lens)
    )

    norm_one, gains, outgoing, qkv_w = local_call(
        project_kernel, "project", (order,), (tokens, own_table),
        [((2 * rows, full), bf16), ((2, full), f32), ((2 * heads, 3 * HD, rows), bf16), ((3 * cols + 16, full), bf16)],
        [((2 * rows, full), bf16), ((3 * cols + 16, full), bf16)], first, copies=10,
        far_in=(0, 1), far_out=(1, 2), far_shards=False, raw_out=(0, 3),
    )
    outgoing, packed = sync((outgoing, packed))
    qkv = deal_out(outgoing)
    arrived = [hop(one, ORDER[at]) if at else one for at, one in enumerate(packed)]
    qkv = sync((qkv,))[0]
    mixed_out, exact, logs = local_call(
        attend_kernel, "attend", (my_lens,), (qkv,),
        [((8, HD, rows), bf16), ((8, HD, rows), f32), ((8, 1, rows), f32)],
        [((8 * rows, HD), bf16)], far_in=(0,), far_out=(0, 1, 2),
    )
    mixed_out, arrived = sync((mixed_out, arrived))
    mixed = deal_out(mixed_out).reshape(2, cols, rows)
    arrived = jnp.stack(arrived)
    near = twin(arrived)
    pair = jnp.stack([jnp.where(core == 0, arrived, near), jnp.where(core == 0, near, arrived)])
    far = across(pair)
    mixed, far = sync((mixed, far))
    four = jnp.concatenate([jnp.where(side == 0, pair, far), jnp.where(side == 0, far, pair)])
    four = jnp.transpose(four, (2, 1, 0, 3, 4)).reshape(2, rows, full)
    grad = local_call(
        place_grad_kernel, "place_grad", (core_at, order), (local_own.reshape(2, rows), four),
        [((2, rows, full), bf16)], [((rows, full), bf16)],
    )

    send, keep, out_w = local_call(
        mix_out_kernel, "mix_out", (core_at, order), (mixed,),
        [((rows, full), bf16), ((rows, full), f32), ((cols, full), bf16)], (), (second_all,), far_in=(0,), far_out=(2,),
    )
    half = add_half(keep, twin(send))
    far = across(half)
    far, grad = sync((far, grad))
    hidden, two_own = local_call(
        norm_two_kernel, "norm_two", (core_at, order), (tokens, half, far, gains),
        [((rows, full), f32), ((rows, full), bf16)], far_in=(0, 3), far_out=(0,),
    )
    two_other = twin(two_own)

    send, keep, act, d_inp, d_gate, result_send, result_keep = local_call(
        feed_kernel, "feed", (order,), (two_own, two_other),
        [((rows, full), bf16), ((rows, full), f32)]
        + [((2 * rows, units), bf16)] * 3
        + [((rows, full), bf16), ((rows, full), f32)],
        [((3 * units, full), bf16), ((2, rows, full), bf16)], (third_all, second_all, grad), copies=25, far_out=(5, 6),
    )
    half_two = add_half(keep, twin(send))
    half_two, act, d_inp, d_gate = sync((half_two, act, d_inp, d_gate))
    far_two = across(half_two)
    feed_grad = local_call(
        weight_grad_kernel, "feed_grad", (order,), (d_inp, d_gate, act, two_own, two_other, grad),
        [((8, 3 * units, width), bf16)], far_out=(0,),
    )
    feed_sum = lax.psum_scatter(feed_grad, "fsdp", scatter_dimension=0, tiled=False)
    far_two, feed_grad = sync((far_two, feed_grad))
    d_hidden, low_own = local_call(
        norm_two_back_kernel, "norm_two_back", (), (hidden, half_two, far_two, grad, gains),
        [((rows, full), f32), ((rows, full), bf16)], far_in=(0, 3, 4), far_out=(0,),
    )
    low_other = twin(low_own)
    d_mixed = local_call(
        mix_back_kernel, "mix_back", (core_at,), (low_own, low_other, out_w),
        [((8, HD, rows), bf16)], far_out=(0,),
    )
    d_mixed, low_own, low_other, result_send, result_keep = sync(
        (d_mixed, low_own, low_other, result_send, result_keep)
    )
    grad_mixed = deal_out(d_mixed)
    out_far, out_near = local_call(
        mix_grad_kernel, "mix_grad", (core_at,), (mixed, low_own, low_other),
        [((4, cols, width), bf16), ((4, cols, width), f32)], far_in=(0, 1, 2), far_out=(1,),
    )
    res_half = add_half(result_keep, twin(result_send))
    out_got = hop(out_far, 1)
    res_far = across(res_half)
    grad_mixed, out_got, res_far = sync((grad_mixed, out_got, res_far))

    d_raw_out = local_call(
        attend_back_kernel, "attend_back", (my_lens,), (qkv, exact, logs, grad_mixed, table),
        [((8, 3 * HD, rows), bf16)],
        [((8 * rows, 2 * HD), bf16), ((HD, 8 * rows), f32), ((HD, 8 * rows), f32)],
        far_in=(0, 1, 2, 3, 4), far_out=(0,),
    )
    d_raw_out, out_got, res_far = sync((d_raw_out, out_got, res_far))
    d_raw = deal_out(d_raw_out).reshape(2, 3 * cols, rows)
    out_own, out_lows = near_sum(out_near, out_got, "out_near")
    packed = local_call(
        result_kernel, "result", (order,), (picks, hidden, res_half, res_far),
        [((8 * halfway, full), bf16)], [((rows, full), bf16)], far_in=(1, 2, 3), far_out=(0,),
    )
    d_raw, out_lows, packed = sync((d_raw, out_lows, packed))

    qkv_far, qkv_near, send, keep = local_call(
        project_back_kernel, "project_back", (core_at,), (d_raw, norm_one, qkv_w),
        [((4, 3 * cols, width), bf16), ((4, 3 * cols, width), f32), ((rows, full), bf16), ((rows, full), f32)],
        far_in=(0, 1, 2), far_out=(1,),
    )
    qkv_got = hop(qkv_far, 1)
    half = add_half(keep, twin(send))
    far = across(half)
    out_got = z_send(out_lows)
    arrived = deal_out(packed.reshape(8, halfway, full))
    input_own = local_call(
        norm_one_back_kernel, "norm_one_back", (core_at, order), (tokens, half, far, d_hidden, gains),
        [((rows, full), bf16)], [((rows, full), f32)], far_in=(0, 3, 4),
    )
    qkv_got, input_own, out_got = sync((qkv_got, input_own, out_got))
    qkv_own, qkv_lows = near_sum(qkv_near, qkv_got, "qkv_near")
    qkv_lows = sync(qkv_lows)
    qkv_got = z_send(qkv_lows)
    qkv_got[0], arrived, input_own, feed_sum = sync((qkv_got[0], arrived, input_own, feed_sum))
    input_other = twin(input_own)
    grad_attn_out = jnp.transpose(far_sum(out_own, out_got))
    inp_sum, gate_sum, down_sum = [feed_sum[at * units : (at + 1) * units].astype(f32) for at in range(3)]
    two_row = jnp.sum(inp_sum * inp_turned.astype(f32) + gate_sum * gate_turned.astype(f32), axis=0)
    grad_in = jnp.stack([jnp.transpose(inp_sum), jnp.transpose(gate_sum)], axis=1)
    grad_down = jnp.transpose(down_sum)
    arrived = arrived.reshape(8 * halfway, full)
    other_side = across(arrived)
    output, input_grad = local_call(
        join_kernel, "join", (core_at, side_at),
        (place_own, arrived, other_side, twin(arrived), twin(other_side), input_own, input_other),
        [((2, rows, full), bf16), ((2, rows, full), bf16)],
    )
    qkv_got, output, input_grad, grad_attn_out, grad_in, grad_down, two_row = sync(
        (qkv_got, output, input_grad, grad_attn_out, grad_in, grad_down, two_row)
    )
    qkv_sum = far_sum(qkv_own, qkv_got)
    one_row = jnp.sum(qkv_sum * turned.astype(f32), axis=0)
    gain_rows = jnp.stack([one_row / gain_one.astype(f32), two_row / gain_two.astype(f32)])
    beyond = lax.ppermute(gain_rows, "tp", [(i, i ^ 3) for i in range(4)])
    gain_rows = (gain_rows + twin(gain_rows)) + (across(gain_rows) + beyond)
    grad_gain_one, grad_gain_two = gain_rows[0], gain_rows[1]
    return (
        output,
        input_grad,
        jnp.transpose(qkv_sum.reshape(heads, 3, HD, width), (3, 1, 0, 2)).reshape(width, 3, cols),
        grad_attn_out,
        grad_in,
        grad_down,
        grad_gain_one,
        grad_gain_two,
    )


def on_device(*operands):
    micro_count, tok_rows = operands[0].shape[0], operands[0].shape[1]
    groups, parts = lax.axis_size("fsdp"), lax.axis_size("tp")
    heads = operands[4].shape[2] // HD
    if groups == 8 and parts == 4 and micro_count == 2 and micro_count * heads == groups and tok_rows % 256 == 0:
        return paired_layer(*operands)
    return general_layer(*operands)


def solution(mesh):
    placed = (
        P(None, "fsdp", None),
        P(None, "fsdp", None),
        P(),
        P(),
        P("fsdp", None, "tp"),
        P("fsdp", "tp"),
        P("fsdp", None, "tp"),
        P("fsdp", "tp"),
        P("fsdp"),
        P("fsdp"),
    )
    return jax.shard_map(
        on_device,
        mesh=mesh,
        in_specs=placed,
        out_specs=(
            P(None, "fsdp", None),
            P(None, "fsdp", None),
            P("fsdp", None, "tp"),
            P("fsdp", "tp"),
            P("fsdp", None, "tp"),
            P("fsdp", "tp"),
            P("fsdp"),
            P("fsdp"),
        ),
        check_vma=False,
    )
```

```python
import math

import jax
import jax.numpy as jnp
from jax import lax
from jax.experimental import pallas as pl
from jax.experimental.pallas import tpu as pltpu
from jax.sharding import PartitionSpec as P

D = 1024
HD = 64


EPS = 1e-05
THETA = 160000.0
key_block = 2048


def layer_norm(values, gain):
    center = values - jnp.mean(values, axis=-1, keepdims=True)
    spread = jnp.mean(center * center, axis=-1, keepdims=True)
    return center * lax.rsqrt(spread + EPS) * gain


def rope_tables(position, width):
    freqs = jnp.power(THETA, -jnp.arange(width // 2, dtype=jnp.float32) * 2.0 / width)
    angle = position.astype(jnp.float32)[:, None] * freqs[None, :]
    angle = jnp.concatenate([angle, angle], axis=-1)
    return (jnp.cos(angle), jnp.sin(angle))


def rotate(values, cosine, sine):
    half = values.shape[-1] // 2
    turned = jnp.concatenate([-values[..., half:], values[..., :half]], axis=-1)
    return values * cosine[:, None, :] + turned * sine[:, None, :]


def running_ends(seq_lens):
    order = jnp.arange(seq_lens.shape[0], dtype=jnp.int32)
    return jnp.sum(jnp.where(order[None, :] <= order[:, None], seq_lens[None, :], 0), axis=1)


def seq_info(anchor, seq_lens):
    ends = running_ends(seq_lens)
    starts = ends - seq_lens
    segment = jnp.sum((anchor[:, None] >= ends[None, :]).astype(jnp.int32), axis=1)
    onehot = segment[:, None] == jnp.arange(seq_lens.shape[0], dtype=jnp.int32)[None, :]
    position = anchor - jnp.sum(jnp.where(onehot, starts[None, :], 0), axis=1)
    return (segment, position)


def blockwise(running, pieces, offset, step_fn):
    piece_len = pieces[0].shape[0]
    if piece_len > key_block and piece_len % key_block == 0:
        block_count = piece_len // key_block
        stacked = tuple((one.reshape((block_count, key_block) + one.shape[1:]) for one in pieces))

        def inner(state_now, scan_item):
            block_index, piece_parts = scan_item
            return (step_fn(state_now, piece_parts, offset + block_index * key_block), None)

        running, _ = lax.scan(inner, running, (jnp.arange(block_count, dtype=jnp.int32), stacked))
        return running
    return step_fn(running, pieces, offset)


def general_layer(
    tokens, cotangent, perm, lengths, w_qkv, w_attn_out, w_in, w_down, gain_one, gain_two
):
    groups = lax.axis_size("fsdp")
    my_index = lax.axis_index("fsdp")
    micro_count = tokens.shape[0]
    tok_rows = tokens.shape[1]
    total_rows = tok_rows * groups
    per_pair = tok_rows // groups
    head_cols = w_qkv.shape[2]
    head_count = head_cols // HD
    unit_cols = w_in.shape[2]
    score_scale = HD ** (-0.5)
    rows_idx = jnp.arange(tok_rows, dtype=jnp.int32)
    f32 = jnp.float32
    bf16 = jnp.bfloat16
    dims_rows = (((0,), (0,)), ((), ()))
    dims_cols = (((1,), (1,)), ((), ()))
    acc_qkv = jnp.zeros((D, 3, head_cols), f32)
    acc_out = jnp.zeros((D, head_cols), f32)
    acc_in = jnp.zeros((D, 2, unit_cols), f32)
    acc_down = jnp.zeros((D, unit_cols), f32)
    acc_gain_one = jnp.zeros((D,), f32)
    acc_gain_two = jnp.zeros((D,), f32)
    outputs = []
    input_grads = []
    for micro_idx in range(micro_count):
        perm_row = perm[micro_idx]
        seq_lens = lengths[micro_idx]
        inverse = (
            jnp.zeros((total_rows,), jnp.int32)
            .at[perm_row]
            .set(jnp.arange(total_rows, dtype=jnp.int32))
        )
        placed = lax.dynamic_slice_in_dim(inverse, my_index * tok_rows, tok_rows)
        send_order = jnp.argsort(placed)
        outgoing = tokens[micro_idx][send_order].reshape(groups, per_pair, D)
        arrived = lax.all_to_all(outgoing, "fsdp", split_axis=0, concat_axis=0, tiled=True).reshape(
            tok_rows, D
        )
        my_tokens = lax.dynamic_slice_in_dim(perm_row, my_index * tok_rows, tok_rows)
        source = my_tokens // tok_rows
        recv_order = jnp.argsort(source * tok_rows + rows_idx)
        recv_slot = jnp.zeros((tok_rows,), jnp.int32).at[recv_order].set(rows_idx)
        dealt = arrived[recv_slot]
        fetched = (
            lax.all_gather(gain_one, "fsdp", axis=0, tiled=True),
            lax.all_gather(gain_two, "fsdp", axis=0, tiled=True),
            lax.all_gather(w_qkv, "fsdp", axis=0, tiled=True),
            lax.all_gather(w_attn_out, "fsdp", axis=0, tiled=True),
            lax.all_gather(w_in, "fsdp", axis=0, tiled=True),
            lax.all_gather(w_down, "fsdp", axis=0, tiled=True),
        )
        gain_first = fetched[0].astype(f32)
        gain_second = fetched[1].astype(f32)
        query_seg, query_pos = seq_info(my_tokens, seq_lens)
        cosine, sine = rope_tables(query_pos, HD)
        x_float = dealt.astype(f32)
        normed_low = layer_norm(x_float, gain_first).astype(bf16)
        raw_proj = jnp.einsum("td,dcf->tcf", normed_low, fetched[2], preferred_element_type=f32)
        raw_heads = raw_proj.reshape(tok_rows, 3, head_count, HD)
        query_low = rotate(raw_heads[:, 0], cosine, sine).astype(bf16)
        key_low = rotate(raw_heads[:, 1], cosine, sine).astype(bf16)
        value_low = raw_heads[:, 2].astype(bf16)

        def forward_step(running, piece_parts, offset):
            run_peak, run_total, run_acc = running
            key_part, value_part = piece_parts
            key_seg, _ = seq_info(
                lax.dynamic_slice_in_dim(perm_row, offset, key_part.shape[0]), seq_lens
            )
            scores = (
                jnp.einsum("qhe,khe->hqk", query_low, key_part, preferred_element_type=f32)
                * score_scale
            )
            same_seq = (query_seg[:, None] == key_seg[None, :])[None]
            block_top = jnp.max(jnp.where(same_seq, scores, -1e30), axis=-1)
            new_peak = jnp.maximum(run_peak, block_top)
            weights = jnp.where(same_seq, jnp.exp(scores - new_peak[..., None]), 0.0)
            fade_factor = jnp.exp(run_peak - new_peak)
            run_acc = run_acc * jnp.transpose(fade_factor)[:, :, None] + jnp.einsum(
                "hqk,khe->qhe", weights.astype(bf16), value_part, preferred_element_type=f32
            )
            run_total = run_total * fade_factor + jnp.sum(weights, axis=-1)
            return (new_peak, run_total, run_acc)

        start_state = (
            jnp.full((head_count, tok_rows), -1e30, f32),
            jnp.zeros((head_count, tok_rows), f32),
            jnp.zeros((tok_rows, head_count, HD), f32),
        )
        run_peak, run_total, run_acc = blockwise(
            start_state,
            (
                lax.all_gather(key_low, "fsdp", axis=0, tiled=True),
                lax.all_gather(value_low, "fsdp", axis=0, tiled=True),
            ),
            jnp.int32(0),
            forward_step,
        )
        log_total = run_peak + jnp.log(run_total)
        mixed_heads = run_acc / jnp.transpose(run_total)[:, :, None]
        mixed_low = mixed_heads.reshape(tok_rows, head_cols).astype(bf16)
        attn_part = lax.dot_general(mixed_low, fetched[3], dims_cols, preferred_element_type=f32)
        branch = lax.psum(attn_part.astype(jnp.bfloat16), "tp").astype(jnp.float32)
        hidden = x_float + branch
        normed_two = layer_norm(hidden, gain_second).astype(bf16)
        ffn_proj = jnp.einsum("td,dcf->tcf", normed_two, fetched[4], preferred_element_type=f32)
        act_low = (jax.nn.gelu(ffn_proj[:, 0], approximate=False) * ffn_proj[:, 1]).astype(bf16)
        ffn_part = lax.dot_general(act_low, fetched[5], dims_cols, preferred_element_type=f32)
        branch_two = lax.psum(ffn_part.astype(jnp.bfloat16), "tp").astype(jnp.float32)
        outputs.append((hidden + branch_two).astype(bf16))
        again = (
            lax.all_gather(gain_one, "fsdp", axis=0, tiled=True),
            lax.all_gather(gain_two, "fsdp", axis=0, tiled=True),
            lax.all_gather(w_qkv, "fsdp", axis=0, tiled=True),
            lax.all_gather(w_attn_out, "fsdp", axis=0, tiled=True),
            lax.all_gather(w_in, "fsdp", axis=0, tiled=True),
            lax.all_gather(w_down, "fsdp", axis=0, tiled=True),
        )
        gain_first = again[0].astype(f32)
        gain_second = again[1].astype(f32)
        grad_low = cotangent[micro_idx]
        grad_float = grad_low.astype(f32)
        acc_down = acc_down + lax.dot_general(
            grad_low, act_low, dims_rows, preferred_element_type=f32
        )
        d_act = jnp.dot(grad_low, again[5], preferred_element_type=f32)
        _, gelu_pull = jax.vjp(
            lambda inputs, gates: jax.nn.gelu(inputs, approximate=False) * gates,
            ffn_proj[:, 0],
            ffn_proj[:, 1],
        )
        d_inputs, d_gates = gelu_pull(d_act)
        d_proj = jnp.stack([d_inputs, d_gates], axis=1).astype(bf16)
        acc_in = acc_in + jnp.einsum("td,tcf->dcf", normed_two, d_proj, preferred_element_type=f32)
        norm_part = jnp.einsum("tcf,dcf->td", d_proj, again[4], preferred_element_type=f32)
        d_norm_two = lax.psum(norm_part.astype(jnp.bfloat16), "tp").astype(jnp.float32)
        _, second_pull = jax.vjp(layer_norm, hidden, gain_second)
        d_hid_norm, d_gain_two = second_pull(d_norm_two)
        acc_gain_two = acc_gain_two + d_gain_two
        d_hidden = grad_float + d_hid_norm
        hidden_low = d_hidden.astype(bf16)
        acc_out = acc_out + lax.dot_general(
            hidden_low, mixed_low, dims_rows, preferred_element_type=f32
        )
        d_mixed = jnp.dot(hidden_low, again[3], preferred_element_type=f32).astype(bf16)
        d_mixed = d_mixed.reshape(tok_rows, head_count, HD)
        delta_rows = jnp.sum(d_mixed.astype(f32) * mixed_heads, axis=-1)
        delta_heads = jnp.transpose(delta_rows)

        def query_step(grad_query, piece_parts, offset):
            key_part, value_part = piece_parts
            key_seg, _ = seq_info(
                lax.dynamic_slice_in_dim(perm_row, offset, key_part.shape[0]), seq_lens
            )
            scores = (
                jnp.einsum("qhe,khe->hqk", query_low, key_part, preferred_element_type=f32)
                * score_scale
            )
            same_seq = (query_seg[:, None] == key_seg[None, :])[None]
            weights = jnp.where(same_seq, jnp.exp(scores - log_total[..., None]), 0.0)
            d_weights = jnp.einsum("qhe,khe->hqk", d_mixed, value_part, preferred_element_type=f32)
            d_scores = (weights * (d_weights - delta_heads[..., None])).astype(bf16)
            return grad_query + score_scale * jnp.einsum(
                "hqk,khe->qhe", d_scores, key_part, preferred_element_type=f32
            )

        query_start = jnp.zeros((tok_rows, head_count, HD), f32)
        grad_query = blockwise(
            query_start,
            (
                lax.all_gather(key_low, "fsdp", axis=0, tiled=True),
                lax.all_gather(value_low, "fsdp", axis=0, tiled=True),
            ),
            jnp.int32(0),
            query_step,
        )
        stat_total, stat_delta = (
            lax.all_gather(jnp.transpose(log_total), "fsdp", axis=0, tiled=True),
            lax.all_gather(delta_rows, "fsdp", axis=0, tiled=True),
        )

        def key_step(running, piece_parts, offset):
            grad_key, grad_value = running
            query_part, dmix_part = piece_parts
            piece_len = query_part.shape[0]
            piece_seg, _ = seq_info(lax.dynamic_slice_in_dim(perm_row, offset, piece_len), seq_lens)
            total_part = jnp.transpose(lax.dynamic_slice_in_dim(stat_total, offset, piece_len))
            delta_part = jnp.transpose(lax.dynamic_slice_in_dim(stat_delta, offset, piece_len))
            scores = (
                jnp.einsum("qhe,khe->hqk", query_part, key_low, preferred_element_type=f32)
                * score_scale
            )
            same_seq = (piece_seg[:, None] == query_seg[None, :])[None]
            weights = jnp.where(same_seq, jnp.exp(scores - total_part[..., None]), 0.0)
            d_weights = jnp.einsum("qhe,khe->hqk", dmix_part, value_low, preferred_element_type=f32)
            d_scores = (weights * (d_weights - delta_part[..., None])).astype(bf16)
            grad_key = grad_key + score_scale * jnp.einsum(
                "hqk,qhe->khe", d_scores, query_part, preferred_element_type=f32
            )
            grad_value = grad_value + jnp.einsum(
                "hqk,qhe->khe", weights.astype(bf16), dmix_part, preferred_element_type=f32
            )
            return (grad_key, grad_value)

        grad_key, grad_value = blockwise(
            (
                jnp.zeros((tok_rows, head_count, HD), f32),
                jnp.zeros((tok_rows, head_count, HD), f32),
            ),
            (
                lax.all_gather(query_low, "fsdp", axis=0, tiled=True),
                lax.all_gather(d_mixed, "fsdp", axis=0, tiled=True),
            ),
            jnp.int32(0),
            key_step,
        )
        _, rope_pull = jax.vjp(lambda heads_in: rotate(heads_in, cosine, sine), raw_heads[:, 0])
        d_raw_query = rope_pull(grad_query)[0]
        d_raw_key = rope_pull(grad_key)[0]
        d_raw = (
            jnp.stack([d_raw_query, d_raw_key, grad_value], axis=1)
            .reshape(tok_rows, 3, head_cols)
            .astype(bf16)
        )
        acc_qkv = acc_qkv + jnp.einsum("td,tcf->dcf", normed_low, d_raw, preferred_element_type=f32)
        first_part = jnp.einsum("tcf,dcf->td", d_raw, again[2], preferred_element_type=f32)
        d_norm_one = lax.psum(first_part.astype(jnp.bfloat16), "tp").astype(jnp.float32)
        _, first_pull = jax.vjp(layer_norm, x_float, gain_first)
        d_x_norm, d_gain_one = first_pull(d_norm_one)
        acc_gain_one = acc_gain_one + d_gain_one
        d_input = (d_hidden + d_x_norm).astype(bf16)
        back_rows = d_input[recv_order].reshape(groups, per_pair, D)
        returned = lax.all_to_all(
            back_rows, "fsdp", split_axis=0, concat_axis=0, tiled=True
        ).reshape(tok_rows, D)
        send_slot = jnp.zeros((tok_rows,), jnp.int32).at[send_order].set(rows_idx)
        input_grads.append(returned[send_slot])
    summed = (
        lax.psum_scatter(acc_qkv, "fsdp", scatter_dimension=0, tiled=True),
        lax.psum_scatter(acc_out, "fsdp", scatter_dimension=0, tiled=True),
        lax.psum_scatter(acc_in, "fsdp", scatter_dimension=0, tiled=True),
        lax.psum_scatter(acc_down, "fsdp", scatter_dimension=0, tiled=True),
        lax.psum_scatter(acc_gain_one, "fsdp", scatter_dimension=0, tiled=True),
        lax.psum_scatter(acc_gain_two, "fsdp", scatter_dimension=0, tiled=True),
    )
    return (
        jnp.stack(outputs),
        jnp.stack(input_grads),
        summed[0],
        summed[1],
        summed[2],
        summed[3],
        summed[4],
        summed[5],
    )


JOIN = 2
COSTS = {"attend": 10, "attend_back": 28, "feed": 8, "norm_one_back": 0, "qkv_near": 0, "feed_grad": 5}
FAR = -1e30
ORDER = (0, 2, 4, 6, 1, 3, 5, 7)
NT = (((1,), (1,)), ((), ()))
TN = (((0,), (0,)), ((), ()))
NN = (((1,), (0,)), ((), ()))
ROOM = 10 * 1024 * 1024


def partial(kernel, *given):
    return lambda *refs: kernel(*given, *refs)


def mm(left, right, dims):
    return lax.dot_general(left, right, dims, preferred_element_type=jnp.float32)


def hop(value, step):
    return lax.ppermute(value, "fsdp", [(i, i ^ step) for i in range(8)])


def twin(value):
    return lax.ppermute(value, "tp", [(i, i ^ 1) for i in range(4)])


def across(value):
    return lax.ppermute(value, "tp", [(i, i ^ 2) for i in range(4)])


def deal_out(value):
    return lax.all_to_all(value, "fsdp", 0, 0, tiled=True)


def after(value, *earlier):
    return lax.optimization_barrier((value,) + earlier)[0]


def sync(values):
    return lax.optimization_barrier(values)


def z_phase(shard):
    return [shard] + [hop(shard, step) for step in ORDER[1:4]]


def y_phase(shards):
    return [hop(one, 1) for one in shards]


def local_call(kernel, name, scalars, arrays, outs, scratch=(), shards=(), copies=8, far_in=(), far_out=(), far_shards=True, raw_out=()):
    shapes = [(one.shape, one.dtype) for one in arrays]
    staged = [shapes[at] for at in far_in] + [outs[at] for at in far_out]
    sems = [pltpu.SemaphoreType.DMA((copies,))] if shards else []
    room = ROOM + sum(math.prod(shape) * jnp.dtype(kind).itemsize for shape, kind in [*shapes, *outs, *scratch])
    counts = (len(scalars), len(arrays), len(shards), len(outs), len(scratch) + len(sems))

    def body(*refs):
        groups = []
        for count in counts:
            groups.append(list(refs[:count]))
            refs = refs[count:]
        given, ins, pieces, results, extra = groups
        if not staged:
            return kernel(*given, *ins, *pieces, *results, *extra)
        stage, sem = refs[:-1], refs[-1]
        incoming, outgoing = [], []
        for slot, at in enumerate(far_in):
            incoming.append(pltpu.make_async_copy(ins[at], stage[slot], sem.at[slot]))
            incoming[-1].start()
            ins[at] = stage[slot]
        for slot, at in enumerate(far_out, len(far_in)):
            outgoing.append(pltpu.make_async_copy(stage[slot], results[at], sem.at[slot]))
            results[at] = stage[slot]
        for copy in incoming:
            copy.wait()
        kernel(*given, *ins, *pieces, *results, *extra)
        for copy in outgoing:
            copy.start()
        for copy in outgoing:
            copy.wait()

    arrays = [pltpu.with_memory_space_constraint(one, pltpu.HBM) if at in far_in else one for at, one in enumerate(arrays)]
    shards = [pltpu.with_memory_space_constraint(one, pltpu.HBM) if far_shards else one for one in shards]

    def space(at, far):
        return pl.BlockSpec(memory_space=pltpu.HBM if at in far else pltpu.VMEM)

    result = pl.pallas_call(
        body,
        in_specs=[pl.BlockSpec(memory_space=pltpu.SMEM)] * len(scalars)
        + [space(at, far_in) for at in range(len(arrays))]
        + [pl.BlockSpec(memory_space=pltpu.HBM if far_shards else pl.ANY)] * len(shards),
        out_specs=[space(at, (*far_out, *raw_out)) for at in range(len(outs))],
        out_shape=[
            pltpu.HBM(shape, kind) if at in (*far_out, *raw_out) else jax.ShapeDtypeStruct(shape, kind)
            for at, (shape, kind) in enumerate(outs)
        ],
        scratch_shapes=[pltpu.VMEM(shape, kind) for shape, kind in scratch]
        + sems
        + [pltpu.VMEM(shape, kind) for shape, kind in staged]
        + ([pltpu.SemaphoreType.DMA((len(staged),))] if staged else []),
        compiler_params=pltpu.CompilerParams(vmem_limit_bytes=room),
        cost_estimate=pl.CostEstimate(flops=COSTS.get(name, 3) * 10**9, transcendentals=0, bytes_accessed=8 * 1024 * 1024),
        name=name,
    )(*scalars, *arrays, *shards)
    return result if len(outs) > 1 else result[0]


def block_at(order_ref, place, width):
    return pl.ds(pl.multiple_of(order_ref[place] * width, width), width)


def shard_copies(shards, low, high, into_ref, sem_ref, base=0):
    width = shards[0].shape[1]
    copies = []
    for place, shard in enumerate(shards):
        span = pl.ds(place * width, width)
        source = shard.at[pl.ds(low, high - low), :]
        copies.append(pltpu.make_async_copy(source, into_ref.at[:, span], sem_ref.at[base + place]))
        copies[-1].start()
    return copies


def gathered_copies(order_ref, source, low, high, into_ref, sem_ref, base=0):
    width = source.shape[2]
    copies = []
    for place in range(8):
        copies.append(
            pltpu.make_async_copy(
                source.at[order_ref[place], pl.ds(low, high - low), :],
                into_ref.at[:, pl.ds(place * width, width)],
                sem_ref.at[base + place],
            )
        )
        copies[-1].start()
    return copies


def finish(copies):
    for copy in copies:
        copy.wait()


def project_kernel(order_ref, x_ref, table_ref, *refs):
    shards = refs[:8]
    norm_out_ref, gains_ref, send_ref, w_out_ref, norm_ref, w_ref, sem_ref = refs[8:]
    width = shards[0].shape[1]
    rows = x_ref.shape[1]
    wide = w_ref.shape[0] - 16
    heads = wide // (3 * HD)
    half = HD // 2
    finish(shard_copies(shards, 0, wide + 16, w_ref, sem_ref))
    outgoing = [pltpu.make_async_copy(w_ref, w_out_ref, sem_ref.at[8]), pltpu.make_async_copy(norm_ref, norm_out_ref, sem_ref.at[9])]
    outgoing[0].start()
    gains_ref[...] = w_ref[wide:, :].astype(jnp.float32)[:2]
    for micro in range(2):
        x = x_ref[micro].astype(jnp.float32)
        mean = jnp.mean(x, axis=-1, keepdims=True)
        center = x - mean
        spread = lax.rsqrt(jnp.mean(center * center, axis=-1, keepdims=True) + EPS)
        for place in range(8):
            piece = x_ref[micro, :, block_at(order_ref, place, width)].astype(jnp.float32)
            span = slice(place * width, (place + 1) * width)
            value = (piece - mean) * spread * gains_ref[0:1, span]
            norm_ref[micro * rows : (micro + 1) * rows, span] = value.astype(jnp.bfloat16)
    outgoing[1].start()
    raw = mm(w_ref[:wide, :], norm_ref[...], NT)
    cosine, sine = table_ref[:half, :], table_ref[half:, :]
    for head in range(heads):
        base = head * 3 * HD
        for kind in range(2):
            upper = raw[base + kind * HD : base + kind * HD + half]
            lower = raw[base + kind * HD + half : base + (kind + 1) * HD]
            first = (upper * cosine - lower * sine).astype(jnp.bfloat16)
            second = (lower * cosine + upper * sine).astype(jnp.bfloat16)
            for micro in range(2):
                span = slice(micro * rows, (micro + 1) * rows)
                send_ref[micro * heads + head, kind * HD : kind * HD + half, :] = first[:, span]
                send_ref[micro * heads + head, kind * HD + half : (kind + 1) * HD, :] = second[:, span]
        value = raw[base + 2 * HD : base + 3 * HD].astype(jnp.bfloat16)
        for micro in range(2):
            send_ref[micro * heads + head, 2 * HD :, :] = value[:, micro * rows : (micro + 1) * rows]
    finish(outgoing)


def key_range(lens_ref, low, high):
    first = jnp.int32(0)
    last = jnp.int32(0)
    total = jnp.int32(0)
    for index in range(lens_ref.shape[0]):
        start = total
        total = total + lens_ref[index]
        first = jnp.where((start <= low) & (low < total), start, first)
        last = jnp.where((start <= high) & (high < total), total, last)
    return first, last


def query_bounds(lens_ref, base, width):
    place = base + lax.broadcasted_iota(jnp.int32, (1, width), 1)
    first = jnp.zeros((1, width), jnp.int32)
    last = jnp.zeros((1, width), jnp.int32)
    total = jnp.int32(0)
    for index in range(lens_ref.shape[0]):
        start = total
        total = total + lens_ref[index]
        inside = (place >= start) & (place < total)
        first = jnp.where(inside, start, first)
        last = jnp.where(inside, total, last)
    return first, last


def lanes(ref, index, count, rows):
    return jnp.concatenate([ref[index * count + at, rows, :] for at in range(count)], axis=1)


def attend_kernel(lens_ref, qkv_ref, mixed_ref, exact_ref, log_ref, key_ref):
    blocks, _, small = qkv_ref.shape
    wide = JOIN * small
    for at in range(blocks):
        block = qkv_ref[at, HD : 2 * HD, :].astype(jnp.float32)
        key_ref[at * small : (at + 1) * small, :] = jnp.transpose(block).astype(jnp.bfloat16)

    def one_query(index, carry):
        base = index * wide
        first, last = key_range(lens_ref, base, base + wide - 1)
        low, high = query_bounds(lens_ref, base, wide)
        query = lanes(qkv_ref, index, JOIN, slice(0, HD)) * jnp.bfloat16(HD**-0.5)

        def one_key(at, state):
            peak, total, acc = state
            start = pl.multiple_of(at * wide, wide)
            scores = mm(key_ref[pl.ds(start, wide), :], query, NN)
            place = start + lax.broadcasted_iota(jnp.int32, (wide, wide), 0)
            scores = jnp.where((place >= low) & (place < high), scores, FAR)
            top = jnp.maximum(peak, jnp.max(scores, axis=0, keepdims=True))
            weights = jnp.exp(scores - top)
            fade = jnp.exp(peak - top)
            total = total * fade + jnp.sum(weights, axis=0, keepdims=True)
            value = lanes(qkv_ref, at, JOIN, slice(2 * HD, 3 * HD))
            acc = acc * fade + mm(value, weights.astype(jnp.bfloat16), NN)
            return top, total, acc

        peak, total, acc = lax.fori_loop(
            first // wide,
            (last + wide - 1) // wide,
            one_key,
            (
                jnp.full((1, wide), FAR, jnp.float32),
                jnp.zeros((1, wide), jnp.float32),
                jnp.zeros((HD, wide), jnp.float32),
            ),
        )
        result = acc / total
        logs = peak + jnp.log(total)
        for at in range(JOIN):
            span = slice(at * small, (at + 1) * small)
            mixed_ref[index * JOIN + at] = result[:, span].astype(jnp.bfloat16)
            exact_ref[index * JOIN + at] = result[:, span]
            log_ref[index * JOIN + at] = logs[:, span]
        return carry

    lax.fori_loop(0, blocks // JOIN, one_query, 0)


def attend_back_kernel(
    lens_ref, qkv_in_ref, exact_in_ref, log_in_ref, grad_in_ref, table_in_ref, raw_out_ref,
    qkv_ref, exact_ref, log_ref, grad_ref, table_ref, raw_ref, pair_ref, dkey_ref, dvalue_ref, sem_ref
):
    pairs = (
        (qkv_in_ref, qkv_ref), (exact_in_ref, exact_ref), (log_in_ref, log_ref), (grad_in_ref, grad_ref),
        (table_in_ref, table_ref), (raw_ref, raw_out_ref),
    )
    copies = [pltpu.make_async_copy(one, two, sem_ref.at[at]) for at, (one, two) in enumerate(pairs)]
    for copy in copies[:5]:
        copy.start()
    copies[0].wait()
    blocks, _, small = qkv_ref.shape
    wide = JOIN * small
    half = HD // 2
    for at in range(blocks):
        block = qkv_ref[at, HD : 3 * HD, :].astype(jnp.float32)
        pair_ref[at * small : (at + 1) * small, :] = jnp.transpose(block).astype(jnp.bfloat16)
    dkey_ref[...] = jnp.zeros(dkey_ref.shape, jnp.float32)
    dvalue_ref[...] = jnp.zeros(dvalue_ref.shape, jnp.float32)
    finish(copies[1:5])

    def unturn(index, grad):
        cosine = table_ref[index, :half, :]
        sine = table_ref[index, half:, :]
        upper, lower = grad[:half], grad[half:]
        return upper * cosine + lower * sine, lower * cosine - upper * sine

    def one_query(index, carry):
        base = index * wide
        first, last = key_range(lens_ref, base, base + wide - 1)
        low, high = query_bounds(lens_ref, base, wide)
        query = lanes(qkv_ref, index, JOIN, slice(0, HD)) * jnp.bfloat16(HD**-0.5)
        grad = lanes(grad_ref, index, JOIN, slice(0, HD))
        logs = lanes(log_ref, index, JOIN, slice(0, 1))
        exact = lanes(exact_ref, index, JOIN, slice(0, HD))
        delta = jnp.sum(grad.astype(jnp.float32) * exact, axis=0, keepdims=True)

        def one_key(at, dquery):
            start = pl.multiple_of(at * wide, wide)
            span = pl.ds(start, wide)
            scores = mm(pair_ref[span, :HD], query, NN)
            dweights = mm(pair_ref[span, HD:], grad, NN)
            place = start + lax.broadcasted_iota(jnp.int32, (wide, wide), 0)
            weights = jnp.where((place >= low) & (place < high), jnp.exp(scores - logs), 0.0)
            dscores = (weights * (dweights - delta)).astype(jnp.bfloat16)
            dkey_ref[:, span] += mm(query, dscores, NT)
            dvalue_ref[:, span] += mm(grad, weights.astype(jnp.bfloat16), NT)
            return dquery + mm(lanes(qkv_ref, at, JOIN, slice(HD, 2 * HD)), dscores, NN)

        dquery = lax.fori_loop(
            first // wide,
            (last + wide - 1) // wide,
            one_key,
            jnp.zeros((HD, wide), jnp.float32),
        ) * (HD**-0.5)
        for at in range(JOIN):
            upper, lower = unturn(index * JOIN + at, dquery[:, at * small : (at + 1) * small])
            raw_ref[index * JOIN + at, :half, :] = upper.astype(jnp.bfloat16)
            raw_ref[index * JOIN + at, half:HD, :] = lower.astype(jnp.bfloat16)
        return carry

    lax.fori_loop(0, blocks // JOIN, one_query, 0)
    for at in range(blocks):
        span = slice(at * small, (at + 1) * small)
        upper, lower = unturn(at, dkey_ref[:, span])
        raw_ref[at, HD : HD + half, :] = upper.astype(jnp.bfloat16)
        raw_ref[at, HD + half : 2 * HD, :] = lower.astype(jnp.bfloat16)
        raw_ref[at, 2 * HD :, :] = dvalue_ref[:, span].astype(jnp.bfloat16)
    copies[5].start()
    copies[5].wait()


def mix_out_kernel(core_ref, order_ref, mixed_ref, all_ref, send_ref, keep_ref, w_ref, sem_ref):
    last = all_ref.shape[1]
    finish(gathered_copies(order_ref, all_ref, last - mixed_ref.shape[1], last, w_ref, sem_ref))
    core = core_ref[0]
    send_ref[...] = mm(mixed_ref[1 - core], w_ref[...], TN).astype(jnp.bfloat16)
    keep_ref[...] = mm(mixed_ref[core], w_ref[...], TN)


def norm_two_kernel(core_ref, order_ref, x_ref, half_ref, far_ref, gains_ref, hidden_ref, norm_ref):
    core = core_ref[0]
    width = x_ref.shape[2] // 8
    for place in range(8):
        span = slice(place * width, (place + 1) * width)
        piece = x_ref[core, :, block_at(order_ref, place, width)].astype(jnp.float32)
        branch = half_ref[:, span].astype(jnp.float32) + far_ref[:, span].astype(jnp.float32)
        hidden_ref[:, span] = piece + branch
    hidden = hidden_ref[...]
    center = hidden - jnp.mean(hidden, axis=-1, keepdims=True)
    spread = lax.rsqrt(jnp.mean(center * center, axis=-1, keepdims=True) + EPS)
    norm_ref[...] = (center * spread * gains_ref[1:2, :]).astype(jnp.bfloat16)


def feed_kernel(
    order_ref, own_ref, other_ref, all_ref, down_ref, source_ref,
    send_ref, keep_ref, act_ref, dinp_ref, dgate_ref, result_send_out, result_keep_out, w_ref, grad_ref,
    result_send_ref, result_keep_ref, sem_ref
):
    units = w_ref.shape[0] // 3
    inp_w, gate_w, down_w = [w_ref.at[pl.ds(at * units, units), :] for at in range(3)]
    rows = own_ref.shape[0]
    inp_copies = gathered_copies(order_ref, all_ref, 0, units, inp_w, sem_ref)
    grad_copy = pltpu.make_async_copy(source_ref, grad_ref, sem_ref.at[24])
    grad_copy.start()
    gate_copies = gathered_copies(order_ref, all_ref, units, 2 * units, gate_w, sem_ref, 16)
    down_copies = gathered_copies(order_ref, down_ref, 0, units, down_w, sem_ref, 8)
    finish(inp_copies)
    for micro, norm_ref in ((1, other_ref), (0, own_ref)):
        span = slice(micro * rows, (micro + 1) * rows)
        inp = mm(norm_ref[...], inp_w[...], NT)
        if micro:
            finish(gate_copies)
        gate = mm(norm_ref[...], gate_w[...], NT)
        if micro:
            finish(down_copies + [grad_copy])
        dact = mm(grad_ref[micro], down_w[...], NT)
        cdf = 0.5 * (1.0 + lax.erf(inp * (0.5**0.5)))
        density = jnp.exp(-0.5 * inp * inp) * ((0.5 / jnp.pi) ** 0.5)
        gelu = inp * cdf
        act = (gelu * gate).astype(jnp.bfloat16)
        act_ref[span, :] = act
        dinp = (dact * gate * (cdf + inp * density)).astype(jnp.bfloat16)
        dgate = (dact * gelu).astype(jnp.bfloat16)
        dinp_ref[span, :] = dinp
        dgate_ref[span, :] = dgate
        result = mm(act, down_w[...], NN)
        if micro:
            result_send_ref[...] = result.astype(jnp.bfloat16)
            outgoing = [pltpu.make_async_copy(result_send_ref, result_send_out, sem_ref.at[25])]
        else:
            result_keep_ref[...] = result
            outgoing.append(pltpu.make_async_copy(result_keep_ref, result_keep_out, sem_ref.at[26]))
        outgoing[-1].start()
        part = mm(dinp, inp_w[...], NN) + mm(dgate, gate_w[...], NN)
        if micro:
            send_ref[...] = part.astype(jnp.bfloat16)
        else:
            keep_ref[...] = part
    finish(outgoing)


def weight_grad_kernel(
    order_ref, dinp_ref, dgate_ref, act_ref, own_ref, other_ref, source_ref, result_ref, grad_ref, out_ref, sem_ref
):
    units = act_ref.shape[1]
    rows = own_ref.shape[0]
    width = out_ref.shape[2]
    grad_copy = pltpu.make_async_copy(source_ref, grad_ref, sem_ref.at[3])
    grad_copy.start()
    copies = []
    for at, (left_ref, rights) in enumerate((
        (dinp_ref, (own_ref, other_ref)),
        (dgate_ref, (own_ref, other_ref)),
        (act_ref, (grad_ref.at[0], grad_ref.at[1])),
    )):
        if at == 2:
            grad_copy.wait()
        total = mm(left_ref[:rows, :], rights[0][...], TN) + mm(left_ref[rows:, :], rights[1][...], TN)
        for place in range(8):
            piece = total[:, place * width : (place + 1) * width].astype(jnp.bfloat16)
            out_ref[order_ref[place], at * units : (at + 1) * units, :] = piece
        span = pl.ds(at * units, units)
        copies.append(pltpu.make_async_copy(out_ref.at[:, span, :], result_ref.at[:, span, :], sem_ref.at[at]))
        copies[-1].start()
    finish(copies)


def near_sum_kernel(near_ref, far_ref, *low_refs):
    for at, low_ref in enumerate(low_refs):
        low_ref[...] = (near_ref[at + 1] + far_ref[at + 1].astype(jnp.float32)).astype(jnp.bfloat16)


def norm_two_back_kernel(hidden_ref, half_ref, far_ref, grad_ref, gains_ref, dhidden_ref, low_ref):
    hidden = hidden_ref[...]
    center = hidden - jnp.mean(hidden, axis=-1, keepdims=True)
    spread = lax.rsqrt(jnp.mean(center * center, axis=-1, keepdims=True) + EPS)
    xhat = center * spread
    dnorm = half_ref[...].astype(jnp.float32) + far_ref[...].astype(jnp.float32)
    scaled = dnorm * gains_ref[1:2, :]
    inner = scaled - jnp.mean(scaled, axis=-1, keepdims=True)
    inner = inner - xhat * jnp.mean(scaled * xhat, axis=-1, keepdims=True)
    total = grad_ref[0].astype(jnp.float32) + inner * spread
    dhidden_ref[...] = total
    low_ref[...] = total.astype(jnp.bfloat16)


def mix_back_kernel(core_ref, own_ref, other_ref, w_ref, send_ref):
    cols = w_ref.shape[0]
    heads = cols // HD
    core = core_ref[0]
    for micro, low_ref in ((core, own_ref), (1 - core, other_ref)):
        total = mm(w_ref[...], low_ref[...], NT).astype(jnp.bfloat16)
        for head in range(heads):
            send_ref[micro * heads + head] = total[head * HD : (head + 1) * HD, :]


def mix_grad_kernel(core_ref, mixed_ref, own_ref, other_ref, far_ref, near_ref):
    core = core_ref[0]
    width = far_ref.shape[2]
    total = mm(mixed_ref[core], own_ref[...], NN) + mm(mixed_ref[1 - core], other_ref[...], NN)
    for place in range(4):
        near_ref[place] = total[:, place * width : (place + 1) * width]
        far_ref[place] = total[:, (4 + place) * width : (5 + place) * width].astype(jnp.bfloat16)


def project_back_kernel(
    core_ref, raw_in_ref, norm_in_ref, w_in_ref, far_ref, near_out_ref, send_ref, keep_ref,
    raw_ref, norm_ref, w_ref, near_ref, sem_ref,
):
    pairs = ((raw_in_ref, raw_ref), (norm_in_ref, norm_ref), (w_in_ref, w_ref), (near_ref, near_out_ref))
    copies = [pltpu.make_async_copy(one, two, sem_ref.at[at]) for at, (one, two) in enumerate(pairs)]
    for copy in copies[:3]:
        copy.start()
    finish(copies[:2])
    wide, width = far_ref.shape[1:]
    rows = raw_ref.shape[2]
    core = core_ref[0]
    total = mm(raw_ref[0], norm_ref[:rows, :], NN) + mm(raw_ref[1], norm_ref[rows:, :], NN)
    for place in range(4):
        near_ref[place] = total[:, place * width : (place + 1) * width]
        far_ref[place] = total[:, (4 + place) * width : (5 + place) * width].astype(jnp.bfloat16)
    copies[3].start()
    copies[2].wait()
    send_ref[...] = mm(raw_ref[1 - core], w_ref[:wide, :], TN).astype(jnp.bfloat16)
    keep_ref[...] = mm(raw_ref[core], w_ref[:wide, :], TN)
    copies[3].wait()


def norm_one_back_kernel(
    core_ref, order_ref, x_ref, half_ref, far_ref, dhidden_ref, gains_ref, grad_ref, xhat_ref
):
    core = core_ref[0]
    width = x_ref.shape[2] // 8
    x = x_ref[core].astype(jnp.float32)
    mean = jnp.mean(x, axis=-1, keepdims=True)
    center = x - mean
    spread = lax.rsqrt(jnp.mean(center * center, axis=-1, keepdims=True) + EPS)
    for place in range(8):
        span = slice(place * width, (place + 1) * width)
        piece = x_ref[core, :, block_at(order_ref, place, width)].astype(jnp.float32)
        xhat_ref[:, span] = (piece - mean) * spread
    xhat = xhat_ref[...]
    dnorm = half_ref[...].astype(jnp.float32) + far_ref[...].astype(jnp.float32)
    scaled = dnorm * gains_ref[0:1, :]
    inner = scaled - jnp.mean(scaled, axis=-1, keepdims=True)
    inner = inner - xhat * jnp.mean(scaled * xhat, axis=-1, keepdims=True)
    total = (dhidden_ref[...] + inner * spread).astype(jnp.bfloat16)
    for place in range(8):
        grad_ref[:, block_at(order_ref, place, width)] = total[:, place * width : (place + 1) * width]


def place_grad_kernel(core_ref, order_ref, local_ref, four_ref, grad_ref, natural_ref):
    rows = grad_ref.shape[1]
    width = grad_ref.shape[2] // 8
    core = core_ref[0]
    for at in range(2):
        micro = core if at == 0 else 1 - core
        place = lax.broadcasted_iota(jnp.int32, (rows, rows), 0)
        onehot = jnp.where(local_ref[pl.ds(micro, 1), :] == place, 1.0, 0.0).astype(jnp.bfloat16)
        natural_ref[...] = mm(onehot, four_ref[micro], NN).astype(jnp.bfloat16)
        for block in range(8):
            span = slice(block * width, (block + 1) * width)
            grad_ref[at, :, span] = natural_ref[:, block_at(order_ref, block, width)]


def result_kernel(order_ref, picks_ref, hidden_ref, half_ref, far_ref, packed_ref, natural_ref):
    rows = hidden_ref.shape[0]
    width = hidden_ref.shape[1] // 8
    branch = half_ref[...].astype(jnp.float32) + far_ref[...].astype(jnp.float32)
    total = (hidden_ref[...] + branch).astype(jnp.bfloat16)
    for block in range(8):
        natural_ref[:, block_at(order_ref, block, width)] = total[:, block * width : (block + 1) * width]
    count = packed_ref.shape[0]
    place = lax.broadcasted_iota(jnp.int32, (rows, count), 0)
    onehot = jnp.where(picks_ref[...] == place, 1.0, 0.0).astype(jnp.bfloat16)
    packed_ref[...] = mm(onehot, natural_ref[...], TN).astype(jnp.bfloat16)


def join_kernel(
    core_ref, side_ref, place_ref, own_ref, far_ref, near_ref, cross_ref, input_own_ref, input_other_ref,
    output_ref, input_ref,
):
    rows = output_ref.shape[1]
    count = own_ref.shape[0]
    halfway = count // 8
    core, side = core_ref[0], side_ref[0]
    row = lax.broadcasted_iota(jnp.int32, (count, rows), 0)
    row = (row // halfway) * (2 * halfway) + row % halfway
    for micro, pieces in ((core, (own_ref, far_ref)), (1 - core, (near_ref, cross_ref))):
        total = jnp.zeros((rows, output_ref.shape[2]), jnp.float32)
        for half, piece in ((side, pieces[0]), (1 - side, pieces[1])):
            wanted = place_ref[pl.ds(micro, 1), :] - half * halfway
            onehot = jnp.where(row == wanted, 1.0, 0.0).astype(jnp.bfloat16)
            total = total + mm(onehot, piece[...], TN)
        output_ref[micro] = total.astype(jnp.bfloat16)
    input_ref[core] = input_own_ref[...]
    input_ref[1 - core] = input_other_ref[...]


def positions(anchor, seq_lens):
    ends = running_ends(seq_lens)
    starts = ends - seq_lens
    inside = (anchor[:, None] >= starts[None, :]) & (anchor[:, None] < ends[None, :])
    return anchor - jnp.sum(jnp.where(inside, starts[None, :], 0), axis=1)


def turn_tables(place):
    freqs = jnp.power(THETA, -jnp.arange(HD // 2, dtype=jnp.float32) * 2.0 / HD)
    angle = freqs[:, None] * place.astype(jnp.float32)[None, :]
    return jnp.concatenate([jnp.cos(angle), jnp.sin(angle)], axis=0)


def paired_layer(
    tokens, cotangent, perm, lengths, w_qkv, w_attn_out, w_in, w_down, gain_one, gain_two
):
    f32, bf16, i32 = jnp.float32, jnp.bfloat16, jnp.int32
    mine = lax.axis_index("fsdp")
    part = lax.axis_index("tp")
    core, side = part & 1, part >> 1
    core_at = core.reshape(1).astype(i32)
    side_at = side.reshape(1).astype(i32)
    rows = tokens.shape[1]
    width = w_qkv.shape[0]
    full = 8 * width
    cols = w_qkv.shape[2]
    heads = cols // HD
    units = w_in.shape[2]
    per_pair = rows // 8
    order = jnp.bitwise_xor(jnp.array(ORDER, i32), mine)

    def pick(value, index):
        return lax.dynamic_index_in_dim(value, index, 0, keepdims=False)

    def add_half(keep, got):
        return (keep + got.astype(f32)).astype(bf16)

    def near_sum(near, far, name):
        shape = near.shape[1:]
        lows = local_call(near_sum_kernel, name, (), (near, far), [(shape, bf16)] * 3, far_in=(0, 1))
        return near[0] + far[0].astype(f32), lows

    def z_send(lows):
        return [hop(low, ORDER[at + 1]) for at, low in enumerate(lows)]

    def far_sum(own, got):
        return own + sum(one.astype(f32) for one in got)

    turned = jnp.transpose(w_qkv.reshape(width, 3, heads, HD), (2, 1, 3, 0)).reshape(3 * cols, width)
    gains_rows = jnp.concatenate([gain_one[None], gain_two[None], jnp.zeros((14, width), bf16)])
    first_same = z_phase(jnp.concatenate([turned, gains_rows], axis=0))
    first = first_same + y_phase(first_same)

    slots = perm.reshape(2, 8, rows)
    from_me = (slots // rows == mine).astype(f32)
    slot_no = jnp.arange(rows, dtype=i32)
    before = (slot_no[:, None] < slot_no[None, :]).astype(f32)
    rank_me = jnp.einsum("mds,st->mdt", from_me, before).astype(i32)
    ranks = jnp.arange(per_pair, dtype=i32)
    chosen = (from_me[..., None] > 0) & (rank_me[..., None] == ranks)
    local = jnp.sum(jnp.where(chosen, (slots % rows)[..., None], 0), axis=2)
    my_slots = lax.dynamic_index_in_dim(slots, mine, 1, keepdims=False)
    target = my_slots // rows
    same = (target[:, :, None] == target[:, None, :]) & (slot_no[:, None] < slot_no[None, :])[None]
    rank_own = jnp.sum(same.astype(i32), axis=1)
    place_own = target * per_pair + rank_own
    quarter = per_pair // 4
    wanted = order[:, None] * per_pair + part * quarter
    wanted = (wanted + jnp.arange(quarter, dtype=i32)[None, :]).reshape(-1)
    packer = (place_own[:, None, :] == wanted[None, :, None]).astype(bf16)
    packed = jnp.einsum("mps,msd->mpd", packer, cotangent, preferred_element_type=f32).astype(bf16)
    packed = packed.reshape(2, 8, quarter, full)
    packed = [packed[:, at] for at in range(8)]
    chosen = order[:, None] == jnp.arange(8, dtype=i32)[None, :]
    local_own = jnp.sum(jnp.where(chosen[None, :, :, None], local[:, None], 0), axis=2)
    anchor = mine * rows + jnp.arange(rows, dtype=i32)
    own_table = jnp.concatenate([turn_tables(positions(anchor, lengths[m])) for m in range(2)], axis=1)
    inp_turned, gate_turned = jnp.transpose(w_in[:, 0]), jnp.transpose(w_in[:, 1])
    second = jnp.concatenate([jnp.transpose(w_down), jnp.transpose(w_attn_out)], axis=0)
    second_all = lax.all_gather(second, "fsdp", axis=0, tiled=False)
    third_all = lax.all_gather(jnp.concatenate([inp_turned, gate_turned], axis=0), "fsdp", axis=0, tiled=False)
    halfway = per_pair // 2
    picks = lax.dynamic_slice_in_dim(pick(local, core), side * halfway, halfway, 1).reshape(1, -1)
    my_lens = lengths[mine // heads]
    all_anchor = jnp.arange(8 * rows, dtype=i32)
    table = turn_tables(positions(all_anchor, my_lens))
    table = jnp.transpose(table.reshape(HD, 8, rows), (1, 0, 2))
    first, packed, own_table, picks, place_own, side_at, table, local_own, order, core_at, core, side, my_lens = sync(
        (first, packed, own_table, picks, place_own, side_at, table, local_own, order, core_at, core, side, my_lens)
    )

    norm_one, gains, outgoing, qkv_w = local_call(
        project_kernel, "project", (order,), (tokens, own_table),
        [((2 * rows, full), bf16), ((2, full), f32), ((2 * heads, 3 * HD, rows), bf16), ((3 * cols + 16, full), bf16)],
        [((2 * rows, full), bf16), ((3 * cols + 16, full), bf16)], first, copies=10,
        far_in=(0, 1), far_out=(1, 2), far_shards=False, raw_out=(0, 3),
    )
    outgoing, packed = sync((outgoing, packed))
    qkv = deal_out(outgoing)
    arrived = [hop(one, ORDER[at]) if at else one for at, one in enumerate(packed)]
    qkv = sync((qkv,))[0]
    mixed_out, exact, logs = local_call(
        attend_kernel, "attend", (my_lens,), (qkv,),
        [((8, HD, rows), bf16), ((8, HD, rows), f32), ((8, 1, rows), f32)],
        [((8 * rows, HD), bf16)], far_in=(0,), far_out=(0, 1, 2),
    )
    mixed_out, arrived = sync((mixed_out, arrived))
    mixed = deal_out(mixed_out).reshape(2, cols, rows)
    arrived = jnp.stack(arrived)
    near = twin(arrived)
    pair = jnp.stack([jnp.where(core == 0, arrived, near), jnp.where(core == 0, near, arrived)])
    far = across(pair)
    mixed, far = sync((mixed, far))
    four = jnp.concatenate([jnp.where(side == 0, pair, far), jnp.where(side == 0, far, pair)])
    four = jnp.transpose(four, (2, 1, 0, 3, 4)).reshape(2, rows, full)
    grad = local_call(
        place_grad_kernel, "place_grad", (core_at, order), (local_own.reshape(2, rows), four),
        [((2, rows, full), bf16)], [((rows, full), bf16)],
    )

    send, keep, out_w = local_call(
        mix_out_kernel, "mix_out", (core_at, order), (mixed,),
        [((rows, full), bf16), ((rows, full), f32), ((cols, full), bf16)], (), (second_all,), far_in=(0,), far_out=(2,),
    )
    half = add_half(keep, twin(send))
    far = across(half)
    far, grad = sync((far, grad))
    hidden, two_own = local_call(
        norm_two_kernel, "norm_two", (core_at, order), (tokens, half, far, gains),
        [((rows, full), f32), ((rows, full), bf16)], far_in=(0, 3), far_out=(0,),
    )
    two_other = twin(two_own)

    send, keep, act, d_inp, d_gate, result_send, result_keep = local_call(
        feed_kernel, "feed", (order,), (two_own, two_other),
        [((rows, full), bf16), ((rows, full), f32)]
        + [((2 * rows, units), bf16)] * 3
        + [((rows, full), bf16), ((rows, full), f32)],
        [((3 * units, full), bf16), ((2, rows, full), bf16), ((rows, full), bf16), ((rows, full), f32)],
        (third_all, second_all, grad), copies=27, raw_out=(5, 6),
    )
    half_two = add_half(keep, twin(send))
    half_two, act, d_inp, d_gate = sync((half_two, act, d_inp, d_gate))
    far_two = across(half_two)
    feed_grad = local_call(
        weight_grad_kernel, "feed_grad", (order,), (d_inp, d_gate, act, two_own, two_other),
        [((8, 3 * units, width), bf16)], [((2, rows, full), bf16), ((8, 3 * units, width), bf16)], (grad,),
        copies=4, raw_out=(0,),
    )
    feed_sum = lax.psum_scatter(feed_grad, "fsdp", scatter_dimension=0, tiled=False)
    far_two, feed_grad = sync((far_two, feed_grad))
    d_hidden, low_own = local_call(
        norm_two_back_kernel, "norm_two_back", (), (hidden, half_two, far_two, grad, gains),
        [((rows, full), f32), ((rows, full), bf16)], far_in=(0, 3, 4), far_out=(0,),
    )
    low_other = twin(low_own)
    d_mixed = local_call(
        mix_back_kernel, "mix_back", (core_at,), (low_own, low_other, out_w),
        [((8, HD, rows), bf16)], far_out=(0,),
    )
    d_mixed, low_own, low_other, result_send, result_keep = sync(
        (d_mixed, low_own, low_other, result_send, result_keep)
    )
    grad_mixed = deal_out(d_mixed)
    out_far, out_near = local_call(
        mix_grad_kernel, "mix_grad", (core_at,), (mixed, low_own, low_other),
        [((4, cols, width), bf16), ((4, cols, width), f32)], far_in=(0, 1, 2), far_out=(1,),
    )
    res_half = add_half(result_keep, twin(result_send))
    out_got = hop(out_far, 1)
    res_far = across(res_half)
    grad_mixed, out_got, res_far = sync((grad_mixed, out_got, res_far))

    d_raw_out = local_call(
        attend_back_kernel, "attend_back", (my_lens,), (),
        [((8, 3 * HD, rows), bf16)],
        [
            ((8, 3 * HD, rows), bf16), ((8, HD, rows), f32), ((8, 1, rows), f32), ((8, HD, rows), bf16),
            ((8, HD, rows), f32), ((8, 3 * HD, rows), bf16),
            ((8 * rows, 2 * HD), bf16), ((HD, 8 * rows), f32), ((HD, 8 * rows), f32),
        ],
        (qkv, exact, logs, grad_mixed, table), copies=6, raw_out=(0,),
    )
    d_raw_out, out_got, res_far = sync((d_raw_out, out_got, res_far))
    d_raw = deal_out(d_raw_out).reshape(2, 3 * cols, rows)
    out_own, out_lows = near_sum(out_near, out_got, "out_near")
    packed = local_call(
        result_kernel, "result", (order,), (picks, hidden, res_half, res_far),
        [((8 * halfway, full), bf16)], [((rows, full), bf16)], far_in=(1, 2, 3), far_out=(0,),
    )
    d_raw, out_lows, packed = sync((d_raw, out_lows, packed))

    qkv_far, qkv_near, send, keep = local_call(
        project_back_kernel, "project_back", (core_at,), (),
        [((4, 3 * cols, width), bf16), ((4, 3 * cols, width), f32), ((rows, full), bf16), ((rows, full), f32)],
        [
            ((2, 3 * cols, rows), bf16), ((2 * rows, full), bf16), ((3 * cols + 16, full), bf16),
            ((4, 3 * cols, width), f32),
        ],
        (d_raw, norm_one, qkv_w), copies=4, raw_out=(1,),
    )
    qkv_got = hop(qkv_far, 1)
    half = add_half(keep, twin(send))
    far = across(half)
    out_got = z_send(out_lows)
    arrived = deal_out(packed.reshape(8, halfway, full))
    input_own = local_call(
        norm_one_back_kernel, "norm_one_back", (core_at, order), (tokens, half, far, d_hidden, gains),
        [((rows, full), bf16)], [((rows, full), f32)], far_in=(0, 3, 4),
    )
    qkv_got, input_own, out_got = sync((qkv_got, input_own, out_got))
    qkv_own, qkv_lows = near_sum(qkv_near, qkv_got, "qkv_near")
    qkv_lows = sync(qkv_lows)
    qkv_got = z_send(qkv_lows)
    qkv_got[0], arrived, input_own, feed_sum = sync((qkv_got[0], arrived, input_own, feed_sum))
    input_other = twin(input_own)
    grad_attn_out = jnp.transpose(far_sum(out_own, out_got))
    inp_sum, gate_sum, down_sum = [feed_sum[at * units : (at + 1) * units].astype(f32) for at in range(3)]
    two_row = jnp.sum(inp_sum * inp_turned.astype(f32) + gate_sum * gate_turned.astype(f32), axis=0)
    grad_in = jnp.stack([jnp.transpose(inp_sum), jnp.transpose(gate_sum)], axis=1)
    grad_down = jnp.transpose(down_sum)
    arrived = arrived.reshape(8 * halfway, full)
    other_side = across(arrived)
    output, input_grad = local_call(
        join_kernel, "join", (core_at, side_at),
        (place_own, arrived, other_side, twin(arrived), twin(other_side), input_own, input_other),
        [((2, rows, full), bf16), ((2, rows, full), bf16)],
    )
    qkv_got, output, input_grad, grad_attn_out, grad_in, grad_down, two_row = sync(
        (qkv_got, output, input_grad, grad_attn_out, grad_in, grad_down, two_row)
    )
    qkv_sum = far_sum(qkv_own, qkv_got)
    one_row = jnp.sum(qkv_sum * turned.astype(f32), axis=0)
    gain_rows = jnp.stack([one_row / gain_one.astype(f32), two_row / gain_two.astype(f32)])
    beyond = lax.ppermute(gain_rows, "tp", [(i, i ^ 3) for i in range(4)])
    gain_rows = (gain_rows + twin(gain_rows)) + (across(gain_rows) + beyond)
    grad_gain_one, grad_gain_two = gain_rows[0], gain_rows[1]
    return (
        output,
        input_grad,
        jnp.transpose(qkv_sum.reshape(heads, 3, HD, width), (3, 1, 0, 2)).reshape(width, 3, cols),
        grad_attn_out,
        grad_in,
        grad_down,
        grad_gain_one,
        grad_gain_two,
    )


def on_device(*operands):
    micro_count, tok_rows = operands[0].shape[0], operands[0].shape[1]
    groups, parts = lax.axis_size("fsdp"), lax.axis_size("tp")
    heads = operands[4].shape[2] // HD
    if groups == 8 and parts == 4 and micro_count == 2 and micro_count * heads == groups and tok_rows % 256 == 0:
        return paired_layer(*operands)
    return general_layer(*operands)


def solution(mesh):
    placed = (
        P(None, "fsdp", None),
        P(None, "fsdp", None),
        P(),
        P(),
        P("fsdp", None, "tp"),
        P("fsdp", "tp"),
        P("fsdp", None, "tp"),
        P("fsdp", "tp"),
        P("fsdp"),
        P("fsdp"),
    )
    return jax.shard_map(
        on_device,
        mesh=mesh,
        in_specs=placed,
        out_specs=(
            P(None, "fsdp", None),
            P(None, "fsdp", None),
            P("fsdp", None, "tp"),
            P("fsdp", "tp"),
            P("fsdp", None, "tp"),
            P("fsdp", "tp"),
            P("fsdp"),
            P("fsdp"),
        ),
        check_vma=False,
    )
```

```python
import math

import jax
import jax.numpy as jnp
from jax import lax
from jax.experimental import pallas as pl
from jax.experimental.pallas import tpu as pltpu
from jax.sharding import PartitionSpec as P

D = 1024
HD = 64


EPS = 1e-05
THETA = 160000.0
key_block = 2048


def layer_norm(values, gain):
    center = values - jnp.mean(values, axis=-1, keepdims=True)
    spread = jnp.mean(center * center, axis=-1, keepdims=True)
    return center * lax.rsqrt(spread + EPS) * gain


def rope_tables(position, width):
    freqs = jnp.power(THETA, -jnp.arange(width // 2, dtype=jnp.float32) * 2.0 / width)
    angle = position.astype(jnp.float32)[:, None] * freqs[None, :]
    angle = jnp.concatenate([angle, angle], axis=-1)
    return (jnp.cos(angle), jnp.sin(angle))


def rotate(values, cosine, sine):
    half = values.shape[-1] // 2
    turned = jnp.concatenate([-values[..., half:], values[..., :half]], axis=-1)
    return values * cosine[:, None, :] + turned * sine[:, None, :]


def running_ends(seq_lens):
    order = jnp.arange(seq_lens.shape[0], dtype=jnp.int32)
    return jnp.sum(jnp.where(order[None, :] <= order[:, None], seq_lens[None, :], 0), axis=1)


def seq_info(anchor, seq_lens):
    ends = running_ends(seq_lens)
    starts = ends - seq_lens
    segment = jnp.sum((anchor[:, None] >= ends[None, :]).astype(jnp.int32), axis=1)
    onehot = segment[:, None] == jnp.arange(seq_lens.shape[0], dtype=jnp.int32)[None, :]
    position = anchor - jnp.sum(jnp.where(onehot, starts[None, :], 0), axis=1)
    return (segment, position)


def blockwise(running, pieces, offset, step_fn):
    piece_len = pieces[0].shape[0]
    if piece_len > key_block and piece_len % key_block == 0:
        block_count = piece_len // key_block
        stacked = tuple((one.reshape((block_count, key_block) + one.shape[1:]) for one in pieces))

        def inner(state_now, scan_item):
            block_index, piece_parts = scan_item
            return (step_fn(state_now, piece_parts, offset + block_index * key_block), None)

        running, _ = lax.scan(inner, running, (jnp.arange(block_count, dtype=jnp.int32), stacked))
        return running
    return step_fn(running, pieces, offset)


def general_layer(
    tokens, cotangent, perm, lengths, w_qkv, w_attn_out, w_in, w_down, gain_one, gain_two
):
    groups = lax.axis_size("fsdp")
    my_index = lax.axis_index("fsdp")
    micro_count = tokens.shape[0]
    tok_rows = tokens.shape[1]
    total_rows = tok_rows * groups
    per_pair = tok_rows // groups
    head_cols = w_qkv.shape[2]
    head_count = head_cols // HD
    unit_cols = w_in.shape[2]
    score_scale = HD ** (-0.5)
    rows_idx = jnp.arange(tok_rows, dtype=jnp.int32)
    f32 = jnp.float32
    bf16 = jnp.bfloat16
    dims_rows = (((0,), (0,)), ((), ()))
    dims_cols = (((1,), (1,)), ((), ()))
    acc_qkv = jnp.zeros((D, 3, head_cols), f32)
    acc_out = jnp.zeros((D, head_cols), f32)
    acc_in = jnp.zeros((D, 2, unit_cols), f32)
    acc_down = jnp.zeros((D, unit_cols), f32)
    acc_gain_one = jnp.zeros((D,), f32)
    acc_gain_two = jnp.zeros((D,), f32)
    outputs = []
    input_grads = []
    for micro_idx in range(micro_count):
        perm_row = perm[micro_idx]
        seq_lens = lengths[micro_idx]
        inverse = (
            jnp.zeros((total_rows,), jnp.int32)
            .at[perm_row]
            .set(jnp.arange(total_rows, dtype=jnp.int32))
        )
        placed = lax.dynamic_slice_in_dim(inverse, my_index * tok_rows, tok_rows)
        send_order = jnp.argsort(placed)
        outgoing = tokens[micro_idx][send_order].reshape(groups, per_pair, D)
        arrived = lax.all_to_all(outgoing, "fsdp", split_axis=0, concat_axis=0, tiled=True).reshape(
            tok_rows, D
        )
        my_tokens = lax.dynamic_slice_in_dim(perm_row, my_index * tok_rows, tok_rows)
        source = my_tokens // tok_rows
        recv_order = jnp.argsort(source * tok_rows + rows_idx)
        recv_slot = jnp.zeros((tok_rows,), jnp.int32).at[recv_order].set(rows_idx)
        dealt = arrived[recv_slot]
        fetched = (
            lax.all_gather(gain_one, "fsdp", axis=0, tiled=True),
            lax.all_gather(gain_two, "fsdp", axis=0, tiled=True),
            lax.all_gather(w_qkv, "fsdp", axis=0, tiled=True),
            lax.all_gather(w_attn_out, "fsdp", axis=0, tiled=True),
            lax.all_gather(w_in, "fsdp", axis=0, tiled=True),
            lax.all_gather(w_down, "fsdp", axis=0, tiled=True),
        )
        gain_first = fetched[0].astype(f32)
        gain_second = fetched[1].astype(f32)
        query_seg, query_pos = seq_info(my_tokens, seq_lens)
        cosine, sine = rope_tables(query_pos, HD)
        x_float = dealt.astype(f32)
        normed_low = layer_norm(x_float, gain_first).astype(bf16)
        raw_proj = jnp.einsum("td,dcf->tcf", normed_low, fetched[2], preferred_element_type=f32)
        raw_heads = raw_proj.reshape(tok_rows, 3, head_count, HD)
        query_low = rotate(raw_heads[:, 0], cosine, sine).astype(bf16)
        key_low = rotate(raw_heads[:, 1], cosine, sine).astype(bf16)
        value_low = raw_heads[:, 2].astype(bf16)

        def forward_step(running, piece_parts, offset):
            run_peak, run_total, run_acc = running
            key_part, value_part = piece_parts
            key_seg, _ = seq_info(
                lax.dynamic_slice_in_dim(perm_row, offset, key_part.shape[0]), seq_lens
            )
            scores = (
                jnp.einsum("qhe,khe->hqk", query_low, key_part, preferred_element_type=f32)
                * score_scale
            )
            same_seq = (query_seg[:, None] == key_seg[None, :])[None]
            block_top = jnp.max(jnp.where(same_seq, scores, -1e30), axis=-1)
            new_peak = jnp.maximum(run_peak, block_top)
            weights = jnp.where(same_seq, jnp.exp(scores - new_peak[..., None]), 0.0)
            fade_factor = jnp.exp(run_peak - new_peak)
            run_acc = run_acc * jnp.transpose(fade_factor)[:, :, None] + jnp.einsum(
                "hqk,khe->qhe", weights.astype(bf16), value_part, preferred_element_type=f32
            )
            run_total = run_total * fade_factor + jnp.sum(weights, axis=-1)
            return (new_peak, run_total, run_acc)

        start_state = (
            jnp.full((head_count, tok_rows), -1e30, f32),
            jnp.zeros((head_count, tok_rows), f32),
            jnp.zeros((tok_rows, head_count, HD), f32),
        )
        run_peak, run_total, run_acc = blockwise(
            start_state,
            (
                lax.all_gather(key_low, "fsdp", axis=0, tiled=True),
                lax.all_gather(value_low, "fsdp", axis=0, tiled=True),
            ),
            jnp.int32(0),
            forward_step,
        )
        log_total = run_peak + jnp.log(run_total)
        mixed_heads = run_acc / jnp.transpose(run_total)[:, :, None]
        mixed_low = mixed_heads.reshape(tok_rows, head_cols).astype(bf16)
        attn_part = lax.dot_general(mixed_low, fetched[3], dims_cols, preferred_element_type=f32)
        branch = lax.psum(attn_part.astype(jnp.bfloat16), "tp").astype(jnp.float32)
        hidden = x_float + branch
        normed_two = layer_norm(hidden, gain_second).astype(bf16)
        ffn_proj = jnp.einsum("td,dcf->tcf", normed_two, fetched[4], preferred_element_type=f32)
        act_low = (jax.nn.gelu(ffn_proj[:, 0], approximate=False) * ffn_proj[:, 1]).astype(bf16)
        ffn_part = lax.dot_general(act_low, fetched[5], dims_cols, preferred_element_type=f32)
        branch_two = lax.psum(ffn_part.astype(jnp.bfloat16), "tp").astype(jnp.float32)
        outputs.append((hidden + branch_two).astype(bf16))
        again = (
            lax.all_gather(gain_one, "fsdp", axis=0, tiled=True),
            lax.all_gather(gain_two, "fsdp", axis=0, tiled=True),
            lax.all_gather(w_qkv, "fsdp", axis=0, tiled=True),
            lax.all_gather(w_attn_out, "fsdp", axis=0, tiled=True),
            lax.all_gather(w_in, "fsdp", axis=0, tiled=True),
            lax.all_gather(w_down, "fsdp", axis=0, tiled=True),
        )
        gain_first = again[0].astype(f32)
        gain_second = again[1].astype(f32)
        grad_low = cotangent[micro_idx]
        grad_float = grad_low.astype(f32)
        acc_down = acc_down + lax.dot_general(
            grad_low, act_low, dims_rows, preferred_element_type=f32
        )
        d_act = jnp.dot(grad_low, again[5], preferred_element_type=f32)
        _, gelu_pull = jax.vjp(
            lambda inputs, gates: jax.nn.gelu(inputs, approximate=False) * gates,
            ffn_proj[:, 0],
            ffn_proj[:, 1],
        )
        d_inputs, d_gates = gelu_pull(d_act)
        d_proj = jnp.stack([d_inputs, d_gates], axis=1).astype(bf16)
        acc_in = acc_in + jnp.einsum("td,tcf->dcf", normed_two, d_proj, preferred_element_type=f32)
        norm_part = jnp.einsum("tcf,dcf->td", d_proj, again[4], preferred_element_type=f32)
        d_norm_two = lax.psum(norm_part.astype(jnp.bfloat16), "tp").astype(jnp.float32)
        _, second_pull = jax.vjp(layer_norm, hidden, gain_second)
        d_hid_norm, d_gain_two = second_pull(d_norm_two)
        acc_gain_two = acc_gain_two + d_gain_two
        d_hidden = grad_float + d_hid_norm
        hidden_low = d_hidden.astype(bf16)
        acc_out = acc_out + lax.dot_general(
            hidden_low, mixed_low, dims_rows, preferred_element_type=f32
        )
        d_mixed = jnp.dot(hidden_low, again[3], preferred_element_type=f32).astype(bf16)
        d_mixed = d_mixed.reshape(tok_rows, head_count, HD)
        delta_rows = jnp.sum(d_mixed.astype(f32) * mixed_heads, axis=-1)
        delta_heads = jnp.transpose(delta_rows)

        def query_step(grad_query, piece_parts, offset):
            key_part, value_part = piece_parts
            key_seg, _ = seq_info(
                lax.dynamic_slice_in_dim(perm_row, offset, key_part.shape[0]), seq_lens
            )
            scores = (
                jnp.einsum("qhe,khe->hqk", query_low, key_part, preferred_element_type=f32)
                * score_scale
            )
            same_seq = (query_seg[:, None] == key_seg[None, :])[None]
            weights = jnp.where(same_seq, jnp.exp(scores - log_total[..., None]), 0.0)
            d_weights = jnp.einsum("qhe,khe->hqk", d_mixed, value_part, preferred_element_type=f32)
            d_scores = (weights * (d_weights - delta_heads[..., None])).astype(bf16)
            return grad_query + score_scale * jnp.einsum(
                "hqk,khe->qhe", d_scores, key_part, preferred_element_type=f32
            )

        query_start = jnp.zeros((tok_rows, head_count, HD), f32)
        grad_query = blockwise(
            query_start,
            (
                lax.all_gather(key_low, "fsdp", axis=0, tiled=True),
                lax.all_gather(value_low, "fsdp", axis=0, tiled=True),
            ),
            jnp.int32(0),
            query_step,
        )
        stat_total, stat_delta = (
            lax.all_gather(jnp.transpose(log_total), "fsdp", axis=0, tiled=True),
            lax.all_gather(delta_rows, "fsdp", axis=0, tiled=True),
        )

        def key_step(running, piece_parts, offset):
            grad_key, grad_value = running
            query_part, dmix_part = piece_parts
            piece_len = query_part.shape[0]
            piece_seg, _ = seq_info(lax.dynamic_slice_in_dim(perm_row, offset, piece_len), seq_lens)
            total_part = jnp.transpose(lax.dynamic_slice_in_dim(stat_total, offset, piece_len))
            delta_part = jnp.transpose(lax.dynamic_slice_in_dim(stat_delta, offset, piece_len))
            scores = (
                jnp.einsum("qhe,khe->hqk", query_part, key_low, preferred_element_type=f32)
                * score_scale
            )
            same_seq = (piece_seg[:, None] == query_seg[None, :])[None]
            weights = jnp.where(same_seq, jnp.exp(scores - total_part[..., None]), 0.0)
            d_weights = jnp.einsum("qhe,khe->hqk", dmix_part, value_low, preferred_element_type=f32)
            d_scores = (weights * (d_weights - delta_part[..., None])).astype(bf16)
            grad_key = grad_key + score_scale * jnp.einsum(
                "hqk,qhe->khe", d_scores, query_part, preferred_element_type=f32
            )
            grad_value = grad_value + jnp.einsum(
                "hqk,qhe->khe", weights.astype(bf16), dmix_part, preferred_element_type=f32
            )
            return (grad_key, grad_value)

        grad_key, grad_value = blockwise(
            (
                jnp.zeros((tok_rows, head_count, HD), f32),
                jnp.zeros((tok_rows, head_count, HD), f32),
            ),
            (
                lax.all_gather(query_low, "fsdp", axis=0, tiled=True),
                lax.all_gather(d_mixed, "fsdp", axis=0, tiled=True),
            ),
            jnp.int32(0),
            key_step,
        )
        _, rope_pull = jax.vjp(lambda heads_in: rotate(heads_in, cosine, sine), raw_heads[:, 0])
        d_raw_query = rope_pull(grad_query)[0]
        d_raw_key = rope_pull(grad_key)[0]
        d_raw = (
            jnp.stack([d_raw_query, d_raw_key, grad_value], axis=1)
            .reshape(tok_rows, 3, head_cols)
            .astype(bf16)
        )
        acc_qkv = acc_qkv + jnp.einsum("td,tcf->dcf", normed_low, d_raw, preferred_element_type=f32)
        first_part = jnp.einsum("tcf,dcf->td", d_raw, again[2], preferred_element_type=f32)
        d_norm_one = lax.psum(first_part.astype(jnp.bfloat16), "tp").astype(jnp.float32)
        _, first_pull = jax.vjp(layer_norm, x_float, gain_first)
        d_x_norm, d_gain_one = first_pull(d_norm_one)
        acc_gain_one = acc_gain_one + d_gain_one
        d_input = (d_hidden + d_x_norm).astype(bf16)
        back_rows = d_input[recv_order].reshape(groups, per_pair, D)
        returned = lax.all_to_all(
            back_rows, "fsdp", split_axis=0, concat_axis=0, tiled=True
        ).reshape(tok_rows, D)
        send_slot = jnp.zeros((tok_rows,), jnp.int32).at[send_order].set(rows_idx)
        input_grads.append(returned[send_slot])
    summed = (
        lax.psum_scatter(acc_qkv, "fsdp", scatter_dimension=0, tiled=True),
        lax.psum_scatter(acc_out, "fsdp", scatter_dimension=0, tiled=True),
        lax.psum_scatter(acc_in, "fsdp", scatter_dimension=0, tiled=True),
        lax.psum_scatter(acc_down, "fsdp", scatter_dimension=0, tiled=True),
        lax.psum_scatter(acc_gain_one, "fsdp", scatter_dimension=0, tiled=True),
        lax.psum_scatter(acc_gain_two, "fsdp", scatter_dimension=0, tiled=True),
    )
    return (
        jnp.stack(outputs),
        jnp.stack(input_grads),
        summed[0],
        summed[1],
        summed[2],
        summed[3],
        summed[4],
        summed[5],
    )


JOIN = 2
COSTS = {"attend": 10, "attend_back": 28, "feed": 8, "norm_one_back": 0, "qkv_near": 0, "feed_grad": 5}
FAR = -1e30
ORDER = (0, 2, 4, 6, 1, 3, 5, 7)
NT = (((1,), (1,)), ((), ()))
TN = (((0,), (0,)), ((), ()))
NN = (((1,), (0,)), ((), ()))
ROOM = 10 * 1024 * 1024


def partial(kernel, *given):
    return lambda *refs: kernel(*given, *refs)


def mm(left, right, dims):
    return lax.dot_general(left, right, dims, preferred_element_type=jnp.float32)


def hop(value, step):
    return lax.ppermute(value, "fsdp", [(i, i ^ step) for i in range(8)])


def twin(value):
    return lax.ppermute(value, "tp", [(i, i ^ 1) for i in range(4)])


def across(value):
    return lax.ppermute(value, "tp", [(i, i ^ 2) for i in range(4)])


def deal_out(value):
    return lax.all_to_all(value, "fsdp", 0, 0, tiled=True)


def after(value, *earlier):
    return lax.optimization_barrier((value,) + earlier)[0]


def sync(values):
    return lax.optimization_barrier(values)


def z_phase(shard):
    return [shard] + [hop(shard, step) for step in ORDER[1:4]]


def y_phase(shards):
    return [hop(one, 1) for one in shards]


def local_call(kernel, name, scalars, arrays, outs, scratch=(), shards=(), copies=8, far_in=(), far_out=(), far_shards=True, raw_out=()):
    shapes = [(one.shape, one.dtype) for one in arrays]
    staged = [shapes[at] for at in far_in] + [outs[at] for at in far_out]
    sems = [pltpu.SemaphoreType.DMA((copies,))] if shards else []
    room = ROOM + sum(math.prod(shape) * jnp.dtype(kind).itemsize for shape, kind in [*shapes, *outs, *scratch])
    counts = (len(scalars), len(arrays), len(shards), len(outs), len(scratch) + len(sems))

    def body(*refs):
        groups = []
        for count in counts:
            groups.append(list(refs[:count]))
            refs = refs[count:]
        given, ins, pieces, results, extra = groups
        if not staged:
            return kernel(*given, *ins, *pieces, *results, *extra)
        stage, sem = refs[:-1], refs[-1]
        incoming, outgoing = [], []
        for slot, at in enumerate(far_in):
            incoming.append(pltpu.make_async_copy(ins[at], stage[slot], sem.at[slot]))
            incoming[-1].start()
            ins[at] = stage[slot]
        for slot, at in enumerate(far_out, len(far_in)):
            outgoing.append(pltpu.make_async_copy(stage[slot], results[at], sem.at[slot]))
            results[at] = stage[slot]
        for copy in incoming:
            copy.wait()
        kernel(*given, *ins, *pieces, *results, *extra)
        for copy in outgoing:
            copy.start()
        for copy in outgoing:
            copy.wait()

    arrays = [pltpu.with_memory_space_constraint(one, pltpu.HBM) if at in far_in else one for at, one in enumerate(arrays)]
    shards = [pltpu.with_memory_space_constraint(one, pltpu.HBM) if far_shards else one for one in shards]

    def space(at, far):
        return pl.BlockSpec(memory_space=pltpu.HBM if at in far else pltpu.VMEM)

    result = pl.pallas_call(
        body,
        in_specs=[pl.BlockSpec(memory_space=pltpu.SMEM)] * len(scalars)
        + [space(at, far_in) for at in range(len(arrays))]
        + [pl.BlockSpec(memory_space=pltpu.HBM if far_shards else pl.ANY)] * len(shards),
        out_specs=[space(at, (*far_out, *raw_out)) for at in range(len(outs))],
        out_shape=[
            pltpu.HBM(shape, kind) if at in (*far_out, *raw_out) else jax.ShapeDtypeStruct(shape, kind)
            for at, (shape, kind) in enumerate(outs)
        ],
        scratch_shapes=[pltpu.VMEM(shape, kind) for shape, kind in scratch]
        + sems
        + [pltpu.VMEM(shape, kind) for shape, kind in staged]
        + ([pltpu.SemaphoreType.DMA((len(staged),))] if staged else []),
        compiler_params=pltpu.CompilerParams(vmem_limit_bytes=room),
        cost_estimate=pl.CostEstimate(flops=COSTS.get(name, 3) * 10**9, transcendentals=0, bytes_accessed=8 * 1024 * 1024),
        name=name,
    )(*scalars, *arrays, *shards)
    return result if len(outs) > 1 else result[0]


def block_at(order_ref, place, width):
    return pl.ds(pl.multiple_of(order_ref[place] * width, width), width)


def shard_copies(shards, low, high, into_ref, sem_ref, base=0):
    width = shards[0].shape[1]
    copies = []
    for place, shard in enumerate(shards):
        span = pl.ds(place * width, width)
        source = shard.at[pl.ds(low, high - low), :]
        copies.append(pltpu.make_async_copy(source, into_ref.at[:, span], sem_ref.at[base + place]))
        copies[-1].start()
    return copies


def gathered_copies(order_ref, source, low, high, into_ref, sem_ref, base=0):
    width = source.shape[2]
    copies = []
    for place in range(8):
        copies.append(
            pltpu.make_async_copy(
                source.at[order_ref[place], pl.ds(low, high - low), :],
                into_ref.at[:, pl.ds(place * width, width)],
                sem_ref.at[base + place],
            )
        )
        copies[-1].start()
    return copies


def finish(copies):
    for copy in copies:
        copy.wait()


def project_kernel(order_ref, x_ref, table_ref, *refs):
    shards = refs[:8]
    norm_out_ref, gains_ref, send_ref, w_out_ref, norm_ref, w_ref, sem_ref = refs[8:]
    width = shards[0].shape[1]
    rows = x_ref.shape[1]
    wide = w_ref.shape[0] - 16
    heads = wide // (3 * HD)
    half = HD // 2
    finish(shard_copies(shards, 0, wide + 16, w_ref, sem_ref))
    outgoing = [pltpu.make_async_copy(w_ref, w_out_ref, sem_ref.at[8]), pltpu.make_async_copy(norm_ref, norm_out_ref, sem_ref.at[9])]
    outgoing[0].start()
    gains_ref[...] = w_ref[wide:, :].astype(jnp.float32)[:2]
    for micro in range(2):
        x = x_ref[micro].astype(jnp.float32)
        mean = jnp.mean(x, axis=-1, keepdims=True)
        center = x - mean
        spread = lax.rsqrt(jnp.mean(center * center, axis=-1, keepdims=True) + EPS)
        for place in range(8):
            piece = x_ref[micro, :, block_at(order_ref, place, width)].astype(jnp.float32)
            span = slice(place * width, (place + 1) * width)
            value = (piece - mean) * spread * gains_ref[0:1, span]
            norm_ref[micro * rows : (micro + 1) * rows, span] = value.astype(jnp.bfloat16)
    outgoing[1].start()
    raw = mm(w_ref[:wide, :], norm_ref[...], NT)
    cosine, sine = table_ref[:half, :], table_ref[half:, :]
    for head in range(heads):
        base = head * 3 * HD
        for kind in range(2):
            upper = raw[base + kind * HD : base + kind * HD + half]
            lower = raw[base + kind * HD + half : base + (kind + 1) * HD]
            first = (upper * cosine - lower * sine).astype(jnp.bfloat16)
            second = (lower * cosine + upper * sine).astype(jnp.bfloat16)
            for micro in range(2):
                span = slice(micro * rows, (micro + 1) * rows)
                send_ref[micro * heads + head, kind * HD : kind * HD + half, :] = first[:, span]
                send_ref[micro * heads + head, kind * HD + half : (kind + 1) * HD, :] = second[:, span]
        value = raw[base + 2 * HD : base + 3 * HD].astype(jnp.bfloat16)
        for micro in range(2):
            send_ref[micro * heads + head, 2 * HD :, :] = value[:, micro * rows : (micro + 1) * rows]
    finish(outgoing)


def key_range(lens_ref, low, high):
    first = jnp.int32(0)
    last = jnp.int32(0)
    total = jnp.int32(0)
    for index in range(lens_ref.shape[0]):
        start = total
        total = total + lens_ref[index]
        first = jnp.where((start <= low) & (low < total), start, first)
        last = jnp.where((start <= high) & (high < total), total, last)
    return first, last


def query_bounds(lens_ref, base, width):
    place = base + lax.broadcasted_iota(jnp.int32, (1, width), 1)
    first = jnp.zeros((1, width), jnp.int32)
    last = jnp.zeros((1, width), jnp.int32)
    total = jnp.int32(0)
    for index in range(lens_ref.shape[0]):
        start = total
        total = total + lens_ref[index]
        inside = (place >= start) & (place < total)
        first = jnp.where(inside, start, first)
        last = jnp.where(inside, total, last)
    return first, last


def lanes(ref, index, count, rows):
    return jnp.concatenate([ref[index * count + at, rows, :] for at in range(count)], axis=1)


def attend_kernel(lens_ref, qkv_ref, mixed_ref, exact_ref, log_ref, key_ref):
    blocks, _, small = qkv_ref.shape
    wide = JOIN * small
    for at in range(blocks):
        block = qkv_ref[at, HD : 2 * HD, :].astype(jnp.float32)
        key_ref[at * small : (at + 1) * small, :] = jnp.transpose(block).astype(jnp.bfloat16)

    def one_query(index, carry):
        base = index * wide
        first, last = key_range(lens_ref, base, base + wide - 1)
        low, high = query_bounds(lens_ref, base, wide)
        query = lanes(qkv_ref, index, JOIN, slice(0, HD)) * jnp.bfloat16(HD**-0.5)

        def one_key(at, state):
            peak, total, acc = state
            start = pl.multiple_of(at * wide, wide)
            scores = mm(key_ref[pl.ds(start, wide), :], query, NN)
            place = start + lax.broadcasted_iota(jnp.int32, (wide, wide), 0)
            scores = jnp.where((place >= low) & (place < high), scores, FAR)
            top = jnp.maximum(peak, jnp.max(scores, axis=0, keepdims=True))
            weights = jnp.exp(scores - top)
            fade = jnp.exp(peak - top)
            total = total * fade + jnp.sum(weights, axis=0, keepdims=True)
            value = lanes(qkv_ref, at, JOIN, slice(2 * HD, 3 * HD))
            acc = acc * fade + mm(value, weights.astype(jnp.bfloat16), NN)
            return top, total, acc

        peak, total, acc = lax.fori_loop(
            first // wide,
            (last + wide - 1) // wide,
            one_key,
            (
                jnp.full((1, wide), FAR, jnp.float32),
                jnp.zeros((1, wide), jnp.float32),
                jnp.zeros((HD, wide), jnp.float32),
            ),
        )
        result = acc / total
        logs = peak + jnp.log(total)
        for at in range(JOIN):
            span = slice(at * small, (at + 1) * small)
            mixed_ref[index * JOIN + at] = result[:, span].astype(jnp.bfloat16)
            exact_ref[index * JOIN + at] = result[:, span]
            log_ref[index * JOIN + at] = logs[:, span]
        return carry

    lax.fori_loop(0, blocks // JOIN, one_query, 0)


def attend_back_kernel(
    lens_ref, qkv_in_ref, exact_in_ref, log_in_ref, grad_in_ref, table_in_ref, raw_out_ref,
    qkv_ref, exact_ref, log_ref, grad_ref, table_ref, raw_ref, pair_ref, dkey_ref, dvalue_ref, sem_ref
):
    pairs = (
        (qkv_in_ref, qkv_ref), (exact_in_ref, exact_ref), (log_in_ref, log_ref), (grad_in_ref, grad_ref),
        (table_in_ref, table_ref), (raw_ref, raw_out_ref),
    )
    copies = [pltpu.make_async_copy(one, two, sem_ref.at[at]) for at, (one, two) in enumerate(pairs)]
    for copy in copies[:5]:
        copy.start()
    copies[0].wait()
    blocks, _, small = qkv_ref.shape
    wide = JOIN * small
    half = HD // 2
    for at in range(blocks):
        block = qkv_ref[at, HD : 3 * HD, :].astype(jnp.float32)
        pair_ref[at * small : (at + 1) * small, :] = jnp.transpose(block).astype(jnp.bfloat16)
    dkey_ref[...] = jnp.zeros(dkey_ref.shape, jnp.float32)
    dvalue_ref[...] = jnp.zeros(dvalue_ref.shape, jnp.float32)
    finish(copies[1:5])

    def unturn(index, grad):
        cosine = table_ref[index, :half, :]
        sine = table_ref[index, half:, :]
        upper, lower = grad[:half], grad[half:]
        return upper * cosine + lower * sine, lower * cosine - upper * sine

    def one_query(index, carry):
        base = index * wide
        first, last = key_range(lens_ref, base, base + wide - 1)
        low, high = query_bounds(lens_ref, base, wide)
        query = lanes(qkv_ref, index, JOIN, slice(0, HD)) * jnp.bfloat16(HD**-0.5)
        grad = lanes(grad_ref, index, JOIN, slice(0, HD))
        logs = lanes(log_ref, index, JOIN, slice(0, 1))
        exact = lanes(exact_ref, index, JOIN, slice(0, HD))
        delta = jnp.sum(grad.astype(jnp.float32) * exact, axis=0, keepdims=True)

        def one_key(at, dquery):
            start = pl.multiple_of(at * wide, wide)
            span = pl.ds(start, wide)
            scores = mm(pair_ref[span, :HD], query, NN)
            dweights = mm(pair_ref[span, HD:], grad, NN)
            place = start + lax.broadcasted_iota(jnp.int32, (wide, wide), 0)
            weights = jnp.where((place >= low) & (place < high), jnp.exp(scores - logs), 0.0)
            dscores = (weights * (dweights - delta)).astype(jnp.bfloat16)
            dkey_ref[:, span] += mm(query, dscores, NT)
            dvalue_ref[:, span] += mm(grad, weights.astype(jnp.bfloat16), NT)
            return dquery + mm(lanes(qkv_ref, at, JOIN, slice(HD, 2 * HD)), dscores, NN)

        dquery = lax.fori_loop(
            first // wide,
            (last + wide - 1) // wide,
            one_key,
            jnp.zeros((HD, wide), jnp.float32),
        ) * (HD**-0.5)
        for at in range(JOIN):
            upper, lower = unturn(index * JOIN + at, dquery[:, at * small : (at + 1) * small])
            raw_ref[index * JOIN + at, :half, :] = upper.astype(jnp.bfloat16)
            raw_ref[index * JOIN + at, half:HD, :] = lower.astype(jnp.bfloat16)
        return carry

    lax.fori_loop(0, blocks // JOIN, one_query, 0)
    for at in range(blocks):
        span = slice(at * small, (at + 1) * small)
        upper, lower = unturn(at, dkey_ref[:, span])
        raw_ref[at, HD : HD + half, :] = upper.astype(jnp.bfloat16)
        raw_ref[at, HD + half : 2 * HD, :] = lower.astype(jnp.bfloat16)
        raw_ref[at, 2 * HD :, :] = dvalue_ref[:, span].astype(jnp.bfloat16)
    copies[5].start()
    copies[5].wait()


def mix_out_kernel(core_ref, order_ref, mixed_ref, all_ref, send_ref, keep_ref, w_ref, sem_ref):
    last = all_ref.shape[1]
    finish(gathered_copies(order_ref, all_ref, last - mixed_ref.shape[1], last, w_ref, sem_ref))
    core = core_ref[0]
    send_ref[...] = mm(mixed_ref[1 - core], w_ref[...], TN).astype(jnp.bfloat16)
    keep_ref[...] = mm(mixed_ref[core], w_ref[...], TN)


def norm_two_kernel(core_ref, order_ref, x_ref, half_ref, far_ref, gains_ref, hidden_ref, norm_ref):
    core = core_ref[0]
    width = x_ref.shape[2] // 8
    for place in range(8):
        span = slice(place * width, (place + 1) * width)
        piece = x_ref[core, :, block_at(order_ref, place, width)].astype(jnp.float32)
        branch = half_ref[:, span].astype(jnp.float32) + far_ref[:, span].astype(jnp.float32)
        hidden_ref[:, span] = piece + branch
    hidden = hidden_ref[...]
    center = hidden - jnp.mean(hidden, axis=-1, keepdims=True)
    spread = lax.rsqrt(jnp.mean(center * center, axis=-1, keepdims=True) + EPS)
    norm_ref[...] = (center * spread * gains_ref[1:2, :]).astype(jnp.bfloat16)


def feed_kernel(
    order_ref, own_ref, other_ref, all_ref, down_ref, source_ref,
    send_ref, keep_ref, act_ref, dinp_ref, dgate_ref, result_send_out, result_keep_out, w_ref, grad_ref,
    result_send_ref, result_keep_ref, sem_ref
):
    units = w_ref.shape[0] // 3
    inp_w, gate_w, down_w = [w_ref.at[pl.ds(at * units, units), :] for at in range(3)]
    rows = own_ref.shape[0]
    inp_copies = gathered_copies(order_ref, all_ref, 0, units, inp_w, sem_ref)
    grad_copy = pltpu.make_async_copy(source_ref, grad_ref, sem_ref.at[24])
    grad_copy.start()
    gate_copies = gathered_copies(order_ref, all_ref, units, 2 * units, gate_w, sem_ref, 16)
    down_copies = gathered_copies(order_ref, down_ref, 0, units, down_w, sem_ref, 8)
    finish(inp_copies)
    for micro, norm_ref in ((1, other_ref), (0, own_ref)):
        span = slice(micro * rows, (micro + 1) * rows)
        inp = mm(norm_ref[...], inp_w[...], NT)
        if micro:
            finish(gate_copies)
        gate = mm(norm_ref[...], gate_w[...], NT)
        if micro:
            finish(down_copies + [grad_copy])
        dact = mm(grad_ref[micro], down_w[...], NT)
        cdf = 0.5 * (1.0 + lax.erf(inp * (0.5**0.5)))
        density = jnp.exp(-0.5 * inp * inp) * ((0.5 / jnp.pi) ** 0.5)
        gelu = inp * cdf
        act = (gelu * gate).astype(jnp.bfloat16)
        act_ref[span, :] = act
        dinp = (dact * gate * (cdf + inp * density)).astype(jnp.bfloat16)
        dgate = (dact * gelu).astype(jnp.bfloat16)
        dinp_ref[span, :] = dinp
        dgate_ref[span, :] = dgate
        result = mm(act, down_w[...], NN)
        if micro:
            result_send_ref[...] = result.astype(jnp.bfloat16)
            outgoing = [pltpu.make_async_copy(result_send_ref, result_send_out, sem_ref.at[25])]
        else:
            result_keep_ref[...] = result
            outgoing.append(pltpu.make_async_copy(result_keep_ref, result_keep_out, sem_ref.at[26]))
        outgoing[-1].start()
        part = mm(dinp, inp_w[...], NN) + mm(dgate, gate_w[...], NN)
        if micro:
            send_ref[...] = part.astype(jnp.bfloat16)
        else:
            keep_ref[...] = part
    finish(outgoing)


def weight_grad_kernel(
    order_ref, dinp_ref, dgate_ref, act_ref, own_ref, other_ref, source_ref, result_ref, grad_ref, out_ref, sem_ref
):
    units = act_ref.shape[1]
    rows = own_ref.shape[0]
    width = out_ref.shape[2]
    grad_copy = pltpu.make_async_copy(source_ref, grad_ref, sem_ref.at[3])
    grad_copy.start()
    copies = []
    for at, (left_ref, rights) in enumerate((
        (dinp_ref, (own_ref, other_ref)),
        (dgate_ref, (own_ref, other_ref)),
        (act_ref, (grad_ref.at[0], grad_ref.at[1])),
    )):
        if at == 2:
            grad_copy.wait()
        total = mm(left_ref[:rows, :], rights[0][...], TN) + mm(left_ref[rows:, :], rights[1][...], TN)
        for place in range(8):
            piece = total[:, place * width : (place + 1) * width].astype(jnp.bfloat16)
            out_ref[order_ref[place], at * units : (at + 1) * units, :] = piece
        span = pl.ds(at * units, units)
        copies.append(pltpu.make_async_copy(out_ref.at[:, span, :], result_ref.at[:, span, :], sem_ref.at[at]))
        copies[-1].start()
    finish(copies)


def near_sum_kernel(near_ref, far_ref, *low_refs):
    for at, low_ref in enumerate(low_refs):
        low_ref[...] = (near_ref[at + 1] + far_ref[at + 1].astype(jnp.float32)).astype(jnp.bfloat16)


def norm_two_back_kernel(
    half_ref, far_ref, hidden_in_ref, grad_in_ref, gains_in_ref, result_ref, low_ref,
    hidden_ref, grad_ref, gains_ref, dhidden_ref, sem_ref,
):
    pairs = ((hidden_in_ref, hidden_ref), (grad_in_ref.at[0], grad_ref), (gains_in_ref, gains_ref), (dhidden_ref, result_ref))
    copies = [pltpu.make_async_copy(one, two, sem_ref.at[at]) for at, (one, two) in enumerate(pairs)]
    for copy in copies[:3]:
        copy.start()
    copies[0].wait()
    hidden = hidden_ref[...]
    center = hidden - jnp.mean(hidden, axis=-1, keepdims=True)
    spread = lax.rsqrt(jnp.mean(center * center, axis=-1, keepdims=True) + EPS)
    xhat = center * spread
    dnorm = half_ref[...].astype(jnp.float32) + far_ref[...].astype(jnp.float32)
    finish(copies[1:3])
    scaled = dnorm * gains_ref[1:2, :]
    inner = scaled - jnp.mean(scaled, axis=-1, keepdims=True)
    inner = inner - xhat * jnp.mean(scaled * xhat, axis=-1, keepdims=True)
    total = grad_ref[...].astype(jnp.float32) + inner * spread
    dhidden_ref[...] = total
    copies[3].start()
    low_ref[...] = total.astype(jnp.bfloat16)
    copies[3].wait()


def mix_back_kernel(core_ref, own_ref, other_ref, w_ref, send_ref):
    cols = w_ref.shape[0]
    heads = cols // HD
    core = core_ref[0]
    for micro, low_ref in ((core, own_ref), (1 - core, other_ref)):
        total = mm(w_ref[...], low_ref[...], NT).astype(jnp.bfloat16)
        for head in range(heads):
            send_ref[micro * heads + head] = total[head * HD : (head + 1) * HD, :]


def mix_grad_kernel(core_ref, mixed_ref, own_ref, other_ref, far_ref, near_ref):
    core = core_ref[0]
    width = far_ref.shape[2]
    total = mm(mixed_ref[core], own_ref[...], NN) + mm(mixed_ref[1 - core], other_ref[...], NN)
    for place in range(4):
        near_ref[place] = total[:, place * width : (place + 1) * width]
        far_ref[place] = total[:, (4 + place) * width : (5 + place) * width].astype(jnp.bfloat16)


def project_back_kernel(
    core_ref, raw_in_ref, norm_in_ref, w_in_ref, far_ref, near_out_ref, send_ref, keep_ref,
    raw_ref, norm_ref, w_ref, near_ref, sem_ref,
):
    pairs = ((raw_in_ref, raw_ref), (norm_in_ref, norm_ref), (w_in_ref, w_ref), (near_ref, near_out_ref))
    copies = [pltpu.make_async_copy(one, two, sem_ref.at[at]) for at, (one, two) in enumerate(pairs)]
    for copy in copies[:3]:
        copy.start()
    finish(copies[:2])
    wide, width = far_ref.shape[1:]
    rows = raw_ref.shape[2]
    core = core_ref[0]
    total = mm(raw_ref[0], norm_ref[:rows, :], NN) + mm(raw_ref[1], norm_ref[rows:, :], NN)
    for place in range(4):
        near_ref[place] = total[:, place * width : (place + 1) * width]
        far_ref[place] = total[:, (4 + place) * width : (5 + place) * width].astype(jnp.bfloat16)
    copies[3].start()
    copies[2].wait()
    send_ref[...] = mm(raw_ref[1 - core], w_ref[:wide, :], TN).astype(jnp.bfloat16)
    keep_ref[...] = mm(raw_ref[core], w_ref[:wide, :], TN)
    copies[3].wait()


def norm_one_back_kernel(
    core_ref, order_ref, x_ref, half_ref, far_ref, dhidden_ref, gains_ref, grad_ref, xhat_ref
):
    core = core_ref[0]
    width = x_ref.shape[2] // 8
    x = x_ref[core].astype(jnp.float32)
    mean = jnp.mean(x, axis=-1, keepdims=True)
    center = x - mean
    spread = lax.rsqrt(jnp.mean(center * center, axis=-1, keepdims=True) + EPS)
    for place in range(8):
        span = slice(place * width, (place + 1) * width)
        piece = x_ref[core, :, block_at(order_ref, place, width)].astype(jnp.float32)
        xhat_ref[:, span] = (piece - mean) * spread
    xhat = xhat_ref[...]
    dnorm = half_ref[...].astype(jnp.float32) + far_ref[...].astype(jnp.float32)
    scaled = dnorm * gains_ref[0:1, :]
    inner = scaled - jnp.mean(scaled, axis=-1, keepdims=True)
    inner = inner - xhat * jnp.mean(scaled * xhat, axis=-1, keepdims=True)
    total = (dhidden_ref[...] + inner * spread).astype(jnp.bfloat16)
    for place in range(8):
        grad_ref[:, block_at(order_ref, place, width)] = total[:, place * width : (place + 1) * width]


def place_grad_kernel(core_ref, order_ref, local_ref, four_ref, grad_ref, natural_ref):
    rows = grad_ref.shape[1]
    width = grad_ref.shape[2] // 8
    core = core_ref[0]
    for at in range(2):
        micro = core if at == 0 else 1 - core
        place = lax.broadcasted_iota(jnp.int32, (rows, rows), 0)
        onehot = jnp.where(local_ref[pl.ds(micro, 1), :] == place, 1.0, 0.0).astype(jnp.bfloat16)
        natural_ref[...] = mm(onehot, four_ref[micro], NN).astype(jnp.bfloat16)
        for block in range(8):
            span = slice(block * width, (block + 1) * width)
            grad_ref[at, :, span] = natural_ref[:, block_at(order_ref, block, width)]


def result_kernel(order_ref, picks_ref, hidden_ref, half_ref, far_ref, packed_ref, natural_ref):
    rows = hidden_ref.shape[0]
    width = hidden_ref.shape[1] // 8
    branch = half_ref[...].astype(jnp.float32) + far_ref[...].astype(jnp.float32)
    total = (hidden_ref[...] + branch).astype(jnp.bfloat16)
    for block in range(8):
        natural_ref[:, block_at(order_ref, block, width)] = total[:, block * width : (block + 1) * width]
    count = packed_ref.shape[0]
    place = lax.broadcasted_iota(jnp.int32, (rows, count), 0)
    onehot = jnp.where(picks_ref[...] == place, 1.0, 0.0).astype(jnp.bfloat16)
    packed_ref[...] = mm(onehot, natural_ref[...], TN).astype(jnp.bfloat16)


def join_kernel(
    core_ref, side_ref, place_ref, own_ref, far_ref, near_ref, cross_ref, input_own_ref, input_other_ref,
    output_ref, input_ref,
):
    rows = output_ref.shape[1]
    count = own_ref.shape[0]
    halfway = count // 8
    core, side = core_ref[0], side_ref[0]
    row = lax.broadcasted_iota(jnp.int32, (count, rows), 0)
    row = (row // halfway) * (2 * halfway) + row % halfway
    for micro, pieces in ((core, (own_ref, far_ref)), (1 - core, (near_ref, cross_ref))):
        total = jnp.zeros((rows, output_ref.shape[2]), jnp.float32)
        for half, piece in ((side, pieces[0]), (1 - side, pieces[1])):
            wanted = place_ref[pl.ds(micro, 1), :] - half * halfway
            onehot = jnp.where(row == wanted, 1.0, 0.0).astype(jnp.bfloat16)
            total = total + mm(onehot, piece[...], TN)
        output_ref[micro] = total.astype(jnp.bfloat16)
    input_ref[core] = input_own_ref[...]
    input_ref[1 - core] = input_other_ref[...]


def positions(anchor, seq_lens):
    ends = running_ends(seq_lens)
    starts = ends - seq_lens
    inside = (anchor[:, None] >= starts[None, :]) & (anchor[:, None] < ends[None, :])
    return anchor - jnp.sum(jnp.where(inside, starts[None, :], 0), axis=1)


def turn_tables(place):
    freqs = jnp.power(THETA, -jnp.arange(HD // 2, dtype=jnp.float32) * 2.0 / HD)
    angle = freqs[:, None] * place.astype(jnp.float32)[None, :]
    return jnp.concatenate([jnp.cos(angle), jnp.sin(angle)], axis=0)


def paired_layer(
    tokens, cotangent, perm, lengths, w_qkv, w_attn_out, w_in, w_down, gain_one, gain_two
):
    f32, bf16, i32 = jnp.float32, jnp.bfloat16, jnp.int32
    mine = lax.axis_index("fsdp")
    part = lax.axis_index("tp")
    core, side = part & 1, part >> 1
    core_at = core.reshape(1).astype(i32)
    side_at = side.reshape(1).astype(i32)
    rows = tokens.shape[1]
    width = w_qkv.shape[0]
    full = 8 * width
    cols = w_qkv.shape[2]
    heads = cols // HD
    units = w_in.shape[2]
    per_pair = rows // 8
    order = jnp.bitwise_xor(jnp.array(ORDER, i32), mine)

    def pick(value, index):
        return lax.dynamic_index_in_dim(value, index, 0, keepdims=False)

    def add_half(keep, got):
        return (keep + got.astype(f32)).astype(bf16)

    def near_sum(near, far, name):
        shape = near.shape[1:]
        lows = local_call(near_sum_kernel, name, (), (near, far), [(shape, bf16)] * 3, far_in=(0, 1))
        return near[0] + far[0].astype(f32), lows

    def z_send(lows):
        return [hop(low, ORDER[at + 1]) for at, low in enumerate(lows)]

    def far_sum(own, got):
        return own + sum(one.astype(f32) for one in got)

    turned = jnp.transpose(w_qkv.reshape(width, 3, heads, HD), (2, 1, 3, 0)).reshape(3 * cols, width)
    gains_rows = jnp.concatenate([gain_one[None], gain_two[None], jnp.zeros((14, width), bf16)])
    first_same = z_phase(jnp.concatenate([turned, gains_rows], axis=0))
    first = first_same + y_phase(first_same)

    slots = perm.reshape(2, 8, rows)
    from_me = (slots // rows == mine).astype(f32)
    slot_no = jnp.arange(rows, dtype=i32)
    before = (slot_no[:, None] < slot_no[None, :]).astype(f32)
    rank_me = jnp.einsum("mds,st->mdt", from_me, before).astype(i32)
    ranks = jnp.arange(per_pair, dtype=i32)
    chosen = (from_me[..., None] > 0) & (rank_me[..., None] == ranks)
    local = jnp.sum(jnp.where(chosen, (slots % rows)[..., None], 0), axis=2)
    my_slots = lax.dynamic_index_in_dim(slots, mine, 1, keepdims=False)
    target = my_slots // rows
    same = (target[:, :, None] == target[:, None, :]) & (slot_no[:, None] < slot_no[None, :])[None]
    rank_own = jnp.sum(same.astype(i32), axis=1)
    place_own = target * per_pair + rank_own
    quarter = per_pair // 4
    wanted = order[:, None] * per_pair + part * quarter
    wanted = (wanted + jnp.arange(quarter, dtype=i32)[None, :]).reshape(-1)
    packer = (place_own[:, None, :] == wanted[None, :, None]).astype(bf16)
    packed = jnp.einsum("mps,msd->mpd", packer, cotangent, preferred_element_type=f32).astype(bf16)
    packed = packed.reshape(2, 8, quarter, full)
    packed = [packed[:, at] for at in range(8)]
    chosen = order[:, None] == jnp.arange(8, dtype=i32)[None, :]
    local_own = jnp.sum(jnp.where(chosen[None, :, :, None], local[:, None], 0), axis=2)
    anchor = mine * rows + jnp.arange(rows, dtype=i32)
    own_table = jnp.concatenate([turn_tables(positions(anchor, lengths[m])) for m in range(2)], axis=1)
    inp_turned, gate_turned = jnp.transpose(w_in[:, 0]), jnp.transpose(w_in[:, 1])
    second = jnp.concatenate([jnp.transpose(w_down), jnp.transpose(w_attn_out)], axis=0)
    second_all = lax.all_gather(second, "fsdp", axis=0, tiled=False)
    third_all = lax.all_gather(jnp.concatenate([inp_turned, gate_turned], axis=0), "fsdp", axis=0, tiled=False)
    halfway = per_pair // 2
    picks = lax.dynamic_slice_in_dim(pick(local, core), side * halfway, halfway, 1).reshape(1, -1)
    my_lens = lengths[mine // heads]
    all_anchor = jnp.arange(8 * rows, dtype=i32)
    table = turn_tables(positions(all_anchor, my_lens))
    table = jnp.transpose(table.reshape(HD, 8, rows), (1, 0, 2))
    first, packed, own_table, picks, place_own, side_at, table, local_own, order, core_at, core, side, my_lens = sync(
        (first, packed, own_table, picks, place_own, side_at, table, local_own, order, core_at, core, side, my_lens)
    )

    norm_one, gains, outgoing, qkv_w = local_call(
        project_kernel, "project", (order,), (tokens, own_table),
        [((2 * rows, full), bf16), ((2, full), f32), ((2 * heads, 3 * HD, rows), bf16), ((3 * cols + 16, full), bf16)],
        [((2 * rows, full), bf16), ((3 * cols + 16, full), bf16)], first, copies=10,
        far_in=(0, 1), far_out=(1, 2), far_shards=False, raw_out=(0, 3),
    )
    outgoing, packed = sync((outgoing, packed))
    qkv = deal_out(outgoing)
    arrived = [hop(one, ORDER[at]) if at else one for at, one in enumerate(packed)]
    qkv = sync((qkv,))[0]
    mixed_out, exact, logs = local_call(
        attend_kernel, "attend", (my_lens,), (qkv,),
        [((8, HD, rows), bf16), ((8, HD, rows), f32), ((8, 1, rows), f32)],
        [((8 * rows, HD), bf16)], far_in=(0,), far_out=(0, 1, 2),
    )
    mixed_out, arrived = sync((mixed_out, arrived))
    mixed = deal_out(mixed_out).reshape(2, cols, rows)
    arrived = jnp.stack(arrived)
    near = twin(arrived)
    pair = jnp.stack([jnp.where(core == 0, arrived, near), jnp.where(core == 0, near, arrived)])
    far = across(pair)
    mixed, far = sync((mixed, far))
    four = jnp.concatenate([jnp.where(side == 0, pair, far), jnp.where(side == 0, far, pair)])
    four = jnp.transpose(four, (2, 1, 0, 3, 4)).reshape(2, rows, full)
    grad = local_call(
        place_grad_kernel, "place_grad", (core_at, order), (local_own.reshape(2, rows), four),
        [((2, rows, full), bf16)], [((rows, full), bf16)],
    )

    send, keep, out_w = local_call(
        mix_out_kernel, "mix_out", (core_at, order), (mixed,),
        [((rows, full), bf16), ((rows, full), f32), ((cols, full), bf16)], (), (second_all,), far_in=(0,), far_out=(2,),
    )
    half = add_half(keep, twin(send))
    far = across(half)
    far, grad = sync((far, grad))
    hidden, two_own = local_call(
        norm_two_kernel, "norm_two", (core_at, order), (tokens, half, far, gains),
        [((rows, full), f32), ((rows, full), bf16)], far_in=(0, 3), far_out=(0,),
    )
    two_other = twin(two_own)

    send, keep, act, d_inp, d_gate, result_send, result_keep = local_call(
        feed_kernel, "feed", (order,), (two_own, two_other),
        [((rows, full), bf16), ((rows, full), f32)]
        + [((2 * rows, units), bf16)] * 3
        + [((rows, full), bf16), ((rows, full), f32)],
        [((3 * units, full), bf16), ((2, rows, full), bf16), ((rows, full), bf16), ((rows, full), f32)],
        (third_all, second_all, grad), copies=27, raw_out=(5, 6),
    )
    half_two = add_half(keep, twin(send))
    half_two, act, d_inp, d_gate = sync((half_two, act, d_inp, d_gate))
    far_two = across(half_two)
    feed_grad = local_call(
        weight_grad_kernel, "feed_grad", (order,), (d_inp, d_gate, act, two_own, two_other),
        [((8, 3 * units, width), bf16)], [((2, rows, full), bf16), ((8, 3 * units, width), bf16)], (grad,),
        copies=4, raw_out=(0,),
    )
    feed_sum = lax.psum_scatter(feed_grad, "fsdp", scatter_dimension=0, tiled=False)
    far_two, feed_grad = sync((far_two, feed_grad))
    d_hidden, low_own = local_call(
        norm_two_back_kernel, "norm_two_back", (), (half_two, far_two),
        [((rows, full), f32), ((rows, full), bf16)],
        [((rows, full), f32), ((rows, full), bf16), ((2, full), f32), ((rows, full), f32)],
        (hidden, grad, gains), copies=4, raw_out=(0,),
    )
    low_other = twin(low_own)
    d_mixed = local_call(
        mix_back_kernel, "mix_back", (core_at,), (low_own, low_other, out_w),
        [((8, HD, rows), bf16)], far_out=(0,),
    )
    d_mixed, low_own, low_other, result_send, result_keep = sync(
        (d_mixed, low_own, low_other, result_send, result_keep)
    )
    grad_mixed = deal_out(d_mixed)
    out_far, out_near = local_call(
        mix_grad_kernel, "mix_grad", (core_at,), (mixed, low_own, low_other),
        [((4, cols, width), bf16), ((4, cols, width), f32)], far_in=(0, 1, 2), far_out=(1,),
    )
    res_half = add_half(result_keep, twin(result_send))
    out_got = hop(out_far, 1)
    res_far = across(res_half)
    grad_mixed, out_got, res_far = sync((grad_mixed, out_got, res_far))

    d_raw_out = local_call(
        attend_back_kernel, "attend_back", (my_lens,), (),
        [((8, 3 * HD, rows), bf16)],
        [
            ((8, 3 * HD, rows), bf16), ((8, HD, rows), f32), ((8, 1, rows), f32), ((8, HD, rows), bf16),
            ((8, HD, rows), f32), ((8, 3 * HD, rows), bf16),
            ((8 * rows, 2 * HD), bf16), ((HD, 8 * rows), f32), ((HD, 8 * rows), f32),
        ],
        (qkv, exact, logs, grad_mixed, table), copies=6, raw_out=(0,),
    )
    d_raw_out, out_got, res_far = sync((d_raw_out, out_got, res_far))
    d_raw = deal_out(d_raw_out).reshape(2, 3 * cols, rows)
    out_own, out_lows = near_sum(out_near, out_got, "out_near")
    packed = local_call(
        result_kernel, "result", (order,), (picks, hidden, res_half, res_far),
        [((8 * halfway, full), bf16)], [((rows, full), bf16)], far_in=(1, 2, 3), far_out=(0,),
    )
    d_raw, out_lows, packed = sync((d_raw, out_lows, packed))

    qkv_far, qkv_near, send, keep = local_call(
        project_back_kernel, "project_back", (core_at,), (),
        [((4, 3 * cols, width), bf16), ((4, 3 * cols, width), f32), ((rows, full), bf16), ((rows, full), f32)],
        [
            ((2, 3 * cols, rows), bf16), ((2 * rows, full), bf16), ((3 * cols + 16, full), bf16),
            ((4, 3 * cols, width), f32),
        ],
        (d_raw, norm_one, qkv_w), copies=4, raw_out=(1,),
    )
    qkv_got = hop(qkv_far, 1)
    half = add_half(keep, twin(send))
    far = across(half)
    out_got = z_send(out_lows)
    arrived = deal_out(packed.reshape(8, halfway, full))
    input_own = local_call(
        norm_one_back_kernel, "norm_one_back", (core_at, order), (tokens, half, far, d_hidden, gains),
        [((rows, full), bf16)], [((rows, full), f32)], far_in=(0, 3, 4),
    )
    qkv_got, input_own, out_got = sync((qkv_got, input_own, out_got))
    qkv_own, qkv_lows = near_sum(qkv_near, qkv_got, "qkv_near")
    qkv_lows = sync(qkv_lows)
    qkv_got = z_send(qkv_lows)
    qkv_got[0], arrived, input_own, feed_sum = sync((qkv_got[0], arrived, input_own, feed_sum))
    input_other = twin(input_own)
    grad_attn_out = jnp.transpose(far_sum(out_own, out_got))
    inp_sum, gate_sum, down_sum = [feed_sum[at * units : (at + 1) * units].astype(f32) for at in range(3)]
    two_row = jnp.sum(inp_sum * inp_turned.astype(f32) + gate_sum * gate_turned.astype(f32), axis=0)
    grad_in = jnp.stack([jnp.transpose(inp_sum), jnp.transpose(gate_sum)], axis=1)
    grad_down = jnp.transpose(down_sum)
    arrived = arrived.reshape(8 * halfway, full)
    other_side = across(arrived)
    output, input_grad = local_call(
        join_kernel, "join", (core_at, side_at),
        (place_own, arrived, other_side, twin(arrived), twin(other_side), input_own, input_other),
        [((2, rows, full), bf16), ((2, rows, full), bf16)],
    )
    qkv_got, output, input_grad, grad_attn_out, grad_in, grad_down, two_row = sync(
        (qkv_got, output, input_grad, grad_attn_out, grad_in, grad_down, two_row)
    )
    qkv_sum = far_sum(qkv_own, qkv_got)
    one_row = jnp.sum(qkv_sum * turned.astype(f32), axis=0)
    gain_rows = jnp.stack([one_row / gain_one.astype(f32), two_row / gain_two.astype(f32)])
    beyond = lax.ppermute(gain_rows, "tp", [(i, i ^ 3) for i in range(4)])
    gain_rows = (gain_rows + twin(gain_rows)) + (across(gain_rows) + beyond)
    grad_gain_one, grad_gain_two = gain_rows[0], gain_rows[1]
    return (
        output,
        input_grad,
        jnp.transpose(qkv_sum.reshape(heads, 3, HD, width), (3, 1, 0, 2)).reshape(width, 3, cols),
        grad_attn_out,
        grad_in,
        grad_down,
        grad_gain_one,
        grad_gain_two,
    )


def on_device(*operands):
    micro_count, tok_rows = operands[0].shape[0], operands[0].shape[1]
    groups, parts = lax.axis_size("fsdp"), lax.axis_size("tp")
    heads = operands[4].shape[2] // HD
    if groups == 8 and parts == 4 and micro_count == 2 and micro_count * heads == groups and tok_rows % 256 == 0:
        return paired_layer(*operands)
    return general_layer(*operands)


def solution(mesh):
    placed = (
        P(None, "fsdp", None),
        P(None, "fsdp", None),
        P(),
        P(),
        P("fsdp", None, "tp"),
        P("fsdp", "tp"),
        P("fsdp", None, "tp"),
        P("fsdp", "tp"),
        P("fsdp"),
        P("fsdp"),
    )
    return jax.shard_map(
        on_device,
        mesh=mesh,
        in_specs=placed,
        out_specs=(
            P(None, "fsdp", None),
            P(None, "fsdp", None),
            P("fsdp", None, "tp"),
            P("fsdp", "tp"),
            P("fsdp", None, "tp"),
            P("fsdp", "tp"),
            P("fsdp"),
            P("fsdp"),
        ),
        check_vma=False,
    )
```
